32 devices in a mesh: rep: 4 (over x, core), fsdp: 8 (over z, y).
Axes of the slice: x: 2, y: 2, z: 4, core: 2. Of those that a mesh axis runs over, the one named last changes fastest.
Arguments:
- inputs: bfloat16 [32, 1024, 512], P(('rep', 'fsdp')), may hold values from -6 to 6
- memory: bfloat16 [32, 1024, 512], P(('rep', 'fsdp')), may hold values from -6 to 6
- memory_length: int32 [32], P(('rep', 'fsdp')), may hold values from 256 to 1024, as said below
- target_pos: int32 [32, 1024], P(('rep', 'fsdp')), may hold values from 0 to 1023, as said below
- cotangent: bfloat16 [32, 1024, 512], P(('rep', 'fsdp')), may hold values from -6 to 6
- attention_weights: float32 [8, 512, 512], P(None, 'fsdp'), as said below
- expand_weights: float32 [512, 2048], P('fsdp'), may hold values from -0.25 to 0.25
- shrink_weights: float32 [2048, 512], P('fsdp'), may hold values from -0.1875 to 0.1875
- expand_bias: float32 [2048], P('fsdp'), may hold values from -3 to 3
- layer_vectors: float32 [10, 512], P(None, 'fsdp'), as said below
- first_attention: float32 [8, 512, 512], P(None, 'fsdp'), may hold values from -112 to 112
- first_expand: float32 [512, 2048], P('fsdp'), may hold values from -112 to 112
- first_shrink: float32 [2048, 512], P('fsdp'), may hold values from -112 to 112
- first_bias: float32 [2048], P('fsdp'), may hold values from -112 to 112
- first_vectors: float32 [10, 512], P(None, 'fsdp'), may hold values from -112 to 112
- second_attention: float32 [8, 512, 512], P(None, 'fsdp'), may hold values from 65.536 to 1638.4
- second_expand: float32 [512, 2048], P('fsdp'), may hold values from 65.536 to 1638.4
- second_shrink: float32 [2048, 512], P('fsdp'), may hold values from 65.536 to 1638.4
- second_bias: float32 [2048], P('fsdp'), may hold values from 65.536 to 1638.4
- second_vectors: float32 [10, 512], P(None, 'fsdp'), may hold values from 65.536 to 1638.4
- hyper_rates: float32 [4], replicated, as said below
- step_count: int32 [], replicated, may hold values from 1 to 3
Outputs:
- outputs: bfloat16 [32, 1024, 512], P(('rep', 'fsdp'))
- input_grad: float32 [32, 1024, 512], P(('rep', 'fsdp'))
- memory_grad: float32 [32, 1024, 512], P(('rep', 'fsdp'))
- new_attention: float32 [8, 512, 512], P(None, 'fsdp')
- new_first_attention: float32 [8, 512, 512], P(None, 'fsdp')
- new_second_attention: float32 [8, 512, 512], P(None, 'fsdp')
- new_expand: float32 [512, 2048], P('fsdp')
- new_first_expand: float32 [512, 2048], P('fsdp')
- new_second_expand: float32 [512, 2048], P('fsdp')
- new_shrink: float32 [2048, 512], P('fsdp')
- new_first_shrink: float32 [2048, 512], P('fsdp')
- new_second_shrink: float32 [2048, 512], P('fsdp')
- new_bias: float32 [2048], P('fsdp')
- new_first_bias: float32 [2048], P('fsdp')
- new_second_bias: float32 [2048], P('fsdp')
- new_vectors: float32 [10, 512], P(None, 'fsdp')
- new_first_vectors: float32 [10, 512], P(None, 'fsdp')
- new_second_vectors: float32 [10, 512], P(None, 'fsdp')
The draws below stay inside these ranges and needn't reach their ends.
Inputs may be any that keep to these rules, and one draw needn't show every extreme that they name: `memory_length`: some row has all 1024 memory tokens and some row only 256. `target_pos`: rows pack documents: the position is 0 at a document's first token (always at a row's first token) and rises by one within it; some row is one document. `attention_weights`: entries of each matrix are independent and of mean zero. `layer_vectors`: gains and omegas are positive. `hyper_rates`: all four are positive, both decays under one.
All inputs are finite; a program needn't handle non-finite values.
Results may differ from the reference program's by a relative error of at most 0.019.
The reference program's roundings to bfloat16 on the way count: a program that leaves them out, or rounds other values in their place, can miss the bound.
Values may be sent and summed in bfloat16 or wider, within the bound.
No kernel may reach another device: no remote copies, remote signals or barrier semaphores. Data moves between devices by JAX's collectives and lax.ppermute only.
A program may use at most 192 MiB of HBM per device.

```python
import math
import jax
import jax.numpy as jnp
from jax import lax

D = 512
FF = 2048
HEADS = 8
HEAD_DIM = 64
SEQ = 1024
SRC = 1024
BATCH = 32


def draw_memory_length(key, part):
    lengths = jax.random.randint(key, (BATCH,), SRC // 4, SRC + 1)
    chosen = jax.random.randint(jax.random.fold_in(key, 3), (), 0, BATCH)
    row_index = jnp.arange(BATCH, dtype=jnp.int32)
    lengths = jnp.where(row_index == chosen, SRC, lengths)
    lengths = jnp.where(row_index == (chosen + 1) % BATCH, SRC // 4, lengths)
    return lengths.astype(jnp.int32)


def draw_target_pos(key, part):
    start_marks = jax.random.randint(key, (BATCH, SEQ), 0, max(SEQ // 2, 2))
    chosen = jax.random.randint(jax.random.fold_in(key, 7), (), 0, BATCH)
    position_index = jnp.arange(SEQ, dtype=jnp.int32)
    row_index = jnp.arange(BATCH, dtype=jnp.int32)
    begins = (start_marks == 0) | (position_index[None, :] == 0)
    begins = jnp.where(row_index[:, None] == chosen, position_index[None, :] == 0, begins)
    starts = lax.cummax(jnp.where(begins, position_index[None, :], 0), axis=1)
    return (position_index[None, :] - starts).astype(jnp.int32)


def draw_attention_weights(key, part):
    values = jax.random.uniform(key, (8, D, D), jnp.float32, -1.0, 1.0)
    slot_index = jnp.arange(8)[:, None, None]
    factor = jnp.where(slot_index % 4 == 3, (3.0 * 64.0 / D) ** 0.5, (3.0 / D) ** 0.5)
    return values * factor


def draw_layer_vectors(key, part):
    uniform_part = jax.random.uniform(key, (10, D), jnp.float32)
    row_index = jnp.arange(10)[:, None]
    gain_rows = 0.6 + 0.8 * uniform_part
    shifts = uniform_part - 0.5
    omegas = 0.7 + 1.3 * uniform_part
    return jnp.where(row_index < 3, gain_rows, jnp.where(row_index < 6, shifts, jnp.where(row_index < 9, omegas, shifts)))


def draw_hyper_rates(key, part):
    uniform_part = jax.random.uniform(key, (4,), jnp.float32)
    low_ends = jnp.array([0.0, 0.8, 0.95, 0.05], jnp.float32)
    spans = jnp.array([0.0, 0.1, 0.04, 0.15], jnp.float32)
    values = low_ends + spans * uniform_part
    learn_rate = 0.2 * jnp.exp(uniform_part[0] * 0.6931472)
    return jnp.concatenate([learn_rate[None], values[1:]])


def block_levels(rng, dims, pieces, least, largest):
    def one(position, blocks):
        draws = jax.random.uniform(jax.random.fold_in(jax.random.fold_in(rng, 6), position), (blocks,), jnp.float32, least / len(pieces), largest / len(pieces))
        return jnp.repeat(jnp.exp(draws), dims[position] // blocks).reshape((-1,) + (1,) * (len(dims) - position - 1))

    loudness = one(*pieces[0])
    for cut in pieces[1:]:
        loudness = loudness * one(*cut)
    return loudness


def scatter_about(key, extent, scale, bound, pieces=(), kind=jnp.bfloat16):
    values = scale * jax.random.normal(key, extent, jnp.float32)
    if pieces:
        values = values * block_levels(key, extent, pieces, -0.22, 0.18)
    return jnp.clip(values, -bound, bound).astype(kind)


def setup_inputs(seed: int = 0) -> dict:
    streams_of = jax.random.split(jax.random.key(seed), 23)
    inputs = scatter_about(streams_of[0], (BATCH, SEQ, D), 1.0, 6.0, ((0, 32),))
    memory = scatter_about(streams_of[1], (BATCH, SRC, D), 1.0, 6.0, ((0, 32),))
    memory_length = draw_memory_length(jax.random.fold_in(streams_of[22], 71), 0)
    target_pos = draw_target_pos(jax.random.fold_in(streams_of[22], 71), 0)
    cotangent = scatter_about(streams_of[4], (BATCH, SEQ, D), 1.0, 6.0, ((0, 32),))
    attention_weights = draw_attention_weights(jax.random.fold_in(streams_of[22], 71), 0)
    expand_weights = scatter_about(streams_of[6], (D, FF), D ** -0.5, 0.25, ((0, 8),), jnp.float32)
    shrink_weights = scatter_about(streams_of[7], (FF, D), (FF // 2) ** -0.5, 0.1875, ((0, 8),), jnp.float32)
    expand_bias = scatter_about(streams_of[8], (FF,), 0.5, 3.0, ((0, 8),), jnp.float32)
    layer_vectors = draw_layer_vectors(jax.random.fold_in(streams_of[22], 71), 0)
    first_attention = scatter_about(streams_of[10], (8, D, D), (0.1 * (BATCH * SEQ) ** 0.5), 112.0, ((1, 8),), jnp.float32)
    first_expand = scatter_about(streams_of[11], (D, FF), (0.1 * (BATCH * SEQ) ** 0.5), 112.0, ((0, 8),), jnp.float32)
    first_shrink = scatter_about(streams_of[12], (FF, D), (0.1 * (BATCH * SEQ) ** 0.5), 112.0, ((0, 8),), jnp.float32)
    first_bias = scatter_about(streams_of[13], (FF,), (0.1 * (BATCH * SEQ) ** 0.5), 112.0, ((0, 8),), jnp.float32)
    first_vectors = scatter_about(streams_of[14], (10, D), (0.1 * (BATCH * SEQ) ** 0.5), 112.0, ((1, 8),), jnp.float32)
    second_attention = jnp.clip(jnp.exp(math.log(1638.4) - 3.218876 * jax.random.uniform(streams_of[15], (8, D, D), jnp.float32) ** block_levels(streams_of[15], (8, D, D), ((1, 8),), -0.2, 0.2)), 65.536, 1638.4)
    second_expand = jnp.clip(jnp.exp(math.log(1638.4) - 3.218876 * jax.random.uniform(streams_of[16], (D, FF), jnp.float32) ** block_levels(streams_of[16], (D, FF), ((0, 8),), -0.2, 0.2)), 65.536, 1638.4)
    second_shrink = jnp.clip(jnp.exp(math.log(1638.4) - 3.218876 * jax.random.uniform(streams_of[17], (FF, D), jnp.float32) ** block_levels(streams_of[17], (FF, D), ((0, 8),), -0.2, 0.2)), 65.536, 1638.4)
    second_bias = jnp.clip(jnp.exp(math.log(1638.4) - 3.218876 * jax.random.uniform(streams_of[18], (FF,), jnp.float32) ** block_levels(streams_of[18], (FF,), ((0, 8),), -0.2, 0.2)), 65.536, 1638.4)
    second_vectors = jnp.clip(jnp.exp(math.log(1638.4) - 3.218876 * jax.random.uniform(streams_of[19], (10, D), jnp.float32) ** block_levels(streams_of[19], (10, D), ((1, 8),), -0.2, 0.2)), 65.536, 1638.4)
    hyper_rates = draw_hyper_rates(jax.random.fold_in(streams_of[22], 71), 0)
    step_count = jax.random.randint(streams_of[21], (), 1, 4).astype(jnp.int32)
    return {"inputs": inputs, "memory": memory, "memory_length": memory_length, "target_pos": target_pos, "cotangent": cotangent, "attention_weights": attention_weights, "expand_weights": expand_weights, "shrink_weights": shrink_weights, "expand_bias": expand_bias, "layer_vectors": layer_vectors, "first_attention": first_attention, "first_expand": first_expand, "first_shrink": first_shrink, "first_bias": first_bias, "first_vectors": first_vectors, "second_attention": second_attention, "second_expand": second_expand, "second_shrink": second_shrink, "second_bias": second_bias, "second_vectors": second_vectors, "hyper_rates": hyper_rates, "step_count": step_count}


@jax.custom_vjp
def low(v):
    return lax.optimization_barrier(v.astype(jnp.bfloat16)).astype(jnp.float32)

@jax.custom_vjp
def low_back(v):
    return v

def low_keep(v):
    return (low(v), None)

def low_pass(kept, grad):
    return (grad,)

def back_keep(v):
    return (v, None)

def back_low(kept, grad):
    return (low(grad),)
low.defvjp(low_keep, low_pass)
low_back.defvjp(back_keep, back_low)

def matmul(left_side, right_side):
    return jnp.dot(left_side, right_side, precision=lax.Precision.HIGHEST)

def smooth_gate(values):
    inner = 0.7978845608028654 * (values + 0.044715 * values * values * values)
    return 0.5 * values * (1.0 + jnp.tanh(inner))

def normalize(summed, gain_row, shift_row):
    center = lax.optimization_barrier(jnp.mean(summed, axis=-1, keepdims=True))
    shifted = summed - center
    spread = lax.optimization_barrier(jnp.mean(shifted * shifted, axis=-1, keepdims=True))
    return shifted * lax.rsqrt(spread + 1e-05) * gain_row + shift_row

def project(source, weight):
    return low_back(low(matmul(source, weight)))

def attend(query_rows, key_rows, value_rows, visible):
    length = query_rows.shape[0]
    query_heads = query_rows.reshape(length, HEADS, HEAD_DIM)
    key_heads = key_rows.reshape(key_rows.shape[0], HEADS, HEAD_DIM)
    value_heads = value_rows.reshape(value_rows.shape[0], HEADS, HEAD_DIM)
    scores = jnp.einsum('qhe,khe->hqk', query_heads, key_heads, precision=lax.Precision.HIGHEST)
    scores = low_back(scores * HEAD_DIM ** (-0.5))
    scores = jnp.where(visible[None], scores, -1000000000.0)
    shifted = scores - lax.optimization_barrier(jnp.max(scores, axis=-1, keepdims=True))
    exponent = jnp.exp(shifted)
    attn_probs = low(exponent / lax.optimization_barrier(jnp.sum(exponent, axis=-1, keepdims=True)))
    mixed_heads = jnp.einsum('hqk,khe->qhe', attn_probs, value_heads, precision=lax.Precision.HIGHEST)
    return low_back(low(mixed_heads.reshape(length, HEADS * HEAD_DIM)))

def decoder_layer(params, given_inputs, source, self_mask, cross_mask):
    attention, expand, shrink, inner_bias, vectors = jax.tree.map(low, params)
    gain_rows = vectors[0:3]
    shift_rows = vectors[3:6]
    omegas = vectors[6:9]
    out_bias = vectors[9]
    query_rows = project(given_inputs, attention[0])
    key_rows = project(given_inputs, attention[1])
    value_rows = project(given_inputs, attention[2])
    branch = low_back(matmul(attend(query_rows, key_rows, value_rows, self_mask), attention[3]))
    first_out = normalize(given_inputs * omegas[0] + branch, gain_rows[0], shift_rows[0])
    cross_query = project(low(first_out), attention[4])
    cross_keys = project(source, attention[5])
    cross_values = project(source, attention[6])
    branch = low_back(matmul(attend(cross_query, cross_keys, cross_values, cross_mask), attention[7]))
    second_out = normalize(first_out * omegas[1] + branch, gain_rows[1], shift_rows[1])
    before = low_back(matmul(low(second_out), expand) + inner_bias)
    hidden = low(smooth_gate(before))
    branch = low_back(matmul(hidden, shrink) + out_bias)
    return normalize(second_out * omegas[2] + branch, gain_rows[2], shift_rows[2])

def adam_update(weight, gradient, moment_one, moment_two, settings, step_float, factor):
    learn_rate = settings[0]
    beta_one = settings[1]
    beta_two = settings[2]
    decay_rate = settings[3]
    first_new = beta_one * moment_one + (1.0 - beta_one) * gradient
    second_new = beta_two * moment_two + (1.0 - beta_two) * gradient * gradient
    first_hat = first_new / (1.0 - beta_one ** step_float)
    second_hat = second_new / (1.0 - beta_two ** step_float)
    change = first_hat / (jnp.sqrt(second_hat) + 1e-08) + factor * decay_rate * weight
    return (weight - learn_rate * change, first_new, second_new)

def reference(inputs, memory, memory_length, target_pos, cotangent, attention_weights, expand_weights, shrink_weights, expand_bias, layer_vectors, first_attention, first_expand, first_shrink, first_bias, first_vectors, second_attention, second_expand, second_shrink, second_bias, second_vectors, hyper_rates, step_count):
    params = (attention_weights, expand_weights, shrink_weights, expand_bias, layer_vectors)
    position_index = jnp.arange(SEQ, dtype=jnp.int32)
    memory_index = jnp.arange(SRC, dtype=jnp.int32)

    def per_row(totals, row_data):
        row_inputs, row_memory, row_length, row_pos, row_cot = row_data
        self_mask = (position_index[None, :] <= position_index[:, None]) & (position_index[None, :] >= (position_index - row_pos)[:, None])
        cross_mask = jnp.broadcast_to(memory_index[None, :] < row_length, (SEQ, SRC))

        def row_layer(weights, given_inputs, source):
            return decoder_layer(weights, given_inputs, source, self_mask, cross_mask)
        result, pullback = jax.vjp(row_layer, params, row_inputs.astype(jnp.float32), row_memory.astype(jnp.float32))
        param_grads, row_input_grad, row_memory_grad = pullback(row_cot.astype(jnp.float32))
        totals = jax.tree.map(jnp.add, totals, param_grads)
        return (totals, (result.astype(jnp.bfloat16), row_input_grad, row_memory_grad))
    start_totals = jax.tree.map(jnp.zeros_like, params)
    grad_total, (outputs, input_grad, memory_grad) = lax.scan(per_row, start_totals, (inputs, memory, memory_length, target_pos, cotangent))
    step_float = step_count.astype(jnp.float32)
    new_attention, new_first_attention, new_second_attention = adam_update(attention_weights, grad_total[0], first_attention, second_attention, hyper_rates, step_float, 1.0)
    new_expand, new_first_expand, new_second_expand = adam_update(expand_weights, grad_total[1], first_expand, second_expand, hyper_rates, step_float, 1.0)
    new_shrink, new_first_shrink, new_second_shrink = adam_update(shrink_weights, grad_total[2], first_shrink, second_shrink, hyper_rates, step_float, 1.0)
    new_bias, new_first_bias, new_second_bias = adam_update(expand_bias, grad_total[3], first_bias, second_bias, hyper_rates, step_float, 0.0)
    new_vectors, new_first_vectors, new_second_vectors = adam_update(layer_vectors, grad_total[4], first_vectors, second_vectors, hyper_rates, step_float, 0.0)
    return (outputs, input_grad, memory_grad, new_attention, new_first_attention, new_second_attention, new_expand, new_first_expand, new_second_expand, new_shrink, new_first_shrink, new_second_shrink, new_bias, new_first_bias, new_second_bias, new_vectors, new_first_vectors, new_second_vectors)
```

```python
import functools

import jax
import jax.numpy as jnp
from jax import lax
from jax.experimental import pallas as pl
from jax.experimental.pallas import tpu as pltpu
from jax.sharding import PartitionSpec as P

BF = jnp.bfloat16
F32 = jnp.float32
HEAD_DIM = 64
PAIR = 128
TILE = 256
MIB = 1 << 20


def dot(left, right, left_dim, right_dim):
    return lax.dot_general(
        left, right, (((left_dim,), (right_dim,)), ((), ())), preferred_element_type=F32
    )


def lanes(size):
    return lax.broadcasted_iota(jnp.int32, (1, size), 1)


def half_masks():
    first = jnp.where(lanes(PAIR) < HEAD_DIM, 1.0, 0.0)
    return first.astype(BF), (1.0 - first).astype(BF)


def rows_at(index, size=TILE):
    return pl.ds(pl.multiple_of(index * size, size), size)


def split_three(column):
    high = column.astype(BF).astype(F32)
    rest = column - high
    middle = rest.astype(BF).astype(F32)
    return high, middle, rest - middle


def with_column(block, column, base, last):
    high, middle, low = split_three(column)
    lane = lanes(PAIR)
    tail = jnp.where(lane == base + 3, last, block)
    return jnp.where(
        lane == base, -high, jnp.where(lane == base + 1, -middle, jnp.where(lane == base + 2, -low, tail))
    ).astype(BF)


def weight(gathered, index, width):
    return gathered[:, index * width : (index + 1) * width, :].reshape(-1, gathered.shape[2])


def key_extra(length_limit, count):
    lane = lanes(PAIR) % HEAD_DIM
    extra = jnp.where(lane < 3, 1.0, 0.0)
    if length_limit is None:
        return jnp.broadcast_to(extra, (count, PAIR)).astype(BF)
    row = lax.broadcasted_iota(jnp.int32, (count, PAIR), 0)
    bias = jnp.where(row < length_limit, 0.0, -1e30)
    return jnp.where(lane == 3, bias, extra).astype(BF)


def visible(start, first_query, first_key, count):
    key = first_key + lax.broadcasted_iota(jnp.int32, (TILE, count), 1)
    seen = key >= start
    if first_key == first_query:
        query = first_query + lax.broadcasted_iota(jnp.int32, (TILE, count), 0)
        seen = seen & (key <= query)
    return seen


def key_spans(tile, count, causal):
    if not causal:
        return [(0, count)]
    spans = [(0, tile * TILE)] if tile else []
    return spans + [(tile * TILE, TILE)]


def attend(q_ref, k_ref, v_ref, extra_ref, start_ref, qa_ref, o_ref):
    length, count = q_ref.shape[0], k_ref.shape[0]
    causal = start_ref is not None
    masks = half_masks()

    @pl.loop(0, q_ref.shape[1] // PAIR)
    def _(pair):
        cols = rows_at(pair, PAIR)
        for tile in range(length // TILE):
            rows = slice(tile * TILE, (tile + 1) * TILE)
            spans = key_spans(tile, count, causal)
            results = []
            for side in (0, 1):
                base = HEAD_DIM * (1 - side)
                lane = lanes(PAIR)
                queries = q_ref[rows, cols] * masks[side]
                queries_f = queries.astype(F32)
                if not causal:
                    queries = jnp.where(lane == base + 3, 1.0, queries_f).astype(BF)
                score_blocks = []
                for first, size in spans:
                    keys = k_ref[first : first + size, cols] * masks[side]
                    if not causal:
                        keys = keys + extra_ref[first : first + size, :] * masks[1 - side]
                    scores = dot(queries, keys, 1, 1)
                    if causal:
                        seen = visible(start_ref[rows, :], tile * TILE, first, size)
                        scores = jnp.where(seen, scores, -1000000000.0)
                    score_blocks.append(scores)
                top = functools.reduce(
                    jnp.maximum, [jnp.max(scores, axis=1, keepdims=True) for scores in score_blocks]
                )
                total = None
                for scores, (first, size) in zip(score_blocks, spans):
                    values = v_ref[first : first + size, cols] * masks[side] + masks[1 - side]
                    probs = jnp.exp(scores - top).astype(BF)
                    part = dot(probs, values, 1, 0)
                    total = part if total is None else total + part
                results.append(total / pltpu.roll(total, HEAD_DIM, 1))
                log_total = top + jnp.log(total[:, base : base + 1])
                qa_ref[rows, pl.ds(pl.multiple_of(pair * 2 * PAIR, PAIR) + side * PAIR, PAIR)] = with_column(
                    queries_f, log_total, base, 0.0 if causal else 1.0
                )
            o_ref[rows, cols] = jnp.where(lanes(PAIR) < HEAD_DIM, results[0], results[1]).astype(BF)


def attend_back(qa_ref, da_ref, k_ref, v_ref, extra_ref, start_ref, dq_ref, dk_ref, dv_ref, dk_sum, dv_sum):
    length, count = qa_ref.shape[0], k_ref.shape[0]
    causal = start_ref is not None
    masks = half_masks()

    @pl.loop(0, k_ref.shape[1] // PAIR)
    def _(pair):
        cols = rows_at(pair, PAIR)
        for tile in reversed(range(length // TILE)):
            rows = slice(tile * TILE, (tile + 1) * TILE)
            query_grads = []
            for side in (0, 1):
                head_cols = pl.ds(pl.multiple_of(pair * 2 * PAIR, PAIR) + side * PAIR, PAIR)
                queries = qa_ref[rows, head_cols]
                grads = da_ref[rows, head_cols]
                query_grad = None
                for first, size in key_spans(tile, count, causal):
                    span = slice(first, first + size)
                    keys = k_ref[span, cols]
                    keys_low = keys * masks[side] + extra_ref[span, :] * masks[1 - side]
                    values = v_ref[span, cols] * masks[side] + masks[1 - side]
                    probs = jnp.exp(dot(queries, keys_low, 1, 1))
                    if causal:
                        seen = visible(start_ref[rows, :], tile * TILE, first, size)
                        probs = jnp.where(seen, probs, 0.0)
                    grad_scores = (probs * dot(grads, values, 1, 1)).astype(BF)
                    value_part = dot(grads, probs.astype(BF), 0, 0)
                    key_part = dot(queries, grad_scores, 0, 0)
                    if tile == length // TILE - 1:
                        dv_sum[side, :, span] = value_part
                        dk_sum[side, :, span] = key_part
                    else:
                        dv_sum[side, :, span] += value_part
                        dk_sum[side, :, span] += key_part
                    part = dot(grad_scores, keys, 1, 0)
                    query_grad = part if query_grad is None else query_grad + part
                query_grads.append(query_grad)
            dq_ref[rows, cols] = (
                jnp.where(lanes(PAIR) < HEAD_DIM, query_grads[0], query_grads[1]) * HEAD_DIM**-0.5
            ).astype(BF)
        for sums, out in ((dk_sum, dk_ref), (dv_sum, dv_ref)):
            joined = jnp.concatenate([sums[0, :HEAD_DIM, :], sums[1, HEAD_DIM:, :]], axis=0)
            out[:, cols] = joined.astype(BF).T


def norm_rows(summed):
    center = jnp.mean(summed, axis=1, keepdims=True)
    shifted = summed - center
    inverse = lax.rsqrt(jnp.mean(shifted * shifted, axis=1, keepdims=True) + 1e-05)
    return shifted * inverse, inverse


def norm_back(grad_out, normed, inverse, gain):
    scaled = grad_out * gain
    first = jnp.mean(scaled, axis=1, keepdims=True)
    second = jnp.mean(scaled * normed, axis=1, keepdims=True)
    return inverse * (scaled - first - normed * second)


def add_rows(ref, row, values):
    ref[row : row + 1, :] += jnp.sum(values, axis=0, keepdims=True)


def place_of(place_ref):
    rep, place = place_ref[0], place_ref[1]
    return lax.rem(rep, 2), lax.div(rep, 2), lax.div(place, 2), lax.rem(place, 2)


def assemble(place_ref, chunk_ref, all_ref):
    core, chip, line, row = place_of(place_ref)
    width = all_ref.shape[1]
    quarter = chunk_ref.shape[4]
    shard = quarter * 4 // 3
    for core_step in (0, 1):
        for chip_step in (0, 1):
            rep = jnp.bitwise_xor(chip, chip_step) * 2 + jnp.bitwise_xor(core, core_step)
            for line_step in range(4):
                for row_step in (0, 1):
                    owner = lax.rem(line - line_step + 4, 4) * 2 + jnp.bitwise_xor(row, row_step)
                    for piece in range(quarter // 16):
                        stacked = rep * quarter + piece * 16
                        matrix = lax.div(stacked, shard)
                        target = matrix * width + owner * shard + (stacked - matrix * shard)
                        all_ref[pl.ds(pl.multiple_of(target, 16), 16), :] = chunk_ref[
                            core_step, chip_step, line_step, row_step, piece * 16 : (piece + 1) * 16, :
                        ]


def self_forward_kernel(staged, *refs):
    if staged:
        place_ref, x_ref, start_ref, chunk_ref, qa_ref, k_ref, v_ref, o_ref, all_ref, q_ref = refs
        assemble(place_ref, chunk_ref, all_ref)
    else:
        x_ref, start_ref, all_ref, qa_ref, k_ref, v_ref, o_ref, q_ref = refs
    length, width = x_ref.shape

    @pl.loop(0, length // TILE)
    def _(tile):
        rows = rows_at(tile)
        source = x_ref[rows, :]
        queries = dot(source, all_ref[:width, :], 1, 0).astype(BF)
        q_ref[rows, :] = queries * jnp.asarray(HEAD_DIM**-0.5, BF)
        k_ref[rows, :] = dot(source, all_ref[width : 2 * width, :], 1, 0).astype(BF)
        v_ref[rows, :] = dot(source, all_ref[2 * width :, :], 1, 0).astype(BF)

    attend(q_ref, k_ref, v_ref, None, start_ref, qa_ref, o_ref)


def cross_forward_kernel(shard, *refs):
    (x_ref, mixed_ref, source_ref, length_ref, vec_ref, w_ref) = refs[:6]
    first_ref, first_inv_ref, qa_ref, k_ref, v_ref, o_ref, n_ref, inv_ref, q_ref, extra_ref = refs[6:]
    length = q_ref.shape[0]
    extra_ref[...] = key_extra(length_ref[0], k_ref.shape[0])

    @pl.loop(0, length // TILE)
    def _(tile):
        rows = rows_at(tile)
        summed = x_ref[rows, :].astype(F32) * vec_ref[6:7, :] + dot(
            mixed_ref[rows, :], weight(w_ref, 0, shard), 1, 0
        )
        normed, inverse = norm_rows(summed)
        first_ref[rows, :] = normed
        first_inv_ref[rows, :] = inverse
        low = (normed * vec_ref[0:1, :] + vec_ref[3:4, :]).astype(BF)
        queries = dot(low, weight(w_ref, 1, shard), 1, 0).astype(BF)
        q_ref[rows, :] = queries * jnp.asarray(HEAD_DIM**-0.5, BF)

    @pl.loop(0, source_ref.shape[0] // TILE)
    def _(tile):
        rows = rows_at(tile)
        source = source_ref[rows, :]
        k_ref[rows, :] = dot(source, weight(w_ref, 2, shard), 1, 0).astype(BF)
        v_ref[rows, :] = dot(source, weight(w_ref, 3, shard), 1, 0).astype(BF)

    attend(q_ref, k_ref, v_ref, extra_ref, None, qa_ref, o_ref)

    @pl.loop(0, length // TILE)
    def _(tile):
        rows = rows_at(tile)
        first_out = first_ref[rows, :] * vec_ref[0:1, :] + vec_ref[3:4, :]
        summed = first_out * vec_ref[7:8, :] + dot(o_ref[rows, :], weight(w_ref, 4, shard), 1, 0)
        normed, inverse = norm_rows(summed)
        n_ref[rows, :] = normed
        inv_ref[rows, :] = inverse


def hidden_kernel(shard, blocks, staged, *refs):
    place_ref = refs[0] if staged else None
    refs = refs[1:] if staged else refs
    (
        n_ref, inv_ref, cot_ref, vec_ref, bias_ref, w_ref,
        out_ref, dz_ref, grad_ref, sums_ref, bias_sum_ref,
        low_ref, h_ref, du_ref, df_ref, slope_ref,
    ) = refs
    length, width = n_ref.shape
    sums_ref[...] = jnp.zeros_like(sums_ref)
    bias_sum_ref[...] = jnp.zeros_like(bias_sum_ref)
    shrink_base = blocks * shard
    shrink_rows = width // w_ref.shape[0] * blocks

    def expand(block):
        return weight(w_ref, block, shard)

    def shrink_all():
        return w_ref[:, shrink_base : shrink_base + shrink_rows, :].reshape(blocks * width, width)

    @pl.loop(0, length // TILE)
    def _(tile):
        rows = rows_at(tile)
        gain, shift = vec_ref[1:2, :], vec_ref[4:5, :]
        second_out = n_ref[rows, :] * gain + shift
        low = second_out.astype(BF)
        low_ref[rows, :] = low
        summed = second_out * vec_ref[8:9, :] + vec_ref[9:10, :]
        shrink = shrink_all()
        for block in range(blocks):
            cols = slice(block * width, (block + 1) * width)
            before = dot(low, expand(block), 1, 0) + bias_ref[:, cols]
            square = before * before
            tangent = jnp.tanh(0.7978845608028654 * (before + 0.044715 * before * square))
            half = 0.5 * (1.0 + tangent)
            slope_ref[:, cols] = half + 0.5 * before * (1.0 - tangent * tangent) * 0.7978845608028654 * (
                1.0 + 3.0 * 0.044715 * square
            )
            hidden = (before * half).astype(BF)
            h_ref[rows, cols] = hidden
            summed = summed + dot(hidden, shrink[cols, :], 1, 0)
        normed, inverse = norm_rows(summed)
        out_ref[rows, :] = (normed * vec_ref[2:3, :] + vec_ref[5:6, :]).astype(BF)
        grad_out = cot_ref[rows, :].astype(F32)
        third = norm_back(grad_out, normed, inverse, vec_ref[2:3, :])
        add_rows(sums_ref, 2, grad_out * normed)
        add_rows(sums_ref, 5, grad_out)
        branch = third.astype(BF)
        df_ref[rows, :] = branch
        add_rows(sums_ref, 9, branch.astype(F32))
        add_rows(sums_ref, 8, second_out * third)
        grad_second = vec_ref[8:9, :] * third
        for block in range(blocks):
            cols = slice(block * width, (block + 1) * width)
            du = (dot(branch, shrink[cols, :], 1, 1) * slope_ref[:, cols]).astype(BF)
            du_ref[rows, cols] = du
            bias_sum_ref[:, cols] += jnp.sum(du.astype(F32), axis=0, keepdims=True)
            grad_second = grad_second + dot(du, expand(block), 1, 1)
        normed_two = n_ref[rows, :]
        dz_ref[rows, :] = norm_back(grad_second, normed_two, inv_ref[rows, :], gain)
        add_rows(sums_ref, 1, grad_second * normed_two)
        add_rows(sums_ref, 4, grad_second)

    devices = w_ref.shape[0]
    for block in range(blocks):
        cols = slice(block * width, (block + 1) * width)
        put_grad(grad_ref, place_ref, block, low_ref[...], du_ref[:, cols])
        grad_shrink = dot(h_ref[:, cols], df_ref[...], 0, 0).astype(grad_ref.dtype)
        if staged:
            core = place_of(place_ref)[0]
            part, half = devices // blocks, shard // 2
            owners = slice(block * part, (block + 1) * part)
            parts = grad_shrink.reshape(part, blocks, 2, half, width)
            for side in (0, 1):
                for piece in range(blocks):
                    first = (blocks + piece) * half
                    grad_ref[jnp.bitwise_xor(core, side), owners, first : first + half, :] = parts[:, piece, side]
        elif devices % blocks == 0:
            part = devices // blocks
            grad_ref[block * part : (block + 1) * part, shrink_base:, :] = grad_shrink.reshape(
                part, shrink_rows, width
            )
        else:
            first = shrink_base + block * width
            grad_ref[0, first : first + width, :] = grad_shrink


def branch_grads(branch, mixed_weight, o_rows, da_ref, rows):
    masks = half_masks()
    mixed_grad = dot(branch, mixed_weight, 1, 1).astype(BF)
    for pair in range(mixed_grad.shape[1] // PAIR):
        cols = slice(pair * PAIR, (pair + 1) * PAIR)
        grad_pair = mixed_grad[:, cols].astype(F32)
        product = grad_pair * o_rows[:, cols].astype(F32)
        for side in (0, 1):
            mask = masks[side].astype(F32)
            inner = jnp.sum(product * mask, axis=1, keepdims=True)
            first = (2 * pair + side) * PAIR
            da_ref[rows, first : first + PAIR] = with_column(
                grad_pair * mask, inner, HEAD_DIM * (1 - side), 0.0
            )


def put_grad(grad_ref, place_ref, index, left, right):
    grad = dot(left, right, 0, 0).astype(grad_ref.dtype)
    if place_ref is None:
        devices = grad_ref.shape[0]
        shard = grad.shape[0] // devices
        grad_ref[:, index * shard : (index + 1) * shard, :] = grad.reshape(devices, shard, -1)
        return
    core = place_of(place_ref)[0]
    devices = grad_ref.shape[1]
    half = grad.shape[0] // devices // 2
    parts = grad.reshape(devices, 2, half, grad.shape[1])
    for side in (0, 1):
        grad_ref[jnp.bitwise_xor(core, side), :, index * half : (index + 1) * half, :] = parts[:, side]


def cross_backward_kernel(shard, staged, *refs):
    place_ref = refs[0] if staged else None
    refs = refs[1:] if staged else refs
    (dz_ref, x_ref, first_ref, inv_ref, source_ref, length_ref, vec_ref, w_ref) = refs[:8]
    (qa_ref, k_ref, v_ref, o_ref, self_o_ref, grad_ref, dfirst_ref, dsource_ref, sums_ref) = refs[8:17]
    low_ref, da_ref, dq_ref, dk_ref, dv_ref, dk_sum, dv_sum, branch_ref, extra_ref = refs[17:]
    length = dz_ref.shape[0]
    sums_ref[...] = jnp.zeros_like(sums_ref)
    extra_ref[...] = key_extra(length_ref[0], k_ref.shape[0])

    @pl.loop(0, length // TILE)
    def _(tile):
        rows = rows_at(tile)
        grad = dz_ref[rows, :]
        branch = grad.astype(BF)
        branch_ref[rows, :] = branch
        first_out = first_ref[rows, :] * vec_ref[0:1, :] + vec_ref[3:4, :]
        low_ref[rows, :] = first_out.astype(BF)
        add_rows(sums_ref, 7, first_out * grad)
        branch_grads(branch, weight(w_ref, 4, shard), o_ref[rows, :], da_ref, rows)

    attend_back(qa_ref, da_ref, k_ref, v_ref, extra_ref, None, dq_ref, dk_ref, dv_ref, dk_sum, dv_sum)

    put_grad(grad_ref, place_ref, 1, low_ref[...], dq_ref[...])
    put_grad(grad_ref, place_ref, 2, source_ref[...], dk_ref[...])
    put_grad(grad_ref, place_ref, 3, source_ref[...], dv_ref[...])
    put_grad(grad_ref, place_ref, 4, o_ref[...], branch_ref[...])

    @pl.loop(0, length // TILE)
    def _(tile):
        rows = rows_at(tile)
        dx = dot(dq_ref[rows, :], weight(w_ref, 1, shard), 1, 1) + vec_ref[7:8, :] * dz_ref[rows, :]
        normed = first_ref[rows, :]
        dfirst = norm_back(dx, normed, inv_ref[rows, :], vec_ref[0:1, :])
        dfirst_ref[rows, :] = dfirst
        add_rows(sums_ref, 0, dx * normed)
        add_rows(sums_ref, 3, dx)
        add_rows(sums_ref, 6, x_ref[rows, :].astype(F32) * dfirst)
        branch_ref[rows, :] = dfirst.astype(BF)

    @pl.loop(0, source_ref.shape[0] // TILE)
    def _(tile):
        rows = rows_at(tile)
        dsource_ref[rows, :] = dot(dk_ref[rows, :], weight(w_ref, 2, shard), 1, 1) + dot(
            dv_ref[rows, :], weight(w_ref, 3, shard), 1, 1
        )

    put_grad(grad_ref, place_ref, 0, self_o_ref[...], branch_ref[...])


def self_backward_kernel(shard, staged, *refs):
    place_ref = refs[0] if staged else None
    refs = refs[1:] if staged else refs
    (dz_ref, x_ref, start_ref, vec_ref, w_ref, all_ref, qa_ref, k_ref, v_ref, o_ref, grad_ref, dx_ref) = refs[:12]
    da_ref, dq_ref, dk_ref, dv_ref, dk_sum, dv_sum, extra_ref = refs[12:]
    length, width = dz_ref.shape
    extra_ref[...] = key_extra(None, k_ref.shape[0])

    @pl.loop(0, length // TILE)
    def _(tile):
        rows = rows_at(tile)
        branch_grads(dz_ref[rows, :].astype(BF), weight(w_ref, 0, shard), o_ref[rows, :], da_ref, rows)

    attend_back(qa_ref, da_ref, k_ref, v_ref, extra_ref, start_ref, dq_ref, dk_ref, dv_ref, dk_sum, dv_sum)

    for index, grads in enumerate((dq_ref, dk_ref, dv_ref)):
        put_grad(grad_ref, place_ref, index, x_ref[...], grads[...])

    @pl.loop(0, length // TILE)
    def _(tile):
        rows = rows_at(tile)
        dx = vec_ref[6:7, :] * dz_ref[rows, :]
        for index, grads in enumerate((dq_ref, dk_ref, dv_ref)):
            dx = dx + dot(grads[rows, :], all_ref[index * width : (index + 1) * width, :], 1, 1)
        dx_ref[rows, :] = dx


def call(kernel, args, outs, scratch, limit, flops, smem=()):
    in_specs = [
        pl.BlockSpec(memory_space=pltpu.SMEM if i in smem else pltpu.VMEM) for i in range(len(args))
    ]
    return pl.pallas_call(
        kernel,
        out_shape=[jax.ShapeDtypeStruct(shape, kind) for shape, kind in outs],
        in_specs=in_specs,
        out_specs=[pl.BlockSpec(memory_space=pltpu.VMEM)] * len(outs),
        scratch_shapes=[pltpu.VMEM(shape, kind) for shape, kind in scratch],
        compiler_params=pltpu.CompilerParams(vmem_limit_bytes=limit * MIB),
        cost_estimate=pl.CostEstimate(flops=flops, bytes_accessed=16 * MIB, transcendentals=0),
    )(*args)


def forward_self(place, x, start, pack, staged):
    length, width = x.shape
    low = ((length, width), BF)
    outs = [((length, 2 * width), BF), low, low, low]
    if staged:
        return call(
            functools.partial(self_forward_kernel, True),
            (place, x, start, pack),
            [*outs, ((3 * width, width), BF)],
            [low],
            48, 10**10, smem=(0,),
        )
    results = call(
        functools.partial(self_forward_kernel, False), (x, start, pack), outs, [low], 48, 10**10
    )
    return (*results, pack)


def forward_cross(x, mixed, source, count, vec, pack, shard):
    length, width = x.shape
    keys = source.shape[0]
    low, full, column = ((length, width), BF), ((length, width), F32), ((length, 1), F32)
    return call(
        functools.partial(cross_forward_kernel, shard),
        (x, mixed, source, count, vec, pack),
        [full, column, ((length, 2 * width), BF), ((keys, width), BF), ((keys, width), BF), low, full, column],
        [low, ((keys, PAIR), BF)],
        48, 10**10, smem=(3,),
    )


def hidden_step(place, normed, inverse, cot, vec, bias, pack, shard, staged):
    length, width = normed.shape
    inner = bias.shape[1]
    args = (normed, inverse, cot, vec, bias, pack)
    low = ((length, width), BF)
    return call(
        functools.partial(hidden_kernel, shard, inner // width, staged),
        (place, *args) if staged else args,
        [low, ((length, width), F32), (grad_shape(pack.shape[0], pack.shape[1], width, staged), BF),
         ((16, width), F32), ((1, inner), F32)],
        [low, ((length, inner), BF), ((length, inner), BF), low, ((TILE, inner), F32)],
        56, 2 * 10**10, smem=(0,) if staged else (),
    )


def grad_shape(devices, rows, width, staged):
    return (2, devices, rows // 2, width) if staged else (devices, rows, width)


def backward_cross(place, dz, x, normed, inverse, source, count, vec, pack, saved, mixed, shard, staged):
    length, width = dz.shape
    keys = source.shape[0]
    args = (dz, x, normed, inverse, source, count, vec, pack, *saved, mixed)
    low, key_low, sums = ((length, width), BF), ((keys, width), BF), ((2, PAIR, keys), F32)
    return call(
        functools.partial(cross_backward_kernel, shard, staged),
        (place, *args) if staged else args,
        [(grad_shape(pack.shape[0], 5 * shard, width, staged), BF), ((length, width), F32),
         ((keys, width), F32), ((16, width), F32)],
        [low, ((length, 2 * width), BF), low, key_low, key_low, sums, sums, low, ((keys, PAIR), BF)],
        56, 2 * 10**10, smem=(0, 6) if staged else (5,),
    )


def backward_self(place, dz, x, start, vec, pack, matrices, saved, shard, staged):
    length, width = dz.shape
    args = (dz, x, start, vec, pack, matrices, *saved)
    low, sums = ((length, width), BF), ((2, PAIR, length), F32)
    return call(
        functools.partial(self_backward_kernel, shard, staged),
        (place, *args) if staged else args,
        [(grad_shape(pack.shape[0], 3 * shard, width, staged), BF), ((length, width), F32)],
        [((length, 2 * width), BF), low, low, low, sums, sums, ((length, PAIR), BF)],
        56, 2 * 10**10, smem=(0,) if staged else (),
    )


CORE_SWAP = [(0, 1), (1, 0), (2, 3), (3, 2)]
CHIP_SWAP = [(0, 2), (2, 0), (1, 3), (3, 1)]
ROW_SWAP = [(i, i ^ 1) for i in range(8)]


def line_shift(step):
    return [(2 * z + y, 2 * ((z + step) % 4) + y) for z in range(4) for y in (0, 1)]


def small_mesh(mesh):
    return mesh.shape["rep"] == 4 and mesh.shape["fsdp"] == 8


def gather_staged(pack):
    quarter = pack.shape[0] // 4
    mine = lax.dynamic_slice_in_dim(pack, lax.axis_index("rep") * quarter, quarter, 0)
    pair = jnp.stack([mine, lax.ppermute(mine, "fsdp", ROW_SWAP)])
    part = jnp.stack([pair] + [lax.ppermute(pair, "fsdp", line_shift(step)) for step in (1, 2, 3)])
    both = jnp.stack([part, lax.ppermute(part, "rep", CHIP_SWAP)])
    return jnp.stack([both, lax.ppermute(both, "rep", CORE_SWAP)])


def low_sum(mine, received):
    return mine.astype(BF).astype(F32) + received.astype(F32)


def join_halves(total, matrices):
    core = lax.axis_index("rep") % 2
    other = lax.ppermute(total, "rep", CORE_SWAP)
    halves = jnp.where(core == 0, jnp.stack([total, other]), jnp.stack([other, total]))
    width = total.shape[-1]
    return halves.reshape(2, matrices, -1, width).transpose(1, 0, 2, 3).reshape(-1, width)


def reduce_halves(grads, matrices):
    joined = low_sum(grads[0], lax.ppermute(grads[1], "rep", CORE_SWAP)).astype(BF)
    part = lax.psum_scatter(joined, "fsdp", scatter_dimension=0)
    return join_halves(low_sum(part, lax.ppermute(part, "rep", CHIP_SWAP)), matrices)


def reduce_lines(grads, matrices):
    place = lax.axis_index("fsdp")
    joined = low_sum(grads[0], lax.ppermute(grads[1], "rep", CORE_SWAP)).astype(BF)
    by_row = joined.reshape(4, 2, -1, joined.shape[-1])
    keep = lax.dynamic_index_in_dim(by_row, place % 2, 1, False)
    send = lax.dynamic_index_in_dim(by_row, 1 - place % 2, 1, False)
    joined = low_sum(keep, lax.ppermute(send, "fsdp", ROW_SWAP)).astype(BF)
    total = lax.dynamic_index_in_dim(joined, place // 2, 0, False).astype(F32)
    for step in (1, 2, 3):
        away = lax.dynamic_index_in_dim(joined, (place // 2 + step) % 4, 0, False)
        total = total + lax.ppermute(away, "fsdp", line_shift(step)).astype(F32)
    total = total.astype(BF)
    return join_halves(low_sum(total, lax.ppermute(total, "rep", CHIP_SWAP)), matrices)


def reduce_plain(grads):
    return lax.psum(lax.psum_scatter(grads, "fsdp", scatter_dimension=0), "rep").astype(F32)


def adam_update(weight_now, gradient, moment_one, moment_two, settings, step_float, factor):
    learn_rate, beta_one, beta_two, decay_rate = settings[0], settings[1], settings[2], settings[3]
    first_new = beta_one * moment_one + (1.0 - beta_one) * gradient
    second_new = beta_two * moment_two + (1.0 - beta_two) * gradient * gradient
    first_hat = first_new / (1.0 - beta_one**step_float)
    second_hat = second_new / (1.0 - beta_two**step_float)
    change = first_hat / (jnp.sqrt(second_hat) + 1e-08) + factor * decay_rate * weight_now
    return (weight_now - learn_rate * change, first_new, second_new)


def per_device(
    small, inputs, memory, memory_length, target_pos, cotangent,
    attention_weights, expand_weights, shrink_weights, expand_bias, layer_vectors,
    first_attention, first_expand, first_shrink, first_bias, first_vectors,
    second_attention, second_expand, second_shrink, second_bias, second_vectors,
    hyper_rates, step_count,
):
    length, width = inputs.shape[1:]
    shard = attention_weights.shape[1]
    count = width // shard
    inner_shard = shrink_weights.shape[0]
    blocks = inner_shard // shard
    whole = shard % 16 != 0
    kernel_shard = width if whole else shard

    def together(pack, parts):
        if not whole:
            return pack
        pieces = []
        for first, rows in parts:
            pieces.append(pack[:, first : first + rows].reshape(-1, width))
        return jnp.concatenate(pieces)[None]

    def apart(pack, parts):
        if not whole:
            return pack
        pieces, at = [], 0
        for _, rows in parts:
            pieces.append(pack[0, at : at + rows * count].reshape(count, rows, width))
            at += rows * count
        return jnp.concatenate(pieces, axis=1)

    self_parts = [(i * shard, shard) for i in range(3)]
    cross_parts = [(i * shard, shard) for i in range(5)]
    hidden_parts = [(i * shard, shard) for i in range(blocks)] + [(blocks * shard, inner_shard)]

    low_attention = attention_weights.astype(BF).reshape(8 * shard, width)
    vector_count = layer_vectors.shape[0]
    flat_size = vector_count * shard + inner_shard
    extra_rows = -(-flat_size // (32 * width)) * 32
    extra = jnp.concatenate([layer_vectors.reshape(-1), expand_bias]).astype(BF)
    extra = jnp.pad(extra, (0, extra_rows * width - flat_size)).reshape(extra_rows, width)
    pack_one = low_attention[: 3 * shard]
    pack_two = jnp.concatenate([low_attention[3 * shard :], extra])
    pack_three = jnp.concatenate(
        [
            expand_weights.astype(BF).reshape(shard, blocks, width).transpose(1, 0, 2).reshape(-1, width),
            shrink_weights.astype(BF),
        ]
    )
    place = jnp.stack([lax.axis_index("rep"), lax.axis_index("fsdp")]).astype(jnp.int32)
    if small:
        one = gather_staged(pack_one)
    else:
        one = lax.all_gather(pack_one, "fsdp", axis=0)
        one = jnp.concatenate([one[:, i : i + rows].reshape(-1, width) for i, rows in self_parts])
    two = lax.all_gather(pack_two, "fsdp", axis=0)
    three = together(lax.all_gather(pack_three, "fsdp", axis=0), hidden_parts)
    flat = two[:, 5 * shard :].reshape(count, -1).astype(F32)
    vec = flat[:, : vector_count * shard].reshape(count, vector_count, shard).transpose(1, 0, 2)
    vec = jnp.pad(vec.reshape(vector_count, width), ((0, 16 - vector_count), (0, 0)))
    bias = flat[:, vector_count * shard : flat_size].reshape(1, -1)
    two = together(two, cross_parts)

    x, source, cot = inputs[0], memory[0], cotangent[0]
    start = (jnp.arange(length, dtype=jnp.int32) - target_pos[0])[:, None]

    *saved_one, matrices = forward_self(place, x, start, one, small)
    norm_one, inv_one, *saved_two, norm_two, inv_two = forward_cross(
        x, saved_one[3], source, memory_length, vec, two, kernel_shard
    )
    outputs, dz_two, grad_three, sums_three, bias_sum = hidden_step(
        place, norm_two, inv_two, cot, vec, bias, three, kernel_shard, small
    )
    grad_two, dz_one, memory_grad, sums_two = backward_cross(
        place, dz_two, x, norm_one, inv_one, source, memory_length, vec, two, saved_two, saved_one[3],
        kernel_shard, small,
    )
    grad_one, input_grad = backward_self(
        place, dz_one, x, start, vec, two, matrices, saved_one, kernel_shard, small
    )
    vector_grad = (sums_two + sums_three)[:vector_count]
    flat = jnp.concatenate(
        [
            vector_grad.reshape(vector_count, count, shard).transpose(1, 0, 2).reshape(count, -1),
            bias_sum.reshape(count, inner_shard),
        ],
        axis=1,
    )
    flat = jnp.pad(flat.astype(BF), ((0, 0), (0, extra_rows * width - flat_size)))
    flat = flat.reshape(count, extra_rows, width)
    if small:
        core = lax.axis_index("rep") % 2
        half = extra_rows // 2
        low, high = flat[:, :half], flat[:, half:]
        extra = jnp.where(core == 0, jnp.stack([low, high]), jnp.stack([high, low]))
        total_three = reduce_halves(grad_three, 2 * blocks)
        core_two = jnp.concatenate([grad_two, extra], axis=2)
        total_two = reduce_halves(core_two, 1)
        half_rows = core_two.shape[2]
        body = total_two.reshape(2, half_rows, width)
        sums_flat = body[:, 5 * shard // 2 :].reshape(-1)
        total_two = body[:, : 5 * shard // 2].reshape(2, 5, -1, width).transpose(1, 0, 2, 3).reshape(-1, width)
        total_one = reduce_lines(grad_one, 3)
    else:
        total_three = reduce_plain(apart(grad_three, hidden_parts))
        total_two = reduce_plain(jnp.concatenate([apart(grad_two, cross_parts), flat], axis=1))
        total_one = reduce_plain(apart(grad_one, self_parts))
        sums_flat = total_two[5 * shard :].reshape(-1)
        total_two = total_two[: 5 * shard]
    grad_attention = jnp.concatenate([total_one, total_two]).reshape(attention_weights.shape)
    grad_expand = total_three[: blocks * shard].reshape(blocks, shard, width).transpose(1, 0, 2).reshape(shard, -1)
    grad_shrink = total_three[blocks * shard :]
    grad_vectors = sums_flat[: vector_count * shard].reshape(vector_count, shard)
    grad_bias = sums_flat[vector_count * shard : flat_size]
    step_float = step_count.astype(F32)
    updated = []
    for now, grad, one_now, two_now, factor in (
        (attention_weights, grad_attention, first_attention, second_attention, 1.0),
        (expand_weights, grad_expand, first_expand, second_expand, 1.0),
        (shrink_weights, grad_shrink, first_shrink, second_shrink, 1.0),
        (expand_bias, grad_bias, first_bias, second_bias, 0.0),
        (layer_vectors, grad_vectors, first_vectors, second_vectors, 0.0),
    ):
        updated.extend(adam_update(now, grad, one_now, two_now, hyper_rates, step_float, factor))
    return (outputs[None], input_grad[None], memory_grad[None], *updated)


def solution(mesh):
    rows = ("rep", "fsdp")
    params = (P(None, "fsdp", None), P("fsdp", None), P("fsdp", None), P("fsdp"), P(None, "fsdp"))
    return jax.shard_map(
        functools.partial(per_device, small_mesh(mesh)),
        mesh=mesh,
        in_specs=(
            P(rows, None, None), P(rows, None, None), P(rows), P(rows, None), P(rows, None, None),
            *params, *params, *params, P(), P(),
        ),
        out_specs=(
            P(rows, None, None), P(rows, None, None), P(rows, None, None),
            *(spec for spec in params for _ in range(3)),
        ),
        check_vma=False,
    )
```

```python
import functools

import jax
import jax.numpy as jnp
from jax import lax
from jax.experimental import pallas as pl
from jax.experimental.pallas import tpu as pltpu
from jax.sharding import PartitionSpec as P

BF = jnp.bfloat16
F32 = jnp.float32
HEAD_DIM = 64
PAIR = 128
TILE = 256
MIB = 1 << 20


def dot(left, right, left_dim, right_dim):
    return lax.dot_general(
        left, right, (((left_dim,), (right_dim,)), ((), ())), preferred_element_type=F32
    )


def lanes(size):
    return lax.broadcasted_iota(jnp.int32, (1, size), 1)


def half_masks():
    first = jnp.where(lanes(PAIR) < HEAD_DIM, 1.0, 0.0)
    return first.astype(BF), (1.0 - first).astype(BF)


def rows_at(index, size=TILE):
    return pl.ds(pl.multiple_of(index * size, size), size)


def split_three(column):
    high = column.astype(BF).astype(F32)
    rest = column - high
    middle = rest.astype(BF).astype(F32)
    return high, middle, rest - middle


def with_column(block, column, base, last):
    high, middle, low = split_three(column)
    lane = lanes(PAIR)
    tail = jnp.where(lane == base + 3, last, block)
    return jnp.where(
        lane == base, -high, jnp.where(lane == base + 1, -middle, jnp.where(lane == base + 2, -low, tail))
    ).astype(BF)


def weight(all_ref, index):
    width = all_ref.shape[1]
    return all_ref[index * width : (index + 1) * width, :]


def key_extra(length_limit, count):
    lane = lanes(PAIR) % HEAD_DIM
    extra = jnp.where(lane < 3, 1.0, 0.0)
    if length_limit is None:
        return jnp.broadcast_to(extra, (count, PAIR)).astype(BF)
    row = lax.broadcasted_iota(jnp.int32, (count, PAIR), 0)
    bias = jnp.where(row < length_limit, 0.0, -1e30)
    return jnp.where(lane == 3, bias, extra).astype(BF)


def visible(start, first_query, first_key, count):
    key = first_key + lax.broadcasted_iota(jnp.int32, (TILE, count), 1)
    seen = key >= start
    if first_key == first_query:
        query = first_query + lax.broadcasted_iota(jnp.int32, (TILE, count), 0)
        seen = seen & (key <= query)
    return seen


def key_spans(tile, count, causal):
    if not causal:
        return [(0, count)]
    spans = [(0, tile * TILE)] if tile else []
    return spans + [(tile * TILE, TILE)]


def attend(q_ref, k_ref, v_ref, extra_ref, start_ref, qa_ref, o_ref):
    length, count = q_ref.shape[0], k_ref.shape[0]
    causal = start_ref is not None
    masks = half_masks()

    @pl.loop(0, q_ref.shape[1] // PAIR)
    def _(pair):
        cols = rows_at(pair, PAIR)
        for tile in range(length // TILE):
            rows = slice(tile * TILE, (tile + 1) * TILE)
            spans = key_spans(tile, count, causal)
            results = []
            for side in (0, 1):
                base = HEAD_DIM * (1 - side)
                lane = lanes(PAIR)
                queries = q_ref[rows, cols] * masks[side]
                queries_f = queries.astype(F32)
                if not causal:
                    queries = jnp.where(lane == base + 3, 1.0, queries_f).astype(BF)
                score_blocks = []
                for first, size in spans:
                    keys = k_ref[first : first + size, cols] * masks[side]
                    if not causal:
                        keys = keys + extra_ref[first : first + size, :] * masks[1 - side]
                    scores = dot(queries, keys, 1, 1)
                    if causal:
                        seen = visible(start_ref[rows, :], tile * TILE, first, size)
                        scores = jnp.where(seen, scores, -1000000000.0)
                    score_blocks.append(scores)
                top = functools.reduce(
                    jnp.maximum, [jnp.max(scores, axis=1, keepdims=True) for scores in score_blocks]
                )
                total = None
                for scores, (first, size) in zip(score_blocks, spans):
                    values = v_ref[first : first + size, cols] * masks[side] + masks[1 - side]
                    probs = jnp.exp(scores - top).astype(BF)
                    part = dot(probs, values, 1, 0)
                    total = part if total is None else total + part
                results.append(total / pltpu.roll(total, HEAD_DIM, 1))
                log_total = top + jnp.log(total[:, base : base + 1])
                qa_ref[rows, pl.ds(pl.multiple_of(pair * 2 * PAIR, PAIR) + side * PAIR, PAIR)] = with_column(
                    queries_f, log_total, base, 0.0 if causal else 1.0
                )
            o_ref[rows, cols] = jnp.where(lanes(PAIR) < HEAD_DIM, results[0], results[1]).astype(BF)


def attend_back(qa_ref, da_ref, k_ref, v_ref, extra_ref, start_ref, dq_ref, dk_ref, dv_ref, dk_sum, dv_sum):
    length, count = qa_ref.shape[0], k_ref.shape[0]
    causal = start_ref is not None
    masks = half_masks()

    @pl.loop(0, k_ref.shape[1] // PAIR)
    def _(pair):
        cols = rows_at(pair, PAIR)
        for tile in reversed(range(length // TILE)):
            rows = slice(tile * TILE, (tile + 1) * TILE)
            query_grads = []
            for side in (0, 1):
                head_cols = pl.ds(pl.multiple_of(pair * 2 * PAIR, PAIR) + side * PAIR, PAIR)
                queries = qa_ref[rows, head_cols]
                grads = da_ref[rows, head_cols]
                query_grad = None
                for first, size in key_spans(tile, count, causal):
                    span = slice(first, first + size)
                    keys = k_ref[span, cols]
                    keys_low = keys * masks[side] + extra_ref[span, :] * masks[1 - side]
                    values = v_ref[span, cols] * masks[side] + masks[1 - side]
                    probs = jnp.exp(dot(queries, keys_low, 1, 1))
                    if causal:
                        seen = visible(start_ref[rows, :], tile * TILE, first, size)
                        probs = jnp.where(seen, probs, 0.0)
                    grad_scores = (probs * dot(grads, values, 1, 1)).astype(BF)
                    value_part = dot(grads, probs.astype(BF), 0, 0)
                    key_part = dot(queries, grad_scores, 0, 0)
                    if tile == length // TILE - 1:
                        dv_sum[side, :, span] = value_part
                        dk_sum[side, :, span] = key_part
                    else:
                        dv_sum[side, :, span] += value_part
                        dk_sum[side, :, span] += key_part
                    part = dot(grad_scores, keys, 1, 0)
                    query_grad = part if query_grad is None else query_grad + part
                query_grads.append(query_grad)
            dq_ref[rows, cols] = (
                jnp.where(lanes(PAIR) < HEAD_DIM, query_grads[0], query_grads[1]) * HEAD_DIM**-0.5
            ).astype(BF)
        for sums, out in ((dk_sum, dk_ref), (dv_sum, dv_ref)):
            joined = jnp.concatenate([sums[0, :HEAD_DIM, :], sums[1, HEAD_DIM:, :]], axis=0)
            out[:, cols] = joined.astype(BF).T


def norm_rows(summed):
    center = jnp.mean(summed, axis=1, keepdims=True)
    shifted = summed - center
    inverse = lax.rsqrt(jnp.mean(shifted * shifted, axis=1, keepdims=True) + 1e-05)
    return shifted * inverse, inverse


def norm_back(grad_out, normed, inverse, gain):
    scaled = grad_out * gain
    first = jnp.mean(scaled, axis=1, keepdims=True)
    second = jnp.mean(scaled * normed, axis=1, keepdims=True)
    return inverse * (scaled - first - normed * second)


def add_rows(ref, row, values):
    ref[row : row + 1, :] += jnp.sum(values, axis=0, keepdims=True)


def place_of(place_ref):
    rep, place = place_ref[0], place_ref[1]
    return lax.rem(rep, 2), lax.div(rep, 2), lax.div(place, 2), lax.rem(place, 2)


def assemble(place_ref, chunk_ref, all_ref):
    core, chip, line, row = place_of(place_ref)
    width = all_ref.shape[1]
    quarter = chunk_ref.shape[4]
    shard = quarter * 4 // 3
    for core_step in (0, 1):
        for chip_step in (0, 1):
            rep = jnp.bitwise_xor(chip, chip_step) * 2 + jnp.bitwise_xor(core, core_step)
            for line_step in range(4):
                for row_step in (0, 1):
                    owner = lax.rem(line - line_step + 4, 4) * 2 + jnp.bitwise_xor(row, row_step)
                    for piece in range(quarter // 16):
                        stacked = rep * quarter + piece * 16
                        matrix = lax.div(stacked, shard)
                        target = matrix * width + owner * shard + (stacked - matrix * shard)
                        all_ref[pl.ds(pl.multiple_of(target, 16), 16), :] = chunk_ref[
                            core_step, chip_step, line_step, row_step, piece * 16 : (piece + 1) * 16, :
                        ]


def assemble_halves(place_ref, mine_ref, other_ref, all_ref, shards):
    core = place_of(place_ref)[0]
    devices, _, half = mine_ref.shape
    for step, ref in ((0, mine_ref), (1, other_ref)):
        cols = pl.ds(pl.multiple_of(jnp.bitwise_xor(core, step) * half, half), half)
        first, target = 0, 0
        for shard in shards:
            for owner in range(devices):
                at = target + owner * shard
                all_ref[at : at + shard, cols] = ref[owner, first : first + shard, :]
            first += shard
            target += shard * devices


def unpack_small(all_ref, base, vec_ref, bias_ref):
    devices = vec_ref.shape[1] // HEAD_DIM
    inner = bias_ref.shape[1] // devices
    for pair in range(devices // 2):
        first = base + 2 * pair * 16
        left = all_ref[first : first + 16, :PAIR].astype(F32)
        right = all_ref[first + 16 : first + 32, :PAIR].astype(F32)
        vec_ref[:, pair * PAIR : (pair + 1) * PAIR] = jnp.where(
            lanes(PAIR) < HEAD_DIM, left, pltpu.roll(right, HEAD_DIM, 1)
        )
    for owner in range(devices):
        rows = all_ref[base + owner * 16 : base + owner * 16 + 16, :inner].astype(F32)
        bias_ref[:, owner * inner : (owner + 1) * inner] = rows[10:11, :]


def self_forward_kernel(staged, *refs):
    if staged:
        place_ref, x_ref, start_ref, chunk_ref, qa_ref, k_ref, v_ref, o_ref, all_ref, q_ref = refs
        assemble(place_ref, chunk_ref, all_ref)
    else:
        x_ref, start_ref, all_ref, qa_ref, k_ref, v_ref, o_ref, q_ref = refs
    length, width = x_ref.shape

    @pl.loop(0, length // TILE)
    def _(tile):
        rows = rows_at(tile)
        source = x_ref[rows, :]
        queries = dot(source, all_ref[:width, :], 1, 0).astype(BF)
        q_ref[rows, :] = queries * jnp.asarray(HEAD_DIM**-0.5, BF)
        k_ref[rows, :] = dot(source, all_ref[width : 2 * width, :], 1, 0).astype(BF)
        v_ref[rows, :] = dot(source, all_ref[2 * width :, :], 1, 0).astype(BF)

    attend(q_ref, k_ref, v_ref, None, start_ref, qa_ref, o_ref)


def cross_forward_kernel(shards, *refs):
    if shards:
        place_ref, x_ref, mixed_ref, source_ref, length_ref, mine_ref, other_ref = refs[:7]
        first_ref, first_inv_ref, qa_ref, k_ref, v_ref, o_ref, n_ref, inv_ref, w_ref, vec_ref, bias_ref = refs[7:18]
        q_ref, extra_ref = refs[18:]
        assemble_halves(place_ref, mine_ref, other_ref, w_ref, shards)
        unpack_small(w_ref, 5 * w_ref.shape[1], vec_ref, bias_ref)
    else:
        (x_ref, mixed_ref, source_ref, length_ref, w_ref, vec_ref) = refs[:6]
        first_ref, first_inv_ref, qa_ref, k_ref, v_ref, o_ref, n_ref, inv_ref, q_ref, extra_ref = refs[6:]
    length = q_ref.shape[0]
    extra_ref[...] = key_extra(length_ref[0], k_ref.shape[0])

    @pl.loop(0, length // TILE)
    def _(tile):
        rows = rows_at(tile)
        summed = x_ref[rows, :].astype(F32) * vec_ref[6:7, :] + dot(
            mixed_ref[rows, :], weight(w_ref, 0), 1, 0
        )
        normed, inverse = norm_rows(summed)
        first_ref[rows, :] = normed
        first_inv_ref[rows, :] = inverse
        low = (normed * vec_ref[0:1, :] + vec_ref[3:4, :]).astype(BF)
        queries = dot(low, weight(w_ref, 1), 1, 0).astype(BF)
        q_ref[rows, :] = queries * jnp.asarray(HEAD_DIM**-0.5, BF)

    @pl.loop(0, source_ref.shape[0] // TILE)
    def _(tile):
        rows = rows_at(tile)
        source = source_ref[rows, :]
        k_ref[rows, :] = dot(source, weight(w_ref, 2), 1, 0).astype(BF)
        v_ref[rows, :] = dot(source, weight(w_ref, 3), 1, 0).astype(BF)

    attend(q_ref, k_ref, v_ref, extra_ref, None, qa_ref, o_ref)

    @pl.loop(0, length // TILE)
    def _(tile):
        rows = rows_at(tile)
        first_out = first_ref[rows, :] * vec_ref[0:1, :] + vec_ref[3:4, :]
        summed = first_out * vec_ref[7:8, :] + dot(o_ref[rows, :], weight(w_ref, 4), 1, 0)
        normed, inverse = norm_rows(summed)
        n_ref[rows, :] = normed
        inv_ref[rows, :] = inverse


def hidden_kernel(shards, *refs):
    place_ref = refs[0] if shards else None
    if shards:
        (
            place_ref, mine_ref, other_ref, n_ref, inv_ref, cot_ref, vec_ref, bias_ref,
            out_ref, dz_ref, keep_ref, send_ref, sums_ref, bias_sum_ref,
            w_ref, low_ref, h_ref, du_ref, df_ref, slope_ref,
        ) = refs
        grad_refs = (keep_ref, send_ref)
        assemble_halves(place_ref, mine_ref, other_ref, w_ref, shards)
    else:
        (
            w_ref, n_ref, inv_ref, cot_ref, vec_ref, bias_ref,
            out_ref, dz_ref, grad_ref, sums_ref, bias_sum_ref,
            low_ref, h_ref, du_ref, df_ref, slope_ref,
        ) = refs
        grad_refs = (grad_ref,)
    length, width = n_ref.shape
    sums_ref[...] = jnp.zeros_like(sums_ref)
    bias_sum_ref[...] = jnp.zeros_like(bias_sum_ref)
    blocks = bias_ref.shape[1] // width

    def expand(block):
        return weight(w_ref, block)

    def shrink_all():
        return w_ref[blocks * width :, :]

    @pl.loop(0, length // TILE)
    def _(tile):
        rows = rows_at(tile)
        gain, shift = vec_ref[1:2, :], vec_ref[4:5, :]
        second_out = n_ref[rows, :] * gain + shift
        low = second_out.astype(BF)
        low_ref[rows, :] = low
        summed = second_out * vec_ref[8:9, :] + vec_ref[9:10, :]
        shrink = shrink_all()
        for block in range(blocks):
            cols = slice(block * width, (block + 1) * width)
            before = dot(low, expand(block), 1, 0) + bias_ref[:, cols]
            square = before * before
            tangent = jnp.tanh(0.7978845608028654 * (before + 0.044715 * before * square))
            half = 0.5 * (1.0 + tangent)
            slope_ref[:, cols] = half + 0.5 * before * (1.0 - tangent * tangent) * 0.7978845608028654 * (
                1.0 + 3.0 * 0.044715 * square
            )
            hidden = (before * half).astype(BF)
            h_ref[rows, cols] = hidden
            summed = summed + dot(hidden, shrink[cols, :], 1, 0)
        normed, inverse = norm_rows(summed)
        out_ref[rows, :] = (normed * vec_ref[2:3, :] + vec_ref[5:6, :]).astype(BF)
        grad_out = cot_ref[rows, :].astype(F32)
        third = norm_back(grad_out, normed, inverse, vec_ref[2:3, :])
        add_rows(sums_ref, 2, grad_out * normed)
        add_rows(sums_ref, 5, grad_out)
        branch = third.astype(BF)
        df_ref[rows, :] = branch
        add_rows(sums_ref, 9, branch.astype(F32))
        add_rows(sums_ref, 8, second_out * third)
        grad_second = vec_ref[8:9, :] * third
        for block in range(blocks):
            cols = slice(block * width, (block + 1) * width)
            du = (dot(branch, shrink[cols, :], 1, 1) * slope_ref[:, cols]).astype(BF)
            du_ref[rows, cols] = du
            bias_sum_ref[:, cols] += jnp.sum(du.astype(F32), axis=0, keepdims=True)
            grad_second = grad_second + dot(du, expand(block), 1, 1)
        normed_two = n_ref[rows, :]
        dz_ref[rows, :] = norm_back(grad_second, normed_two, inv_ref[rows, :], gain)
        add_rows(sums_ref, 1, grad_second * normed_two)
        add_rows(sums_ref, 4, grad_second)

    for block in range(blocks):
        cols = slice(block * width, (block + 1) * width)
        put_grad(grad_refs, place_ref, block, low_ref[...], du_ref, block * width)
        put_shrink(grad_refs, place_ref, block, blocks, h_ref[:, cols], df_ref)


def branch_grads(branch, mixed_weight, o_rows, da_ref, rows):
    masks = half_masks()
    mixed_grad = dot(branch, mixed_weight, 1, 1).astype(BF)
    for pair in range(mixed_grad.shape[1] // PAIR):
        cols = slice(pair * PAIR, (pair + 1) * PAIR)
        grad_pair = mixed_grad[:, cols].astype(F32)
        product = grad_pair * o_rows[:, cols].astype(F32)
        for side in (0, 1):
            mask = masks[side].astype(F32)
            inner = jnp.sum(product * mask, axis=1, keepdims=True)
            first = (2 * pair + side) * PAIR
            da_ref[rows, first : first + PAIR] = with_column(
                grad_pair * mask, inner, HEAD_DIM * (1 - side), 0.0
            )


def put_grad(grad_refs, place_ref, index, left, right_ref, first=0):
    width = left.shape[1]
    if place_ref is None:
        grad = dot(left, right_ref[:, first : first + width], 0, 0)
        grad_refs[0][index * width : (index + 1) * width, :] = grad.astype(BF)
        return
    core, _, _, row = place_of(place_ref)
    half = width // 2
    shard = width // 8
    for step, grad_ref in enumerate(grad_refs):
        cols = pl.ds(pl.multiple_of(first + jnp.bitwise_xor(core, step) * half, half), half)
        grad = dot(left, right_ref[:, cols], 0, 0).astype(BF).reshape(4, 2, shard, half)
        for side in (0, 1):
            slot = jnp.bitwise_xor(row, side)
            grad_ref[slot, :, index * shard : (index + 1) * shard, :] = grad[:, side]


def put_shrink(grad_refs, place_ref, block, blocks, left, right_ref):
    width = left.shape[1]
    if place_ref is None:
        first = (blocks + block) * width
        grad_refs[0][first : first + width, :] = dot(left, right_ref[...], 0, 0).astype(BF)
        return
    core, _, _, row = place_of(place_ref)
    half, shard = width // 2, width * blocks // 8
    base = width // 8 * blocks
    for step, grad_ref in enumerate(grad_refs):
        cols = pl.ds(pl.multiple_of(jnp.bitwise_xor(core, step) * half, half), half)
        grad = dot(left, right_ref[:, cols], 0, 0).astype(BF).reshape(width // shard, shard, half)
        for part in range(width // shard):
            owner = block * (width // shard) + part
            grad_ref[jnp.bitwise_xor(row, owner % 2), owner // 2, base:, :] = grad[part]


def put_small(grad_refs, place_ref, base, sums, bias_sum):
    core, _, _, row = place_of(place_ref)
    half = grad_refs[0].shape[3]
    inner = bias_sum.shape[1] // 8
    index = lax.broadcasted_iota(jnp.int32, (16, half), 0)
    for owner in range(8):
        block = sums[:, owner // 2 * PAIR : (owner // 2 + 1) * PAIR]
        if owner % 2:
            block = pltpu.roll(block, HEAD_DIM, 1)
        block = jnp.concatenate([block, jnp.zeros((16, half - PAIR), F32)], axis=1)
        block = jnp.where(index == 10, bias_sum[:, owner * inner : (owner + 1) * inner], block)
        high = block.astype(BF)
        low = (block - high.astype(F32)).astype(BF)
        slot = jnp.bitwise_xor(row, owner % 2)
        first = (core == 0).astype(F32)
        for step, grad_ref in enumerate(grad_refs):
            is_high = first if step == 0 else 1.0 - first
            mixed = high.astype(F32) * is_high + low.astype(F32) * (1.0 - is_high)
            grad_ref[slot, owner // 2, base : base + 16, :] = mixed.astype(BF)


def cross_backward_kernel(staged, *refs):
    place_ref = refs[0] if staged else None
    refs = refs[1:] if staged else refs
    (dz_ref, x_ref, first_ref, inv_ref, source_ref, length_ref, vec_ref, w_ref) = refs[:8]
    (qa_ref, k_ref, v_ref, o_ref, self_o_ref) = refs[8:13]
    if staged:
        sums_three_ref, bias_sum_ref, keep_ref, send_ref, dfirst_ref, dsource_ref, sums_ref = refs[13:20]
        scratch, grad_refs = refs[20:], (keep_ref, send_ref)
    else:
        grad_ref, dfirst_ref, dsource_ref, sums_ref = refs[13:17]
        scratch, grad_refs = refs[17:], (grad_ref,)
    low_ref, da_ref, dq_ref, dk_ref, dv_ref, dk_sum, dv_sum, branch_ref, extra_ref = scratch
    length = dz_ref.shape[0]
    sums_ref[...] = jnp.zeros_like(sums_ref)
    extra_ref[...] = key_extra(length_ref[0], k_ref.shape[0])

    @pl.loop(0, length // TILE)
    def _(tile):
        rows = rows_at(tile)
        grad = dz_ref[rows, :]
        branch = grad.astype(BF)
        branch_ref[rows, :] = branch
        first_out = first_ref[rows, :] * vec_ref[0:1, :] + vec_ref[3:4, :]
        low_ref[rows, :] = first_out.astype(BF)
        add_rows(sums_ref, 7, first_out * grad)
        branch_grads(branch, weight(w_ref, 4), o_ref[rows, :], da_ref, rows)

    attend_back(qa_ref, da_ref, k_ref, v_ref, extra_ref, None, dq_ref, dk_ref, dv_ref, dk_sum, dv_sum)

    put_grad(grad_refs, place_ref, 1, low_ref[...], dq_ref)
    put_grad(grad_refs, place_ref, 2, source_ref[...], dk_ref)
    put_grad(grad_refs, place_ref, 3, source_ref[...], dv_ref)
    put_grad(grad_refs, place_ref, 4, o_ref[...], branch_ref)

    @pl.loop(0, length // TILE)
    def _(tile):
        rows = rows_at(tile)
        dx = dot(dq_ref[rows, :], weight(w_ref, 1), 1, 1) + vec_ref[7:8, :] * dz_ref[rows, :]
        normed = first_ref[rows, :]
        dfirst = norm_back(dx, normed, inv_ref[rows, :], vec_ref[0:1, :])
        dfirst_ref[rows, :] = dfirst
        add_rows(sums_ref, 0, dx * normed)
        add_rows(sums_ref, 3, dx)
        add_rows(sums_ref, 6, x_ref[rows, :].astype(F32) * dfirst)
        branch_ref[rows, :] = dfirst.astype(BF)

    @pl.loop(0, source_ref.shape[0] // TILE)
    def _(tile):
        rows = rows_at(tile)
        dsource_ref[rows, :] = dot(dk_ref[rows, :], weight(w_ref, 2), 1, 1) + dot(
            dv_ref[rows, :], weight(w_ref, 3), 1, 1
        )

    put_grad(grad_refs, place_ref, 0, self_o_ref[...], branch_ref)
    if staged:
        put_small(
            grad_refs, place_ref, 5 * (w_ref.shape[1] // 8), sums_ref[...] + sums_three_ref[...], bias_sum_ref[...]
        )


def self_backward_kernel(staged, *refs):
    place_ref = refs[0] if staged else None
    refs = refs[1:] if staged else refs
    (dz_ref, x_ref, start_ref, vec_ref, w_ref, all_ref, qa_ref, k_ref, v_ref, o_ref) = refs[:10]
    count = 2 if staged else 1
    grad_refs, dx_ref, scratch = refs[10 : 10 + count], refs[10 + count], refs[11 + count :]
    da_ref, dq_ref, dk_ref, dv_ref, dk_sum, dv_sum, extra_ref = scratch
    length, width = dz_ref.shape
    extra_ref[...] = key_extra(None, k_ref.shape[0])

    @pl.loop(0, length // TILE)
    def _(tile):
        rows = rows_at(tile)
        branch_grads(dz_ref[rows, :].astype(BF), weight(w_ref, 0), o_ref[rows, :], da_ref, rows)

    attend_back(qa_ref, da_ref, k_ref, v_ref, extra_ref, start_ref, dq_ref, dk_ref, dv_ref, dk_sum, dv_sum)

    for index, grads in enumerate((dq_ref, dk_ref, dv_ref)):
        put_grad(grad_refs, place_ref, index, x_ref[...], grads)

    @pl.loop(0, length // TILE)
    def _(tile):
        rows = rows_at(tile)
        dx = vec_ref[6:7, :] * dz_ref[rows, :]
        for index, grads in enumerate((dq_ref, dk_ref, dv_ref)):
            dx = dx + dot(grads[rows, :], all_ref[index * width : (index + 1) * width, :], 1, 1)
        dx_ref[rows, :] = dx


def call(kernel, args, outs, scratch, limit, flops, smem=()):
    in_specs = [
        pl.BlockSpec(memory_space=pltpu.SMEM if i in smem else pltpu.VMEM) for i in range(len(args))
    ]
    return pl.pallas_call(
        kernel,
        out_shape=[jax.ShapeDtypeStruct(shape, kind) for shape, kind in outs],
        in_specs=in_specs,
        out_specs=[pl.BlockSpec(memory_space=pltpu.VMEM)] * len(outs),
        scratch_shapes=[pltpu.VMEM(shape, kind) for shape, kind in scratch],
        compiler_params=pltpu.CompilerParams(vmem_limit_bytes=limit * MIB),
        cost_estimate=pl.CostEstimate(flops=flops, bytes_accessed=16 * MIB, transcendentals=0),
    )(*args)


def forward_self(place, x, start, pack, staged):
    length, width = x.shape
    low = ((length, width), BF)
    outs = [((length, 2 * width), BF), low, low, low]
    if staged:
        return call(
            functools.partial(self_forward_kernel, True),
            (place, x, start, pack),
            [*outs, ((3 * width, width), BF)],
            [low],
            48, 10**10, smem=(0,),
        )
    results = call(
        functools.partial(self_forward_kernel, False), (x, start, pack), outs, [low], 48, 10**10
    )
    return (*results, pack)


def forward_cross(place, x, mixed, source, count, packs, small, shards):
    length, width = x.shape
    keys = source.shape[0]
    low, full, column = ((length, width), BF), ((length, width), F32), ((length, 1), F32)
    outs = [full, column, ((length, 2 * width), BF), ((keys, width), BF), ((keys, width), BF), low, full, column]
    scratch = [low, ((keys, PAIR), BF)]
    if shards:
        return call(
            functools.partial(cross_forward_kernel, shards),
            (place, x, mixed, source, count, *packs),
            [*outs, ((8 * sum(shards), width), BF), ((16, width), F32), ((1, 8 * shards[0] * 4), F32)],
            scratch,
            48, 10**10, smem=(0, 4),
        )
    vec, bias = small
    results = call(
        functools.partial(cross_forward_kernel, None),
        (x, mixed, source, count, packs, vec),
        outs, scratch, 48, 10**10, smem=(3,),
    )
    return (*results, packs, vec, bias)


def grad_outs(rows, width, staged):
    return [((2, 4, rows, width // 2), BF)] * 2 if staged else [((rows, width), BF)]


def hidden_step(place, packs, normed, inverse, cot, vec, bias, shards):
    length, width = normed.shape
    inner = bias.shape[1]
    args = (normed, inverse, cot, vec, bias)
    low = ((length, width), BF)
    scratch = [low, ((length, inner), BF), ((length, inner), BF), low, ((TILE, inner), F32)]
    matrices = ((2 * inner, width), BF)
    rows = sum(shards) if shards else 2 * inner
    return call(
        functools.partial(hidden_kernel, shards),
        (place, *packs, *args) if shards else (packs, *args),
        [low, ((length, width), F32), *grad_outs(rows, width, shards), ((16, width), F32), ((1, inner), F32)],
        [matrices, *scratch] if shards else scratch,
        60, 2 * 10**10, smem=(0,) if shards else (),
    )


def backward_cross(place, dz, x, normed, inverse, source, count, vec, matrices, saved, mixed, small):
    length, width = dz.shape
    keys = source.shape[0]
    args = (dz, x, normed, inverse, source, count, vec, matrices, *saved, mixed)
    low, key_low, sums = ((length, width), BF), ((keys, width), BF), ((2, PAIR, keys), F32)
    return call(
        functools.partial(cross_backward_kernel, small is not None),
        (place, *args, *small) if small else args,
        [*grad_outs(5 * width // 8 + 16 if small else 5 * width, width, small), ((length, width), F32),
         ((keys, width), F32), ((16, width), F32)],
        [low, ((length, 2 * width), BF), low, key_low, key_low, sums, sums, low, ((keys, PAIR), BF)],
        60, 2 * 10**10, smem=(0, 6) if small else (5,),
    )


def backward_self(place, dz, x, start, vec, cross_matrices, matrices, saved, staged):
    length, width = dz.shape
    args = (dz, x, start, vec, cross_matrices, matrices, *saved)
    low, sums = ((length, width), BF), ((2, PAIR, length), F32)
    return call(
        functools.partial(self_backward_kernel, staged),
        (place, *args) if staged else args,
        [*grad_outs(3 * width // 8 if staged else 3 * width, width, staged), ((length, width), F32)],
        [((length, 2 * width), BF), low, low, low, sums, sums, ((length, PAIR), BF)],
        60, 2 * 10**10, smem=(0,) if staged else (),
    )


def adam_step(settings_ref, now, grad, one, two, decay):
    beta_one, beta_two = settings_ref[1], settings_ref[2]
    first = beta_one * one + (1.0 - beta_one) * grad
    second = beta_two * two + (1.0 - beta_two) * grad * grad
    change = (first / settings_ref[4]) / (jnp.sqrt(second / settings_ref[5]) + 1e-08)
    if decay:
        change = change + settings_ref[3] * now
    return now - settings_ref[0] * change, first, second


def store_step(refs, where, results):
    for ref, value in zip(refs, results):
        ref[where] = value


def hidden_adam_kernel(place_ref, settings_ref, mine_ref, other_ref, *refs):
    core = place_of(place_ref)[0]
    expand, shrink = refs[0:3], refs[3:6]
    new_expand, new_shrink = refs[6:9], refs[9:12]
    half = mine_ref.shape[1]
    shard = expand[0].shape[0]
    blocks = expand[0].shape[1] // (2 * half)
    for step, ref in ((0, mine_ref), (1, other_ref)):
        side = jnp.bitwise_xor(core, step) * half
        cols = pl.ds(pl.multiple_of(side, half), half)
        for block in range(blocks):
            where = (slice(None), pl.ds(pl.multiple_of(block * 2 * half + side, half), half))
            grad = ref[block * shard : (block + 1) * shard, :]
            now, one, two = (r[where] for r in expand)
            store_step(new_expand, where, adam_step(settings_ref, now, grad, one, two, True))
        where = (slice(None), cols)
        now, one, two = (r[where] for r in shrink)
        store_step(new_shrink, where, adam_step(settings_ref, now, ref[blocks * shard :, :], one, two, True))


def attention_adam_kernel(place_ref, settings_ref, mine_one, other_one, mine_two, other_two, *refs):
    core = place_of(place_ref)[0]
    matrices, bias, vectors = refs[0:3], refs[3:6], refs[6:9]
    new_matrices, new_bias, new_vectors = refs[9:12], refs[12:15], refs[15:18]
    half = mine_one.shape[1]
    shard = matrices[0].shape[1]
    for step, one_ref, two_ref in ((0, mine_one, mine_two), (1, other_one, other_two)):
        cols = pl.ds(pl.multiple_of(jnp.bitwise_xor(core, step) * half, half), half)
        for index in range(8):
            ref, at = (one_ref, index) if index < 3 else (two_ref, index - 3)
            where = (index, slice(None), cols)
            now, one, two = (r[where] for r in matrices)
            grad = ref[at * shard : (at + 1) * shard, :]
            store_step(new_matrices, where, adam_step(settings_ref, now, grad, one, two, True))
    small = mine_two[5 * shard :, :] + other_two[5 * shard :, :]
    for group, new, grad in (
        (bias, new_bias, small[10:11, : bias[0].shape[1]]),
        (vectors, new_vectors, small[:10, : vectors[0].shape[1]]),
    ):
        now, one, two = (r[...] for r in group)
        store_step(new, ..., adam_step(settings_ref, now, grad, one, two, False))


def adam_call(kernel, scalars, grads, params):
    return call(
        kernel, (*scalars, *grads, *params), [(p.shape, F32) for p in params], [], 32, 10**7, smem=(0, 1)
    )


CORE_SWAP = [(0, 1), (1, 0), (2, 3), (3, 2)]
CHIP_SWAP = [(0, 2), (2, 0), (1, 3), (3, 1)]
ROW_SWAP = [(i, i ^ 1) for i in range(8)]


LINES = [[0, 2, 4, 6], [1, 3, 5, 7]]


def line_shift(step):
    return [(2 * z + y, 2 * ((z + step) % 4) + y) for z in range(4) for y in (0, 1)]


def small_mesh(mesh):
    return mesh.shape["rep"] == 4 and mesh.shape["fsdp"] == 8


def gather_staged(pack):
    quarter = pack.shape[0] // 4
    mine = lax.dynamic_slice_in_dim(pack, lax.axis_index("rep") * quarter, quarter, 0)
    pair = jnp.stack([mine, lax.ppermute(mine, "fsdp", ROW_SWAP)])
    part = jnp.stack([pair] + [lax.ppermute(pair, "fsdp", line_shift(step)) for step in (1, 2, 3)])
    both = jnp.stack([part, lax.ppermute(part, "rep", CHIP_SWAP)])
    return jnp.stack([both, lax.ppermute(both, "rep", CORE_SWAP)])


def gather_halves(pack):
    half = pack.shape[1] // 2
    mine = lax.dynamic_slice_in_dim(pack, lax.axis_index("rep") % 2 * half, half, 1)
    mine = lax.all_gather(mine, "fsdp", axis=0)
    return mine, lax.ppermute(mine, "rep", CORE_SWAP)


def low_sum(mine, received):
    return (mine.astype(F32) + received.astype(F32)).astype(BF)


def reduce_rows(keep, send):
    received = lax.ppermute(send, "rep", CORE_SWAP)
    away = lax.ppermute(low_sum(keep[1], received[1]), "fsdp", ROW_SWAP)
    return low_sum(low_sum(keep[0], received[0]), away)


def reduce_last(part):
    total = part.astype(F32) + lax.ppermute(part, "rep", CHIP_SWAP).astype(F32)
    return total, lax.ppermute(total, "rep", CORE_SWAP)


def reduce_line(grads):
    return reduce_last(
        lax.psum_scatter(
            reduce_rows(*grads), "fsdp", scatter_dimension=0, axis_index_groups=LINES
        ).reshape(grads[0].shape[2:])
    )


def reduce_shifts(grads):
    line = lax.axis_index("fsdp") // 2
    joined = reduce_rows(*grads)
    total = lax.dynamic_index_in_dim(joined, line, 0, False).astype(F32)
    for step in (1, 2, 3):
        away = lax.dynamic_index_in_dim(joined, (line + step) % 4, 0, False)
        total = total + lax.ppermute(away, "fsdp", line_shift(step)).astype(F32)
    return reduce_last(total.astype(BF))


def reduce_plain(grads):
    return lax.psum(lax.psum_scatter(grads, "fsdp", scatter_dimension=0), "rep").astype(F32)


def adam_update(weight_now, gradient, moment_one, moment_two, settings, step_float, factor):
    learn_rate, beta_one, beta_two, decay_rate = settings[0], settings[1], settings[2], settings[3]
    first_new = beta_one * moment_one + (1.0 - beta_one) * gradient
    second_new = beta_two * moment_two + (1.0 - beta_two) * gradient * gradient
    first_hat = first_new / (1.0 - beta_one**step_float)
    second_hat = second_new / (1.0 - beta_two**step_float)
    change = first_hat / (jnp.sqrt(second_hat) + 1e-08) + factor * decay_rate * weight_now
    return (weight_now - learn_rate * change, first_new, second_new)


def per_device(
    small, inputs, memory, memory_length, target_pos, cotangent,
    attention_weights, expand_weights, shrink_weights, expand_bias, layer_vectors,
    first_attention, first_expand, first_shrink, first_bias, first_vectors,
    second_attention, second_expand, second_shrink, second_bias, second_vectors,
    hyper_rates, step_count,
):
    length, width = inputs.shape[1:]
    shard = attention_weights.shape[1]
    count = width // shard
    inner_shard = shrink_weights.shape[0]
    blocks = inner_shard // shard
    low_attention = attention_weights.astype(BF).reshape(8 * shard, width)
    pack_one = low_attention[: 3 * shard]
    pack_three = jnp.concatenate(
        [
            expand_weights.astype(BF).reshape(shard, blocks, width).transpose(1, 0, 2).reshape(-1, width),
            shrink_weights.astype(BF),
        ]
    )
    x, source, cot = inputs[0], memory[0], cotangent[0]
    start = (jnp.arange(length, dtype=jnp.int32) - target_pos[0])[:, None]
    step_float = step_count.astype(F32)

    if small:
        place = jnp.stack([lax.axis_index("rep"), lax.axis_index("fsdp")]).astype(jnp.int32)
        small_rows = jnp.concatenate(
            [
                jnp.pad(layer_vectors, ((0, 0), (0, inner_shard - shard))),
                expand_bias[None],
                jnp.zeros((5, inner_shard), F32),
            ]
        )
        small_rows = jnp.pad(small_rows, ((0, 0), (0, width - inner_shard))).astype(BF)
        pack_two = jnp.concatenate([low_attention[3 * shard :], small_rows])
        one = gather_staged(pack_one)
        two = gather_halves(pack_two)
        three = gather_halves(pack_three)
        given = None
        cross_shards = (*(shard,) * 5, 16)
        hidden_shards = (*(shard,) * blocks, inner_shard)
    else:
        place, cross_shards, hidden_shards = None, None, None
        flat = jnp.concatenate([layer_vectors.reshape(-1), expand_bias]).astype(BF)
        flat = lax.all_gather(flat, "fsdp", axis=0).astype(F32)
        vector_size = layer_vectors.size
        vec = flat[:, :vector_size].reshape(count, -1, shard).transpose(1, 0, 2).reshape(-1, width)
        given = jnp.pad(vec, ((0, 16 - vec.shape[0]), (0, 0))), flat[:, vector_size:].reshape(1, -1)

        def gather_all(pack, shards):
            full = lax.all_gather(pack, "fsdp", axis=0)
            pieces, first = [], 0
            for rows in shards:
                pieces.append(full[:, first : first + rows].reshape(-1, width))
                first += rows
            return jnp.concatenate(pieces)

        def owners(grads, shards):
            pieces, first = [], 0
            for rows in shards:
                pieces.append(grads[first : first + rows * count].reshape(count, rows, width))
                first += rows * count
            return jnp.concatenate(pieces, axis=1)

        one = gather_all(pack_one, (shard,) * 3)
        two = gather_all(low_attention[3 * shard :], (shard,) * 5)
        three = gather_all(pack_three, (*(shard,) * blocks, inner_shard))

    *saved_one, matrices = forward_self(place, x, start, one, small)
    norm_one, inv_one, *saved_two, norm_two, inv_two, cross_matrices, vec, bias = forward_cross(
        place, x, saved_one[3], source, memory_length, two, given, cross_shards
    )
    outputs, dz_two, *grad_three, sums_three, bias_sum = hidden_step(
        place, three, norm_two, inv_two, cot, vec, bias, hidden_shards
    )
    *grad_two, dz_one, memory_grad, sums_two = backward_cross(
        place, dz_two, x, norm_one, inv_one, source, memory_length, vec, cross_matrices, saved_two, saved_one[3],
        (sums_three, bias_sum) if small else None,
    )
    *grad_one, input_grad = backward_self(
        place, dz_one, x, start, vec, cross_matrices, matrices, saved_one, small
    )

    attention = (attention_weights, first_attention, second_attention)
    expand = (expand_weights, first_expand, second_expand)
    shrink = (shrink_weights, first_shrink, second_shrink)
    bias = (expand_bias, first_bias, second_bias)
    vectors = (layer_vectors, first_vectors, second_vectors)
    if small:
        powers = 1.0 - hyper_rates[1:3] ** step_float
        scalars = place, jnp.concatenate([hyper_rates, powers])
        total_three = reduce_line(grad_three)
        total_two = reduce_line(grad_two)
        total_one = reduce_shifts(grad_one)
        hidden_new = adam_call(hidden_adam_kernel, scalars, total_three, (*expand, *shrink))
        rows = tuple(b[None] for b in bias)
        other_new = adam_call(
            attention_adam_kernel, scalars, (*total_one, *total_two), (*attention, *rows, *vectors)
        )
        new_bias = tuple(b[0] for b in other_new[3:6])
        updated = (*other_new[:3], *hidden_new, *new_bias, *other_new[6:])
    else:
        sums = (sums_two + sums_three)[: layer_vectors.shape[0]]
        flat = jnp.concatenate(
            [
                sums.reshape(-1, count, shard).transpose(1, 0, 2).reshape(count, -1),
                bias_sum.reshape(count, inner_shard),
            ],
            axis=1,
        )
        total_three = reduce_plain(owners(grad_three[0], (*(shard,) * blocks, inner_shard)))
        total_two = reduce_plain(owners(grad_two[0], (shard,) * 5))
        total_one = reduce_plain(owners(grad_one[0], (shard,) * 3))
        flat = lax.psum(lax.psum_scatter(flat, "fsdp", scatter_dimension=0), "rep")
        grad_attention = jnp.concatenate([total_one, total_two]).reshape(attention_weights.shape)
        grad_expand = total_three[: blocks * shard].reshape(blocks, shard, width).transpose(1, 0, 2)
        updated = []
        for (now, one_now, two_now), grad, factor in (
            (attention, grad_attention, 1.0),
            (expand, grad_expand.reshape(shard, -1), 1.0),
            (shrink, total_three[blocks * shard :], 1.0),
            (bias, flat[layer_vectors.size :], 0.0),
            (vectors, flat[: layer_vectors.size].reshape(-1, shard), 0.0),
        ):
            updated.extend(adam_update(now, grad, one_now, two_now, hyper_rates, step_float, factor))
    return (outputs[None], input_grad[None], memory_grad[None], *updated)


def solution(mesh):
    rows = ("rep", "fsdp")
    params = (P(None, "fsdp", None), P("fsdp", None), P("fsdp", None), P("fsdp"), P(None, "fsdp"))
    return jax.shard_map(
        functools.partial(per_device, small_mesh(mesh)),
        mesh=mesh,
        in_specs=(
            P(rows, None, None), P(rows, None, None), P(rows), P(rows, None), P(rows, None, None),
            *params, *params, *params, P(), P(),
        ),
        out_specs=(
            P(rows, None, None), P(rows, None, None), P(rows, None, None),
            *(spec for spec in params for _ in range(3)),
        ),
        check_vma=False,
    )
```

```python
import functools

import jax
import jax.numpy as jnp
from jax import lax
from jax.experimental import pallas as pl
from jax.experimental.pallas import tpu as pltpu
from jax.sharding import PartitionSpec as P

BF = jnp.bfloat16
F32 = jnp.float32
HEAD_DIM = 64
PAIR = 128
TILE = 256
MIB = 1 << 20


def dot(left, right, left_dim, right_dim):
    return lax.dot_general(
        left, right, (((left_dim,), (right_dim,)), ((), ())), preferred_element_type=F32
    )


def lanes(size):
    return lax.broadcasted_iota(jnp.int32, (1, size), 1)


def half_masks():
    first = jnp.where(lanes(PAIR) < HEAD_DIM, 1.0, 0.0)
    return first.astype(BF), (1.0 - first).astype(BF)


def rows_at(index, size=TILE):
    return pl.ds(pl.multiple_of(index * size, size), size)


def split_three(column):
    high = column.astype(BF).astype(F32)
    rest = column - high
    middle = rest.astype(BF).astype(F32)
    return high, middle, rest - middle


def with_column(block, column, base, last):
    high, middle, low = split_three(column)
    lane = lanes(PAIR)
    tail = jnp.where(lane == base + 3, last, block)
    return jnp.where(
        lane == base, -high, jnp.where(lane == base + 1, -middle, jnp.where(lane == base + 2, -low, tail))
    ).astype(BF)


def weight(all_ref, index):
    width = all_ref.shape[1]
    return all_ref[index * width : (index + 1) * width, :]


def key_extra(length_limit, count):
    lane = lanes(PAIR) % HEAD_DIM
    extra = jnp.where(lane < 3, 1.0, 0.0)
    if length_limit is None:
        return jnp.broadcast_to(extra, (count, PAIR)).astype(BF)
    row = lax.broadcasted_iota(jnp.int32, (count, PAIR), 0)
    bias = jnp.where(row < length_limit, 0.0, -1e30)
    return jnp.where(lane == 3, bias, extra).astype(BF)


def put_start(pos_ref, start_ref):
    length = start_ref.shape[0]
    query = lax.broadcasted_iota(jnp.int32, (8, length), 1)
    first = (query - pos_ref[...]).astype(F32)
    start_ref[...] = first.T[:, :1].astype(jnp.int32)


def visible(start, first_query, first_key, count):
    key = first_key + lax.broadcasted_iota(jnp.int32, (TILE, count), 1)
    seen = key >= start
    if first_key == first_query:
        query = first_query + lax.broadcasted_iota(jnp.int32, (TILE, count), 0)
        seen = seen & (key <= query)
    return seen


def key_spans(tile, count, causal):
    if not causal:
        return [(0, count)]
    spans = [(0, tile * TILE)] if tile else []
    return spans + [(tile * TILE, TILE)]


def attend(q_ref, k_ref, v_ref, extra_ref, start_ref, qa_ref, o_ref):
    length, count = q_ref.shape[0], k_ref.shape[0]
    causal = start_ref is not None
    masks = half_masks()

    @pl.loop(0, q_ref.shape[1] // PAIR)
    def _(pair):
        cols = rows_at(pair, PAIR)
        for tile in range(length // TILE):
            rows = slice(tile * TILE, (tile + 1) * TILE)
            spans = key_spans(tile, count, causal)
            results = []
            for side in (0, 1):
                base = HEAD_DIM * (1 - side)
                lane = lanes(PAIR)
                queries = q_ref[rows, cols] * masks[side]
                queries_f = queries.astype(F32)
                if not causal:
                    queries = jnp.where(lane == base + 3, 1.0, queries_f).astype(BF)
                score_blocks = []
                for first, size in spans:
                    keys = k_ref[first : first + size, cols] * masks[side]
                    if not causal:
                        keys = keys + extra_ref[first : first + size, :] * masks[1 - side]
                    scores = dot(queries, keys, 1, 1)
                    if causal:
                        seen = visible(start_ref[rows, :], tile * TILE, first, size)
                        scores = jnp.where(seen, scores, -1000000000.0)
                    score_blocks.append(scores)
                top = functools.reduce(
                    jnp.maximum, [jnp.max(scores, axis=1, keepdims=True) for scores in score_blocks]
                )
                total = None
                for scores, (first, size) in zip(score_blocks, spans):
                    values = v_ref[first : first + size, cols] * masks[side] + masks[1 - side]
                    probs = jnp.exp(scores - top).astype(BF)
                    part = dot(probs, values, 1, 0)
                    total = part if total is None else total + part
                results.append(total / pltpu.roll(total, HEAD_DIM, 1))
                log_total = top + jnp.log(total[:, base : base + 1])
                qa_ref[rows, pl.ds(pl.multiple_of(pair * 2 * PAIR, PAIR) + side * PAIR, PAIR)] = with_column(
                    queries_f, log_total, base, 0.0 if causal else 1.0
                )
            o_ref[rows, cols] = jnp.where(lanes(PAIR) < HEAD_DIM, results[0], results[1]).astype(BF)


def attend_back(qa_ref, da_ref, k_ref, v_ref, extra_ref, start_ref, dq_ref, dk_ref, dv_ref, dk_sum, dv_sum):
    length, count = qa_ref.shape[0], k_ref.shape[0]
    causal = start_ref is not None
    masks = half_masks()

    @pl.loop(0, k_ref.shape[1] // PAIR)
    def _(pair):
        cols = rows_at(pair, PAIR)
        for tile in reversed(range(length // TILE)):
            rows = slice(tile * TILE, (tile + 1) * TILE)
            query_grads = []
            for side in (0, 1):
                head_cols = pl.ds(pl.multiple_of(pair * 2 * PAIR, PAIR) + side * PAIR, PAIR)
                queries = qa_ref[rows, head_cols]
                grads = da_ref[rows, head_cols]
                query_grad = None
                for first, size in key_spans(tile, count, causal):
                    span = slice(first, first + size)
                    keys = k_ref[span, cols]
                    keys_low = keys * masks[side] + extra_ref[span, :] * masks[1 - side]
                    values = v_ref[span, cols] * masks[side] + masks[1 - side]
                    probs = jnp.exp(dot(queries, keys_low, 1, 1))
                    if causal:
                        seen = visible(start_ref[rows, :], tile * TILE, first, size)
                        probs = jnp.where(seen, probs, 0.0)
                    grad_scores = (probs * dot(grads, values, 1, 1)).astype(BF)
                    value_part = dot(grads, probs.astype(BF), 0, 0)
                    key_part = dot(queries, grad_scores, 0, 0)
                    if tile == length // TILE - 1:
                        dv_sum[side, :, span] = value_part
                        dk_sum[side, :, span] = key_part
                    else:
                        dv_sum[side, :, span] += value_part
                        dk_sum[side, :, span] += key_part
                    part = dot(grad_scores, keys, 1, 0)
                    query_grad = part if query_grad is None else query_grad + part
                query_grads.append(query_grad)
            dq_ref[rows, cols] = (
                jnp.where(lanes(PAIR) < HEAD_DIM, query_grads[0], query_grads[1]) * HEAD_DIM**-0.5
            ).astype(BF)
        for sums, out in ((dk_sum, dk_ref), (dv_sum, dv_ref)):
            joined = jnp.concatenate([sums[0, :HEAD_DIM, :], sums[1, HEAD_DIM:, :]], axis=0)
            out[:, cols] = joined.astype(BF).T


def norm_rows(summed):
    center = jnp.mean(summed, axis=1, keepdims=True)
    shifted = summed - center
    inverse = lax.rsqrt(jnp.mean(shifted * shifted, axis=1, keepdims=True) + 1e-05)
    return shifted * inverse, inverse


def norm_back(grad_out, normed, inverse, gain):
    scaled = grad_out * gain
    first = jnp.mean(scaled, axis=1, keepdims=True)
    second = jnp.mean(scaled * normed, axis=1, keepdims=True)
    return inverse * (scaled - first - normed * second)


def add_rows(ref, row, values):
    ref[row : row + 1, :] += jnp.sum(values, axis=0, keepdims=True)


def place_of(place_ref):
    rep, place = place_ref[0], place_ref[1]
    return lax.rem(rep, 2), lax.div(rep, 2), lax.div(place, 2), lax.rem(place, 2)


def assemble(place_ref, chunk_refs, all_ref):
    core, chip, line, row = place_of(place_ref)
    width = all_ref.shape[1]
    quarter = chunk_refs[0].shape[3]
    shard = quarter * 4 // 3
    for core_step, chunk_ref in enumerate(chunk_refs):
        for chip_step in (0, 1):
            rep = jnp.bitwise_xor(chip, chip_step) * 2 + jnp.bitwise_xor(core, core_step)
            for line_step in range(4):
                for row_step in (0, 1):
                    owner = lax.rem(line - line_step + 4, 4) * 2 + jnp.bitwise_xor(row, row_step)
                    for piece in range(quarter // 16):
                        stacked = rep * quarter + piece * 16
                        matrix = lax.div(stacked, shard)
                        target = matrix * width + owner * shard + (stacked - matrix * shard)
                        all_ref[pl.ds(pl.multiple_of(target, 16), 16), :] = chunk_ref[
                            chip_step, line_step, row_step, piece * 16 : (piece + 1) * 16, :
                        ]


def assemble_halves(place_ref, mine_ref, other_ref, all_ref, shards):
    core = place_of(place_ref)[0]
    devices, _, half = mine_ref.shape
    for step, ref in ((0, mine_ref), (1, other_ref)):
        cols = pl.ds(pl.multiple_of(jnp.bitwise_xor(core, step) * half, half), half)
        first, target = 0, 0
        for shard in shards:
            for owner in range(devices):
                at = target + owner * shard
                all_ref[at : at + shard, cols] = ref[owner, first : first + shard, :]
            first += shard
            target += shard * devices


def unpack_small(all_ref, base, vec_ref, bias_ref):
    devices = vec_ref.shape[1] // HEAD_DIM
    inner = bias_ref.shape[1] // devices
    for pair in range(devices // 2):
        first = base + 2 * pair * 16
        left = all_ref[first : first + 16, :PAIR].astype(F32)
        right = all_ref[first + 16 : first + 32, :PAIR].astype(F32)
        vec_ref[:, pair * PAIR : (pair + 1) * PAIR] = jnp.where(
            lanes(PAIR) < HEAD_DIM, left, pltpu.roll(right, HEAD_DIM, 1)
        )
    for owner in range(devices):
        rows = all_ref[base + owner * 16 : base + owner * 16 + 16, :inner].astype(F32)
        bias_ref[:, owner * inner : (owner + 1) * inner] = rows[10:11, :]


def self_forward_kernel(staged, *refs):
    if staged:
        place_ref, x_ref, pos_ref, chunk_ref, other_ref, qa_ref, k_ref, v_ref, o_ref, all_ref, q_ref, start_ref = refs
        assemble(place_ref, (chunk_ref, other_ref), all_ref)
    else:
        x_ref, pos_ref, all_ref, qa_ref, k_ref, v_ref, o_ref, q_ref, start_ref = refs
    length, width = x_ref.shape
    put_start(pos_ref, start_ref)

    @pl.loop(0, length // TILE)
    def _(tile):
        rows = rows_at(tile)
        source = x_ref[rows, :]
        queries = dot(source, all_ref[:width, :], 1, 0).astype(BF)
        q_ref[rows, :] = queries * jnp.asarray(HEAD_DIM**-0.5, BF)
        k_ref[rows, :] = dot(source, all_ref[width : 2 * width, :], 1, 0).astype(BF)
        v_ref[rows, :] = dot(source, all_ref[2 * width :, :], 1, 0).astype(BF)

    attend(q_ref, k_ref, v_ref, None, start_ref, qa_ref, o_ref)


def cross_forward_kernel(shards, *refs):
    if shards:
        place_ref, x_ref, mixed_ref, source_ref, length_ref, mine_ref, other_ref = refs[:7]
        first_ref, first_inv_ref, qa_ref, k_ref, v_ref, o_ref, n_ref, inv_ref, w_ref, vec_ref, bias_ref = refs[7:18]
        q_ref, extra_ref = refs[18:]
        assemble_halves(place_ref, mine_ref, other_ref, w_ref, shards)
        unpack_small(w_ref, 5 * w_ref.shape[1], vec_ref, bias_ref)
    else:
        (x_ref, mixed_ref, source_ref, length_ref, w_ref, vec_ref) = refs[:6]
        first_ref, first_inv_ref, qa_ref, k_ref, v_ref, o_ref, n_ref, inv_ref, q_ref, extra_ref = refs[6:]
    length = q_ref.shape[0]
    extra_ref[...] = key_extra(length_ref[0], k_ref.shape[0])

    @pl.loop(0, length // TILE)
    def _(tile):
        rows = rows_at(tile)
        summed = x_ref[rows, :].astype(F32) * vec_ref[6:7, :] + dot(
            mixed_ref[rows, :], weight(w_ref, 0), 1, 0
        )
        normed, inverse = norm_rows(summed)
        first_ref[rows, :] = normed
        first_inv_ref[rows, :] = inverse
        low = (normed * vec_ref[0:1, :] + vec_ref[3:4, :]).astype(BF)
        queries = dot(low, weight(w_ref, 1), 1, 0).astype(BF)
        q_ref[rows, :] = queries * jnp.asarray(HEAD_DIM**-0.5, BF)

    @pl.loop(0, source_ref.shape[0] // TILE)
    def _(tile):
        rows = rows_at(tile)
        source = source_ref[rows, :]
        k_ref[rows, :] = dot(source, weight(w_ref, 2), 1, 0).astype(BF)
        v_ref[rows, :] = dot(source, weight(w_ref, 3), 1, 0).astype(BF)

    attend(q_ref, k_ref, v_ref, extra_ref, None, qa_ref, o_ref)

    @pl.loop(0, length // TILE)
    def _(tile):
        rows = rows_at(tile)
        first_out = first_ref[rows, :] * vec_ref[0:1, :] + vec_ref[3:4, :]
        summed = first_out * vec_ref[7:8, :] + dot(o_ref[rows, :], weight(w_ref, 4), 1, 0)
        normed, inverse = norm_rows(summed)
        n_ref[rows, :] = normed
        inv_ref[rows, :] = inverse


def hidden_kernel(shards, *refs):
    place_ref = refs[0] if shards else None
    if shards:
        (
            place_ref, mine_ref, other_ref, n_ref, inv_ref, cot_ref, vec_ref, bias_ref,
            out_ref, dz_ref, keep_ref, send_ref, sums_ref, bias_sum_ref,
            w_ref, low_ref, h_ref, du_ref, df_ref, slope_ref,
        ) = refs
        grad_refs = (keep_ref, send_ref)
        assemble_halves(place_ref, mine_ref, other_ref, w_ref, shards)
    else:
        (
            w_ref, n_ref, inv_ref, cot_ref, vec_ref, bias_ref,
            out_ref, dz_ref, grad_ref, sums_ref, bias_sum_ref,
            low_ref, h_ref, du_ref, df_ref, slope_ref,
        ) = refs
        grad_refs = (grad_ref,)
    length, width = n_ref.shape
    sums_ref[...] = jnp.zeros_like(sums_ref)
    bias_sum_ref[...] = jnp.zeros_like(bias_sum_ref)
    blocks = bias_ref.shape[1] // width

    def expand(block):
        return weight(w_ref, block)

    def shrink_all():
        return w_ref[blocks * width :, :]

    @pl.loop(0, length // TILE)
    def _(tile):
        rows = rows_at(tile)
        gain, shift = vec_ref[1:2, :], vec_ref[4:5, :]
        second_out = n_ref[rows, :] * gain + shift
        low = second_out.astype(BF)
        low_ref[rows, :] = low
        summed = second_out * vec_ref[8:9, :] + vec_ref[9:10, :]
        shrink = shrink_all()
        for block in range(blocks):
            cols = slice(block * width, (block + 1) * width)
            before = dot(low, expand(block), 1, 0) + bias_ref[:, cols]
            square = before * before
            tangent = jnp.tanh(0.7978845608028654 * (before + 0.044715 * before * square))
            half = 0.5 * (1.0 + tangent)
            slope_ref[:, cols] = half + 0.5 * before * (1.0 - tangent * tangent) * 0.7978845608028654 * (
                1.0 + 3.0 * 0.044715 * square
            )
            hidden = (before * half).astype(BF)
            h_ref[rows, cols] = hidden
            summed = summed + dot(hidden, shrink[cols, :], 1, 0)
        normed, inverse = norm_rows(summed)
        out_ref[rows, :] = (normed * vec_ref[2:3, :] + vec_ref[5:6, :]).astype(BF)
        grad_out = cot_ref[rows, :].astype(F32)
        third = norm_back(grad_out, normed, inverse, vec_ref[2:3, :])
        add_rows(sums_ref, 2, grad_out * normed)
        add_rows(sums_ref, 5, grad_out)
        branch = third.astype(BF)
        df_ref[rows, :] = branch
        add_rows(sums_ref, 9, branch.astype(F32))
        add_rows(sums_ref, 8, second_out * third)
        grad_second = vec_ref[8:9, :] * third
        for block in range(blocks):
            cols = slice(block * width, (block + 1) * width)
            du = (dot(branch, shrink[cols, :], 1, 1) * slope_ref[:, cols]).astype(BF)
            du_ref[rows, cols] = du
            bias_sum_ref[:, cols] += jnp.sum(du.astype(F32), axis=0, keepdims=True)
            grad_second = grad_second + dot(du, expand(block), 1, 1)
        normed_two = n_ref[rows, :]
        dz_ref[rows, :] = norm_back(grad_second, normed_two, inv_ref[rows, :], gain)
        add_rows(sums_ref, 1, grad_second * normed_two)
        add_rows(sums_ref, 4, grad_second)

    for block in range(blocks):
        cols = slice(block * width, (block + 1) * width)
        put_grad(grad_refs, place_ref, block, low_ref[...], du_ref, block * width)
        put_shrink(grad_refs, place_ref, block, blocks, h_ref[:, cols], df_ref)


def branch_grads(branch, mixed_weight, o_rows, da_ref, rows):
    masks = half_masks()
    mixed_grad = dot(branch, mixed_weight, 1, 1).astype(BF)
    for pair in range(mixed_grad.shape[1] // PAIR):
        cols = slice(pair * PAIR, (pair + 1) * PAIR)
        grad_pair = mixed_grad[:, cols].astype(F32)
        product = grad_pair * o_rows[:, cols].astype(F32)
        for side in (0, 1):
            mask = masks[side].astype(F32)
            inner = jnp.sum(product * mask, axis=1, keepdims=True)
            first = (2 * pair + side) * PAIR
            da_ref[rows, first : first + PAIR] = with_column(
                grad_pair * mask, inner, HEAD_DIM * (1 - side), 0.0
            )


def put_grad(grad_refs, place_ref, index, left, right_ref, first=0):
    width = left.shape[1]
    if place_ref is None:
        grad = dot(left, right_ref[:, first : first + width], 0, 0)
        grad_refs[0][index * width : (index + 1) * width, :] = grad.astype(BF)
        return
    core, _, _, row = place_of(place_ref)
    half = width // 2
    shard = width // 8
    for step, grad_ref in enumerate(grad_refs):
        cols = pl.ds(pl.multiple_of(first + jnp.bitwise_xor(core, step) * half, half), half)
        grad = dot(left, right_ref[:, cols], 0, 0).astype(BF).reshape(4, 2, shard, half)
        for side in (0, 1):
            slot = jnp.bitwise_xor(row, side)
            grad_ref[slot, :, index * shard : (index + 1) * shard, :] = grad[:, side]


def put_shrink(grad_refs, place_ref, block, blocks, left, right_ref):
    width = left.shape[1]
    if place_ref is None:
        first = (blocks + block) * width
        grad_refs[0][first : first + width, :] = dot(left, right_ref[...], 0, 0).astype(BF)
        return
    core, _, _, row = place_of(place_ref)
    half, shard = width // 2, width * blocks // 8
    base = width // 8 * blocks
    for step, grad_ref in enumerate(grad_refs):
        cols = pl.ds(pl.multiple_of(jnp.bitwise_xor(core, step) * half, half), half)
        grad = dot(left, right_ref[:, cols], 0, 0).astype(BF).reshape(width // shard, shard, half)
        for part in range(width // shard):
            owner = block * (width // shard) + part
            grad_ref[jnp.bitwise_xor(row, owner % 2), owner // 2, base:, :] = grad[part]


def put_small(grad_refs, place_ref, base, sums, bias_sum):
    core, _, _, row = place_of(place_ref)
    half = grad_refs[0].shape[3]
    inner = bias_sum.shape[1] // 8
    index = lax.broadcasted_iota(jnp.int32, (16, half), 0)
    for owner in range(8):
        block = sums[:, owner // 2 * PAIR : (owner // 2 + 1) * PAIR]
        if owner % 2:
            block = pltpu.roll(block, HEAD_DIM, 1)
        block = jnp.concatenate([block, jnp.zeros((16, half - PAIR), F32)], axis=1)
        block = jnp.where(index == 10, bias_sum[:, owner * inner : (owner + 1) * inner], block)
        high = block.astype(BF)
        low = (block - high.astype(F32)).astype(BF)
        slot = jnp.bitwise_xor(row, owner % 2)
        first = (core == 0).astype(F32)
        for step, grad_ref in enumerate(grad_refs):
            is_high = first if step == 0 else 1.0 - first
            mixed = high.astype(F32) * is_high + low.astype(F32) * (1.0 - is_high)
            grad_ref[slot, owner // 2, base : base + 16, :] = mixed.astype(BF)


def cross_backward_kernel(staged, *refs):
    place_ref = refs[0] if staged else None
    refs = refs[1:] if staged else refs
    (dz_ref, x_ref, first_ref, inv_ref, source_ref, length_ref, vec_ref, w_ref) = refs[:8]
    (qa_ref, k_ref, v_ref, o_ref, self_o_ref) = refs[8:13]
    if staged:
        sums_three_ref, bias_sum_ref, keep_ref, send_ref, dfirst_ref, dsource_ref, sums_ref = refs[13:20]
        scratch, grad_refs = refs[20:], (keep_ref, send_ref)
    else:
        grad_ref, dfirst_ref, dsource_ref, sums_ref = refs[13:17]
        scratch, grad_refs = refs[17:], (grad_ref,)
    low_ref, da_ref, dq_ref, dk_ref, dv_ref, dk_sum, dv_sum, branch_ref, extra_ref = scratch
    length = dz_ref.shape[0]
    sums_ref[...] = jnp.zeros_like(sums_ref)
    extra_ref[...] = key_extra(length_ref[0], k_ref.shape[0])

    @pl.loop(0, length // TILE)
    def _(tile):
        rows = rows_at(tile)
        grad = dz_ref[rows, :]
        branch = grad.astype(BF)
        branch_ref[rows, :] = branch
        first_out = first_ref[rows, :] * vec_ref[0:1, :] + vec_ref[3:4, :]
        low_ref[rows, :] = first_out.astype(BF)
        add_rows(sums_ref, 7, first_out * grad)
        branch_grads(branch, weight(w_ref, 4), o_ref[rows, :], da_ref, rows)

    attend_back(qa_ref, da_ref, k_ref, v_ref, extra_ref, None, dq_ref, dk_ref, dv_ref, dk_sum, dv_sum)

    put_grad(grad_refs, place_ref, 1, low_ref[...], dq_ref)
    put_grad(grad_refs, place_ref, 2, source_ref[...], dk_ref)
    put_grad(grad_refs, place_ref, 3, source_ref[...], dv_ref)
    put_grad(grad_refs, place_ref, 4, o_ref[...], branch_ref)

    @pl.loop(0, length // TILE)
    def _(tile):
        rows = rows_at(tile)
        dx = dot(dq_ref[rows, :], weight(w_ref, 1), 1, 1) + vec_ref[7:8, :] * dz_ref[rows, :]
        normed = first_ref[rows, :]
        dfirst = norm_back(dx, normed, inv_ref[rows, :], vec_ref[0:1, :])
        dfirst_ref[rows, :] = dfirst
        add_rows(sums_ref, 0, dx * normed)
        add_rows(sums_ref, 3, dx)
        add_rows(sums_ref, 6, x_ref[rows, :].astype(F32) * dfirst)
        branch_ref[rows, :] = dfirst.astype(BF)

    @pl.loop(0, source_ref.shape[0] // TILE)
    def _(tile):
        rows = rows_at(tile)
        dsource_ref[rows, :] = dot(dk_ref[rows, :], weight(w_ref, 2), 1, 1) + dot(
            dv_ref[rows, :], weight(w_ref, 3), 1, 1
        )

    put_grad(grad_refs, place_ref, 0, self_o_ref[...], branch_ref)
    if staged:
        put_small(
            grad_refs, place_ref, 5 * (w_ref.shape[1] // 8), sums_ref[...] + sums_three_ref[...], bias_sum_ref[...]
        )


def self_backward_kernel(staged, *refs):
    place_ref = refs[0] if staged else None
    refs = refs[1:] if staged else refs
    (dz_ref, x_ref, pos_ref, vec_ref, w_ref, all_ref, qa_ref, k_ref, v_ref, o_ref) = refs[:10]
    count = 2 if staged else 1
    grad_refs, dx_ref, scratch = refs[10 : 10 + count], refs[10 + count], refs[11 + count :]
    da_ref, dq_ref, dk_ref, dv_ref, dk_sum, dv_sum, extra_ref, start_ref = scratch
    length, width = dz_ref.shape
    put_start(pos_ref, start_ref)
    extra_ref[...] = key_extra(None, k_ref.shape[0])

    @pl.loop(0, length // TILE)
    def _(tile):
        rows = rows_at(tile)
        branch_grads(dz_ref[rows, :].astype(BF), weight(w_ref, 0), o_ref[rows, :], da_ref, rows)

    attend_back(qa_ref, da_ref, k_ref, v_ref, extra_ref, start_ref, dq_ref, dk_ref, dv_ref, dk_sum, dv_sum)

    for index, grads in enumerate((dq_ref, dk_ref, dv_ref)):
        put_grad(grad_refs, place_ref, index, x_ref[...], grads)

    @pl.loop(0, length // TILE)
    def _(tile):
        rows = rows_at(tile)
        dx = vec_ref[6:7, :] * dz_ref[rows, :]
        for index, grads in enumerate((dq_ref, dk_ref, dv_ref)):
            dx = dx + dot(grads[rows, :], all_ref[index * width : (index + 1) * width, :], 1, 1)
        dx_ref[rows, :] = dx


def call(kernel, args, outs, scratch, limit, flops, smem=()):
    in_specs = [
        pl.BlockSpec(memory_space=pltpu.SMEM if i in smem else pltpu.VMEM) for i in range(len(args))
    ]
    return pl.pallas_call(
        kernel,
        out_shape=[jax.ShapeDtypeStruct(shape, kind) for shape, kind in outs],
        in_specs=in_specs,
        out_specs=[pl.BlockSpec(memory_space=pltpu.VMEM)] * len(outs),
        scratch_shapes=[pltpu.VMEM(shape, kind) for shape, kind in scratch],
        compiler_params=pltpu.CompilerParams(vmem_limit_bytes=limit * MIB),
        cost_estimate=pl.CostEstimate(flops=flops, bytes_accessed=16 * MIB, transcendentals=0),
    )(*args)


def forward_self(place, x, start, pack, staged):
    length, width = x.shape
    low = ((length, width), BF)
    outs = [((length, 2 * width), BF), low, low, low]
    if staged:
        return call(
            functools.partial(self_forward_kernel, True),
            (place, x, start, *pack),
            [*outs, ((3 * width, width), BF)],
            [low, ((length, 1), jnp.int32)],
            48, 10**10, smem=(0,),
        )
    results = call(
        functools.partial(self_forward_kernel, False), (x, start, pack), outs, [low, ((length, 1), jnp.int32)], 48, 10**10
    )
    return (*results, pack)


def forward_cross(place, x, mixed, source, count, packs, small, shards):
    length, width = x.shape
    keys = source.shape[0]
    low, full, column = ((length, width), BF), ((length, width), F32), ((length, 1), F32)
    outs = [full, column, ((length, 2 * width), BF), ((keys, width), BF), ((keys, width), BF), low, full, column]
    scratch = [low, ((keys, PAIR), BF)]
    if shards:
        return call(
            functools.partial(cross_forward_kernel, shards),
            (place, x, mixed, source, count, *packs),
            [*outs, ((8 * sum(shards), width), BF), ((16, width), F32), ((1, 8 * shards[0] * 4), F32)],
            scratch,
            48, 10**10, smem=(0, 4),
        )
    vec, bias = small
    results = call(
        functools.partial(cross_forward_kernel, None),
        (x, mixed, source, count, packs, vec),
        outs, scratch, 48, 10**10, smem=(3,),
    )
    return (*results, packs, vec, bias)


def grad_outs(rows, width, staged):
    return [((2, 4, rows, width // 2), BF)] * 2 if staged else [((rows, width), BF)]


def hidden_step(place, packs, normed, inverse, cot, vec, bias, shards):
    length, width = normed.shape
    inner = bias.shape[1]
    args = (normed, inverse, cot, vec, bias)
    low = ((length, width), BF)
    scratch = [low, ((length, inner), BF), ((length, inner), BF), low, ((TILE, inner), F32)]
    matrices = ((2 * inner, width), BF)
    rows = sum(shards) if shards else 2 * inner
    return call(
        functools.partial(hidden_kernel, shards),
        (place, *packs, *args) if shards else (packs, *args),
        [low, ((length, width), F32), *grad_outs(rows, width, shards), ((16, width), F32), ((1, inner), F32)],
        [matrices, *scratch] if shards else scratch,
        60, 2 * 10**10, smem=(0,) if shards else (),
    )


def backward_cross(place, dz, x, normed, inverse, source, count, vec, matrices, saved, mixed, small):
    length, width = dz.shape
    keys = source.shape[0]
    args = (dz, x, normed, inverse, source, count, vec, matrices, *saved, mixed)
    low, key_low, sums = ((length, width), BF), ((keys, width), BF), ((2, PAIR, keys), F32)
    return call(
        functools.partial(cross_backward_kernel, small is not None),
        (place, *args, *small) if small else args,
        [*grad_outs(5 * width // 8 + 16 if small else 5 * width, width, small), ((length, width), F32),
         ((keys, width), F32), ((16, width), F32)],
        [low, ((length, 2 * width), BF), low, key_low, key_low, sums, sums, low, ((keys, PAIR), BF)],
        60, 2 * 10**10, smem=(0, 6) if small else (5,),
    )


def backward_self(place, dz, x, start, vec, cross_matrices, matrices, saved, staged):
    length, width = dz.shape
    args = (dz, x, start, vec, cross_matrices, matrices, *saved)
    low, sums = ((length, width), BF), ((2, PAIR, length), F32)
    return call(
        functools.partial(self_backward_kernel, staged),
        (place, *args) if staged else args,
        [*grad_outs(3 * width // 8 if staged else 3 * width, width, staged), ((length, width), F32)],
        [((length, 2 * width), BF), low, low, low, sums, sums, ((length, PAIR), BF), ((length, 1), jnp.int32)],
        60, 2 * 10**10, smem=(0,) if staged else (),
    )


def adam_step(settings_ref, now, grad, one, two, decay):
    beta_one, beta_two = settings_ref[1], settings_ref[2]
    first = beta_one * one + (1.0 - beta_one) * grad
    second = beta_two * two + (1.0 - beta_two) * grad * grad
    change = (first / settings_ref[4]) / (jnp.sqrt(second / settings_ref[5]) + 1e-08)
    if decay:
        change = change + settings_ref[3] * now
    return now - settings_ref[0] * change, first, second


def store_step(refs, where, results):
    for ref, value in zip(refs, results):
        ref[where] = value


def hidden_adam_kernel(place_ref, settings_ref, mine_ref, other_ref, *refs):
    core = place_of(place_ref)[0]
    expand, shrink = refs[0:3], refs[3:6]
    new_expand, new_shrink = refs[6:9], refs[9:12]
    half = mine_ref.shape[1]
    shard = expand[0].shape[0]
    blocks = expand[0].shape[1] // (2 * half)
    for step, ref in ((0, mine_ref), (1, other_ref)):
        side = jnp.bitwise_xor(core, step) * half
        cols = pl.ds(pl.multiple_of(side, half), half)
        for block in range(blocks):
            where = (slice(None), pl.ds(pl.multiple_of(block * 2 * half + side, half), half))
            grad = ref[block * shard : (block + 1) * shard, :]
            now, one, two = (r[where] for r in expand)
            store_step(new_expand, where, adam_step(settings_ref, now, grad, one, two, True))
        where = (slice(None), cols)
        now, one, two = (r[where] for r in shrink)
        store_step(new_shrink, where, adam_step(settings_ref, now, ref[blocks * shard :, :], one, two, True))


def attention_adam_kernel(place_ref, settings_ref, mine_one, other_one, mine_two, other_two, *refs):
    core = place_of(place_ref)[0]
    matrices, bias, vectors = refs[0:3], refs[3:6], refs[6:9]
    new_matrices, new_bias, new_vectors = refs[9:12], refs[12:15], refs[15:18]
    half = mine_one.shape[1]
    shard = matrices[0].shape[1]
    for step, one_ref, two_ref in ((0, mine_one, mine_two), (1, other_one, other_two)):
        cols = pl.ds(pl.multiple_of(jnp.bitwise_xor(core, step) * half, half), half)
        for index in range(8):
            ref, at = (one_ref, index) if index < 3 else (two_ref, index - 3)
            where = (index, slice(None), cols)
            now, one, two = (r[where] for r in matrices)
            grad = ref[at * shard : (at + 1) * shard, :]
            store_step(new_matrices, where, adam_step(settings_ref, now, grad, one, two, True))
    small = mine_two[5 * shard :, :] + other_two[5 * shard :, :]
    for group, new, grad in (
        (bias, new_bias, small[10:11, : bias[0].shape[1]]),
        (vectors, new_vectors, small[:10, : vectors[0].shape[1]]),
    ):
        now, one, two = (r[...] for r in group)
        store_step(new, ..., adam_step(settings_ref, now, grad, one, two, False))


def adam_call(kernel, scalars, grads, params):
    return call(
        kernel, (*scalars, *grads, *params), [(p.shape, F32) for p in params], [], 32, 10**7, smem=(0, 1)
    )


CORE_SWAP = [(0, 1), (1, 0), (2, 3), (3, 2)]
CHIP_SWAP = [(0, 2), (2, 0), (1, 3), (3, 1)]
ROW_SWAP = [(i, i ^ 1) for i in range(8)]


LINES = [[0, 2, 4, 6], [1, 3, 5, 7]]


def line_shift(step):
    return [(2 * z + y, 2 * ((z + step) % 4) + y) for z in range(4) for y in (0, 1)]


def small_mesh(mesh):
    return mesh.shape["rep"] == 4 and mesh.shape["fsdp"] == 8


def gather_staged(pack):
    quarter = pack.shape[0] // 4
    mine = lax.dynamic_slice_in_dim(pack, lax.axis_index("rep") * quarter, quarter, 0)
    pair = jnp.stack([mine, lax.ppermute(mine, "fsdp", ROW_SWAP)])
    part = jnp.stack([pair] + [lax.ppermute(pair, "fsdp", line_shift(step)) for step in (1, 2, 3)])
    both = jnp.stack([part, lax.ppermute(part, "rep", CHIP_SWAP)])
    return both, lax.ppermute(both, "rep", CORE_SWAP)


def after(value, *done):
    return lax.optimization_barrier((value, *done))[0]


def gather_half(pack):
    half = pack.shape[1] // 2
    mine = lax.dynamic_slice_in_dim(pack, lax.axis_index("rep") % 2 * half, half, 1)
    return lax.all_gather(mine, "fsdp", axis=0)


def both_halves(mine, done):
    mine = after(mine, done)
    return mine, lax.ppermute(mine, "rep", CORE_SWAP)


def low_sum(mine, received):
    return (mine.astype(F32) + received.astype(F32)).astype(BF)


def reduce_cores(keep, send):
    received = lax.ppermute(send, "rep", CORE_SWAP)
    return low_sum(keep[0], received[0]), low_sum(keep[1], received[1])


def send_rows(send):
    return lax.ppermute(send, "fsdp", ROW_SWAP)


def reduce_rows(keep, received, done):
    return low_sum(keep, after(received, done))


def reduce_last(part):
    total = part.astype(F32) + lax.ppermute(part, "rep", CHIP_SWAP).astype(F32)
    return total, lax.ppermute(total, "rep", CORE_SWAP)


def reduce_line(joined):
    part = lax.psum_scatter(joined, "fsdp", scatter_dimension=0, axis_index_groups=LINES)
    return part.reshape(joined.shape[1:])


def reduce_shifts(joined):
    line = lax.axis_index("fsdp") // 2
    total = lax.dynamic_index_in_dim(joined, line, 0, False).astype(F32)
    for step in (1, 2, 3):
        away = lax.dynamic_index_in_dim(joined, (line + step) % 4, 0, False)
        total = total + lax.ppermute(away, "fsdp", line_shift(step)).astype(F32)
    return total.astype(BF)


def reduce_plain(grads):
    return lax.psum(lax.psum_scatter(grads, "fsdp", scatter_dimension=0), "rep").astype(F32)


def adam_update(weight_now, gradient, moment_one, moment_two, settings, step_float, factor):
    learn_rate, beta_one, beta_two, decay_rate = settings[0], settings[1], settings[2], settings[3]
    first_new = beta_one * moment_one + (1.0 - beta_one) * gradient
    second_new = beta_two * moment_two + (1.0 - beta_two) * gradient * gradient
    first_hat = first_new / (1.0 - beta_one**step_float)
    second_hat = second_new / (1.0 - beta_two**step_float)
    change = first_hat / (jnp.sqrt(second_hat) + 1e-08) + factor * decay_rate * weight_now
    return (weight_now - learn_rate * change, first_new, second_new)


def per_device(
    small, inputs, memory, memory_length, target_pos, cotangent,
    attention_weights, expand_weights, shrink_weights, expand_bias, layer_vectors,
    first_attention, first_expand, first_shrink, first_bias, first_vectors,
    second_attention, second_expand, second_shrink, second_bias, second_vectors,
    hyper_rates, step_count,
):
    length, width = inputs.shape[1:]
    shard = attention_weights.shape[1]
    count = width // shard
    inner_shard = shrink_weights.shape[0]
    blocks = inner_shard // shard
    low_attention = attention_weights.astype(BF).reshape(8 * shard, width)
    pack_one = low_attention[: 3 * shard]
    pack_three = jnp.concatenate(
        [
            expand_weights.astype(BF).reshape(shard, blocks, width).transpose(1, 0, 2).reshape(-1, width),
            shrink_weights.astype(BF),
        ]
    )
    x, source, cot = inputs[0], memory[0], cotangent[0]
    start = target_pos
    step_float = step_count.astype(F32)

    if small:
        place = jnp.stack([lax.axis_index("rep"), lax.axis_index("fsdp")]).astype(jnp.int32)
        small_rows = jnp.concatenate(
            [
                jnp.pad(layer_vectors, ((0, 0), (0, inner_shard - shard))),
                expand_bias[None],
                jnp.zeros((5, inner_shard), F32),
            ]
        )
        small_rows = jnp.pad(small_rows, ((0, 0), (0, width - inner_shard))).astype(BF)
        pack_two = jnp.concatenate([low_attention[3 * shard :], small_rows])
        one = gather_staged(pack_one)
        two = gather_half(pack_two)
        three = gather_half(pack_three)
        given = None
        cross_shards = (*(shard,) * 5, 16)
        hidden_shards = (*(shard,) * blocks, inner_shard)
    else:
        place, cross_shards, hidden_shards = None, None, None
        flat = jnp.concatenate([layer_vectors.reshape(-1), expand_bias]).astype(BF)
        flat = lax.all_gather(flat, "fsdp", axis=0).astype(F32)
        vector_size = layer_vectors.size
        vec = flat[:, :vector_size].reshape(count, -1, shard).transpose(1, 0, 2).reshape(-1, width)
        given = jnp.pad(vec, ((0, 16 - vec.shape[0]), (0, 0))), flat[:, vector_size:].reshape(1, -1)

        def gather_all(pack, shards):
            full = lax.all_gather(pack, "fsdp", axis=0)
            pieces, first = [], 0
            for rows in shards:
                pieces.append(full[:, first : first + rows].reshape(-1, width))
                first += rows
            return jnp.concatenate(pieces)

        def owners(grads, shards):
            pieces, first = [], 0
            for rows in shards:
                pieces.append(grads[first : first + rows * count].reshape(count, rows, width))
                first += rows * count
            return jnp.concatenate(pieces, axis=1)

        one = gather_all(pack_one, (shard,) * 3)
        two = gather_all(low_attention[3 * shard :], (shard,) * 5)
        three = gather_all(pack_three, (*(shard,) * blocks, inner_shard))

    *saved_one, matrices = forward_self(place, x, start, one, small)
    two = both_halves(two, saved_one[3]) if small else two
    norm_one, inv_one, *saved_two, norm_two, inv_two, cross_matrices, vec, bias = forward_cross(
        place, x, saved_one[3], source, memory_length, two, given, cross_shards
    )
    three = both_halves(three, norm_two) if small else three
    outputs, dz_two, *grad_three, sums_three, bias_sum = hidden_step(
        place, three, norm_two, inv_two, cot, vec, bias, hidden_shards
    )
    if small:
        keep_three, send_three = reduce_cores(*grad_three)
        dz_two = after(dz_two, keep_three, send_three)
        received_three = send_rows(send_three)
    *grad_two, dz_one, memory_grad, sums_two = backward_cross(
        place, dz_two, x, norm_one, inv_one, source, memory_length, vec, cross_matrices, saved_two, saved_one[3],
        (sums_three, bias_sum) if small else None,
    )
    if small:
        joined_three = reduce_rows(keep_three, received_three, dz_one)
        keep_two, send_two = reduce_cores(grad_two[0], after(grad_two[1], joined_three))
        dz_one = after(dz_one, joined_three, keep_two, send_two)
        received_two = send_rows(send_two)
    *grad_one, input_grad = backward_self(
        place, dz_one, x, start, vec, cross_matrices, matrices, saved_one, small
    )

    attention = (attention_weights, first_attention, second_attention)
    expand = (expand_weights, first_expand, second_expand)
    shrink = (shrink_weights, first_shrink, second_shrink)
    bias = (expand_bias, first_bias, second_bias)
    vectors = (layer_vectors, first_vectors, second_vectors)
    if small:
        powers = 1.0 - hyper_rates[1:3] ** step_float
        scalars = place, jnp.concatenate([hyper_rates, powers])
        part_three = reduce_line(joined_three)
        part_two = reduce_line(reduce_rows(keep_two, received_two, input_grad))
        keep_one, send_one = reduce_cores(*grad_one)
        part_one = reduce_shifts(reduce_rows(keep_one, send_rows(send_one), input_grad))
        total_three = reduce_last(after(part_three, input_grad))
        total_two = reduce_last(part_two)
        total_one = reduce_last(part_one)
        hidden_new = adam_call(hidden_adam_kernel, scalars, total_three, (*expand, *shrink))
        rows = tuple(b[None] for b in bias)
        other_new = adam_call(
            attention_adam_kernel, scalars, (*total_one, *total_two), (*attention, *rows, *vectors)
        )
        new_bias = tuple(b[0] for b in other_new[3:6])
        updated = (*other_new[:3], *hidden_new, *new_bias, *other_new[6:])
    else:
        sums = (sums_two + sums_three)[: layer_vectors.shape[0]]
        flat = jnp.concatenate(
            [
                sums.reshape(-1, count, shard).transpose(1, 0, 2).reshape(count, -1),
                bias_sum.reshape(count, inner_shard),
            ],
            axis=1,
        )
        total_three = reduce_plain(owners(grad_three[0], (*(shard,) * blocks, inner_shard)))
        total_two = reduce_plain(owners(grad_two[0], (shard,) * 5))
        total_one = reduce_plain(owners(grad_one[0], (shard,) * 3))
        flat = lax.psum(lax.psum_scatter(flat, "fsdp", scatter_dimension=0), "rep")
        grad_attention = jnp.concatenate([total_one, total_two]).reshape(attention_weights.shape)
        grad_expand = total_three[: blocks * shard].reshape(blocks, shard, width).transpose(1, 0, 2)
        updated = []
        for (now, one_now, two_now), grad, factor in (
            (attention, grad_attention, 1.0),
            (expand, grad_expand.reshape(shard, -1), 1.0),
            (shrink, total_three[blocks * shard :], 1.0),
            (bias, flat[layer_vectors.size :], 0.0),
            (vectors, flat[: layer_vectors.size].reshape(-1, shard), 0.0),
        ):
            updated.extend(adam_update(now, grad, one_now, two_now, hyper_rates, step_float, factor))
    return (outputs[None], input_grad[None], memory_grad[None], *updated)


def solution(mesh):
    rows = ("rep", "fsdp")
    params = (P(None, "fsdp", None), P("fsdp", None), P("fsdp", None), P("fsdp"), P(None, "fsdp"))
    return jax.shard_map(
        functools.partial(per_device, small_mesh(mesh)),
        mesh=mesh,
        in_specs=(
            P(rows, None, None), P(rows, None, None), P(rows), P(rows, None), P(rows, None, None),
            *params, *params, *params, P(), P(),
        ),
        out_specs=(
            P(rows, None, None), P(rows, None, None), P(rows, None, None),
            *(spec for spec in params for _ in range(3)),
        ),
        check_vma=False,
    )
```

```python
import functools

import jax
import jax.numpy as jnp
from jax import lax
from jax.experimental import pallas as pl
from jax.experimental.pallas import tpu as pltpu
from jax.sharding import PartitionSpec as P

BF = jnp.bfloat16
F32 = jnp.float32
HEAD_DIM = 64
PAIR = 128
TILE = 256
MIB = 1 << 20


def dot(left, right, left_dim, right_dim):
    return lax.dot_general(
        left, right, (((left_dim,), (right_dim,)), ((), ())), preferred_element_type=F32
    )


def lanes(size):
    return lax.broadcasted_iota(jnp.int32, (1, size), 1)


def half_masks():
    first = jnp.where(lanes(PAIR) < HEAD_DIM, 1.0, 0.0)
    return first.astype(BF), (1.0 - first).astype(BF)


def rows_at(index, size=TILE):
    return pl.ds(pl.multiple_of(index * size, size), size)


def split_three(column):
    high = column.astype(BF).astype(F32)
    rest = column - high
    middle = rest.astype(BF).astype(F32)
    return high, middle, rest - middle


def with_column(block, column, base, last):
    high, middle, low = split_three(column)
    lane = lanes(PAIR)
    tail = jnp.where(lane == base + 3, last, block)
    return jnp.where(
        lane == base, -high, jnp.where(lane == base + 1, -middle, jnp.where(lane == base + 2, -low, tail))
    ).astype(BF)


class Mover:
    def __init__(self, sems):
        self.sems, self.used, self.leaving = sems, 0, []

    def take(self, count=1):
        self.used += count
        return self.used - count

    def load(self, source, target):
        copy = pltpu.make_async_copy(source, target, self.sems.at[self.take()])
        copy.start()
        return copy

    def load_rows(self, source, target):
        count = source.shape[0] // TILE
        first = self.take(count)

        def copy(tile):
            rows = rows_at(tile)
            return pltpu.make_async_copy(source.at[rows], target.at[rows], self.sems.at[first + tile])

        for tile in range(count):
            copy(tile).start()
        return lambda tile: copy(tile).wait()

    def store(self, source, target):
        self.leaving.append(self.load(source, target))

    def store_parts(self, source, target, count, where):
        first = self.take(count)

        def copy(part):
            return pltpu.make_async_copy(source.at[where(part)], target.at[where(part)], self.sems.at[first + part])

        self.leaving.extend(copy(part) for part in range(count))
        return lambda part: copy(part).start()

    def store_rows(self, source, target):
        return self.store_parts(source, target, source.shape[0] // TILE, rows_at)

    def finish(self):
        for copy in self.leaving:
            copy.wait()


def columns_at(size):
    return lambda part: (slice(None), rows_at(part, size))


def load_matrices(mover, core, sources, targets):
    waits, first = [], 0
    for index, target in enumerate(targets):
        if core is None:
            copies = [mover.load(sources[index], target)]
        else:
            rows, half = target.shape[1], target.shape[2] // 2
            copies = []
            for step, source in enumerate(sources):
                cols = pl.ds(pl.multiple_of(jnp.bitwise_xor(core, step) * half, half), half)
                copies.append(mover.load(source.at[:, first : first + rows, :], target.at[:, :, cols]))
            first += rows
        waits.append(lambda copies=copies: [copy.wait() for copy in copies])
    return waits


def whole(ref):
    return ref[...].reshape(-1, ref.shape[-1])


def key_extra(length_limit, count):
    lane = lanes(PAIR) % HEAD_DIM
    extra = jnp.where(lane < 3, 1.0, 0.0)
    if length_limit is None:
        return jnp.broadcast_to(extra, (count, PAIR)).astype(BF)
    row = lax.broadcasted_iota(jnp.int32, (count, PAIR), 0)
    bias = jnp.where(row < length_limit, 0.0, -1e30)
    return jnp.where(lane == 3, bias, extra).astype(BF)


def put_start(pos_ref, start_ref):
    length = start_ref.shape[0]
    query = lax.broadcasted_iota(jnp.int32, (8, length), 1)
    first = (query - pos_ref[...]).astype(F32)
    start_ref[...] = first.T[:, :1].astype(jnp.int32)


def visible(start, first_query, first_key, count):
    key = first_key + lax.broadcasted_iota(jnp.int32, (TILE, count), 1)
    seen = key >= start
    if first_key == first_query:
        query = first_query + lax.broadcasted_iota(jnp.int32, (TILE, count), 0)
        seen = seen & (key <= query)
    return seen


def key_spans(tile, count, causal):
    if not causal:
        return [(0, count)]
    spans = [(0, tile * TILE)] if tile else []
    return spans + [(tile * TILE, TILE)]


def attend(q_ref, k_ref, v_ref, extra_ref, start_ref, qa_ref, o_ref, finished):
    length, count = q_ref.shape[0], k_ref.shape[0]
    causal = start_ref is not None
    masks = half_masks()

    @pl.loop(0, q_ref.shape[1] // PAIR)
    def _(pair):
        cols = rows_at(pair, PAIR)
        for tile in range(length // TILE):
            rows = slice(tile * TILE, (tile + 1) * TILE)
            spans = key_spans(tile, count, causal)
            results = []
            for side in (0, 1):
                base = HEAD_DIM * (1 - side)
                lane = lanes(PAIR)
                queries = q_ref[rows, cols] * masks[side]
                queries_f = queries.astype(F32)
                if not causal:
                    queries = jnp.where(lane == base + 3, 1.0, queries_f).astype(BF)
                score_blocks = []
                for first, size in spans:
                    keys = k_ref[first : first + size, cols] * masks[side]
                    if not causal:
                        keys = keys + extra_ref[first : first + size, :] * masks[1 - side]
                    scores = dot(queries, keys, 1, 1)
                    if causal:
                        seen = visible(start_ref[rows, :], tile * TILE, first, size)
                        scores = jnp.where(seen, scores, -1000000000.0)
                    score_blocks.append(scores)
                top = functools.reduce(
                    jnp.maximum, [jnp.max(scores, axis=1, keepdims=True) for scores in score_blocks]
                )
                total = None
                for scores, (first, size) in zip(score_blocks, spans):
                    values = v_ref[first : first + size, cols] * masks[side] + masks[1 - side]
                    probs = jnp.exp(scores - top).astype(BF)
                    part = dot(probs, values, 1, 0)
                    total = part if total is None else total + part
                results.append(total / pltpu.roll(total, HEAD_DIM, 1))
                log_total = top + jnp.log(total[:, base : base + 1])
                qa_ref[rows, pl.ds(pl.multiple_of(pair * 2 * PAIR, PAIR) + side * PAIR, PAIR)] = with_column(
                    queries_f, log_total, base, 0.0 if causal else 1.0
                )
            o_ref[rows, cols] = jnp.where(lanes(PAIR) < HEAD_DIM, results[0], results[1]).astype(BF)
        for start_store in finished:
            start_store(pair)


def attend_back(qa_ref, da_ref, k_ref, v_ref, extra_ref, start_ref, dq_ref, dk_ref, dv_ref, dk_sum, dv_sum):
    length, count = qa_ref.shape[0], k_ref.shape[0]
    causal = start_ref is not None
    masks = half_masks()

    @pl.loop(0, k_ref.shape[1] // PAIR)
    def _(pair):
        cols = rows_at(pair, PAIR)
        for tile in reversed(range(length // TILE)):
            rows = slice(tile * TILE, (tile + 1) * TILE)
            query_grads = []
            for side in (0, 1):
                head_cols = pl.ds(pl.multiple_of(pair * 2 * PAIR, PAIR) + side * PAIR, PAIR)
                queries = qa_ref[rows, head_cols]
                grads = da_ref[rows, head_cols]
                query_grad = None
                for first, size in key_spans(tile, count, causal):
                    span = slice(first, first + size)
                    keys = k_ref[span, cols]
                    keys_low = keys * masks[side] + extra_ref[span, :] * masks[1 - side]
                    values = v_ref[span, cols] * masks[side] + masks[1 - side]
                    probs = jnp.exp(dot(queries, keys_low, 1, 1))
                    if causal:
                        seen = visible(start_ref[rows, :], tile * TILE, first, size)
                        probs = jnp.where(seen, probs, 0.0)
                    grad_scores = (probs * dot(grads, values, 1, 1)).astype(BF)
                    value_part = dot(grads, probs.astype(BF), 0, 0)
                    key_part = dot(queries, grad_scores, 0, 0)
                    if tile == length // TILE - 1:
                        dv_sum[side, :, span] = value_part
                        dk_sum[side, :, span] = key_part
                    else:
                        dv_sum[side, :, span] += value_part
                        dk_sum[side, :, span] += key_part
                    part = dot(grad_scores, keys, 1, 0)
                    query_grad = part if query_grad is None else query_grad + part
                query_grads.append(query_grad)
            dq_ref[rows, cols] = (
                jnp.where(lanes(PAIR) < HEAD_DIM, query_grads[0], query_grads[1]) * HEAD_DIM**-0.5
            ).astype(BF)
        for sums, out in ((dk_sum, dk_ref), (dv_sum, dv_ref)):
            joined = jnp.concatenate([sums[0, :HEAD_DIM, :], sums[1, HEAD_DIM:, :]], axis=0)
            out[:, cols] = joined.astype(BF).T


def norm_rows(summed):
    center = jnp.mean(summed, axis=1, keepdims=True)
    shifted = summed - center
    inverse = lax.rsqrt(jnp.mean(shifted * shifted, axis=1, keepdims=True) + 1e-05)
    return shifted * inverse, inverse


def norm_back(grad_out, normed, inverse, gain):
    scaled = grad_out * gain
    first = jnp.mean(scaled, axis=1, keepdims=True)
    second = jnp.mean(scaled * normed, axis=1, keepdims=True)
    return inverse * (scaled - first - normed * second)


def add_rows(ref, row, values):
    ref[row : row + 1, :] += jnp.sum(values, axis=0, keepdims=True)


def place_of(place_ref):
    rep, place = place_ref[0], place_ref[1]
    return lax.rem(rep, 2), lax.div(rep, 2), lax.div(place, 2), lax.rem(place, 2)


def assemble(place_ref, chunk_refs, all_ref):
    core, chip, line, row = place_of(place_ref)
    width = all_ref.shape[1]
    quarter = chunk_refs[0].shape[3]
    shard = quarter * 4 // 3
    for core_step, chunk_ref in enumerate(chunk_refs):
        for chip_step in (0, 1):
            rep = jnp.bitwise_xor(chip, chip_step) * 2 + jnp.bitwise_xor(core, core_step)
            for line_step in range(4):
                for row_step in (0, 1):
                    owner = lax.rem(line - line_step + 4, 4) * 2 + jnp.bitwise_xor(row, row_step)
                    for piece in range(quarter // 16):
                        stacked = rep * quarter + piece * 16
                        matrix = lax.div(stacked, shard)
                        target = matrix * width + owner * shard + (stacked - matrix * shard)
                        all_ref[pl.ds(pl.multiple_of(target, 16), 16), :] = chunk_ref[
                            chip_step, line_step, row_step, piece * 16 : (piece + 1) * 16, :
                        ]


def assemble_halves(place_ref, mine_ref, other_ref, all_ref, shards):
    core = place_of(place_ref)[0]
    devices, _, half = mine_ref.shape
    for step, ref in ((0, mine_ref), (1, other_ref)):
        cols = pl.ds(pl.multiple_of(jnp.bitwise_xor(core, step) * half, half), half)
        first, target = 0, 0
        for shard in shards:
            for owner in range(devices):
                at = target + owner * shard
                all_ref[at : at + shard, cols] = ref[owner, first : first + shard, :]
            first += shard
            target += shard * devices


def unpack_small(all_ref, base, vec_ref, bias_ref):
    devices = vec_ref.shape[1] // HEAD_DIM
    inner = bias_ref.shape[1] // devices
    for pair in range(devices // 2):
        first = base + 2 * pair * 16
        left = all_ref[first : first + 16, :PAIR].astype(F32)
        right = all_ref[first + 16 : first + 32, :PAIR].astype(F32)
        vec_ref[:, pair * PAIR : (pair + 1) * PAIR] = jnp.where(
            lanes(PAIR) < HEAD_DIM, left, pltpu.roll(right, HEAD_DIM, 1)
        )
    for owner in range(devices):
        rows = all_ref[base + owner * 16 : base + owner * 16 + 16, :inner].astype(F32)
        bias_ref[:, owner * inner : (owner + 1) * inner] = rows[10:11, :]


def self_forward_kernel(staged, *refs):
    if staged:
        place_ref, pos_ref, x_hbm, chunk_hbm, other_hbm = refs[:5]
        refs = refs[5:]
    else:
        pos_ref, x_hbm, all_hbm = refs[:3]
        refs = refs[3:]
    qa_hbm, k_hbm, v_hbm, o_hbm = refs[:4]
    refs = refs[4:]
    if staged:
        all_out, refs = refs[0], refs[1:]
    x_ref, all_ref, qa_ref, k_ref, v_ref, o_ref, q_ref, start_ref = refs[:8]
    mover = Mover(refs[-1])
    length, width = x_ref.shape
    if staged:
        chunk_refs = refs[8:10]
        loads = [mover.load(a, b) for a, b in zip((chunk_hbm, other_hbm), chunk_refs)]
    else:
        loads = [mover.load(all_hbm, all_ref)]
    x_load = mover.load(x_hbm, x_ref)
    put_start(pos_ref, start_ref)
    for load in loads:
        load.wait()
    if staged:
        assemble(place_ref, chunk_refs, all_ref)
        mover.store(all_ref, all_out)
    x_load.wait()

    @pl.loop(0, length // TILE)
    def _(tile):
        rows = rows_at(tile)
        source = x_ref[rows, :]
        queries = dot(source, all_ref[:width, :], 1, 0).astype(BF)
        q_ref[rows, :] = queries * jnp.asarray(HEAD_DIM**-0.5, BF)
        k_ref[rows, :] = dot(source, all_ref[width : 2 * width, :], 1, 0).astype(BF)
        v_ref[rows, :] = dot(source, all_ref[2 * width :, :], 1, 0).astype(BF)

    mover.store(k_ref, k_hbm)
    mover.store(v_ref, v_hbm)
    pairs = width // PAIR
    finished = (
        mover.store_parts(qa_ref, qa_hbm, pairs, columns_at(2 * PAIR)),
        mover.store_parts(o_ref, o_hbm, pairs, columns_at(PAIR)),
    )
    attend(q_ref, k_ref, v_ref, None, start_ref, qa_ref, o_ref, finished)
    mover.finish()


def unpack_small(small_ref, vec_ref, bias_ref):
    devices = vec_ref.shape[1] // HEAD_DIM
    inner = bias_ref.shape[1] // devices
    for pair in range(devices // 2):
        left = small_ref[0, 2 * pair, :, :PAIR].astype(F32)
        right = small_ref[0, 2 * pair + 1, :, :PAIR].astype(F32)
        vec_ref[:, pair * PAIR : (pair + 1) * PAIR] = jnp.where(
            lanes(PAIR) < HEAD_DIM, left, pltpu.roll(right, HEAD_DIM, 1)
        )
    for owner in range(devices):
        rows = small_ref[0, owner, :, :inner].astype(F32)
        bias_ref[:, owner * inner : (owner + 1) * inner] = rows[10:11, :]


def cross_forward_kernel(staged, *refs):
    place_ref, core = None, None
    if staged:
        place_ref, refs = refs[0], refs[1:]
        core = place_of(place_ref)[0]
    length_ref, refs = refs[0], refs[1:]
    if staged:
        x_hbm, mixed_hbm, source_hbm, *packs = refs[:5]
        refs = refs[5:]
    else:
        vec_ref, x_hbm, mixed_hbm, source_hbm, *packs = refs[:9]
        refs = refs[9:]
    first_hbm, first_inv_hbm, qa_hbm, k_hbm, v_hbm, o_hbm, n_hbm, inv_hbm = refs[:8]
    refs = refs[8:]
    if staged:
        vec_ref, bias_ref, refs = refs[0], refs[1], refs[2:]
    x_ref, mixed_ref, source_ref, first_ref, first_inv_ref, qa_ref, k_ref, v_ref, o_ref, n_ref, inv_ref = refs[:11]
    q_ref, extra_ref, *w_refs = refs[11:18]
    mover = Mover(refs[-1])
    length, width = q_ref.shape

    if staged:
        small_ref = refs[18]
        rows = packs[0].shape[1]
        small = [
            mover.load(pack.at[:, rows - 16 :, :], small_ref.at[jnp.bitwise_xor(core, step)])
            for step, pack in enumerate(packs)
        ]
    source_load = mover.load_rows(source_hbm, source_ref)
    order = (2, 3, 0, 1, 4)
    waits = [None] * 5
    if staged:
        half = width // 2
        shard = w_refs[0].shape[1]
        for index in order:
            copies = []
            for step, pack in enumerate(packs):
                cols = pl.ds(pl.multiple_of(jnp.bitwise_xor(core, step) * half, half), half)
                copies.append(
                    mover.load(pack.at[:, index * shard : (index + 1) * shard, :], w_refs[index].at[:, :, cols])
                )
            waits[index] = lambda copies=copies: [copy.wait() for copy in copies]
    else:
        for index in order:
            waits[index] = mover.load(packs[index], w_refs[index]).wait
    mixed_load = mover.load_rows(mixed_hbm, mixed_ref)
    x_load = mover.load_rows(x_hbm, x_ref)
    extra_ref[...] = key_extra(length_ref[0], k_ref.shape[0])
    waits[2]()
    waits[3]()

    @pl.loop(0, source_ref.shape[0] // TILE)
    def _(tile):
        rows = rows_at(tile)
        source_load(tile)
        source = source_ref[rows, :]
        k_ref[rows, :] = dot(source, whole(w_refs[2]), 1, 0).astype(BF)
        v_ref[rows, :] = dot(source, whole(w_refs[3]), 1, 0).astype(BF)

    mover.store(k_ref, k_hbm)
    mover.store(v_ref, v_hbm)
    if staged:
        for load in small:
            load.wait()
        unpack_small(small_ref, vec_ref, bias_ref)
    waits[0]()
    waits[1]()

    @pl.loop(0, length // TILE)
    def _(tile):
        rows = rows_at(tile)
        mixed_load(tile)
        x_load(tile)
        summed = x_ref[rows, :].astype(F32) * vec_ref[6:7, :] + dot(mixed_ref[rows, :], whole(w_refs[0]), 1, 0)
        normed, inverse = norm_rows(summed)
        first_ref[rows, :] = normed
        first_inv_ref[rows, :] = inverse
        low = (normed * vec_ref[0:1, :] + vec_ref[3:4, :]).astype(BF)
        queries = dot(low, whole(w_refs[1]), 1, 0).astype(BF)
        q_ref[rows, :] = queries * jnp.asarray(HEAD_DIM**-0.5, BF)

    mover.store(first_ref, first_hbm)
    mover.store(first_inv_ref, first_inv_hbm)
    pairs = width // PAIR
    finished = (
        mover.store_parts(qa_ref, qa_hbm, pairs, columns_at(2 * PAIR)),
        mover.store_parts(o_ref, o_hbm, pairs, columns_at(PAIR)),
    )
    attend(q_ref, k_ref, v_ref, extra_ref, None, qa_ref, o_ref, finished)
    waits[4]()
    n_store, inv_store = mover.store_rows(n_ref, n_hbm), mover.store_rows(inv_ref, inv_hbm)

    @pl.loop(0, length // TILE)
    def _(tile):
        rows = rows_at(tile)
        first_out = first_ref[rows, :] * vec_ref[0:1, :] + vec_ref[3:4, :]
        summed = first_out * vec_ref[7:8, :] + dot(o_ref[rows, :], whole(w_refs[4]), 1, 0)
        normed, inverse = norm_rows(summed)
        n_ref[rows, :] = normed
        inv_ref[rows, :] = inverse
        n_store(tile)
        inv_store(tile)

    mover.finish()


def hidden_kernel(staged, *refs):
    place_ref, core = None, None
    if staged:
        place_ref, refs = refs[0], refs[1:]
        core = place_of(place_ref)[0]
    vec_ref, bias_ref, *packs = refs[: 4 if staged else 7]
    n_hbm, inv_hbm, cot_hbm = refs[len(packs) + 2 : len(packs) + 5]
    refs = refs[len(packs) + 5 :]
    count = 2 if staged else 1
    sums_ref, bias_sum_ref, out_hbm, dz_hbm = refs[:4]
    grad_hbms, refs = refs[4 : 4 + count], refs[4 + count :]
    grad_refs, refs = refs[:count], refs[count:]
    n_ref, inv_ref, cot_ref, out_ref, dz_ref, low_ref, h_ref, du_ref, df_ref, slope_ref = refs[:10]
    blocks = bias_ref.shape[1] // vec_ref.shape[1]
    *e_refs, s_ref = refs[10 : 11 + blocks]
    mover = Mover(refs[-1])
    length, width = n_ref.shape

    n_load = mover.load_rows(n_hbm, n_ref)
    waits = load_matrices(mover, core, packs, (*e_refs, s_ref))
    inv_load = mover.load_rows(inv_hbm, inv_ref)
    cot_load = mover.load_rows(cot_hbm, cot_ref)
    sums_ref[...] = jnp.zeros_like(sums_ref)
    bias_sum_ref[...] = jnp.zeros_like(bias_sum_ref)
    out_store, dz_store = mover.store_rows(out_ref, out_hbm), mover.store_rows(dz_ref, dz_hbm)
    for wait in waits:
        wait()

    @pl.loop(0, length // TILE)
    def _(tile):
        rows = rows_at(tile)
        n_load(tile)
        gain, shift = vec_ref[1:2, :], vec_ref[4:5, :]
        second_out = n_ref[rows, :] * gain + shift
        low = second_out.astype(BF)
        low_ref[rows, :] = low
        summed = second_out * vec_ref[8:9, :] + vec_ref[9:10, :]
        shrink = whole(s_ref)
        for block in range(blocks):
            cols = slice(block * width, (block + 1) * width)
            before = dot(low, whole(e_refs[block]), 1, 0) + bias_ref[:, cols]
            square = before * before
            tangent = jnp.tanh(0.7978845608028654 * (before + 0.044715 * before * square))
            half = 0.5 * (1.0 + tangent)
            slope_ref[:, cols] = half + 0.5 * before * (1.0 - tangent * tangent) * 0.7978845608028654 * (
                1.0 + 3.0 * 0.044715 * square
            )
            hidden = (before * half).astype(BF)
            h_ref[rows, cols] = hidden
            summed = summed + dot(hidden, shrink[cols, :], 1, 0)
        normed, inverse = norm_rows(summed)
        cot_load(tile)
        inv_load(tile)
        out_ref[rows, :] = (normed * vec_ref[2:3, :] + vec_ref[5:6, :]).astype(BF)
        out_store(tile)
        grad_out = cot_ref[rows, :].astype(F32)
        third = norm_back(grad_out, normed, inverse, vec_ref[2:3, :])
        add_rows(sums_ref, 2, grad_out * normed)
        add_rows(sums_ref, 5, grad_out)
        branch = third.astype(BF)
        df_ref[rows, :] = branch
        add_rows(sums_ref, 9, branch.astype(F32))
        add_rows(sums_ref, 8, second_out * third)
        grad_second = vec_ref[8:9, :] * third
        for block in range(blocks):
            cols = slice(block * width, (block + 1) * width)
            du = (dot(branch, shrink[cols, :], 1, 1) * slope_ref[:, cols]).astype(BF)
            du_ref[rows, cols] = du
            bias_sum_ref[:, cols] += jnp.sum(du.astype(F32), axis=0, keepdims=True)
            grad_second = grad_second + dot(du, whole(e_refs[block]), 1, 1)
        normed_two = n_ref[rows, :]
        dz_ref[rows, :] = norm_back(grad_second, normed_two, inv_ref[rows, :], gain)
        dz_store(tile)
        add_rows(sums_ref, 1, grad_second * normed_two)
        add_rows(sums_ref, 4, grad_second)

    for step in reversed(range(count)):
        for block in range(blocks):
            cols = slice(block * width, (block + 1) * width)
            put_grad(grad_refs, step, place_ref, block, low_ref[...], du_ref, block * width)
            put_shrink(grad_refs, step, place_ref, block, blocks, h_ref[:, cols], df_ref)
        mover.store(grad_refs[step], grad_hbms[step])
    mover.finish()


def branch_grads(branch, mixed_weight, o_rows, da_ref, rows):
    masks = half_masks()
    mixed_grad = dot(branch, mixed_weight, 1, 1).astype(BF)
    for pair in range(mixed_grad.shape[1] // PAIR):
        cols = slice(pair * PAIR, (pair + 1) * PAIR)
        grad_pair = mixed_grad[:, cols].astype(F32)
        product = grad_pair * o_rows[:, cols].astype(F32)
        for side in (0, 1):
            mask = masks[side].astype(F32)
            inner = jnp.sum(product * mask, axis=1, keepdims=True)
            first = (2 * pair + side) * PAIR
            da_ref[rows, first : first + PAIR] = with_column(
                grad_pair * mask, inner, HEAD_DIM * (1 - side), 0.0
            )


def put_grad(grad_refs, step, place_ref, index, left, right_ref, first=0):
    width = left.shape[1]
    if place_ref is None:
        grad = dot(left, right_ref[:, first : first + width], 0, 0)
        grad_refs[0][index * width : (index + 1) * width, :] = grad.astype(BF)
        return
    core, _, _, row = place_of(place_ref)
    half = width // 2
    shard = width // 8
    cols = pl.ds(pl.multiple_of(first + jnp.bitwise_xor(core, step) * half, half), half)
    grad = dot(left, right_ref[:, cols], 0, 0).astype(BF).reshape(4, 2, shard, half)
    for side in (0, 1):
        slot = jnp.bitwise_xor(row, side)
        grad_refs[step][slot, :, index * shard : (index + 1) * shard, :] = grad[:, side]


def put_shrink(grad_refs, step, place_ref, block, blocks, left, right_ref):
    width = left.shape[1]
    if place_ref is None:
        first = (blocks + block) * width
        grad_refs[0][first : first + width, :] = dot(left, right_ref[...], 0, 0).astype(BF)
        return
    core, _, _, row = place_of(place_ref)
    half, shard = width // 2, width * blocks // 8
    base = width // 8 * blocks
    cols = pl.ds(pl.multiple_of(jnp.bitwise_xor(core, step) * half, half), half)
    grad = dot(left, right_ref[:, cols], 0, 0).astype(BF).reshape(width // shard, shard, half)
    for part in range(width // shard):
        owner = block * (width // shard) + part
        grad_refs[step][jnp.bitwise_xor(row, owner % 2), owner // 2, base:, :] = grad[part]


def put_small(grad_refs, place_ref, base, sums, bias_sum):
    core, _, _, row = place_of(place_ref)
    half = grad_refs[0].shape[3]
    inner = bias_sum.shape[1] // 8
    index = lax.broadcasted_iota(jnp.int32, (16, half), 0)
    for owner in range(8):
        block = sums[:, owner // 2 * PAIR : (owner // 2 + 1) * PAIR]
        if owner % 2:
            block = pltpu.roll(block, HEAD_DIM, 1)
        block = jnp.concatenate([block, jnp.zeros((16, half - PAIR), F32)], axis=1)
        block = jnp.where(index == 10, bias_sum[:, owner * inner : (owner + 1) * inner], block)
        high = block.astype(BF)
        low = (block - high.astype(F32)).astype(BF)
        slot = jnp.bitwise_xor(row, owner % 2)
        first = (core == 0).astype(F32)
        for step, grad_ref in enumerate(grad_refs):
            is_high = first if step == 0 else 1.0 - first
            mixed = high.astype(F32) * is_high + low.astype(F32) * (1.0 - is_high)
            grad_ref[slot, owner // 2, base : base + 16, :] = mixed.astype(BF)


def cross_backward_kernel(staged, *refs):
    place_ref, core = None, None
    if staged:
        place_ref, refs = refs[0], refs[1:]
        core = place_of(place_ref)[0]
    length_ref, vec_ref, refs = refs[0], refs[1], refs[2:]
    if staged:
        sums_three_ref, bias_sum_ref, refs = refs[0], refs[1], refs[2:]
    packs, refs = refs[: 2 if staged else 5], refs[2 if staged else 5 :]
    dz_hbm, x_hbm, first_hbm, inv_hbm, source_hbm, qa_hbm, k_hbm, v_hbm, o_hbm, self_o_hbm = refs[:10]
    sums_ref, dfirst_hbm, dsource_hbm = refs[10:13]
    count = 2 if staged else 1
    grad_hbms, refs = refs[13 : 13 + count], refs[13 + count :]
    grad_refs, refs = refs[:count], refs[count:]
    dz_ref, x_ref, first_ref, inv_ref, source_ref, qa_ref, k_ref, v_ref, o_ref, self_o_ref = refs[:10]
    dfirst_ref, dsource_ref, *w_refs = refs[10:17]
    low_ref, da_ref, dq_ref, dk_ref, dv_ref, dk_sum, dv_sum, branch_ref, extra_ref = refs[17:26]
    mover = Mover(refs[-1])
    length, width = dz_ref.shape

    dz_load, o_load = mover.load_rows(dz_hbm, dz_ref), mover.load_rows(o_hbm, o_ref)
    waits = load_matrices(mover, core, packs, w_refs)
    first_load = mover.load_rows(first_hbm, first_ref)
    middle = [mover.load(a, b) for a, b in ((k_hbm, k_ref), (v_hbm, v_ref), (qa_hbm, qa_ref))]
    sums_ref[...] = jnp.zeros_like(sums_ref)
    extra_ref[...] = key_extra(length_ref[0], k_ref.shape[0])
    for wait in waits:
        wait()

    @pl.loop(0, length // TILE)
    def _(tile):
        rows = rows_at(tile)
        dz_load(tile)
        o_load(tile)
        first_load(tile)
        grad = dz_ref[rows, :]
        branch = grad.astype(BF)
        branch_ref[rows, :] = branch
        first_out = first_ref[rows, :] * vec_ref[0:1, :] + vec_ref[3:4, :]
        low_ref[rows, :] = first_out.astype(BF)
        add_rows(sums_ref, 7, first_out * grad)
        branch_grads(branch, whole(w_refs[4]), o_ref[rows, :], da_ref, rows)

    last = [
        mover.load(a, b)
        for a, b in ((source_hbm, source_ref), (x_hbm, x_ref), (inv_hbm, inv_ref), (self_o_hbm, self_o_ref))
    ]
    for load in middle:
        load.wait()
    attend_back(qa_ref, da_ref, k_ref, v_ref, extra_ref, None, dq_ref, dk_ref, dv_ref, dk_sum, dv_sum)
    for load in last:
        load.wait()

    dsource_store = mover.store_rows(dsource_ref, dsource_hbm)

    @pl.loop(0, source_ref.shape[0] // TILE)
    def _(tile):
        rows = rows_at(tile)
        dsource_ref[rows, :] = dot(dk_ref[rows, :], whole(w_refs[2]), 1, 1) + dot(
            dv_ref[rows, :], whole(w_refs[3]), 1, 1
        )
        dsource_store(tile)

    for step in range(count):
        put_grad(grad_refs, step, place_ref, 4, o_ref[...], branch_ref)
    dfirst_store = mover.store_rows(dfirst_ref, dfirst_hbm)

    @pl.loop(0, length // TILE)
    def _(tile):
        rows = rows_at(tile)
        dx = dot(dq_ref[rows, :], whole(w_refs[1]), 1, 1) + vec_ref[7:8, :] * dz_ref[rows, :]
        normed = first_ref[rows, :]
        dfirst = norm_back(dx, normed, inv_ref[rows, :], vec_ref[0:1, :])
        dfirst_ref[rows, :] = dfirst
        dfirst_store(tile)
        add_rows(sums_ref, 0, dx * normed)
        add_rows(sums_ref, 3, dx)
        add_rows(sums_ref, 6, x_ref[rows, :].astype(F32) * dfirst)
        branch_ref[rows, :] = dfirst.astype(BF)

    if staged:
        put_small(grad_refs, place_ref, 5 * (width // 8), sums_ref[...] + sums_three_ref[...], bias_sum_ref[...])
    for step in reversed(range(count)):
        put_grad(grad_refs, step, place_ref, 1, low_ref[...], dq_ref)
        put_grad(grad_refs, step, place_ref, 2, source_ref[...], dk_ref)
        put_grad(grad_refs, step, place_ref, 3, source_ref[...], dv_ref)
        put_grad(grad_refs, step, place_ref, 0, self_o_ref[...], branch_ref)
        mover.store(grad_refs[step], grad_hbms[step])
    mover.finish()


def self_backward_kernel(staged, *refs):
    place_ref, core = None, None
    if staged:
        place_ref, refs = refs[0], refs[1:]
        core = place_of(place_ref)[0]
    pos_ref, vec_ref, refs = refs[0], refs[1], refs[2:]
    count = 2 if staged else 1
    packs, refs = refs[:count], refs[count:]
    dz_hbm, x_hbm, all_hbm, qa_hbm, k_hbm, v_hbm, o_hbm, dx_hbm = refs[:8]
    grad_hbms, refs = refs[8 : 8 + count], refs[8 + count :]
    grad_refs, refs = refs[:count], refs[count:]
    dz_ref, x_ref, all_ref, qa_ref, k_ref, v_ref, o_ref, dx_ref, w_ref = refs[:9]
    da_ref, dq_ref, dk_ref, dv_ref, dk_sum, dv_sum, extra_ref, start_ref = refs[9:17]
    mover = Mover(refs[-1])
    length, width = dz_ref.shape

    dz_load = mover.load_rows(dz_hbm, dz_ref)
    waits = load_matrices(mover, core, packs, (w_ref,))
    o_load = mover.load_rows(o_hbm, o_ref)
    middle = [mover.load(a, b) for a, b in ((k_hbm, k_ref), (v_hbm, v_ref), (qa_hbm, qa_ref))]
    put_start(pos_ref, start_ref)
    extra_ref[...] = key_extra(None, k_ref.shape[0])
    waits[0]()

    @pl.loop(0, length // TILE)
    def _(tile):
        rows = rows_at(tile)
        dz_load(tile)
        o_load(tile)
        branch_grads(dz_ref[rows, :].astype(BF), whole(w_ref), o_ref[rows, :], da_ref, rows)

    last = [mover.load(a, b) for a, b in ((x_hbm, x_ref), (all_hbm, all_ref))]
    for load in middle:
        load.wait()
    attend_back(qa_ref, da_ref, k_ref, v_ref, extra_ref, start_ref, dq_ref, dk_ref, dv_ref, dk_sum, dv_sum)
    for load in last:
        load.wait()

    dx_store = mover.store_rows(dx_ref, dx_hbm)

    @pl.loop(0, length // TILE)
    def _(tile):
        rows = rows_at(tile)
        dx = vec_ref[6:7, :] * dz_ref[rows, :]
        for index, grads in enumerate((dq_ref, dk_ref, dv_ref)):
            dx = dx + dot(grads[rows, :], all_ref[index * width : (index + 1) * width, :], 1, 1)
        dx_ref[rows, :] = dx
        dx_store(tile)

    for step in reversed(range(count)):
        for index, grads in enumerate((dq_ref, dk_ref, dv_ref)):
            put_grad(grad_refs, step, place_ref, index, x_ref[...], grads)
        mover.store(grad_refs[step], grad_hbms[step])
    mover.finish()


def call(kernel, args, outs, scratch, limit, flops, smem=(), near=(), near_outs=(), copies=0):
    spaces = [pltpu.SMEM if i in smem else pltpu.VMEM if i in near else pl.ANY for i in range(len(args))]
    out_spaces = [pltpu.VMEM if i in near_outs else pl.ANY for i in range(len(outs))]
    buffers = [pltpu.VMEM(shape, kind) for shape, kind in scratch]
    if copies:
        buffers.append(pltpu.SemaphoreType.DMA((copies,)))
    return pl.pallas_call(
        kernel,
        out_shape=[jax.ShapeDtypeStruct(shape, kind) for shape, kind in outs],
        in_specs=[pl.BlockSpec(memory_space=space) for space in spaces],
        out_specs=[pl.BlockSpec(memory_space=space) for space in out_spaces],
        scratch_shapes=buffers,
        compiler_params=pltpu.CompilerParams(vmem_limit_bytes=limit * MIB),
        cost_estimate=pl.CostEstimate(flops=flops, bytes_accessed=16 * MIB, transcendentals=0),
    )(*args)


def like(*arrays):
    return [(a.shape, a.dtype) for a in arrays]


def forward_self(place, x, pos, pack, staged):
    length, width = x.shape
    low = ((length, width), BF)
    outs = [((length, 2 * width), BF), low, low, low]
    matrices = ((3 * width, width), BF)
    scratch = [low, matrices, *outs, low, ((length, 1), jnp.int32)]
    if staged:
        return call(
            functools.partial(self_forward_kernel, True),
            (place, pos, x, *pack),
            [*outs, matrices],
            [*scratch, *like(*pack)],
            40, 10**10, smem=(0,), near=(1,), copies=16,
        )
    results = call(
        functools.partial(self_forward_kernel, False),
        (pos, x, pack), outs, scratch, 40, 10**10, near=(0,), copies=16,
    )
    return (*results, pack)


def matrix_buffers(shards, width):
    return [((8 if rows < width else 1, rows, width), BF) for rows in shards]


def forward_cross(place, x, mixed, source, count, packs, given, shards):
    length, width = x.shape
    keys = source.shape[0]
    low, full, column, key_low = ((length, width), BF), ((length, width), F32), ((length, 1), F32), ((keys, width), BF)
    outs = [full, column, ((length, 2 * width), BF), key_low, key_low, low, full, column]
    scratch = [low, low, key_low, *outs, low, ((keys, PAIR), BF)]
    if place is not None:
        return call(
            functools.partial(cross_forward_kernel, True),
            (place, count, x, mixed, source, *packs),
            [*outs, ((16, width), F32), ((1, 4 * width), F32)],
            [*scratch, *matrix_buffers(shards, width), ((2, 8, 16, width // 2), BF)],
            44, 10**10, smem=(0, 1), near_outs=(8, 9), copies=64,
        )
    vec, bias = given
    results = call(
        functools.partial(cross_forward_kernel, False),
        (count, vec, x, mixed, source, *packs),
        outs, [*scratch, *like(*packs)],
        44, 10**10, smem=(0,), near=(1,), copies=64,
    )
    return (*results, vec, bias)


def grad_outs(rows, width, staged):
    return [((2, 4, rows, width // 2), BF)] * 2 if staged else [((rows, width), BF)]


def hidden_step(place, packs, normed, inverse, cot, vec, bias, shards):
    length, width = normed.shape
    inner = bias.shape[1]
    staged = place is not None
    low = ((length, width), BF)
    grads = grad_outs(sum(shards) if staged else 2 * inner, width, staged)
    args = (vec, bias, *packs, normed, inverse, cot)
    matrices = matrix_buffers(shards, width) if staged else like(*packs)
    return call(
        functools.partial(hidden_kernel, staged),
        (place, *args) if staged else args,
        [((16, width), F32), ((1, inner), F32), low, ((length, width), F32), *grads],
        [*grads, *like(normed, inverse, cot), low, ((length, width), F32), low, ((length, inner), BF),
         ((length, inner), BF), low, ((TILE, inner), F32), *matrices],
        44, 2 * 10**10, smem=(0,) if staged else (), near=(1, 2) if staged else (0, 1), near_outs=(0, 1), copies=64,
    )


def backward_cross(place, packs, dz, x, normed, inverse, source, count, vec, saved, mixed, small, shards):
    length, width = dz.shape
    keys = source.shape[0]
    staged = place is not None
    arrays = (dz, x, normed, inverse, source, *saved, mixed)
    low, key_low, sums = ((length, width), BF), ((keys, width), BF), ((2, PAIR, keys), F32)
    grads = grad_outs(5 * width // 8 + 16 if staged else 5 * width, width, staged)
    full, key_full = ((length, width), F32), ((keys, width), F32)
    return call(
        functools.partial(cross_backward_kernel, staged),
        (place, count, vec, *small, *packs, *arrays) if staged else (count, vec, *packs, *arrays),
        [((16, width), F32), full, key_full, *grads],
        [*grads, *like(*arrays), full, key_full, *(matrix_buffers(shards, width) if staged else like(*packs)),
         low, ((length, 2 * width), BF), low, key_low, key_low, sums, sums, low, ((keys, PAIR), BF)],
        48, 2 * 10**10, smem=(0, 1) if staged else (0,), near=(2, 3, 4) if staged else (1,), near_outs=(0,), copies=64,
    )


def backward_self(place, packs, dz, x, pos, vec, matrices, saved, shards):
    length, width = dz.shape
    staged = place is not None
    arrays = (dz, x, matrices, *saved)
    low, sums, full = ((length, width), BF), ((2, PAIR, length), F32), ((length, width), F32)
    grads = grad_outs(3 * width // 8 if staged else 3 * width, width, staged)
    first = matrix_buffers(shards[:1], width) if staged else like(*packs)
    return call(
        functools.partial(self_backward_kernel, staged),
        (place, pos, vec, *packs, *arrays) if staged else (pos, vec, *packs, *arrays),
        [full, *grads],
        [*grads, *like(*arrays), full, *first,
         ((length, 2 * width), BF), low, low, low, sums, sums, ((length, PAIR), BF), ((length, 1), jnp.int32)],
        48, 2 * 10**10, smem=(0,) if staged else (), near=(1, 2) if staged else (0, 1), copies=64,
    )


def adam_step(settings_ref, now, grad, one, two, decay):
    beta_one, beta_two = settings_ref[1], settings_ref[2]
    first = beta_one * one + (1.0 - beta_one) * grad
    second = beta_two * two + (1.0 - beta_two) * grad * grad
    change = (first / settings_ref[4]) / (jnp.sqrt(second / settings_ref[5]) + 1e-08)
    if decay:
        change = change + settings_ref[3] * now
    return now - settings_ref[0] * change, first, second


def store_step(refs, where, results):
    for ref, value in zip(refs, results):
        ref[where] = value


def hidden_adam_kernel(place_ref, settings_ref, mine_ref, other_ref, *refs):
    core = place_of(place_ref)[0]
    expand, shrink = refs[0:3], refs[3:6]
    new_expand, new_shrink = refs[6:9], refs[9:12]
    half = mine_ref.shape[1]
    shard = expand[0].shape[0]
    blocks = expand[0].shape[1] // (2 * half)
    for step, ref in ((0, mine_ref), (1, other_ref)):
        side = jnp.bitwise_xor(core, step) * half
        cols = pl.ds(pl.multiple_of(side, half), half)
        for block in range(blocks):
            where = (slice(None), pl.ds(pl.multiple_of(block * 2 * half + side, half), half))
            grad = ref[block * shard : (block + 1) * shard, :]
            now, one, two = (r[where] for r in expand)
            store_step(new_expand, where, adam_step(settings_ref, now, grad, one, two, True))
        where = (slice(None), cols)
        now, one, two = (r[where] for r in shrink)
        store_step(new_shrink, where, adam_step(settings_ref, now, ref[blocks * shard :, :], one, two, True))


def attention_adam_kernel(place_ref, settings_ref, mine_one, other_one, mine_two, other_two, *refs):
    core = place_of(place_ref)[0]
    matrices, bias, vectors = refs[0:3], refs[3:6], refs[6:9]
    new_matrices, new_bias, new_vectors = refs[9:12], refs[12:15], refs[15:18]
    half = mine_one.shape[1]
    shard = matrices[0].shape[1]
    for step, one_ref, two_ref in ((0, mine_one, mine_two), (1, other_one, other_two)):
        cols = pl.ds(pl.multiple_of(jnp.bitwise_xor(core, step) * half, half), half)
        for index in range(8):
            ref, at = (one_ref, index) if index < 3 else (two_ref, index - 3)
            where = (index, slice(None), cols)
            now, one, two = (r[where] for r in matrices)
            grad = ref[at * shard : (at + 1) * shard, :]
            store_step(new_matrices, where, adam_step(settings_ref, now, grad, one, two, True))
    small = mine_two[5 * shard :, :] + other_two[5 * shard :, :]
    for group, new, grad in (
        (bias, new_bias, small[10:11, : bias[0].shape[1]]),
        (vectors, new_vectors, small[:10, : vectors[0].shape[1]]),
    ):
        now, one, two = (r[...] for r in group)
        store_step(new, ..., adam_step(settings_ref, now, grad, one, two, False))


def adam_call(kernel, scalars, grads, params):
    return call(
        kernel, (*scalars, *grads, *params), [(p.shape, F32) for p in params], [], 32, 10**7, smem=(0, 1),
        near=range(2, 2 + len(grads) + len(params)), near_outs=range(len(params)),
    )


CORE_SWAP = [(0, 1), (1, 0), (2, 3), (3, 2)]
CHIP_SWAP = [(0, 2), (2, 0), (1, 3), (3, 1)]
ROW_SWAP = [(i, i ^ 1) for i in range(8)]


LINES = [[0, 2, 4, 6], [1, 3, 5, 7]]


def line_shift(step):
    return [(2 * z + y, 2 * ((z + step) % 4) + y) for z in range(4) for y in (0, 1)]


def small_mesh(mesh):
    return mesh.shape["rep"] == 4 and mesh.shape["fsdp"] == 8


def gather_staged(pack):
    quarter = pack.shape[0] // 4
    mine = lax.dynamic_slice_in_dim(pack, lax.axis_index("rep") * quarter, quarter, 0)
    pair = jnp.stack([mine, lax.ppermute(mine, "fsdp", ROW_SWAP)])
    part = jnp.stack([pair] + [lax.ppermute(pair, "fsdp", line_shift(step)) for step in (1, 2, 3)])
    both = jnp.stack([part, lax.ppermute(part, "rep", CHIP_SWAP)])
    return both, lax.ppermute(both, "rep", CORE_SWAP)


def after(value, *done):
    return lax.optimization_barrier((value, *done))[0]


def gather_half(pack):
    half = pack.shape[1] // 2
    mine = lax.dynamic_slice_in_dim(pack, lax.axis_index("rep") % 2 * half, half, 1)
    return lax.all_gather(mine, "fsdp", axis=0)


def both_halves(mine, done):
    mine = after(mine, done)
    return mine, lax.ppermute(mine, "rep", CORE_SWAP)


def low_sum(mine, received):
    return (mine.astype(F32) + received.astype(F32)).astype(BF)


def reduce_cores(keep, send):
    received = lax.ppermute(send, "rep", CORE_SWAP)
    return low_sum(keep[0], received[0]), low_sum(keep[1], received[1])


def send_rows(send):
    return lax.ppermute(send, "fsdp", ROW_SWAP)


def reduce_rows(keep, received, done):
    return low_sum(keep, after(received, done))


def reduce_last(part):
    total = part.astype(F32) + lax.ppermute(part, "rep", CHIP_SWAP).astype(F32)
    return total, lax.ppermute(total, "rep", CORE_SWAP)


def reduce_line(joined):
    part = lax.psum_scatter(joined, "fsdp", scatter_dimension=0, axis_index_groups=LINES)
    return part.reshape(joined.shape[1:])


def reduce_shifts(joined):
    line = lax.axis_index("fsdp") // 2
    total = lax.dynamic_index_in_dim(joined, line, 0, False).astype(F32)
    for step in (1, 2, 3):
        away = lax.dynamic_index_in_dim(joined, (line + step) % 4, 0, False)
        total = total + lax.ppermute(away, "fsdp", line_shift(step)).astype(F32)
    return total.astype(BF)


def reduce_plain(grads):
    return lax.psum(lax.psum_scatter(grads, "fsdp", scatter_dimension=0), "rep").astype(F32)


def adam_update(weight_now, gradient, moment_one, moment_two, settings, step_float, factor):
    learn_rate, beta_one, beta_two, decay_rate = settings[0], settings[1], settings[2], settings[3]
    first_new = beta_one * moment_one + (1.0 - beta_one) * gradient
    second_new = beta_two * moment_two + (1.0 - beta_two) * gradient * gradient
    first_hat = first_new / (1.0 - beta_one**step_float)
    second_hat = second_new / (1.0 - beta_two**step_float)
    change = first_hat / (jnp.sqrt(second_hat) + 1e-08) + factor * decay_rate * weight_now
    return (weight_now - learn_rate * change, first_new, second_new)


def per_device(
    small, inputs, memory, memory_length, target_pos, cotangent,
    attention_weights, expand_weights, shrink_weights, expand_bias, layer_vectors,
    first_attention, first_expand, first_shrink, first_bias, first_vectors,
    second_attention, second_expand, second_shrink, second_bias, second_vectors,
    hyper_rates, step_count,
):
    length, width = inputs.shape[1:]
    shard = attention_weights.shape[1]
    count = width // shard
    inner_shard = shrink_weights.shape[0]
    blocks = inner_shard // shard
    low_attention = attention_weights.astype(BF).reshape(8 * shard, width)
    pack_one = low_attention[: 3 * shard]
    pack_three = jnp.concatenate(
        [
            expand_weights.astype(BF).reshape(shard, blocks, width).transpose(1, 0, 2).reshape(-1, width),
            shrink_weights.astype(BF),
        ]
    )
    x, source, cot = inputs[0], memory[0], cotangent[0]
    step_float = step_count.astype(F32)

    if small:
        place = jnp.stack([lax.axis_index("rep"), lax.axis_index("fsdp")]).astype(jnp.int32)
        small_rows = jnp.concatenate(
            [
                jnp.pad(layer_vectors, ((0, 0), (0, inner_shard - shard))),
                expand_bias[None],
                jnp.zeros((5, inner_shard), F32),
            ]
        )
        small_rows = jnp.pad(small_rows, ((0, 0), (0, width - inner_shard))).astype(BF)
        pack_two = jnp.concatenate([low_attention[3 * shard :], small_rows])
        one = gather_staged(pack_one)
        two = gather_half(pack_two)
        three = gather_half(pack_three)
        given = None
        cross_shards = (shard,) * 5
        hidden_shards = (*(shard,) * blocks, inner_shard)
    else:
        place, cross_shards, hidden_shards = None, None, None
        flat = jnp.concatenate([layer_vectors.reshape(-1), expand_bias]).astype(BF)
        flat = lax.all_gather(flat, "fsdp", axis=0).astype(F32)
        vector_size = layer_vectors.size
        vec = flat[:, :vector_size].reshape(count, -1, shard).transpose(1, 0, 2).reshape(-1, width)
        given = jnp.pad(vec, ((0, 16 - vec.shape[0]), (0, 0))), flat[:, vector_size:].reshape(1, -1)

        def gather_all(pack, shards):
            full = lax.all_gather(pack, "fsdp", axis=0)
            pieces, first = [], 0
            for rows in shards:
                pieces.append(full[:, first : first + rows].reshape(-1, width))
                first += rows
            return pieces

        def owners(grads, shards):
            pieces, first = [], 0
            for rows in shards:
                pieces.append(grads[first : first + rows * count].reshape(count, rows, width))
                first += rows * count
            return jnp.concatenate(pieces, axis=1)

        one = jnp.concatenate(gather_all(pack_one, (shard,) * 3))
        two = [m[None] for m in gather_all(low_attention[3 * shard :], (shard,) * 5)]
        three = [m[None] for m in gather_all(pack_three, (*(shard,) * blocks, inner_shard))]

    *saved_one, matrices = forward_self(place, x, target_pos, one, small)
    two = both_halves(two, saved_one[3]) if small else two
    norm_one, inv_one, *saved_two, norm_two, inv_two, vec, bias = forward_cross(
        place, x, saved_one[3], source, memory_length, two, given, cross_shards
    )
    three = both_halves(three, norm_two) if small else three
    sums_three, bias_sum, outputs, dz_two, *grad_three = hidden_step(
        place, three, norm_two, inv_two, cot, vec, bias, hidden_shards
    )
    if small:
        keep_three, send_three = reduce_cores(*grad_three)
        dz_two = after(dz_two, keep_three, send_three)
        received_three = send_rows(send_three)
    sums_two, dz_one, memory_grad, *grad_two = backward_cross(
        place, two, dz_two, x, norm_one, inv_one, source, memory_length, vec, saved_two, saved_one[3],
        (sums_three, bias_sum), cross_shards,
    )
    if small:
        joined_three = reduce_rows(keep_three, received_three, dz_one)
        keep_two, send_two = reduce_cores(grad_two[0], after(grad_two[1], joined_three))
        dz_one = after(dz_one, joined_three, keep_two, send_two)
        received_two = send_rows(send_two)
    input_grad, *grad_one = backward_self(
        place, two if small else two[:1], dz_one, x, target_pos, vec, matrices, saved_one, cross_shards
    )

    attention = (attention_weights, first_attention, second_attention)
    expand = (expand_weights, first_expand, second_expand)
    shrink = (shrink_weights, first_shrink, second_shrink)
    bias = (expand_bias, first_bias, second_bias)
    vectors = (layer_vectors, first_vectors, second_vectors)
    if small:
        powers = 1.0 - hyper_rates[1:3] ** step_float
        scalars = place, jnp.concatenate([hyper_rates, powers])
        part_three = reduce_line(joined_three)
        part_two = reduce_line(reduce_rows(keep_two, received_two, input_grad))
        keep_one, send_one = reduce_cores(*grad_one)
        part_one = reduce_shifts(reduce_rows(keep_one, send_rows(send_one), input_grad))
        total_three = reduce_last(after(part_three, input_grad))
        total_two = reduce_last(part_two)
        total_one = reduce_last(part_one)
        hidden_new = adam_call(hidden_adam_kernel, scalars, total_three, (*expand, *shrink))
        rows = tuple(b[None] for b in bias)
        other_new = adam_call(
            attention_adam_kernel, scalars, (*total_one, *total_two), (*attention, *rows, *vectors)
        )
        new_bias = tuple(b[0] for b in other_new[3:6])
        updated = (*other_new[:3], *hidden_new, *new_bias, *other_new[6:])
    else:
        sums = (sums_two + sums_three)[: layer_vectors.shape[0]]
        flat = jnp.concatenate(
            [
                sums.reshape(-1, count, shard).transpose(1, 0, 2).reshape(count, -1),
                bias_sum.reshape(count, inner_shard),
            ],
            axis=1,
        )
        total_three = reduce_plain(owners(grad_three[0], (*(shard,) * blocks, inner_shard)))
        total_two = reduce_plain(owners(grad_two[0], (shard,) * 5))
        total_one = reduce_plain(owners(grad_one[0], (shard,) * 3))
        flat = lax.psum(lax.psum_scatter(flat, "fsdp", scatter_dimension=0), "rep")
        grad_attention = jnp.concatenate([total_one, total_two]).reshape(attention_weights.shape)
        grad_expand = total_three[: blocks * shard].reshape(blocks, shard, width).transpose(1, 0, 2)
        updated = []
        for (now, one_now, two_now), grad, factor in (
            (attention, grad_attention, 1.0),
            (expand, grad_expand.reshape(shard, -1), 1.0),
            (shrink, total_three[blocks * shard :], 1.0),
            (bias, flat[layer_vectors.size :], 0.0),
            (vectors, flat[: layer_vectors.size].reshape(-1, shard), 0.0),
        ):
            updated.extend(adam_update(now, grad, one_now, two_now, hyper_rates, step_float, factor))
    return (outputs[None], input_grad[None], memory_grad[None], *updated)


def solution(mesh):
    rows = ("rep", "fsdp")
    params = (P(None, "fsdp", None), P("fsdp", None), P("fsdp", None), P("fsdp"), P(None, "fsdp"))
    return jax.shard_map(
        functools.partial(per_device, small_mesh(mesh)),
        mesh=mesh,
        in_specs=(
            P(rows, None, None), P(rows, None, None), P(rows), P(rows, None), P(rows, None, None),
            *params, *params, *params, P(), P(),
        ),
        out_specs=(
            P(rows, None, None), P(rows, None, None), P(rows, None, None),
            *(spec for spec in params for _ in range(3)),
        ),
        check_vma=False,
    )
```

```python
import functools

import jax
import jax.numpy as jnp
from jax import lax
from jax.experimental import pallas as pl
from jax.experimental.pallas import tpu as pltpu
from jax.sharding import PartitionSpec as P

BF = jnp.bfloat16
F32 = jnp.float32
HEAD_DIM = 64
PAIR = 128
TILE = 256
MIB = 1 << 20


def dot(left, right, left_dim, right_dim):
    return lax.dot_general(
        left, right, (((left_dim,), (right_dim,)), ((), ())), preferred_element_type=F32
    )


def lanes(size):
    return lax.broadcasted_iota(jnp.int32, (1, size), 1)


def half_masks():
    first = jnp.where(lanes(PAIR) < HEAD_DIM, 1.0, 0.0)
    return first.astype(BF), (1.0 - first).astype(BF)


def rows_at(index, size=TILE):
    return pl.ds(pl.multiple_of(index * size, size), size)


def split_three(column):
    high = column.astype(BF).astype(F32)
    rest = column - high
    middle = rest.astype(BF).astype(F32)
    return high, middle, rest - middle


def with_column(block, column, base, last):
    high, middle, low = split_three(column)
    lane = lanes(PAIR)
    tail = jnp.where(lane == base + 3, last, block)
    return jnp.where(
        lane == base, -high, jnp.where(lane == base + 1, -middle, jnp.where(lane == base + 2, -low, tail))
    ).astype(BF)


class Mover:
    def __init__(self, sems):
        self.sems, self.used, self.leaving = sems, 0, []

    def take(self, count=1):
        self.used += count
        return self.used - count

    def load(self, source, target):
        copy = pltpu.make_async_copy(source, target, self.sems.at[self.take()])
        copy.start()
        return copy

    def load_rows(self, source, target):
        count = source.shape[0] // TILE
        first = self.take(count)

        def copy(tile):
            rows = rows_at(tile)
            return pltpu.make_async_copy(source.at[rows], target.at[rows], self.sems.at[first + tile])

        for tile in range(count):
            copy(tile).start()
        return lambda tile: copy(tile).wait()

    def store(self, source, target):
        self.leaving.append(self.load(source, target))

    def store_parts(self, source, target, count, where):
        first = self.take(count)

        def copy(part):
            return pltpu.make_async_copy(source.at[where(part)], target.at[where(part)], self.sems.at[first + part])

        self.leaving.extend(copy(part) for part in range(count))
        return lambda part: copy(part).start()

    def store_rows(self, source, target):
        return self.store_parts(source, target, source.shape[0] // TILE, rows_at)

    def finish(self):
        for copy in self.leaving:
            copy.wait()


def columns_at(size):
    return lambda part: (slice(None), rows_at(part, size))


def load_matrices(mover, core, sources, targets, which=None):
    waits, first = [], 0
    for index, target in enumerate(targets):
        if which is not None and index not in which:
            first += target.shape[1]
            continue
        if core is None:
            copies = [mover.load(sources[index], target)]
        else:
            rows, half = target.shape[1], target.shape[2] // 2
            copies = []
            for step, source in enumerate(sources):
                cols = pl.ds(pl.multiple_of(jnp.bitwise_xor(core, step) * half, half), half)
                copies.append(mover.load(source.at[:, first : first + rows, :], target.at[:, :, cols]))
            first += rows
        waits.append(lambda copies=copies: [copy.wait() for copy in copies])
    return waits


def whole(ref):
    return ref[...].reshape(-1, ref.shape[-1])


def key_extra(length_limit, count):
    lane = lanes(PAIR) % HEAD_DIM
    extra = jnp.where(lane < 3, 1.0, 0.0)
    if length_limit is None:
        return jnp.broadcast_to(extra, (count, PAIR)).astype(BF)
    row = lax.broadcasted_iota(jnp.int32, (count, PAIR), 0)
    bias = jnp.where(row < length_limit, 0.0, -1e30)
    return jnp.where(lane == 3, bias, extra).astype(BF)


def put_start(pos_ref, start_ref):
    length = start_ref.shape[0]
    query = lax.broadcasted_iota(jnp.int32, (8, length), 1)
    first = (query - pos_ref[...]).astype(F32)
    start_ref[...] = first.T[:, :1].astype(jnp.int32)


def visible(start, first_query, first_key, count):
    key = first_key + lax.broadcasted_iota(jnp.int32, (TILE, count), 1)
    seen = key >= start
    if first_key == first_query:
        query = first_query + lax.broadcasted_iota(jnp.int32, (TILE, count), 0)
        seen = seen & (key <= query)
    return seen


def key_spans(tile, count, causal):
    if not causal:
        return [(0, count)]
    spans = [(0, tile * TILE)] if tile else []
    return spans + [(tile * TILE, TILE)]


class ProbStore:
    def __init__(self, mover, hbm, ref, causal):
        self.hbm, self.ref, self.mover = hbm, ref, mover
        self.tiles = ref.shape[2] // TILE
        self.causal = causal
        self.first = mover.take(2 * self.tiles)

    def views(self, pair, slot, tile):
        rows = slice(tile * TILE, (tile + 1) * TILE)
        keys = slice(0, (tile + 1) * TILE) if self.causal else slice(0, self.ref.shape[3])
        sem = self.mover.sems.at[self.first + slot * self.tiles + tile]
        return self.hbm.at[pair, :, rows, keys], self.ref.at[slot, :, rows, keys], sem

    def copy(self, pair, slot, tile, out):
        far, near, sem = self.views(pair, slot, tile)
        return pltpu.make_async_copy(near, far, sem) if out else pltpu.make_async_copy(far, near, sem)


def two_pairs(pairs, body):
    @pl.loop(0, pairs // 2)
    def _(step):
        for slot in (0, 1):
            body(2 * step + slot, slot, step)


def attend(q_ref, k_ref, v_ref, extra_ref, start_ref, o_ref, store, finished):
    length, count = q_ref.shape[0], k_ref.shape[0]
    causal = start_ref is not None
    masks = half_masks()
    pairs = q_ref.shape[1] // PAIR

    def one_pair(pair, slot, step):
        cols = rows_at(pair, PAIR)

        @pl.when(step > 0)
        def _():
            for tile in range(store.tiles):
                store.copy(pair - 2, slot, tile, True).wait()

        for tile in range(length // TILE):
            rows = slice(tile * TILE, (tile + 1) * TILE)
            spans = key_spans(tile, count, causal)
            results = []
            for side in (0, 1):
                base = HEAD_DIM * (1 - side)
                queries = q_ref[rows, cols] * masks[side]
                if not causal:
                    queries = jnp.where(lanes(PAIR) == base + 3, 1.0, queries.astype(F32)).astype(BF)
                score_blocks = []
                for first, size in spans:
                    keys = k_ref[first : first + size, cols]
                    if not causal:
                        keys = keys * masks[side] + extra_ref[first : first + size, :] * masks[1 - side]
                    scores = dot(queries, keys, 1, 1)
                    if causal:
                        seen = visible(start_ref[rows, :], tile * TILE, first, size)
                        scores = jnp.where(seen, scores, -1000000000.0)
                    score_blocks.append(scores)
                top = functools.reduce(
                    jnp.maximum, [jnp.max(scores, axis=1, keepdims=True) for scores in score_blocks]
                )
                exponents = [jnp.exp(scores - top) for scores in score_blocks]
                inverse = 1.0 / sum(jnp.sum(exponent, axis=1, keepdims=True) for exponent in exponents)
                total = None
                for exponent, (first, size) in zip(exponents, spans):
                    probs = (exponent * inverse).astype(BF)
                    store.ref[slot, side, rows, first : first + size] = probs
                    part = dot(probs, v_ref[first : first + size, cols], 1, 0)
                    total = part if total is None else total + part
                results.append(total)
            o_ref[rows, cols] = jnp.where(lanes(PAIR) < HEAD_DIM, results[0], results[1]).astype(BF)
        for tile in range(store.tiles):
            store.copy(pair, slot, tile, True).start()
        for start_store in finished:
            start_store(pair)

    two_pairs(pairs, one_pair)
    for slot in (0, 1):
        for tile in range(store.tiles):
            store.mover.leaving.append(store.copy(pairs - 2 + slot, slot, tile, True))


def load_probs(store, slot):
    for tile in reversed(range(store.tiles)):
        store.copy(slot, slot, tile, False).start()


def attend_back(q_ref, da_ref, k_ref, v_ref, store, dq_ref, dk_ref, dv_ref, dk_sum, dv_sum, values_ref):
    length, count = q_ref.shape[0], k_ref.shape[0]
    masks = half_masks()
    pairs = k_ref.shape[1] // PAIR

    def one_pair(pair, slot, step):
        cols = rows_at(pair, PAIR)
        for tile in range(store.tiles):
            store.copy(pair, slot, tile, False).wait()
        for side in (0, 1):
            values_ref[side] = v_ref[:, cols] * masks[side] + masks[1 - side]
        for tile in reversed(range(length // TILE)):
            rows = slice(tile * TILE, (tile + 1) * TILE)
            span = slice(0, (tile + 1) * TILE if store.causal else count)
            query_grads = []
            for side in (0, 1):
                head_cols = pl.ds(pl.multiple_of(pair * 2 * PAIR, PAIR) + side * PAIR, PAIR)
                grads = da_ref[rows, head_cols]
                probs = store.ref[slot, side, rows, span]
                value_part = dot(grads, probs, 0, 0)
                grad_scores = (probs.astype(F32) * dot(grads, values_ref[side, span, :], 1, 1)).astype(BF)
                key_part = dot(q_ref[rows, cols], grad_scores, 0, 0)
                if tile == length // TILE - 1:
                    dv_sum[side, :, span] = value_part
                    dk_sum[side, :, span] = key_part
                else:
                    dv_sum[side, :, span] += value_part
                    dk_sum[side, :, span] += key_part
                query_grads.append(dot(grad_scores, k_ref[span, cols], 1, 0))
            dq_ref[rows, cols] = (
                jnp.where(lanes(PAIR) < HEAD_DIM, query_grads[0], query_grads[1]) * HEAD_DIM**-0.5
            ).astype(BF)
        for sums, out in ((dk_sum, dk_ref), (dv_sum, dv_ref)):
            joined = jnp.concatenate([sums[0, :HEAD_DIM, :], sums[1, HEAD_DIM:, :]], axis=0)
            out[:, cols] = joined.astype(BF).T

        @pl.when(step < pairs // 2 - 1)
        def _():
            for tile in range(store.tiles):
                store.copy(pair + 2, slot, tile, False).start()

    two_pairs(pairs, one_pair)


def norm_rows(summed):
    center = jnp.mean(summed, axis=1, keepdims=True)
    shifted = summed - center
    inverse = lax.rsqrt(jnp.mean(shifted * shifted, axis=1, keepdims=True) + 1e-05)
    return shifted * inverse, inverse


def norm_back(grad_out, normed, inverse, gain):
    scaled = grad_out * gain
    first = jnp.mean(scaled, axis=1, keepdims=True)
    second = jnp.mean(scaled * normed, axis=1, keepdims=True)
    return inverse * (scaled - first - normed * second)


def add_rows(ref, row, values):
    ref[row : row + 1, :] += jnp.sum(values, axis=0, keepdims=True)


def place_of(place_ref):
    rep, place = place_ref[0], place_ref[1]
    return lax.rem(rep, 2), lax.div(rep, 2), lax.div(place, 2), lax.rem(place, 2)


def assemble(place_ref, chunk_refs, all_ref):
    core, chip, line, row = place_of(place_ref)
    width = all_ref.shape[1]
    quarter = chunk_refs[0].shape[3]
    shard = quarter * 4 // 3
    for core_step, chunk_ref in enumerate(chunk_refs):
        for chip_step in (0, 1):
            rep = jnp.bitwise_xor(chip, chip_step) * 2 + jnp.bitwise_xor(core, core_step)
            for line_step in range(4):
                for row_step in (0, 1):
                    owner = lax.rem(line - line_step + 4, 4) * 2 + jnp.bitwise_xor(row, row_step)
                    for piece in range(quarter // 16):
                        stacked = rep * quarter + piece * 16
                        matrix = lax.div(stacked, shard)
                        target = matrix * width + owner * shard + (stacked - matrix * shard)
                        all_ref[pl.ds(pl.multiple_of(target, 16), 16), :] = chunk_ref[
                            chip_step, line_step, row_step, piece * 16 : (piece + 1) * 16, :
                        ]


def assemble_halves(place_ref, mine_ref, other_ref, all_ref, shards):
    core = place_of(place_ref)[0]
    devices, _, half = mine_ref.shape
    for step, ref in ((0, mine_ref), (1, other_ref)):
        cols = pl.ds(pl.multiple_of(jnp.bitwise_xor(core, step) * half, half), half)
        first, target = 0, 0
        for shard in shards:
            for owner in range(devices):
                at = target + owner * shard
                all_ref[at : at + shard, cols] = ref[owner, first : first + shard, :]
            first += shard
            target += shard * devices


def unpack_small(all_ref, base, vec_ref, bias_ref):
    devices = vec_ref.shape[1] // HEAD_DIM
    inner = bias_ref.shape[1] // devices
    for pair in range(devices // 2):
        first = base + 2 * pair * 16
        left = all_ref[first : first + 16, :PAIR].astype(F32)
        right = all_ref[first + 16 : first + 32, :PAIR].astype(F32)
        vec_ref[:, pair * PAIR : (pair + 1) * PAIR] = jnp.where(
            lanes(PAIR) < HEAD_DIM, left, pltpu.roll(right, HEAD_DIM, 1)
        )
    for owner in range(devices):
        rows = all_ref[base + owner * 16 : base + owner * 16 + 16, :inner].astype(F32)
        bias_ref[:, owner * inner : (owner + 1) * inner] = rows[10:11, :]


def self_forward_kernel(staged, *refs):
    if staged:
        place_ref, pos_ref, x_hbm, chunk_hbm, other_hbm = refs[:5]
        refs = refs[5:]
    else:
        pos_ref, x_hbm, all_hbm = refs[:3]
        refs = refs[3:]
    p_hbm, q_hbm, k_hbm, v_hbm, o_hbm = refs[:5]
    refs = refs[5:]
    if staged:
        all_out, refs = refs[0], refs[1:]
    x_ref, all_ref, q_ref, k_ref, v_ref, o_ref, p_ref, start_ref = refs[:8]
    mover = Mover(refs[-1])
    length, width = x_ref.shape
    if staged:
        chunk_refs = refs[8:10]
        loads = [mover.load(a, b) for a, b in zip((chunk_hbm, other_hbm), chunk_refs)]
    else:
        loads = [mover.load(all_hbm, all_ref)]
    x_load = mover.load(x_hbm, x_ref)
    put_start(pos_ref, start_ref)
    for load in loads:
        load.wait()
    if staged:
        assemble(place_ref, chunk_refs, all_ref)
        mover.store(all_ref, all_out)
    x_load.wait()

    @pl.loop(0, length // TILE)
    def _(tile):
        rows = rows_at(tile)
        source = x_ref[rows, :]
        queries = dot(source, all_ref[:width, :], 1, 0).astype(BF)
        q_ref[rows, :] = queries * jnp.asarray(HEAD_DIM**-0.5, BF)
        k_ref[rows, :] = dot(source, all_ref[width : 2 * width, :], 1, 0).astype(BF)
        v_ref[rows, :] = dot(source, all_ref[2 * width :, :], 1, 0).astype(BF)

    mover.store(k_ref, k_hbm)
    mover.store(v_ref, v_hbm)
    mover.store(q_ref, q_hbm)
    finished = (mover.store_parts(o_ref, o_hbm, width // PAIR, columns_at(PAIR)),)
    attend(q_ref, k_ref, v_ref, None, start_ref, o_ref, ProbStore(mover, p_hbm, p_ref, True), finished)
    mover.finish()


def unpack_small(small_ref, vec_ref, bias_ref):
    devices = vec_ref.shape[1] // HEAD_DIM
    inner = bias_ref.shape[1] // devices
    for pair in range(devices // 2):
        left = small_ref[0, 2 * pair, :, :PAIR].astype(F32)
        right = small_ref[0, 2 * pair + 1, :, :PAIR].astype(F32)
        vec_ref[:, pair * PAIR : (pair + 1) * PAIR] = jnp.where(
            lanes(PAIR) < HEAD_DIM, left, pltpu.roll(right, HEAD_DIM, 1)
        )
    for owner in range(devices):
        rows = small_ref[0, owner, :, :inner].astype(F32)
        bias_ref[:, owner * inner : (owner + 1) * inner] = rows[10:11, :]


def cross_forward_kernel(staged, *refs):
    place_ref, core = None, None
    if staged:
        place_ref, refs = refs[0], refs[1:]
        core = place_of(place_ref)[0]
    length_ref, refs = refs[0], refs[1:]
    if staged:
        x_hbm, mixed_hbm, source_hbm, *packs = refs[:5]
        refs = refs[5:]
    else:
        vec_ref, x_hbm, mixed_hbm, source_hbm, *packs = refs[:9]
        refs = refs[9:]
    first_hbm, first_inv_hbm, p_hbm, q_hbm, k_hbm, v_hbm, o_hbm, n_hbm, inv_hbm = refs[:9]
    refs = refs[9:]
    if staged:
        vec_ref, bias_ref, refs = refs[0], refs[1], refs[2:]
    x_ref, mixed_ref, source_ref, first_ref, first_inv_ref, q_ref, k_ref, v_ref, o_ref, n_ref, inv_ref = refs[:11]
    p_ref, extra_ref, *w_refs = refs[11:18]
    mover = Mover(refs[-1])
    length, width = q_ref.shape

    if staged:
        small_ref = refs[18]
        rows = packs[0].shape[1]
        small = [
            mover.load(pack.at[:, rows - 16 :, :], small_ref.at[jnp.bitwise_xor(core, step)])
            for step, pack in enumerate(packs)
        ]
    source_load = mover.load_rows(source_hbm, source_ref)
    order = (2, 3, 0, 1, 4)
    waits = [None] * 5
    if staged:
        half = width // 2
        shard = w_refs[0].shape[1]
        for index in order:
            copies = []
            for step, pack in enumerate(packs):
                cols = pl.ds(pl.multiple_of(jnp.bitwise_xor(core, step) * half, half), half)
                copies.append(
                    mover.load(pack.at[:, index * shard : (index + 1) * shard, :], w_refs[index].at[:, :, cols])
                )
            waits[index] = lambda copies=copies: [copy.wait() for copy in copies]
    else:
        for index in order:
            waits[index] = mover.load(packs[index], w_refs[index]).wait
    mixed_load = mover.load_rows(mixed_hbm, mixed_ref)
    x_load = mover.load_rows(x_hbm, x_ref)
    extra_ref[...] = key_extra(length_ref[0], k_ref.shape[0])
    waits[2]()
    waits[3]()

    @pl.loop(0, source_ref.shape[0] // TILE)
    def _(tile):
        rows = rows_at(tile)
        source_load(tile)
        source = source_ref[rows, :]
        k_ref[rows, :] = dot(source, whole(w_refs[2]), 1, 0).astype(BF)
        v_ref[rows, :] = dot(source, whole(w_refs[3]), 1, 0).astype(BF)

    mover.store(k_ref, k_hbm)
    mover.store(v_ref, v_hbm)
    if staged:
        for load in small:
            load.wait()
        unpack_small(small_ref, vec_ref, bias_ref)
    waits[0]()
    waits[1]()

    @pl.loop(0, length // TILE)
    def _(tile):
        rows = rows_at(tile)
        mixed_load(tile)
        x_load(tile)
        summed = x_ref[rows, :].astype(F32) * vec_ref[6:7, :] + dot(mixed_ref[rows, :], whole(w_refs[0]), 1, 0)
        normed, inverse = norm_rows(summed)
        first_ref[rows, :] = normed
        first_inv_ref[rows, :] = inverse
        low = (normed * vec_ref[0:1, :] + vec_ref[3:4, :]).astype(BF)
        queries = dot(low, whole(w_refs[1]), 1, 0).astype(BF)
        q_ref[rows, :] = queries * jnp.asarray(HEAD_DIM**-0.5, BF)

    mover.store(first_ref, first_hbm)
    mover.store(first_inv_ref, first_inv_hbm)
    mover.store(q_ref, q_hbm)
    finished = (mover.store_parts(o_ref, o_hbm, width // PAIR, columns_at(PAIR)),)
    attend(q_ref, k_ref, v_ref, extra_ref, None, o_ref, ProbStore(mover, p_hbm, p_ref, False), finished)
    waits[4]()
    n_store, inv_store = mover.store_rows(n_ref, n_hbm), mover.store_rows(inv_ref, inv_hbm)

    @pl.loop(0, length // TILE)
    def _(tile):
        rows = rows_at(tile)
        first_out = first_ref[rows, :] * vec_ref[0:1, :] + vec_ref[3:4, :]
        summed = first_out * vec_ref[7:8, :] + dot(o_ref[rows, :], whole(w_refs[4]), 1, 0)
        normed, inverse = norm_rows(summed)
        n_ref[rows, :] = normed
        inv_ref[rows, :] = inverse
        n_store(tile)
        inv_store(tile)

    mover.finish()


def hidden_kernel(staged, *refs):
    place_ref, core = None, None
    if staged:
        place_ref, refs = refs[0], refs[1:]
        core = place_of(place_ref)[0]
    vec_ref, bias_ref, *packs = refs[: 4 if staged else 7]
    n_hbm, inv_hbm, cot_hbm = refs[len(packs) + 2 : len(packs) + 5]
    refs = refs[len(packs) + 5 :]
    count = 2 if staged else 1
    sums_ref, bias_sum_ref, out_hbm, dz_hbm = refs[:4]
    grad_hbms, refs = refs[4 : 4 + count], refs[4 + count :]
    grad_refs, refs = refs[:count], refs[count:]
    n_ref, inv_ref, cot_ref, out_ref, dz_ref, low_ref, h_ref, du_ref, df_ref, slope_ref, third_ref = refs[:11]
    blocks = bias_ref.shape[1] // vec_ref.shape[1]
    *e_refs, s_ref = refs[11 : 12 + blocks]
    mover = Mover(refs[-1])
    length, width = n_ref.shape

    n_load = mover.load_rows(n_hbm, n_ref)
    waits = load_matrices(mover, core, packs, (*e_refs, s_ref))
    cot_load = mover.load_rows(cot_hbm, cot_ref)
    inv_load = mover.load_rows(inv_hbm, inv_ref)
    out_store, dz_store = mover.store_rows(out_ref, out_hbm), mover.store_rows(dz_ref, dz_hbm)
    tiles = [slice(tile * TILE, (tile + 1) * TILE) for tile in range(length // TILE)]
    parts = [slice(block * width, (block + 1) * width) for block in range(blocks)]
    sums = {row: 0.0 for row in (1, 2, 4, 5, 8, 9)}
    bias_sums = [0.0] * blocks

    def add(row, values):
        sums[row] = sums[row] + jnp.sum(values, axis=0, keepdims=True)

    def second_out(rows):
        return n_ref[rows, :] * vec_ref[1:2, :] + vec_ref[4:5, :]

    def staggered(first, then, count):
        ready = first(0)
        for index in range(count):
            following = first(index + 1) if index + 1 < count else None
            then(index, ready)
            ready = following

    for tile, rows in enumerate(tiles):
        n_load(tile)
        low_ref[rows, :] = second_out(rows).astype(BF)
    steps = [(block, rows) for block in range(blocks) for rows in tiles]

    def expand(index):
        block, rows = steps[index]
        if index % len(tiles) == 0:
            waits[block]()
        return dot(low_ref[rows, :], whole(e_refs[block]), 1, 0) + bias_ref[:, parts[block]]

    def activate(index, before):
        block, rows = steps[index]
        square = before * before
        tangent = jnp.tanh(before * (0.7978845608028654 + 0.7978845608028654 * 0.044715 * square))
        half = 0.5 * (1.0 + tangent)
        slope_ref[rows, parts[block]] = half + before * (half * (1.0 - tangent)) * (
            0.7978845608028654 + 3.0 * 0.7978845608028654 * 0.044715 * square
        )
        h_ref[rows, parts[block]] = (before * half).astype(BF)

    staggered(expand, activate, len(steps))
    waits[blocks]()
    for tile in range(len(tiles)):
        cot_load(tile)
        inv_load(tile)

    def shrink(tile):
        return dot(h_ref[tiles[tile], :], whole(s_ref), 1, 0)

    def outer_norm(tile, branch_out):
        rows = tiles[tile]
        second = second_out(rows)
        normed, inverse = norm_rows(second * vec_ref[8:9, :] + vec_ref[9:10, :] + branch_out)
        out_ref[rows, :] = (normed * vec_ref[2:3, :] + vec_ref[5:6, :]).astype(BF)
        grad_out = cot_ref[rows, :].astype(F32)
        third = norm_back(grad_out, normed, inverse, vec_ref[2:3, :])
        third_ref[rows, :] = third
        add(2, grad_out * normed)
        add(5, grad_out)
        branch = third.astype(BF)
        df_ref[rows, :] = branch
        add(9, branch.astype(F32))
        add(8, second * third)

    staggered(shrink, outer_norm, len(tiles))
    for tile in range(len(tiles)):
        out_store(tile)

    def shrink_back(index):
        block, rows = steps[index]
        return dot(df_ref[rows, :], whole(s_ref)[parts[block], :], 1, 1)

    def slope_back(index, grad_hidden):
        block, rows = steps[index]
        du = (grad_hidden * slope_ref[rows, parts[block]]).astype(BF)
        du_ref[rows, parts[block]] = du
        bias_sums[block] = bias_sums[block] + jnp.sum(du.astype(F32), axis=0, keepdims=True)

    staggered(shrink_back, slope_back, len(steps))

    def expand_back(tile):
        rows = tiles[tile]
        return sum(dot(du_ref[rows, parts[block]], whole(e_refs[block]), 1, 1) for block in range(blocks))

    def inner_norm(tile, grad_expanded):
        rows = tiles[tile]
        grad = vec_ref[8:9, :] * third_ref[rows, :] + grad_expanded
        normed = n_ref[rows, :]
        dz_ref[rows, :] = norm_back(grad, normed, inv_ref[rows, :], vec_ref[1:2, :])
        add(1, grad * normed)
        add(4, grad)

    staggered(expand_back, inner_norm, len(tiles))
    for tile in range(len(tiles)):
        dz_store(tile)
    sums_ref[...] = jnp.zeros_like(sums_ref)
    for row, values in sums.items():
        sums_ref[row : row + 1, :] = values
    for block, values in enumerate(bias_sums):
        bias_sum_ref[:, parts[block]] = values
    for step in reversed(range(count)):
        for block in range(blocks):
            put_grad(grad_refs, step, place_ref, block, low_ref[...], du_ref, block * width)
            put_shrink(grad_refs, step, place_ref, block, blocks, h_ref[:, parts[block]], df_ref)
        mover.store(grad_refs[step], grad_hbms[step])
    mover.finish()


def branch_grads(branch, mixed_weight, o_rows, da_ref, rows):
    masks = half_masks()
    mixed_grad = dot(branch, mixed_weight, 1, 1).astype(BF)
    for pair in range(mixed_grad.shape[1] // PAIR):
        cols = slice(pair * PAIR, (pair + 1) * PAIR)
        grad_pair = mixed_grad[:, cols].astype(F32)
        product = grad_pair * o_rows[:, cols].astype(F32)
        for side in (0, 1):
            mask = masks[side].astype(F32)
            inner = jnp.sum(product * mask, axis=1, keepdims=True)
            first = (2 * pair + side) * PAIR
            da_ref[rows, first : first + PAIR] = with_column(
                grad_pair * mask, inner, HEAD_DIM * (1 - side), 0.0
            )


def put_grad(grad_refs, step, place_ref, index, left, right_ref, first=0):
    width = left.shape[1]
    if place_ref is None:
        grad = dot(left, right_ref[:, first : first + width], 0, 0)
        grad_refs[0][index * width : (index + 1) * width, :] = grad.astype(BF)
        return
    core, _, _, row = place_of(place_ref)
    half = width // 2
    shard = width // 8
    cols = pl.ds(pl.multiple_of(first + jnp.bitwise_xor(core, step) * half, half), half)
    grad = dot(left, right_ref[:, cols], 0, 0).astype(BF).reshape(4, 2, shard, half)
    for side in (0, 1):
        slot = jnp.bitwise_xor(row, side)
        grad_refs[step][slot, :, index * shard : (index + 1) * shard, :] = grad[:, side]


def put_shrink(grad_refs, step, place_ref, block, blocks, left, right_ref):
    width = left.shape[1]
    if place_ref is None:
        first = (blocks + block) * width
        grad_refs[0][first : first + width, :] = dot(left, right_ref[...], 0, 0).astype(BF)
        return
    core, _, _, row = place_of(place_ref)
    half, shard = width // 2, width * blocks // 8
    base = width // 8 * blocks
    cols = pl.ds(pl.multiple_of(jnp.bitwise_xor(core, step) * half, half), half)
    grad = dot(left, right_ref[:, cols], 0, 0).astype(BF).reshape(width // shard, shard, half)
    for part in range(width // shard):
        owner = block * (width // shard) + part
        grad_refs[step][jnp.bitwise_xor(row, owner % 2), owner // 2, base:, :] = grad[part]


def put_small(grad_refs, place_ref, base, sums, bias_sum):
    core, _, _, row = place_of(place_ref)
    half = grad_refs[0].shape[3]
    inner = bias_sum.shape[1] // 8
    index = lax.broadcasted_iota(jnp.int32, (16, half), 0)
    for owner in range(8):
        block = sums[:, owner // 2 * PAIR : (owner // 2 + 1) * PAIR]
        if owner % 2:
            block = pltpu.roll(block, HEAD_DIM, 1)
        block = jnp.concatenate([block, jnp.zeros((16, half - PAIR), F32)], axis=1)
        block = jnp.where(index == 10, bias_sum[:, owner * inner : (owner + 1) * inner], block)
        high = block.astype(BF)
        low = (block - high.astype(F32)).astype(BF)
        slot = jnp.bitwise_xor(row, owner % 2)
        first = (core == 0).astype(F32)
        for step, grad_ref in enumerate(grad_refs):
            is_high = first if step == 0 else 1.0 - first
            mixed = high.astype(F32) * is_high + low.astype(F32) * (1.0 - is_high)
            grad_ref[slot, owner // 2, base : base + 16, :] = mixed.astype(BF)


def cross_backward_kernel(staged, *refs):
    place_ref, core = None, None
    if staged:
        place_ref, refs = refs[0], refs[1:]
        core = place_of(place_ref)[0]
    vec_ref, refs = refs[0], refs[1:]
    if staged:
        sums_three_ref, bias_sum_ref, refs = refs[0], refs[1], refs[2:]
    packs, refs = refs[: 2 if staged else 5], refs[2 if staged else 5 :]
    p_hbm, dz_hbm, x_hbm, first_hbm, inv_hbm, source_hbm, q_hbm, k_hbm, v_hbm, o_hbm, self_o_hbm = refs[:11]
    sums_ref, dfirst_hbm, dsource_hbm = refs[11:14]
    count = 2 if staged else 1
    grad_hbms, refs = refs[14 : 14 + count], refs[14 + count :]
    grad_refs, refs = refs[:count], refs[count:]
    dz_ref, x_ref, first_ref, inv_ref, source_ref, q_ref, k_ref, v_ref, o_ref, self_o_ref = refs[:10]
    dfirst_ref, dsource_ref, *w_refs = refs[10:17]
    low_ref, da_ref, dq_ref, dk_ref, dv_ref, dk_sum, dv_sum, branch_ref, values_ref, p_ref = refs[17:27]
    mover = Mover(refs[-1])
    length, width = dz_ref.shape

    dz_load, o_load = mover.load_rows(dz_hbm, dz_ref), mover.load_rows(o_hbm, o_ref)
    waits = load_matrices(mover, core, packs, w_refs, (4,))
    sums_ref[...] = jnp.zeros_like(sums_ref)
    waits[0]()
    store = ProbStore(mover, p_hbm, p_ref, False)
    load_probs(store, 0)
    middle = [mover.load(a, b) for a, b in ((v_hbm, v_ref), (q_hbm, q_ref), (k_hbm, k_ref))]

    @pl.loop(0, length // TILE)
    def _(tile):
        rows = rows_at(tile)
        dz_load(tile)
        o_load(tile)
        branch = dz_ref[rows, :].astype(BF)
        branch_ref[rows, :] = branch
        branch_grads(branch, whole(w_refs[4]), o_ref[rows, :], da_ref, rows)

    for step in range(count):
        put_grad(grad_refs, step, place_ref, 4, o_ref[...], branch_ref)
    load_probs(store, 1)
    first_load = mover.load_rows(first_hbm, first_ref)
    waits = load_matrices(mover, core, packs, w_refs, (1, 2, 3))
    last = [
        mover.load(a, b)
        for a, b in ((source_hbm, source_ref), (x_hbm, x_ref), (inv_hbm, inv_ref), (self_o_hbm, self_o_ref))
    ]
    for load in middle:
        load.wait()
    attend_back(q_ref, da_ref, k_ref, v_ref, store, dq_ref, dk_ref, dv_ref, dk_sum, dv_sum, values_ref)
    for load in last:
        load.wait()
    for wait in waits:
        wait()
    for tile in range(length // TILE):
        first_load(tile)

    dsource_store = mover.store_rows(dsource_ref, dsource_hbm)

    @pl.loop(0, source_ref.shape[0] // TILE)
    def _(tile):
        rows = rows_at(tile)
        dsource_ref[rows, :] = dot(dk_ref[rows, :], whole(w_refs[2]), 1, 1) + dot(
            dv_ref[rows, :], whole(w_refs[3]), 1, 1
        )
        dsource_store(tile)

    dfirst_store = mover.store_rows(dfirst_ref, dfirst_hbm)

    @pl.loop(0, length // TILE)
    def _(tile):
        rows = rows_at(tile)
        grad = dz_ref[rows, :]
        dx = dot(dq_ref[rows, :], whole(w_refs[1]), 1, 1) + vec_ref[7:8, :] * grad
        normed = first_ref[rows, :]
        first_out = normed * vec_ref[0:1, :] + vec_ref[3:4, :]
        low_ref[rows, :] = first_out.astype(BF)
        add_rows(sums_ref, 7, first_out * grad)
        dfirst = norm_back(dx, normed, inv_ref[rows, :], vec_ref[0:1, :])
        dfirst_ref[rows, :] = dfirst
        dfirst_store(tile)
        add_rows(sums_ref, 0, dx * normed)
        add_rows(sums_ref, 3, dx)
        add_rows(sums_ref, 6, x_ref[rows, :].astype(F32) * dfirst)
        branch_ref[rows, :] = dfirst.astype(BF)

    if staged:
        put_small(grad_refs, place_ref, 5 * (width // 8), sums_ref[...] + sums_three_ref[...], bias_sum_ref[...])
    for step in reversed(range(count)):
        put_grad(grad_refs, step, place_ref, 1, low_ref[...], dq_ref)
        put_grad(grad_refs, step, place_ref, 2, source_ref[...], dk_ref)
        put_grad(grad_refs, step, place_ref, 3, source_ref[...], dv_ref)
        put_grad(grad_refs, step, place_ref, 0, self_o_ref[...], branch_ref)
        mover.store(grad_refs[step], grad_hbms[step])
    mover.finish()


def self_backward_kernel(staged, *refs):
    place_ref, core = None, None
    if staged:
        place_ref, refs = refs[0], refs[1:]
        core = place_of(place_ref)[0]
    count = 2 if staged else 1
    packs, refs = refs[:count], refs[count:]
    p_hbm, dz_hbm, x_hbm, q_hbm, k_hbm, v_hbm, o_hbm, *head_hbms = refs[:10]
    grad_hbms, refs = refs[10 : 10 + count], refs[10 + count :]
    grad_refs, refs = refs[:count], refs[count:]
    dz_ref, x_ref, q_ref, k_ref, v_ref, o_ref, w_ref = refs[:7]
    da_ref, dq_ref, dk_ref, dv_ref, dk_sum, dv_sum, values_ref, p_ref = refs[7:15]
    mover = Mover(refs[-1])
    length, width = dz_ref.shape

    dz_load = mover.load_rows(dz_hbm, dz_ref)
    waits = load_matrices(mover, core, packs, (w_ref,))
    o_load = mover.load_rows(o_hbm, o_ref)
    waits[0]()
    store = ProbStore(mover, p_hbm, p_ref, True)
    load_probs(store, 0)
    middle = [mover.load(a, b) for a, b in ((v_hbm, v_ref), (q_hbm, q_ref), (k_hbm, k_ref))]

    @pl.loop(0, length // TILE)
    def _(tile):
        rows = rows_at(tile)
        dz_load(tile)
        o_load(tile)
        branch_grads(dz_ref[rows, :].astype(BF), whole(w_ref), o_ref[rows, :], da_ref, rows)

    load_probs(store, 1)
    x_load = mover.load(x_hbm, x_ref)
    for load in middle:
        load.wait()
    attend_back(q_ref, da_ref, k_ref, v_ref, store, dq_ref, dk_ref, dv_ref, dk_sum, dv_sum, values_ref)
    for near, far in zip((dq_ref, dk_ref, dv_ref), head_hbms):
        mover.store(near, far)
    x_load.wait()
    for step in reversed(range(count)):
        for index, grads in enumerate((dq_ref, dk_ref, dv_ref)):
            put_grad(grad_refs, step, place_ref, index, x_ref[...], grads)
        mover.store(grad_refs[step], grad_hbms[step])
    mover.finish()


def input_grad_kernel(vec_ref, dz_hbm, all_hbm, dq_hbm, dk_hbm, dv_hbm, dx_hbm, *refs):
    dz_ref, all_ref, dq_ref, dk_ref, dv_ref, dx_ref, sems = refs
    mover = Mover(sems)
    width = dz_ref.shape[1]
    all_load = mover.load(all_hbm, all_ref)
    heads = (dq_ref, dk_ref, dv_ref)
    loads = [mover.load_rows(a, b) for a, b in zip((dq_hbm, dk_hbm, dv_hbm), heads)]
    loads.append(mover.load_rows(dz_hbm, dz_ref))
    dx_store = mover.store_rows(dx_ref, dx_hbm)
    all_load.wait()

    @pl.loop(0, dz_ref.shape[0] // TILE)
    def _(tile):
        rows = rows_at(tile)
        for load in loads:
            load(tile)
        dx = vec_ref[6:7, :] * dz_ref[rows, :]
        for index, grads in enumerate(heads):
            dx = dx + dot(grads[rows, :], all_ref[index * width : (index + 1) * width, :], 1, 1)
        dx_ref[rows, :] = dx
        dx_store(tile)

    mover.finish()


def call(kernel, args, outs, scratch, limit, flops, smem=(), near=(), near_outs=(), copies=0):
    spaces = [pltpu.SMEM if i in smem else pltpu.VMEM if i in near else pl.ANY for i in range(len(args))]
    out_spaces = [pltpu.VMEM if i in near_outs else pl.ANY for i in range(len(outs))]
    buffers = [pltpu.VMEM(shape, kind) for shape, kind in scratch]
    if copies:
        buffers.append(pltpu.SemaphoreType.DMA((copies,)))
    return pl.pallas_call(
        kernel,
        out_shape=[jax.ShapeDtypeStruct(shape, kind) for shape, kind in outs],
        in_specs=[pl.BlockSpec(memory_space=space) for space in spaces],
        out_specs=[pl.BlockSpec(memory_space=space) for space in out_spaces],
        scratch_shapes=buffers,
        compiler_params=pltpu.CompilerParams(vmem_limit_bytes=(63 if copies else limit) * MIB),
        cost_estimate=pl.CostEstimate(flops=flops, bytes_accessed=16 * MIB, transcendentals=0),
    )(*args)


def like(*arrays):
    return [(a.shape, a.dtype) for a in arrays]


def prob_shape(queries, keys, width):
    return (width // PAIR, 2, queries, keys), BF


def forward_self(place, x, pos, pack, staged):
    length, width = x.shape
    low = ((length, width), BF)
    outs = [prob_shape(length, length, width), low, low, low, low]
    matrices = ((3 * width, width), BF)
    scratch = [low, matrices, low, low, low, low, ((2, 2, length, length), BF), ((length, 1), jnp.int32)]
    if staged:
        return call(
            functools.partial(self_forward_kernel, True),
            (place, pos, x, *pack),
            [*outs, matrices],
            [*scratch, *like(*pack)],
            40, 10**10, smem=(0,), near=(1,), copies=24,
        )
    results = call(
        functools.partial(self_forward_kernel, False),
        (pos, x, pack), outs, scratch, 40, 10**10, near=(0,), copies=24,
    )
    return (*results, pack)


def matrix_buffers(shards, width):
    return [((8 if rows < width else 1, rows, width), BF) for rows in shards]


def forward_cross(place, x, mixed, source, count, packs, given, shards):
    length, width = x.shape
    keys = source.shape[0]
    low, full, column, key_low = ((length, width), BF), ((length, width), F32), ((length, 1), F32), ((keys, width), BF)
    outs = [full, column, prob_shape(length, keys, width), low, key_low, key_low, low, full, column]
    near = [full, column, low, key_low, key_low, low, full, column]
    scratch = [low, low, key_low, *near, ((2, 2, length, keys), BF), ((keys, PAIR), BF)]
    if place is not None:
        return call(
            functools.partial(cross_forward_kernel, True),
            (place, count, x, mixed, source, *packs),
            [*outs, ((16, width), F32), ((1, 4 * width), F32)],
            [*scratch, *matrix_buffers(shards, width), ((2, 8, 16, width // 2), BF)],
            44, 10**10, smem=(0, 1), near_outs=(9, 10), copies=64,
        )
    vec, bias = given
    results = call(
        functools.partial(cross_forward_kernel, False),
        (count, vec, x, mixed, source, *packs),
        outs, [*scratch, *like(*packs)],
        44, 10**10, smem=(0,), near=(1,), copies=64,
    )
    return (*results, vec, bias)


def grad_outs(rows, width, staged):
    return [((2, 4, rows, width // 2), BF)] * 2 if staged else [((rows, width), BF)]


def hidden_step(place, packs, normed, inverse, cot, vec, bias, shards):
    length, width = normed.shape
    inner = bias.shape[1]
    staged = place is not None
    low = ((length, width), BF)
    grads = grad_outs(sum(shards) if staged else 2 * inner, width, staged)
    args = (vec, bias, *packs, normed, inverse, cot)
    matrices = matrix_buffers(shards, width) if staged else like(*packs)
    return call(
        functools.partial(hidden_kernel, staged),
        (place, *args) if staged else args,
        [((16, width), F32), ((1, inner), F32), low, ((length, width), F32), *grads],
        [*grads, *like(normed, inverse, cot), low, ((length, width), F32), low, ((length, inner), BF),
         ((length, inner), BF), low, ((length, inner), F32), ((length, width), F32), *matrices],
        44, 2 * 10**10, smem=(0,) if staged else (), near=(1, 2) if staged else (0, 1), near_outs=(0, 1), copies=64,
    )


def backward_cross(place, packs, dz, x, normed, inverse, source, vec, saved, mixed, small, shards):
    length, width = dz.shape
    keys = source.shape[0]
    staged = place is not None
    probs, *saved = saved
    arrays = (dz, x, normed, inverse, source, *saved, mixed)
    low, key_low, sums = ((length, width), BF), ((keys, width), BF), ((2, PAIR, keys), F32)
    grads = grad_outs(5 * width // 8 + 16 if staged else 5 * width, width, staged)
    full, key_full = ((length, width), F32), ((keys, width), F32)
    return call(
        functools.partial(cross_backward_kernel, staged),
        (place, vec, *small, *packs, probs, *arrays) if staged else (vec, *packs, probs, *arrays),
        [((16, width), F32), full, key_full, *grads],
        [*grads, *like(*arrays), full, key_full, *(matrix_buffers(shards, width) if staged else like(*packs)),
         low, ((length, 2 * width), BF), low, key_low, key_low, sums, sums, low, ((2, keys, PAIR), BF),
         ((2, 2, length, keys), BF)],
        48, 2 * 10**10, smem=(0,) if staged else (), near=(1, 2, 3) if staged else (0,), near_outs=(0,), copies=72,
    )


def backward_self(place, packs, dz, x, saved, shards):
    length, width = dz.shape
    staged = place is not None
    probs, *saved = saved
    arrays = (dz, x, *saved)
    low, sums = ((length, width), BF), ((2, PAIR, length), F32)
    grads = grad_outs(3 * width // 8 if staged else 3 * width, width, staged)
    first = matrix_buffers(shards[:1], width) if staged else like(*packs)
    return call(
        functools.partial(self_backward_kernel, staged),
        (place, *packs, probs, *arrays) if staged else (*packs, probs, *arrays),
        [low, low, low, *grads],
        [*grads, *like(*arrays), *first, ((length, 2 * width), BF), low, low, low, sums, sums,
         ((2, length, PAIR), BF), ((2, 2, length, length), BF)],
        48, 2 * 10**10, smem=(0,) if staged else (), copies=64,
    )


def input_gradient(vec, dz, matrices, heads):
    arrays = (dz, matrices, *heads)
    return call(
        input_grad_kernel, (vec, *arrays), like(dz), [*like(*arrays), *like(dz)], 40, 2 * 10**9, near=(0,), copies=24
    )[0]


def adam_step(settings_ref, now, grad, one, two, decay):
    beta_one, beta_two = settings_ref[1], settings_ref[2]
    first = beta_one * one + (1.0 - beta_one) * grad
    second = beta_two * two + (1.0 - beta_two) * grad * grad
    change = (first / settings_ref[4]) / (jnp.sqrt(second / settings_ref[5]) + 1e-08)
    if decay:
        change = change + settings_ref[3] * now
    return now - settings_ref[0] * change, first, second


def store_step(refs, where, results):
    for ref, value in zip(refs, results):
        ref[where] = value


def hidden_adam_kernel(place_ref, settings_ref, mine_ref, other_ref, *refs):
    core = place_of(place_ref)[0]
    expand, shrink = refs[0:3], refs[3:6]
    new_expand, new_shrink = refs[6:9], refs[9:12]
    half = mine_ref.shape[1]
    shard = expand[0].shape[0]
    blocks = expand[0].shape[1] // (2 * half)
    for step, ref in ((0, mine_ref), (1, other_ref)):
        side = jnp.bitwise_xor(core, step) * half
        cols = pl.ds(pl.multiple_of(side, half), half)
        for block in range(blocks):
            where = (slice(None), pl.ds(pl.multiple_of(block * 2 * half + side, half), half))
            grad = ref[block * shard : (block + 1) * shard, :]
            now, one, two = (r[where] for r in expand)
            store_step(new_expand, where, adam_step(settings_ref, now, grad, one, two, True))
        where = (slice(None), cols)
        now, one, two = (r[where] for r in shrink)
        store_step(new_shrink, where, adam_step(settings_ref, now, ref[blocks * shard :, :], one, two, True))


def attention_adam_kernel(place_ref, settings_ref, mine_one, other_one, mine_two, other_two, *refs):
    core = place_of(place_ref)[0]
    matrices, bias, vectors = refs[0:3], refs[3:6], refs[6:9]
    new_matrices, new_bias, new_vectors = refs[9:12], refs[12:15], refs[15:18]
    half = mine_one.shape[1]
    shard = matrices[0].shape[1]
    for step, one_ref, two_ref in ((0, mine_one, mine_two), (1, other_one, other_two)):
        cols = pl.ds(pl.multiple_of(jnp.bitwise_xor(core, step) * half, half), half)
        for index in range(8):
            ref, at = (one_ref, index) if index < 3 else (two_ref, index - 3)
            where = (index, slice(None), cols)
            now, one, two = (r[where] for r in matrices)
            grad = ref[at * shard : (at + 1) * shard, :]
            store_step(new_matrices, where, adam_step(settings_ref, now, grad, one, two, True))
    small = mine_two[5 * shard :, :] + other_two[5 * shard :, :]
    for group, new, grad in (
        (bias, new_bias, small[10:11, : bias[0].shape[1]]),
        (vectors, new_vectors, small[:10, : vectors[0].shape[1]]),
    ):
        now, one, two = (r[...] for r in group)
        store_step(new, ..., adam_step(settings_ref, now, grad, one, two, False))


def adam_call(kernel, scalars, grads, params):
    return call(
        kernel, (*scalars, *grads, *params), [(p.shape, F32) for p in params], [], 32, 10**7, smem=(0, 1),
        near=range(2, 2 + len(grads) + len(params)), near_outs=range(len(params)),
    )


CORE_SWAP = [(0, 1), (1, 0), (2, 3), (3, 2)]
CHIP_SWAP = [(0, 2), (2, 0), (1, 3), (3, 1)]
ROW_SWAP = [(i, i ^ 1) for i in range(8)]


LINES = [[0, 2, 4, 6], [1, 3, 5, 7]]


def line_shift(step):
    return [(2 * z + y, 2 * ((z + step) % 4) + y) for z in range(4) for y in (0, 1)]


def small_mesh(mesh):
    return mesh.shape["rep"] == 4 and mesh.shape["fsdp"] == 8


def gather_staged(pack):
    quarter = pack.shape[0] // 4
    mine = lax.dynamic_slice_in_dim(pack, lax.axis_index("rep") * quarter, quarter, 0)
    pair = jnp.stack([mine, lax.ppermute(mine, "fsdp", ROW_SWAP)])
    part = jnp.stack([pair] + [lax.ppermute(pair, "fsdp", line_shift(step)) for step in (1, 2, 3)])
    both = jnp.stack([part, lax.ppermute(part, "rep", CHIP_SWAP)])
    return both, lax.ppermute(both, "rep", CORE_SWAP)


def after(value, *done):
    return lax.optimization_barrier((value, *done))[0]


def gather_half(pack):
    half = pack.shape[1] // 2
    mine = lax.dynamic_slice_in_dim(pack, lax.axis_index("rep") % 2 * half, half, 1)
    return lax.all_gather(mine, "fsdp", axis=0)


def both_halves(mine, done):
    mine = after(mine, done)
    return mine, lax.ppermute(mine, "rep", CORE_SWAP)


def low_sum(mine, received):
    return (mine.astype(F32) + received.astype(F32)).astype(BF)


def reduce_cores(keep, send):
    received = lax.ppermute(send, "rep", CORE_SWAP)
    return low_sum(keep[0], received[0]), low_sum(keep[1], received[1])


def send_rows(send):
    return lax.ppermute(send, "fsdp", ROW_SWAP)


def reduce_rows(keep, received, done):
    return low_sum(keep, after(received, done))


def reduce_last(part):
    total = part.astype(F32) + lax.ppermute(part, "rep", CHIP_SWAP).astype(F32)
    return total, lax.ppermute(total, "rep", CORE_SWAP)


def reduce_line(joined):
    part = lax.psum_scatter(joined, "fsdp", scatter_dimension=0, axis_index_groups=LINES)
    return part.reshape(joined.shape[1:])


def reduce_shifts(joined, done):
    line = lax.axis_index("fsdp") // 2
    total = lax.dynamic_index_in_dim(joined, line, 0, False).astype(F32)
    for step in (1, 2, 3):
        away = lax.dynamic_index_in_dim(joined, (line + step) % 4, 0, False)
        total = total + after(lax.ppermute(away, "fsdp", line_shift(step)), done).astype(F32)
    return total.astype(BF)


def reduce_plain(grads):
    return lax.psum(lax.psum_scatter(grads, "fsdp", scatter_dimension=0), "rep").astype(F32)


def adam_update(weight_now, gradient, moment_one, moment_two, settings, step_float, factor):
    learn_rate, beta_one, beta_two, decay_rate = settings[0], settings[1], settings[2], settings[3]
    first_new = beta_one * moment_one + (1.0 - beta_one) * gradient
    second_new = beta_two * moment_two + (1.0 - beta_two) * gradient * gradient
    first_hat = first_new / (1.0 - beta_one**step_float)
    second_hat = second_new / (1.0 - beta_two**step_float)
    change = first_hat / (jnp.sqrt(second_hat) + 1e-08) + factor * decay_rate * weight_now
    return (weight_now - learn_rate * change, first_new, second_new)


def per_device(
    small, inputs, memory, memory_length, target_pos, cotangent,
    attention_weights, expand_weights, shrink_weights, expand_bias, layer_vectors,
    first_attention, first_expand, first_shrink, first_bias, first_vectors,
    second_attention, second_expand, second_shrink, second_bias, second_vectors,
    hyper_rates, step_count,
):
    length, width = inputs.shape[1:]
    shard = attention_weights.shape[1]
    count = width // shard
    inner_shard = shrink_weights.shape[0]
    blocks = inner_shard // shard
    low_attention = attention_weights.astype(BF).reshape(8 * shard, width)
    pack_one = low_attention[: 3 * shard]
    pack_three = jnp.concatenate(
        [
            expand_weights.astype(BF).reshape(shard, blocks, width).transpose(1, 0, 2).reshape(-1, width),
            shrink_weights.astype(BF),
        ]
    )
    x, source, cot = inputs[0], memory[0], cotangent[0]
    step_float = step_count.astype(F32)

    if small:
        place = jnp.stack([lax.axis_index("rep"), lax.axis_index("fsdp")]).astype(jnp.int32)
        small_rows = jnp.concatenate(
            [
                jnp.pad(layer_vectors, ((0, 0), (0, inner_shard - shard))),
                expand_bias[None],
                jnp.zeros((5, inner_shard), F32),
            ]
        )
        small_rows = jnp.pad(small_rows, ((0, 0), (0, width - inner_shard))).astype(BF)
        pack_two = jnp.concatenate([low_attention[3 * shard :], small_rows])
        one = gather_staged(pack_one)
        two = gather_half(pack_two)
        three = gather_half(pack_three)
        given = None
        cross_shards = (shard,) * 5
        hidden_shards = (*(shard,) * blocks, inner_shard)
    else:
        place, cross_shards, hidden_shards = None, None, None
        flat = jnp.concatenate([layer_vectors.reshape(-1), expand_bias]).astype(BF)
        flat = lax.all_gather(flat, "fsdp", axis=0).astype(F32)
        vector_size = layer_vectors.size
        vec = flat[:, :vector_size].reshape(count, -1, shard).transpose(1, 0, 2).reshape(-1, width)
        given = jnp.pad(vec, ((0, 16 - vec.shape[0]), (0, 0))), flat[:, vector_size:].reshape(1, -1)

        def gather_all(pack, shards):
            full = lax.all_gather(pack, "fsdp", axis=0)
            pieces, first = [], 0
            for rows in shards:
                pieces.append(full[:, first : first + rows].reshape(-1, width))
                first += rows
            return pieces

        def owners(grads, shards):
            pieces, first = [], 0
            for rows in shards:
                pieces.append(grads[first : first + rows * count].reshape(count, rows, width))
                first += rows * count
            return jnp.concatenate(pieces, axis=1)

        one = jnp.concatenate(gather_all(pack_one, (shard,) * 3))
        two = [m[None] for m in gather_all(low_attention[3 * shard :], (shard,) * 5)]
        three = [m[None] for m in gather_all(pack_three, (*(shard,) * blocks, inner_shard))]

    *saved_one, matrices = forward_self(place, x, target_pos, one, small)
    two = both_halves(two, saved_one[4]) if small else two
    norm_one, inv_one, *saved_two, norm_two, inv_two, vec, bias = forward_cross(
        place, x, saved_one[4], source, memory_length, two, given, cross_shards
    )
    three = both_halves(three, norm_two) if small else three
    sums_three, bias_sum, outputs, dz_two, *grad_three = hidden_step(
        place, three, norm_two, inv_two, cot, vec, bias, hidden_shards
    )
    if small:
        keep_three, send_three = reduce_cores(*grad_three)
        dz_two = after(dz_two, keep_three, send_three)
        received_three = send_rows(send_three)
    sums_two, dz_one, memory_grad, *grad_two = backward_cross(
        place, two, dz_two, x, norm_one, inv_one, source, vec, saved_two, saved_one[4],
        (sums_three, bias_sum), cross_shards,
    )
    if small:
        joined_three = reduce_rows(keep_three, received_three, dz_one)
        keep_two, send_two = reduce_cores(grad_two[0], after(grad_two[1], joined_three))
        dz_one = after(dz_one, joined_three, keep_two, send_two)
        received_two = send_rows(send_two)
    *heads, grad_keep, grad_send = (
        *backward_self(place, two if small else two[:1], dz_one, x, saved_one, cross_shards),
        *((None,) if not small else ()),
    )
    input_grad = input_gradient(vec, dz_one, matrices, heads)

    attention = (attention_weights, first_attention, second_attention)
    expand = (expand_weights, first_expand, second_expand)
    shrink = (shrink_weights, first_shrink, second_shrink)
    bias = (expand_bias, first_bias, second_bias)
    vectors = (layer_vectors, first_vectors, second_vectors)
    if small:
        powers = 1.0 - hyper_rates[1:3] ** step_float
        scalars = place, jnp.concatenate([hyper_rates, powers])
        part_three = reduce_line(joined_three)
        part_two = reduce_line(reduce_rows(keep_two, received_two, heads[0]))
        total_three = reduce_last(after(part_three, heads[0]))
        total_two = reduce_last(part_two)
        keep_one, send_one = reduce_cores(grad_keep, grad_send)
        joined_one = reduce_rows(keep_one, send_rows(send_one), input_grad)
        hidden_new = adam_call(hidden_adam_kernel, scalars, total_three, (*expand, *shrink))
        total_one = reduce_last(reduce_shifts(joined_one, hidden_new[0]))
        rows = tuple(b[None] for b in bias)
        other_new = adam_call(
            attention_adam_kernel, scalars, (*total_one, *total_two), (*attention, *rows, *vectors)
        )
        new_bias = tuple(b[0] for b in other_new[3:6])
        updated = (*other_new[:3], *hidden_new, *new_bias, *other_new[6:])
    else:
        sums = (sums_two + sums_three)[: layer_vectors.shape[0]]
        flat = jnp.concatenate(
            [
                sums.reshape(-1, count, shard).transpose(1, 0, 2).reshape(count, -1),
                bias_sum.reshape(count, inner_shard),
            ],
            axis=1,
        )
        total_three = reduce_plain(owners(grad_three[0], (*(shard,) * blocks, inner_shard)))
        total_two = reduce_plain(owners(grad_two[0], (shard,) * 5))
        total_one = reduce_plain(owners(grad_keep, (shard,) * 3))
        flat = lax.psum(lax.psum_scatter(flat, "fsdp", scatter_dimension=0), "rep")
        grad_attention = jnp.concatenate([total_one, total_two]).reshape(attention_weights.shape)
        grad_expand = total_three[: blocks * shard].reshape(blocks, shard, width).transpose(1, 0, 2)
        updated = []
        for (now, one_now, two_now), grad, factor in (
            (attention, grad_attention, 1.0),
            (expand, grad_expand.reshape(shard, -1), 1.0),
            (shrink, total_three[blocks * shard :], 1.0),
            (bias, flat[layer_vectors.size :], 0.0),
            (vectors, flat[: layer_vectors.size].reshape(-1, shard), 0.0),
        ):
            updated.extend(adam_update(now, grad, one_now, two_now, hyper_rates, step_float, factor))
    return (outputs[None], input_grad[None], memory_grad[None], *updated)


def solution(mesh):
    rows = ("rep", "fsdp")
    params = (P(None, "fsdp", None), P("fsdp", None), P("fsdp", None), P("fsdp"), P(None, "fsdp"))
    return jax.shard_map(
        functools.partial(per_device, small_mesh(mesh)),
        mesh=mesh,
        in_specs=(
            P(rows, None, None), P(rows, None, None), P(rows), P(rows, None), P(rows, None, None),
            *params, *params, *params, P(), P(),
        ),
        out_specs=(
            P(rows, None, None), P(rows, None, None), P(rows, None, None),
            *(spec for spec in params for _ in range(3)),
        ),
        check_vma=False,
    )
```

```python
import functools

import jax
import jax.numpy as jnp
from jax import lax
from jax.experimental import pallas as pl
from jax.experimental.pallas import tpu as pltpu
from jax.sharding import PartitionSpec as P

BF = jnp.bfloat16
F32 = jnp.float32
HEAD_DIM = 64
PAIR = 128
TILE = 256
MIB = 1 << 20


def dot(left, right, left_dim, right_dim):
    return lax.dot_general(
        left, right, (((left_dim,), (right_dim,)), ((), ())), preferred_element_type=F32
    )


def lanes(size):
    return lax.broadcasted_iota(jnp.int32, (1, size), 1)


def half_masks():
    first = jnp.where(lanes(PAIR) < HEAD_DIM, 1.0, 0.0)
    return first.astype(BF), (1.0 - first).astype(BF)


def rows_at(index, size=TILE):
    return pl.ds(pl.multiple_of(index * size, size), size)


def split_three(column):
    high = column.astype(BF).astype(F32)
    rest = column - high
    middle = rest.astype(BF).astype(F32)
    return high, middle, rest - middle


def with_column(block, column, base, last):
    high, middle, low = split_three(column)
    lane = lanes(PAIR)
    tail = jnp.where(lane == base + 3, last, block)
    return jnp.where(
        lane == base, -high, jnp.where(lane == base + 1, -middle, jnp.where(lane == base + 2, -low, tail))
    ).astype(BF)


class Mover:
    def __init__(self, sems):
        self.sems, self.used, self.leaving = sems, 0, []

    def take(self, count=1):
        self.used += count
        return self.used - count

    def load(self, source, target):
        copy = pltpu.make_async_copy(source, target, self.sems.at[self.take()])
        copy.start()
        return copy

    def load_rows(self, source, target):
        count = source.shape[0] // TILE
        first = self.take(count)

        def copy(tile):
            rows = rows_at(tile)
            return pltpu.make_async_copy(source.at[rows], target.at[rows], self.sems.at[first + tile])

        for tile in range(count):
            copy(tile).start()
        return lambda tile: copy(tile).wait()

    def store(self, source, target):
        self.leaving.append(self.load(source, target))

    def store_parts(self, source, target, count, where):
        first = self.take(count)

        def copy(part):
            return pltpu.make_async_copy(source.at[where(part)], target.at[where(part)], self.sems.at[first + part])

        self.leaving.extend(copy(part) for part in range(count))
        return lambda part: copy(part).start()

    def store_rows(self, source, target):
        return self.store_parts(source, target, source.shape[0] // TILE, rows_at)

    def finish(self):
        for copy in self.leaving:
            copy.wait()


def columns_at(size):
    return lambda part: (slice(None), rows_at(part, size))


def load_matrices(mover, core, sources, targets, which=None):
    waits, first = [], 0
    for index, target in enumerate(targets):
        if which is not None and index not in which:
            first += target.shape[1]
            continue
        if core is None:
            copies = [mover.load(sources[index], target)]
        else:
            rows, half = target.shape[1], target.shape[2] // 2
            copies = []
            for step, source in enumerate(sources):
                cols = pl.ds(pl.multiple_of(jnp.bitwise_xor(core, step) * half, half), half)
                copies.append(mover.load(source.at[:, first : first + rows, :], target.at[:, :, cols]))
            first += rows
        waits.append(lambda copies=copies: [copy.wait() for copy in copies])
    return waits


def load_quarters(mover, place_ref, packs, expand_ref, shrink_ref):
    core, chip, line, row = place_of(place_ref)
    half, cut = expand_ref.shape[3] // 2, expand_ref.shape[2] // 2
    loads = ([], [])
    for index, pack in enumerate(packs):
        core_step, chip_step = divmod(index, 2)
        cols = pl.ds(pl.multiple_of(jnp.bitwise_xor(core, core_step) * half, half), half)
        side = jnp.bitwise_xor(chip, chip_step)
        rows = pl.ds(pl.multiple_of(side * cut, cut), cut)
        for line_step in range(4):
            for row_step in (0, 1):
                owner = lax.rem(line - line_step + 4, 4) * 2 + jnp.bitwise_xor(row, row_step)
                source = pack.at[line_step, row_step]
                loads[0].append((source.at[0], expand_ref.at[:, owner, rows, cols]))
                loads[1].append((source.at[1], shrink_ref.at[owner, side, :, :, cols]))
    return [[mover.load(*pair) for pair in pairs] for pairs in loads]


def whole(ref):
    return ref[...].reshape(-1, ref.shape[-1])


def key_extra(length_limit, count):
    lane = lanes(PAIR) % HEAD_DIM
    extra = jnp.where(lane < 3, 1.0, 0.0)
    if length_limit is None:
        return jnp.broadcast_to(extra, (count, PAIR)).astype(BF)
    row = lax.broadcasted_iota(jnp.int32, (count, PAIR), 0)
    bias = jnp.where(row < length_limit, 0.0, -1e30)
    return jnp.where(lane == 3, bias, extra).astype(BF)


def put_start(pos_ref, start_ref):
    length = start_ref.shape[0]
    query = lax.broadcasted_iota(jnp.int32, (8, length), 1)
    first = (query - pos_ref[...]).astype(F32)
    start_ref[...] = first.T[:, :1].astype(jnp.int32)


def visible(start, first_query, first_key, count):
    key = first_key + lax.broadcasted_iota(jnp.int32, (TILE, count), 1)
    seen = key >= start
    if first_key == first_query:
        query = first_query + lax.broadcasted_iota(jnp.int32, (TILE, count), 0)
        seen = seen & (key <= query)
    return seen


def key_spans(tile, count, causal):
    if not causal:
        return [(0, count)]
    spans = [(0, tile * TILE)] if tile else []
    return spans + [(tile * TILE, TILE)]


def staggered(first, then, count):
    ready = first(0)
    for index in range(count):
        following = first(index + 1) if index + 1 < count else None
        then(index, ready)
        ready = following


class ProbStore:
    def __init__(self, mover, hbm, ref, causal):
        self.hbm, self.ref, self.mover = hbm, ref, mover
        self.tiles = ref.shape[2] // TILE
        self.causal = causal
        self.first = mover.take(2 * self.tiles)

    def views(self, pair, slot, tile):
        rows = slice(tile * TILE, (tile + 1) * TILE)
        keys = slice(0, (tile + 1) * TILE) if self.causal else slice(0, self.ref.shape[3])
        sem = self.mover.sems.at[self.first + slot * self.tiles + tile]
        return self.hbm.at[pair, :, rows, keys], self.ref.at[slot, :, rows, keys], sem

    def copy(self, pair, slot, tile, out):
        far, near, sem = self.views(pair, slot, tile)
        return pltpu.make_async_copy(near, far, sem) if out else pltpu.make_async_copy(far, near, sem)


def two_pairs(pairs, body):
    @pl.loop(0, pairs // 2)
    def _(step):
        for slot in (0, 1):
            body(2 * step + slot, slot, step)


def attend(q_ref, k_ref, v_ref, extra_ref, start_ref, o_ref, store, finished):
    length, count = q_ref.shape[0], k_ref.shape[0]
    causal = start_ref is not None
    masks = half_masks()
    pairs = q_ref.shape[1] // PAIR

    def one_pair(pair, slot, step):
        cols = rows_at(pair, PAIR)

        @pl.when(step > 0)
        def _():
            for tile in range(store.tiles):
                store.copy(pair - 2, slot, tile, True).wait()

        steps = [(tile, side) for tile in range(length // TILE) for side in (0, 1)]
        results = {}

        def scores_of(index):
            tile, side = steps[index]
            rows = slice(tile * TILE, (tile + 1) * TILE)
            queries = q_ref[rows, cols] * masks[side]
            if not causal:
                base = HEAD_DIM * (1 - side)
                queries = jnp.where(lanes(PAIR) == base + 3, 1.0, queries.astype(F32)).astype(BF)
            blocks = []
            for first, size in key_spans(tile, count, causal):
                keys = k_ref[first : first + size, cols]
                if not causal:
                    keys = keys * masks[side] + extra_ref[first : first + size, :] * masks[1 - side]
                scores = dot(queries, keys, 1, 1)
                if causal:
                    seen = visible(start_ref[rows, :], tile * TILE, first, size)
                    scores = jnp.where(seen, scores, -1000000000.0)
                blocks.append(scores)
            return blocks

        def mix(index, score_blocks):
            tile, side = steps[index]
            rows = slice(tile * TILE, (tile + 1) * TILE)
            spans = key_spans(tile, count, causal)
            top = functools.reduce(
                jnp.maximum, [jnp.max(scores, axis=1, keepdims=True) for scores in score_blocks]
            )
            exponents = [jnp.exp(scores - top) for scores in score_blocks]
            inverse = 1.0 / sum(jnp.sum(exponent, axis=1, keepdims=True) for exponent in exponents)
            total = None
            for exponent, (first, size) in zip(exponents, spans):
                probs = (exponent * inverse).astype(BF)
                store.ref[slot, side, rows, first : first + size] = probs
                part = dot(probs, v_ref[first : first + size, cols], 1, 0)
                total = part if total is None else total + part
            results[side] = total
            if side == 1:
                o_ref[rows, cols] = jnp.where(lanes(PAIR) < HEAD_DIM, results[0], results[1]).astype(BF)

        staggered(scores_of, mix, len(steps))
        for tile in range(store.tiles):
            store.copy(pair, slot, tile, True).start()
        for start_store in finished:
            start_store(pair)

    two_pairs(pairs, one_pair)
    for slot in (0, 1):
        for tile in range(store.tiles):
            store.mover.leaving.append(store.copy(pairs - 2 + slot, slot, tile, True))


def load_probs(store, slot):
    for tile in reversed(range(store.tiles)):
        store.copy(slot, slot, tile, False).start()


def attend_back(q_ref, da_ref, k_ref, v_ref, store, dq_ref, dk_ref, dv_ref, dk_sum, dv_sum, values_ref):
    length, count = q_ref.shape[0], k_ref.shape[0]
    masks = half_masks()
    pairs = k_ref.shape[1] // PAIR

    def one_pair(pair, slot, step):
        cols = rows_at(pair, PAIR)
        for tile in range(store.tiles):
            store.copy(pair, slot, tile, False).wait()
        for side in (0, 1):
            values_ref[side] = v_ref[:, cols] * masks[side] + masks[1 - side]
        for tile in reversed(range(length // TILE)):
            rows = slice(tile * TILE, (tile + 1) * TILE)
            span = slice(0, (tile + 1) * TILE if store.causal else count)
            query_grads = []
            for side in (0, 1):
                head_cols = pl.ds(pl.multiple_of(pair * 2 * PAIR, PAIR) + side * PAIR, PAIR)
                grads = da_ref[rows, head_cols]
                probs = store.ref[slot, side, rows, span]
                value_part = dot(grads, probs, 0, 0)
                grad_scores = (probs.astype(F32) * dot(grads, values_ref[side, span, :], 1, 1)).astype(BF)
                key_part = dot(q_ref[rows, cols], grad_scores, 0, 0)
                if tile == length // TILE - 1:
                    dv_sum[side, :, span] = value_part
                    dk_sum[side, :, span] = key_part
                else:
                    dv_sum[side, :, span] += value_part
                    dk_sum[side, :, span] += key_part
                query_grads.append(dot(grad_scores, k_ref[span, cols], 1, 0))
            dq_ref[rows, cols] = (
                jnp.where(lanes(PAIR) < HEAD_DIM, query_grads[0], query_grads[1]) * HEAD_DIM**-0.5
            ).astype(BF)
        for sums, out in ((dk_sum, dk_ref), (dv_sum, dv_ref)):
            joined = jnp.concatenate([sums[0, :HEAD_DIM, :], sums[1, HEAD_DIM:, :]], axis=0)
            out[:, cols] = joined.astype(BF).T

        @pl.when(step < pairs // 2 - 1)
        def _():
            for tile in range(store.tiles):
                store.copy(pair + 2, slot, tile, False).start()

    two_pairs(pairs, one_pair)


def norm_rows(summed):
    center = jnp.mean(summed, axis=1, keepdims=True)
    shifted = summed - center
    inverse = lax.rsqrt(jnp.mean(shifted * shifted, axis=1, keepdims=True) + 1e-05)
    return shifted * inverse, inverse


def norm_back(grad_out, normed, inverse, gain):
    scaled = grad_out * gain
    first = jnp.mean(scaled, axis=1, keepdims=True)
    second = jnp.mean(scaled * normed, axis=1, keepdims=True)
    return inverse * (scaled - first - normed * second)


def add_rows(ref, row, values):
    ref[row : row + 1, :] += jnp.sum(values, axis=0, keepdims=True)


def place_of(place_ref):
    rep, place = place_ref[0], place_ref[1]
    return lax.rem(rep, 2), lax.div(rep, 2), lax.div(place, 2), lax.rem(place, 2)


def assemble(place_ref, chunk_refs, all_ref):
    core, chip, line, row = place_of(place_ref)
    width = all_ref.shape[1]
    quarter = chunk_refs[0].shape[3]
    shard = quarter * 4 // 3
    for core_step, chunk_ref in enumerate(chunk_refs):
        for chip_step in (0, 1):
            rep = jnp.bitwise_xor(chip, chip_step) * 2 + jnp.bitwise_xor(core, core_step)
            for line_step in range(4):
                for row_step in (0, 1):
                    owner = lax.rem(line - line_step + 4, 4) * 2 + jnp.bitwise_xor(row, row_step)
                    for piece in range(quarter // 16):
                        stacked = rep * quarter + piece * 16
                        matrix = lax.div(stacked, shard)
                        target = matrix * width + owner * shard + (stacked - matrix * shard)
                        all_ref[pl.ds(pl.multiple_of(target, 16), 16), :] = chunk_ref[
                            chip_step, line_step, row_step, piece * 16 : (piece + 1) * 16, :
                        ]


def assemble_halves(place_ref, mine_ref, other_ref, all_ref, shards):
    core = place_of(place_ref)[0]
    devices, _, half = mine_ref.shape
    for step, ref in ((0, mine_ref), (1, other_ref)):
        cols = pl.ds(pl.multiple_of(jnp.bitwise_xor(core, step) * half, half), half)
        first, target = 0, 0
        for shard in shards:
            for owner in range(devices):
                at = target + owner * shard
                all_ref[at : at + shard, cols] = ref[owner, first : first + shard, :]
            first += shard
            target += shard * devices


def unpack_small(all_ref, base, vec_ref, bias_ref):
    devices = vec_ref.shape[1] // HEAD_DIM
    inner = bias_ref.shape[1] // devices
    for pair in range(devices // 2):
        first = base + 2 * pair * 16
        left = all_ref[first : first + 16, :PAIR].astype(F32)
        right = all_ref[first + 16 : first + 32, :PAIR].astype(F32)
        vec_ref[:, pair * PAIR : (pair + 1) * PAIR] = jnp.where(
            lanes(PAIR) < HEAD_DIM, left, pltpu.roll(right, HEAD_DIM, 1)
        )
    for owner in range(devices):
        rows = all_ref[base + owner * 16 : base + owner * 16 + 16, :inner].astype(F32)
        bias_ref[:, owner * inner : (owner + 1) * inner] = rows[10:11, :]


def self_forward_kernel(staged, *refs):
    if staged:
        place_ref, pos_ref, x_hbm, chunk_hbm, other_hbm = refs[:5]
        refs = refs[5:]
    else:
        pos_ref, x_hbm, all_hbm = refs[:3]
        refs = refs[3:]
    p_hbm, q_hbm, k_hbm, v_hbm, o_hbm = refs[:5]
    refs = refs[5:]
    if staged:
        all_out, refs = refs[0], refs[1:]
    x_ref, all_ref, q_ref, k_ref, v_ref, o_ref, p_ref, start_ref = refs[:8]
    mover = Mover(refs[-1])
    length, width = x_ref.shape
    if staged:
        chunk_refs = refs[8:10]
        loads = [mover.load(a, b) for a, b in zip((chunk_hbm, other_hbm), chunk_refs)]
    else:
        loads = [mover.load(all_hbm, all_ref)]
    x_load = mover.load(x_hbm, x_ref)
    put_start(pos_ref, start_ref)
    for load in loads:
        load.wait()
    if staged:
        assemble(place_ref, chunk_refs, all_ref)
        mover.store(all_ref, all_out)
    x_load.wait()

    @pl.loop(0, length // TILE)
    def _(tile):
        rows = rows_at(tile)
        source = x_ref[rows, :]
        queries = dot(source, all_ref[:width, :], 1, 0).astype(BF)
        q_ref[rows, :] = queries * jnp.asarray(HEAD_DIM**-0.5, BF)
        k_ref[rows, :] = dot(source, all_ref[width : 2 * width, :], 1, 0).astype(BF)
        v_ref[rows, :] = dot(source, all_ref[2 * width :, :], 1, 0).astype(BF)

    mover.store(k_ref, k_hbm)
    mover.store(v_ref, v_hbm)
    mover.store(q_ref, q_hbm)
    finished = (mover.store_parts(o_ref, o_hbm, width // PAIR, columns_at(PAIR)),)
    attend(q_ref, k_ref, v_ref, None, start_ref, o_ref, ProbStore(mover, p_hbm, p_ref, True), finished)
    mover.finish()


def unpack_small(small_ref, vec_ref, bias_ref):
    devices = vec_ref.shape[1] // HEAD_DIM
    inner = bias_ref.shape[1] // devices
    for pair in range(devices // 2):
        left = small_ref[0, 2 * pair, :, :PAIR].astype(F32)
        right = small_ref[0, 2 * pair + 1, :, :PAIR].astype(F32)
        vec_ref[:, pair * PAIR : (pair + 1) * PAIR] = jnp.where(
            lanes(PAIR) < HEAD_DIM, left, pltpu.roll(right, HEAD_DIM, 1)
        )
    for owner in range(devices):
        rows = small_ref[0, owner, :, :inner].astype(F32)
        bias_ref[:, owner * inner : (owner + 1) * inner] = rows[10:11, :]


def cross_forward_kernel(staged, *refs):
    place_ref, core = None, None
    if staged:
        place_ref, refs = refs[0], refs[1:]
        core = place_of(place_ref)[0]
    length_ref, refs = refs[0], refs[1:]
    if staged:
        x_hbm, mixed_hbm, source_hbm, *packs = refs[:5]
        refs = refs[5:]
    else:
        vec_ref, x_hbm, mixed_hbm, source_hbm, *packs = refs[:9]
        refs = refs[9:]
    first_hbm, first_inv_hbm, p_hbm, q_hbm, k_hbm, v_hbm, o_hbm, n_hbm, inv_hbm = refs[:9]
    refs = refs[9:]
    if staged:
        vec_ref, bias_ref, refs = refs[0], refs[1], refs[2:]
    x_ref, mixed_ref, source_ref, first_ref, first_inv_ref, q_ref, k_ref, v_ref, o_ref, n_ref, inv_ref = refs[:11]
    p_ref, extra_ref, *w_refs = refs[11:18]
    mover = Mover(refs[-1])
    length, width = q_ref.shape

    if staged:
        small_ref = refs[18]
        rows = packs[0].shape[1]
        small = [
            mover.load(pack.at[:, rows - 16 :, :], small_ref.at[jnp.bitwise_xor(core, step)])
            for step, pack in enumerate(packs)
        ]
    source_load = mover.load_rows(source_hbm, source_ref)
    order = (2, 3, 0, 1, 4)
    waits = [None] * 5
    if staged:
        half = width // 2
        shard = w_refs[0].shape[1]
        for index in order:
            copies = []
            for step, pack in enumerate(packs):
                cols = pl.ds(pl.multiple_of(jnp.bitwise_xor(core, step) * half, half), half)
                copies.append(
                    mover.load(pack.at[:, index * shard : (index + 1) * shard, :], w_refs[index].at[:, :, cols])
                )
            waits[index] = lambda copies=copies: [copy.wait() for copy in copies]
    else:
        for index in order:
            waits[index] = mover.load(packs[index], w_refs[index]).wait
    mixed_load = mover.load_rows(mixed_hbm, mixed_ref)
    x_load = mover.load_rows(x_hbm, x_ref)
    extra_ref[...] = key_extra(length_ref[0], k_ref.shape[0])
    waits[2]()
    waits[3]()

    @pl.loop(0, source_ref.shape[0] // TILE)
    def _(tile):
        rows = rows_at(tile)
        source_load(tile)
        source = source_ref[rows, :]
        k_ref[rows, :] = dot(source, whole(w_refs[2]), 1, 0).astype(BF)
        v_ref[rows, :] = dot(source, whole(w_refs[3]), 1, 0).astype(BF)

    mover.store(k_ref, k_hbm)
    mover.store(v_ref, v_hbm)
    if staged:
        for load in small:
            load.wait()
        unpack_small(small_ref, vec_ref, bias_ref)
    waits[0]()
    waits[1]()

    @pl.loop(0, length // TILE)
    def _(tile):
        rows = rows_at(tile)
        mixed_load(tile)
        x_load(tile)
        summed = x_ref[rows, :].astype(F32) * vec_ref[6:7, :] + dot(mixed_ref[rows, :], whole(w_refs[0]), 1, 0)
        normed, inverse = norm_rows(summed)
        first_ref[rows, :] = normed
        first_inv_ref[rows, :] = inverse
        low = (normed * vec_ref[0:1, :] + vec_ref[3:4, :]).astype(BF)
        queries = dot(low, whole(w_refs[1]), 1, 0).astype(BF)
        q_ref[rows, :] = queries * jnp.asarray(HEAD_DIM**-0.5, BF)

    mover.store(first_ref, first_hbm)
    mover.store(first_inv_ref, first_inv_hbm)
    mover.store(q_ref, q_hbm)
    finished = (mover.store_parts(o_ref, o_hbm, width // PAIR, columns_at(PAIR)),)
    attend(q_ref, k_ref, v_ref, extra_ref, None, o_ref, ProbStore(mover, p_hbm, p_ref, False), finished)
    waits[4]()
    n_store, inv_store = mover.store_rows(n_ref, n_hbm), mover.store_rows(inv_ref, inv_hbm)

    @pl.loop(0, length // TILE)
    def _(tile):
        rows = rows_at(tile)
        first_out = first_ref[rows, :] * vec_ref[0:1, :] + vec_ref[3:4, :]
        summed = first_out * vec_ref[7:8, :] + dot(o_ref[rows, :], whole(w_refs[4]), 1, 0)
        normed, inverse = norm_rows(summed)
        n_ref[rows, :] = normed
        inv_ref[rows, :] = inverse
        n_store(tile)
        inv_store(tile)

    mover.finish()


def hidden_kernel(staged, *refs):
    place_ref, core = None, None
    if staged:
        place_ref, refs = refs[0], refs[1:]
        core = place_of(place_ref)[0]
    vec_ref, bias_ref, *packs = refs[: 6 if staged else 4]
    n_hbm, inv_hbm, cot_hbm = refs[len(packs) + 2 : len(packs) + 5]
    refs = refs[len(packs) + 5 :]
    count = 2 if staged else 1
    sums_ref, bias_sum_ref, out_hbm, dz_hbm = refs[:4]
    grad_hbms, refs = refs[4 : 4 + count], refs[4 + count :]
    grad_refs, refs = refs[:count], refs[count:]
    n_ref, inv_ref, cot_ref, out_ref, dz_ref, low_ref, h_ref, du_ref, df_ref, slope_ref, third_ref = refs[:11]
    blocks = bias_ref.shape[1] // vec_ref.shape[1]
    e_ref, s_ref = refs[11:13]
    mover = Mover(refs[-1])
    length, width = n_ref.shape

    n_load = mover.load_rows(n_hbm, n_ref)
    if staged:
        expand_loads, shrink_loads = load_quarters(mover, place_ref, packs, e_ref, s_ref)
    else:
        expand_loads, shrink_loads = [mover.load(packs[0], e_ref)], [mover.load(packs[1], s_ref)]
    cot_load = mover.load_rows(cot_hbm, cot_ref)
    inv_load = mover.load_rows(inv_hbm, inv_ref)
    out_store, dz_store = mover.store_rows(out_ref, out_hbm), mover.store_rows(dz_ref, dz_hbm)
    tiles = [slice(tile * TILE, (tile + 1) * TILE) for tile in range(length // TILE)]
    parts = [slice(block * width, (block + 1) * width) for block in range(blocks)]
    sums = {row: 0.0 for row in (1, 2, 4, 5, 8, 9)}
    bias_sums = [0.0] * blocks

    def add(row, values):
        sums[row] = sums[row] + jnp.sum(values, axis=0, keepdims=True)

    def second_out(rows):
        return n_ref[rows, :] * vec_ref[1:2, :] + vec_ref[4:5, :]

    for tile, rows in enumerate(tiles):
        n_load(tile)
        low_ref[rows, :] = second_out(rows).astype(BF)
    steps = [(block, rows) for block in range(blocks) for rows in tiles]

    def expand(index):
        block, rows = steps[index]
        return dot(low_ref[rows, :], whole(e_ref.at[block]), 1, 0) + bias_ref[:, parts[block]]

    def activate(index, before):
        block, rows = steps[index]
        square = before * before
        tangent = jnp.tanh(before * (0.7978845608028654 + 0.7978845608028654 * 0.044715 * square))
        half = 0.5 * (1.0 + tangent)
        slope_ref[rows, parts[block]] = half + before * (half * (1.0 - tangent)) * (
            0.7978845608028654 + 3.0 * 0.7978845608028654 * 0.044715 * square
        )
        h_ref[rows, parts[block]] = (before * half).astype(BF)

    for load in expand_loads:
        load.wait()
    staggered(expand, activate, len(steps))
    for load in shrink_loads:
        load.wait()
    for tile in range(len(tiles)):
        cot_load(tile)
        inv_load(tile)

    def shrink(tile):
        return dot(h_ref[tiles[tile], :], whole(s_ref), 1, 0)

    def outer_norm(tile, branch_out):
        rows = tiles[tile]
        second = second_out(rows)
        normed, inverse = norm_rows(second * vec_ref[8:9, :] + vec_ref[9:10, :] + branch_out)
        out_ref[rows, :] = (normed * vec_ref[2:3, :] + vec_ref[5:6, :]).astype(BF)
        grad_out = cot_ref[rows, :].astype(F32)
        third = norm_back(grad_out, normed, inverse, vec_ref[2:3, :])
        third_ref[rows, :] = third
        add(2, grad_out * normed)
        add(5, grad_out)
        branch = third.astype(BF)
        df_ref[rows, :] = branch
        add(9, branch.astype(F32))
        add(8, second * third)

    staggered(shrink, outer_norm, len(tiles))
    for tile in range(len(tiles)):
        out_store(tile)

    def shrink_back(index):
        block, rows = steps[index]
        return dot(df_ref[rows, :], whole(s_ref)[parts[block], :], 1, 1)

    def slope_back(index, grad_hidden):
        block, rows = steps[index]
        du = (grad_hidden * slope_ref[rows, parts[block]]).astype(BF)
        du_ref[rows, parts[block]] = du
        bias_sums[block] = bias_sums[block] + jnp.sum(du.astype(F32), axis=0, keepdims=True)

    staggered(shrink_back, slope_back, len(steps))

    def expand_back(tile):
        rows = tiles[tile]
        return sum(dot(du_ref[rows, parts[block]], whole(e_ref.at[block]), 1, 1) for block in range(blocks))

    def inner_norm(tile, grad_expanded):
        rows = tiles[tile]
        grad = vec_ref[8:9, :] * third_ref[rows, :] + grad_expanded
        normed = n_ref[rows, :]
        dz_ref[rows, :] = norm_back(grad, normed, inv_ref[rows, :], vec_ref[1:2, :])
        add(1, grad * normed)
        add(4, grad)

    staggered(expand_back, inner_norm, len(tiles))
    for tile in range(len(tiles)):
        dz_store(tile)
    sums_ref[...] = jnp.zeros_like(sums_ref)
    for row, values in sums.items():
        sums_ref[row : row + 1, :] = values
    for block, values in enumerate(bias_sums):
        bias_sum_ref[:, parts[block]] = values
    for step in reversed(range(count)):
        for block in range(blocks):
            put_grad(grad_refs, step, place_ref, block, low_ref[...], du_ref, block * width)
            put_shrink(grad_refs, step, place_ref, block, blocks, h_ref[:, parts[block]], df_ref)
        mover.store(grad_refs[step], grad_hbms[step])
    mover.finish()


def branch_grads(branch, mixed_weight, o_rows, da_ref, rows):
    masks = half_masks()
    mixed_grad = dot(branch, mixed_weight, 1, 1).astype(BF)
    for pair in range(mixed_grad.shape[1] // PAIR):
        cols = slice(pair * PAIR, (pair + 1) * PAIR)
        grad_pair = mixed_grad[:, cols].astype(F32)
        product = grad_pair * o_rows[:, cols].astype(F32)
        for side in (0, 1):
            mask = masks[side].astype(F32)
            inner = jnp.sum(product * mask, axis=1, keepdims=True)
            first = (2 * pair + side) * PAIR
            da_ref[rows, first : first + PAIR] = with_column(
                grad_pair * mask, inner, HEAD_DIM * (1 - side), 0.0
            )


def put_grad(grad_refs, step, place_ref, index, left, right_ref, first=0):
    width = left.shape[1]
    if place_ref is None:
        grad = dot(left, right_ref[:, first : first + width], 0, 0)
        grad_refs[0][index * width : (index + 1) * width, :] = grad.astype(BF)
        return
    core, _, _, row = place_of(place_ref)
    half = width // 2
    shard = width // 8
    cols = pl.ds(pl.multiple_of(first + jnp.bitwise_xor(core, step) * half, half), half)
    grad = dot(left, right_ref[:, cols], 0, 0).astype(BF).reshape(4, 2, shard, half)
    for side in (0, 1):
        slot = jnp.bitwise_xor(row, side)
        grad_refs[step][slot, :, index * shard : (index + 1) * shard, :] = grad[:, side]


def put_shrink(grad_refs, step, place_ref, block, blocks, left, right_ref):
    width = left.shape[1]
    if place_ref is None:
        first = (blocks + block) * width
        grad_refs[0][first : first + width, :] = dot(left, right_ref[...], 0, 0).astype(BF)
        return
    core, _, _, row = place_of(place_ref)
    half, shard = width // 2, width * blocks // 8
    base = width // 8 * blocks
    cols = pl.ds(pl.multiple_of(jnp.bitwise_xor(core, step) * half, half), half)
    grad = dot(left, right_ref[:, cols], 0, 0).astype(BF).reshape(width // shard, shard, half)
    for part in range(width // shard):
        owner = block * (width // shard) + part
        grad_refs[step][jnp.bitwise_xor(row, owner % 2), owner // 2, base:, :] = grad[part]


def put_small(grad_refs, place_ref, base, sums, bias_sum):
    core, _, _, row = place_of(place_ref)
    half = grad_refs[0].shape[3]
    inner = bias_sum.shape[1] // 8
    index = lax.broadcasted_iota(jnp.int32, (16, half), 0)
    for owner in range(8):
        block = sums[:, owner // 2 * PAIR : (owner // 2 + 1) * PAIR]
        if owner % 2:
            block = pltpu.roll(block, HEAD_DIM, 1)
        block = jnp.concatenate([block, jnp.zeros((16, half - PAIR), F32)], axis=1)
        block = jnp.where(index == 10, bias_sum[:, owner * inner : (owner + 1) * inner], block)
        high = block.astype(BF)
        low = (block - high.astype(F32)).astype(BF)
        slot = jnp.bitwise_xor(row, owner % 2)
        first = (core == 0).astype(F32)
        for step, grad_ref in enumerate(grad_refs):
            is_high = first if step == 0 else 1.0 - first
            mixed = high.astype(F32) * is_high + low.astype(F32) * (1.0 - is_high)
            grad_ref[slot, owner // 2, base : base + 16, :] = mixed.astype(BF)


def cross_backward_kernel(staged, *refs):
    place_ref, core = None, None
    if staged:
        place_ref, refs = refs[0], refs[1:]
        core = place_of(place_ref)[0]
    vec_ref, refs = refs[0], refs[1:]
    if staged:
        sums_three_ref, bias_sum_ref, refs = refs[0], refs[1], refs[2:]
    packs, refs = refs[: 2 if staged else 5], refs[2 if staged else 5 :]
    p_hbm, dz_hbm, x_hbm, first_hbm, inv_hbm, source_hbm, q_hbm, k_hbm, v_hbm, o_hbm, self_o_hbm = refs[:11]
    sums_ref, dfirst_hbm, dsource_hbm = refs[11:14]
    count = 2 if staged else 1
    grad_hbms, refs = refs[14 : 14 + count], refs[14 + count :]
    grad_refs, refs = refs[:count], refs[count:]
    dz_ref, x_ref, first_ref, inv_ref, source_ref, q_ref, k_ref, v_ref, o_ref, self_o_ref = refs[:10]
    dfirst_ref, dsource_ref, *w_refs = refs[10:17]
    low_ref, da_ref, dq_ref, dk_ref, dv_ref, dk_sum, dv_sum, branch_ref, values_ref, p_ref = refs[17:27]
    mover = Mover(refs[-1])
    length, width = dz_ref.shape

    dz_load, o_load = mover.load_rows(dz_hbm, dz_ref), mover.load_rows(o_hbm, o_ref)
    waits = load_matrices(mover, core, packs, w_refs, (4,))
    sums_ref[...] = jnp.zeros_like(sums_ref)
    waits[0]()
    store = ProbStore(mover, p_hbm, p_ref, False)
    load_probs(store, 0)
    middle = [mover.load(a, b) for a, b in ((v_hbm, v_ref), (q_hbm, q_ref), (k_hbm, k_ref))]

    @pl.loop(0, length // TILE)
    def _(tile):
        rows = rows_at(tile)
        dz_load(tile)
        o_load(tile)
        branch = dz_ref[rows, :].astype(BF)
        branch_ref[rows, :] = branch
        branch_grads(branch, whole(w_refs[4]), o_ref[rows, :], da_ref, rows)

    for step in range(count):
        put_grad(grad_refs, step, place_ref, 4, o_ref[...], branch_ref)
    load_probs(store, 1)
    first_load = mover.load_rows(first_hbm, first_ref)
    waits = load_matrices(mover, core, packs, w_refs, (1, 2, 3))
    last = [
        mover.load(a, b)
        for a, b in ((source_hbm, source_ref), (x_hbm, x_ref), (inv_hbm, inv_ref), (self_o_hbm, self_o_ref))
    ]
    for load in middle:
        load.wait()
    attend_back(q_ref, da_ref, k_ref, v_ref, store, dq_ref, dk_ref, dv_ref, dk_sum, dv_sum, values_ref)
    for load in last:
        load.wait()
    for wait in waits:
        wait()
    for tile in range(length // TILE):
        first_load(tile)

    dsource_store = mover.store_rows(dsource_ref, dsource_hbm)

    @pl.loop(0, source_ref.shape[0] // TILE)
    def _(tile):
        rows = rows_at(tile)
        dsource_ref[rows, :] = dot(dk_ref[rows, :], whole(w_refs[2]), 1, 1) + dot(
            dv_ref[rows, :], whole(w_refs[3]), 1, 1
        )
        dsource_store(tile)

    dfirst_store = mover.store_rows(dfirst_ref, dfirst_hbm)

    @pl.loop(0, length // TILE)
    def _(tile):
        rows = rows_at(tile)
        grad = dz_ref[rows, :]
        dx = dot(dq_ref[rows, :], whole(w_refs[1]), 1, 1) + vec_ref[7:8, :] * grad
        normed = first_ref[rows, :]
        first_out = normed * vec_ref[0:1, :] + vec_ref[3:4, :]
        low_ref[rows, :] = first_out.astype(BF)
        add_rows(sums_ref, 7, first_out * grad)
        dfirst = norm_back(dx, normed, inv_ref[rows, :], vec_ref[0:1, :])
        dfirst_ref[rows, :] = dfirst
        dfirst_store(tile)
        add_rows(sums_ref, 0, dx * normed)
        add_rows(sums_ref, 3, dx)
        add_rows(sums_ref, 6, x_ref[rows, :].astype(F32) * dfirst)
        branch_ref[rows, :] = dfirst.astype(BF)

    if staged:
        put_small(grad_refs, place_ref, 5 * (width // 8), sums_ref[...] + sums_three_ref[...], bias_sum_ref[...])
    for step in reversed(range(count)):
        put_grad(grad_refs, step, place_ref, 1, low_ref[...], dq_ref)
        put_grad(grad_refs, step, place_ref, 2, source_ref[...], dk_ref)
        put_grad(grad_refs, step, place_ref, 3, source_ref[...], dv_ref)
        put_grad(grad_refs, step, place_ref, 0, self_o_ref[...], branch_ref)
        mover.store(grad_refs[step], grad_hbms[step])
    mover.finish()


def self_backward_kernel(staged, *refs):
    place_ref, core = None, None
    if staged:
        place_ref, refs = refs[0], refs[1:]
        core = place_of(place_ref)[0]
    count = 2 if staged else 1
    packs, refs = refs[:count], refs[count:]
    p_hbm, dz_hbm, x_hbm, q_hbm, k_hbm, v_hbm, o_hbm, *head_hbms = refs[:10]
    grad_hbms, refs = refs[10 : 10 + count], refs[10 + count :]
    grad_refs, refs = refs[:count], refs[count:]
    dz_ref, x_ref, q_ref, k_ref, v_ref, o_ref, w_ref = refs[:7]
    da_ref, dq_ref, dk_ref, dv_ref, dk_sum, dv_sum, values_ref, p_ref = refs[7:15]
    mover = Mover(refs[-1])
    length, width = dz_ref.shape

    dz_load = mover.load_rows(dz_hbm, dz_ref)
    waits = load_matrices(mover, core, packs, (w_ref,))
    o_load = mover.load_rows(o_hbm, o_ref)
    waits[0]()
    store = ProbStore(mover, p_hbm, p_ref, True)
    load_probs(store, 0)
    middle = [mover.load(a, b) for a, b in ((v_hbm, v_ref), (q_hbm, q_ref), (k_hbm, k_ref))]

    @pl.loop(0, length // TILE)
    def _(tile):
        rows = rows_at(tile)
        dz_load(tile)
        o_load(tile)
        branch_grads(dz_ref[rows, :].astype(BF), whole(w_ref), o_ref[rows, :], da_ref, rows)

    load_probs(store, 1)
    x_load = mover.load(x_hbm, x_ref)
    for load in middle:
        load.wait()
    attend_back(q_ref, da_ref, k_ref, v_ref, store, dq_ref, dk_ref, dv_ref, dk_sum, dv_sum, values_ref)
    for near, far in zip((dq_ref, dk_ref, dv_ref), head_hbms):
        mover.store(near, far)
    x_load.wait()
    for step in reversed(range(count)):
        for index, grads in enumerate((dq_ref, dk_ref, dv_ref)):
            put_grad(grad_refs, step, place_ref, index, x_ref[...], grads)
        mover.store(grad_refs[step], grad_hbms[step])
    mover.finish()


def input_grad_kernel(vec_ref, dz_hbm, all_hbm, dq_hbm, dk_hbm, dv_hbm, dx_hbm, *refs):
    dz_ref, all_ref, dq_ref, dk_ref, dv_ref, dx_ref, sems = refs
    mover = Mover(sems)
    width = dz_ref.shape[1]
    all_load = mover.load(all_hbm, all_ref)
    heads = (dq_ref, dk_ref, dv_ref)
    loads = [mover.load_rows(a, b) for a, b in zip((dq_hbm, dk_hbm, dv_hbm), heads)]
    loads.append(mover.load_rows(dz_hbm, dz_ref))
    dx_store = mover.store_rows(dx_ref, dx_hbm)
    all_load.wait()

    @pl.loop(0, dz_ref.shape[0] // TILE)
    def _(tile):
        rows = rows_at(tile)
        for load in loads:
            load(tile)
        dx = vec_ref[6:7, :] * dz_ref[rows, :]
        for index, grads in enumerate(heads):
            dx = dx + dot(grads[rows, :], all_ref[index * width : (index + 1) * width, :], 1, 1)
        dx_ref[rows, :] = dx
        dx_store(tile)

    mover.finish()


def call(kernel, args, outs, scratch, limit, flops, smem=(), near=(), near_outs=(), copies=0):
    spaces = [pltpu.SMEM if i in smem else pltpu.VMEM if i in near else pl.ANY for i in range(len(args))]
    out_spaces = [pltpu.VMEM if i in near_outs else pl.ANY for i in range(len(outs))]
    buffers = [pltpu.VMEM(shape, kind) for shape, kind in scratch]
    if copies:
        buffers.append(pltpu.SemaphoreType.DMA((copies,)))
    return pl.pallas_call(
        kernel,
        out_shape=[jax.ShapeDtypeStruct(shape, kind) for shape, kind in outs],
        in_specs=[pl.BlockSpec(memory_space=space) for space in spaces],
        out_specs=[pl.BlockSpec(memory_space=space) for space in out_spaces],
        scratch_shapes=buffers,
        compiler_params=pltpu.CompilerParams(vmem_limit_bytes=(63 if copies else limit) * MIB),
        cost_estimate=pl.CostEstimate(flops=flops, bytes_accessed=16 * MIB, transcendentals=0),
    )(*args)


def like(*arrays):
    return [(a.shape, a.dtype) for a in arrays]


def prob_shape(queries, keys, width):
    return (width // PAIR, 2, queries, keys), BF


def forward_self(place, x, pos, pack, staged):
    length, width = x.shape
    low = ((length, width), BF)
    outs = [prob_shape(length, length, width), low, low, low, low]
    matrices = ((3 * width, width), BF)
    scratch = [low, matrices, low, low, low, low, ((2, 2, length, length), BF), ((length, 1), jnp.int32)]
    if staged:
        return call(
            functools.partial(self_forward_kernel, True),
            (place, pos, x, *pack),
            [*outs, matrices],
            [*scratch, *like(*pack)],
            40, 10**10, smem=(0,), near=(1,), copies=24,
        )
    results = call(
        functools.partial(self_forward_kernel, False),
        (pos, x, pack), outs, scratch, 40, 10**10, near=(0,), copies=24,
    )
    return (*results, pack)


def matrix_buffers(shards, width):
    return [((8 if rows < width else 1, rows, width), BF) for rows in shards]


def forward_cross(place, x, mixed, source, count, packs, given, shards):
    length, width = x.shape
    keys = source.shape[0]
    low, full, column, key_low = ((length, width), BF), ((length, width), F32), ((length, 1), F32), ((keys, width), BF)
    outs = [full, column, prob_shape(length, keys, width), low, key_low, key_low, low, full, column]
    near = [full, column, low, key_low, key_low, low, full, column]
    scratch = [low, low, key_low, *near, ((2, 2, length, keys), BF), ((keys, PAIR), BF)]
    if place is not None:
        return call(
            functools.partial(cross_forward_kernel, True),
            (place, count, x, mixed, source, *packs),
            [*outs, ((16, width), F32), ((1, 4 * width), F32)],
            [*scratch, *matrix_buffers(shards, width), ((2, 8, 16, width // 2), BF)],
            44, 10**10, smem=(0, 1), near_outs=(9, 10), copies=64,
        )
    vec, bias = given
    results = call(
        functools.partial(cross_forward_kernel, False),
        (count, vec, x, mixed, source, *packs),
        outs, [*scratch, *like(*packs)],
        44, 10**10, smem=(0,), near=(1,), copies=64,
    )
    return (*results, vec, bias)


def grad_outs(rows, width, staged):
    return [((2, 4, rows, width // 2), BF)] * 2 if staged else [((rows, width), BF)]


def hidden_step(place, packs, normed, inverse, cot, vec, bias):
    length, width = normed.shape
    inner = bias.shape[1]
    blocks = inner // width
    staged = place is not None
    low, full = ((length, width), BF), ((length, width), F32)
    grads = grad_outs(2 * inner // 8 if staged else 2 * inner, width, staged)
    args = (vec, bias, *packs, normed, inverse, cot)
    matrices = like(*packs)
    if staged:
        rows = width // 8
        matrices = [((blocks, 8, rows, width), BF), ((8, 2, blocks, rows // 2, width), BF)]
    return call(
        functools.partial(hidden_kernel, staged),
        (place, *args) if staged else args,
        [((16, width), F32), ((1, inner), F32), low, full, *grads],
        [*grads, *like(normed, inverse, cot), low, full, low, ((length, inner), BF), ((length, inner), BF), low,
         ((length, inner), F32), full, *matrices],
        44, 2 * 10**10, smem=(0,) if staged else (), near=(1, 2) if staged else (0, 1), near_outs=(0, 1),
        copies=96,
    )


def backward_cross(place, packs, dz, x, normed, inverse, source, vec, saved, mixed, small, shards):
    length, width = dz.shape
    keys = source.shape[0]
    staged = place is not None
    probs, *saved = saved
    arrays = (dz, x, normed, inverse, source, *saved, mixed)
    low, key_low, sums = ((length, width), BF), ((keys, width), BF), ((2, PAIR, keys), F32)
    grads = grad_outs(5 * width // 8 + 16 if staged else 5 * width, width, staged)
    full, key_full = ((length, width), F32), ((keys, width), F32)
    return call(
        functools.partial(cross_backward_kernel, staged),
        (place, vec, *small, *packs, probs, *arrays) if staged else (vec, *packs, probs, *arrays),
        [((16, width), F32), full, key_full, *grads],
        [*grads, *like(*arrays), full, key_full, *(matrix_buffers(shards, width) if staged else like(*packs)),
         low, ((length, 2 * width), BF), low, key_low, key_low, sums, sums, low, ((2, keys, PAIR), BF),
         ((2, 2, length, keys), BF)],
        48, 2 * 10**10, smem=(0,) if staged else (), near=(1, 2, 3) if staged else (0,), near_outs=(0,), copies=72,
    )


def backward_self(place, packs, dz, x, saved, shards):
    length, width = dz.shape
    staged = place is not None
    probs, *saved = saved
    arrays = (dz, x, *saved)
    low, sums = ((length, width), BF), ((2, PAIR, length), F32)
    grads = grad_outs(3 * width // 8 if staged else 3 * width, width, staged)
    first = matrix_buffers(shards[:1], width) if staged else like(*packs)
    return call(
        functools.partial(self_backward_kernel, staged),
        (place, *packs, probs, *arrays) if staged else (*packs, probs, *arrays),
        [low, low, low, *grads],
        [*grads, *like(*arrays), *first, ((length, 2 * width), BF), low, low, low, sums, sums,
         ((2, length, PAIR), BF), ((2, 2, length, length), BF)],
        48, 2 * 10**10, smem=(0,) if staged else (), copies=64,
    )


def input_gradient(vec, dz, matrices, heads):
    arrays = (dz, matrices, *heads)
    return call(
        input_grad_kernel, (vec, *arrays), like(dz), [*like(*arrays), *like(dz)], 40, 2 * 10**9, near=(0,), copies=24
    )[0]


def adam_step(settings_ref, now, grad, one, two, decay):
    beta_one, beta_two = settings_ref[1], settings_ref[2]
    first = beta_one * one + (1.0 - beta_one) * grad
    second = beta_two * two + (1.0 - beta_two) * grad * grad
    change = (first / settings_ref[4]) / (jnp.sqrt(second / settings_ref[5]) + 1e-08)
    if decay:
        change = change + settings_ref[3] * now
    return now - settings_ref[0] * change, first, second


def store_step(refs, where, results):
    for ref, value in zip(refs, results):
        ref[where] = value


def hidden_adam_kernel(place_ref, settings_ref, mine_ref, other_ref, *refs):
    core = place_of(place_ref)[0]
    expand, shrink = refs[0:3], refs[3:6]
    new_expand, new_shrink = refs[6:9], refs[9:12]
    half = mine_ref.shape[1]
    shard = expand[0].shape[0]
    blocks = expand[0].shape[1] // (2 * half)
    for step, ref in ((0, mine_ref), (1, other_ref)):
        side = jnp.bitwise_xor(core, step) * half
        cols = pl.ds(pl.multiple_of(side, half), half)
        for block in range(blocks):
            where = (slice(None), pl.ds(pl.multiple_of(block * 2 * half + side, half), half))
            grad = ref[block * shard : (block + 1) * shard, :]
            now, one, two = (r[where] for r in expand)
            store_step(new_expand, where, adam_step(settings_ref, now, grad, one, two, True))
        where = (slice(None), cols)
        now, one, two = (r[where] for r in shrink)
        store_step(new_shrink, where, adam_step(settings_ref, now, ref[blocks * shard :, :], one, two, True))


def attention_adam_kernel(place_ref, settings_ref, mine_one, other_one, mine_two, other_two, *refs):
    core = place_of(place_ref)[0]
    matrices, bias, vectors = refs[0:3], refs[3:6], refs[6:9]
    new_matrices, new_bias, new_vectors = refs[9:12], refs[12:15], refs[15:18]
    half = mine_one.shape[1]
    shard = matrices[0].shape[1]
    for step, one_ref, two_ref in ((0, mine_one, mine_two), (1, other_one, other_two)):
        cols = pl.ds(pl.multiple_of(jnp.bitwise_xor(core, step) * half, half), half)
        for index in range(8):
            ref, at = (one_ref, index) if index < 3 else (two_ref, index - 3)
            where = (index, slice(None), cols)
            now, one, two = (r[where] for r in matrices)
            grad = ref[at * shard : (at + 1) * shard, :]
            store_step(new_matrices, where, adam_step(settings_ref, now, grad, one, two, True))
    small = mine_two[5 * shard :, :] + other_two[5 * shard :, :]
    for group, new, grad in (
        (bias, new_bias, small[10:11, : bias[0].shape[1]]),
        (vectors, new_vectors, small[:10, : vectors[0].shape[1]]),
    ):
        now, one, two = (r[...] for r in group)
        store_step(new, ..., adam_step(settings_ref, now, grad, one, two, False))


def adam_call(kernel, scalars, grads, params):
    return call(
        kernel, (*scalars, *grads, *params), [(p.shape, F32) for p in params], [], 32, 10**7, smem=(0, 1),
        near=range(2, 2 + len(grads) + len(params)), near_outs=range(len(params)),
    )


CORE_SWAP = [(0, 1), (1, 0), (2, 3), (3, 2)]
CHIP_SWAP = [(0, 2), (2, 0), (1, 3), (3, 1)]
ROW_SWAP = [(i, i ^ 1) for i in range(8)]


LINES = [[0, 2, 4, 6], [1, 3, 5, 7]]


def line_shift(step):
    return [(2 * z + y, 2 * ((z + step) % 4) + y) for z in range(4) for y in (0, 1)]


def small_mesh(mesh):
    return mesh.shape["rep"] == 4 and mesh.shape["fsdp"] == 8


class StagedGather:
    def rows(self, mine, done):
        self.mine = mine
        self.other = lax.ppermute(after(mine, done), "fsdp", ROW_SWAP)

    def line(self, done):
        self.pair = after(jnp.stack([self.mine, self.other]), done)
        self.received = [lax.ppermute(self.pair, "fsdp", line_shift(step)) for step in (1, 2, 3)]

    def chips(self, done):
        self.part = jnp.stack([self.pair, *(after(received, done) for received in self.received)])
        self.far = lax.ppermute(self.part, "rep", CHIP_SWAP)

    def cores(self, done):
        far = after(self.far, done)
        part = after(self.part, done)
        return part, far, lax.ppermute(part, "rep", CORE_SWAP), lax.ppermute(far, "rep", CORE_SWAP)


def gather_staged(pack):
    quarter = pack.shape[0] // 4
    mine = lax.dynamic_slice_in_dim(pack, lax.axis_index("rep") * quarter, quarter, 0)
    pair = jnp.stack([mine, lax.ppermute(mine, "fsdp", ROW_SWAP)])
    part = jnp.stack([pair] + [lax.ppermute(pair, "fsdp", line_shift(step)) for step in (1, 2, 3)])
    both = jnp.stack([part, lax.ppermute(part, "rep", CHIP_SWAP)])
    return pair, part, both


def after(value, *done):
    return lax.optimization_barrier((value, *done))[0]


def gather_half(pack):
    half = pack.shape[1] // 2
    mine = lax.dynamic_slice_in_dim(pack, lax.axis_index("rep") % 2 * half, half, 1)
    return lax.all_gather(mine, "fsdp", axis=0)


def both_halves(mine, done):
    mine = after(mine, done)
    return mine, lax.ppermute(mine, "rep", CORE_SWAP)


def low_sum(mine, received):
    return mine + received


def reduce_cores(keep, send):
    received = lax.ppermute(send, "rep", CORE_SWAP)
    return low_sum(keep[0], received[0]), low_sum(keep[1], received[1])


def send_rows(send):
    return lax.ppermute(send, "fsdp", ROW_SWAP)


def reduce_rows(keep, received, done):
    return low_sum(keep, after(received, done))


def reduce_last(part, *done):
    total = part.astype(F32) + after(lax.ppermute(part, "rep", CHIP_SWAP), *done).astype(F32)
    return total, lax.ppermute(total, "rep", CORE_SWAP)


def reduce_line(joined):
    part = lax.psum_scatter(joined, "fsdp", scatter_dimension=0, axis_index_groups=LINES)
    return part.reshape(joined.shape[1:])


def reduce_shifts(joined, done):
    line = lax.axis_index("fsdp") // 2
    total = lax.dynamic_index_in_dim(joined, line, 0, False).astype(F32)
    for step in (1, 2, 3):
        away = lax.dynamic_index_in_dim(joined, (line + step) % 4, 0, False)
        total = total + after(lax.ppermute(away, "fsdp", line_shift(step)), done).astype(F32)
    return total.astype(BF)


def reduce_plain(grads):
    return lax.psum(lax.psum_scatter(grads, "fsdp", scatter_dimension=0), "rep").astype(F32)


def adam_update(weight_now, gradient, moment_one, moment_two, settings, step_float, factor):
    learn_rate, beta_one, beta_two, decay_rate = settings[0], settings[1], settings[2], settings[3]
    first_new = beta_one * moment_one + (1.0 - beta_one) * gradient
    second_new = beta_two * moment_two + (1.0 - beta_two) * gradient * gradient
    first_hat = first_new / (1.0 - beta_one**step_float)
    second_hat = second_new / (1.0 - beta_two**step_float)
    change = first_hat / (jnp.sqrt(second_hat) + 1e-08) + factor * decay_rate * weight_now
    return (weight_now - learn_rate * change, first_new, second_new)


def per_device(
    small, inputs, memory, memory_length, target_pos, cotangent,
    attention_weights, expand_weights, shrink_weights, expand_bias, layer_vectors,
    first_attention, first_expand, first_shrink, first_bias, first_vectors,
    second_attention, second_expand, second_shrink, second_bias, second_vectors,
    hyper_rates, step_count,
):
    length, width = inputs.shape[1:]
    shard = attention_weights.shape[1]
    count = width // shard
    inner_shard = shrink_weights.shape[0]
    blocks = inner_shard // shard
    low_attention = attention_weights.astype(BF).reshape(8 * shard, width)
    pack_one = low_attention[: 3 * shard]
    expand_low = expand_weights.astype(BF).reshape(shard, blocks, width)
    shrink_low = shrink_weights.astype(BF)
    x, source, cot = inputs[0], memory[0], cotangent[0]
    step_float = step_count.astype(F32)

    if small:
        place = jnp.stack([lax.axis_index("rep"), lax.axis_index("fsdp")]).astype(jnp.int32)
        small_rows = jnp.concatenate(
            [
                jnp.pad(layer_vectors, ((0, 0), (0, inner_shard - shard))),
                expand_bias[None],
                jnp.zeros((5, inner_shard), F32),
            ]
        )
        small_rows = jnp.pad(small_rows, ((0, 0), (0, width - inner_shard))).astype(BF)
        pack_two = jnp.concatenate([low_attention[3 * shard :], small_rows])
        two = gather_half(pack_two)
        pair_one, part_one, one = gather_staged(pack_one)
        half = shard // 2
        halves = expand_low.reshape(2, half, blocks, width).transpose(0, 2, 1, 3)
        quarters = jnp.stack([halves, shrink_low.reshape(2, blocks, half, width)], axis=1)
        core, chip = place[0] % 2, place[0] // 2
        quarter = lax.dynamic_slice(
            quarters, (chip, 0, 0, 0, core * (width // 2)), (1, *quarters.shape[1:4], width // 2)
        )
        three = StagedGather()
        three.rows(quarter[0], pair_one)
        one = both_halves(one, three.other)
        three.line(part_one)
        given = None
        cross_shards = (shard,) * 5
    else:
        place, cross_shards = None, None
        flat = jnp.concatenate([layer_vectors.reshape(-1), expand_bias]).astype(BF)
        flat = lax.all_gather(flat, "fsdp", axis=0).astype(F32)
        vector_size = layer_vectors.size
        vec = flat[:, :vector_size].reshape(count, -1, shard).transpose(1, 0, 2).reshape(-1, width)
        given = jnp.pad(vec, ((0, 16 - vec.shape[0]), (0, 0))), flat[:, vector_size:].reshape(1, -1)

        def gather_all(pack, shards):
            full = lax.all_gather(pack, "fsdp", axis=0)
            pieces, first = [], 0
            for rows in shards:
                pieces.append(full[:, first : first + rows].reshape(-1, width))
                first += rows
            return pieces

        def owners(grads, shards):
            pieces, first = [], 0
            for rows in shards:
                pieces.append(grads[first : first + rows * count].reshape(count, rows, width))
                first += rows * count
            return jnp.concatenate(pieces, axis=1)

        one = jnp.concatenate(gather_all(pack_one, (shard,) * 3))
        two = [m[None] for m in gather_all(low_attention[3 * shard :], (shard,) * 5)]
        pack = jnp.concatenate([expand_low.transpose(1, 0, 2).reshape(-1, width), shrink_low])
        *expand_all, shrink_all = gather_all(pack, (*(shard,) * blocks, inner_shard))
        three = jnp.stack(expand_all)[:, None], shrink_all[None]

    *saved_one, matrices = forward_self(place, x, target_pos, one, small)
    if small:
        three.chips(saved_one[4])
        two = both_halves(two, three.part)
    norm_one, inv_one, *saved_two, norm_two, inv_two, vec, bias = forward_cross(
        place, x, saved_one[4], source, memory_length, two, given, cross_shards
    )
    three = three.cores(norm_two) if small else three
    sums_three, bias_sum, outputs, dz_two, *grad_three = hidden_step(
        place, three, norm_two, inv_two, cot, vec, bias
    )
    if small:
        keep_three, send_three = reduce_cores(*grad_three)
        dz_two = after(dz_two, keep_three, send_three)
        received_three = send_rows(send_three)
    sums_two, dz_one, memory_grad, *grad_two = backward_cross(
        place, two, dz_two, x, norm_one, inv_one, source, vec, saved_two, saved_one[4],
        (sums_three, bias_sum), cross_shards,
    )
    if small:
        joined_three = reduce_rows(keep_three, received_three, dz_one)
        keep_two, send_two = reduce_cores(grad_two[0], after(grad_two[1], joined_three))
        dz_one = after(dz_one, joined_three, keep_two, send_two)
        received_two = send_rows(send_two)
    *heads, grad_keep, grad_send = (
        *backward_self(place, two if small else two[:1], dz_one, x, saved_one, cross_shards),
        *((None,) if not small else ()),
    )
    if small:
        joined_two = reduce_rows(keep_two, received_two, heads[0])
        keep_one, send_one = reduce_cores(grad_keep, after(grad_send, joined_two))
        heads = after(tuple(heads), keep_one, send_one)
        received_one = send_rows(send_one)
    input_grad = input_gradient(vec, dz_one, matrices, heads)

    attention = (attention_weights, first_attention, second_attention)
    expand = (expand_weights, first_expand, second_expand)
    shrink = (shrink_weights, first_shrink, second_shrink)
    bias = (expand_bias, first_bias, second_bias)
    vectors = (layer_vectors, first_vectors, second_vectors)
    if small:
        powers = 1.0 - hyper_rates[1:3] ** step_float
        scalars = place, jnp.concatenate([hyper_rates, powers])
        part_three = reduce_line(joined_three)
        part_two = reduce_line(joined_two)
        total_three = reduce_last(after(part_three, heads[0]), input_grad)
        joined_one = reduce_rows(keep_one, received_one, input_grad)
        hidden_new = adam_call(hidden_adam_kernel, scalars, total_three, (*expand, *shrink))
        total_two = reduce_last(part_two)
        total_one = reduce_last(reduce_shifts(joined_one, hidden_new[0]))
        rows = tuple(b[None] for b in bias)
        other_new = adam_call(
            attention_adam_kernel, scalars, (*total_one, *total_two), (*attention, *rows, *vectors)
        )
        new_bias = tuple(b[0] for b in other_new[3:6])
        updated = (*other_new[:3], *hidden_new, *new_bias, *other_new[6:])
    else:
        sums = (sums_two + sums_three)[: layer_vectors.shape[0]]
        flat = jnp.concatenate(
            [
                sums.reshape(-1, count, shard).transpose(1, 0, 2).reshape(count, -1),
                bias_sum.reshape(count, inner_shard),
            ],
            axis=1,
        )
        total_three = reduce_plain(owners(grad_three[0], (*(shard,) * blocks, inner_shard)))
        total_two = reduce_plain(owners(grad_two[0], (shard,) * 5))
        total_one = reduce_plain(owners(grad_keep, (shard,) * 3))
        flat = lax.psum(lax.psum_scatter(flat, "fsdp", scatter_dimension=0), "rep")
        grad_attention = jnp.concatenate([total_one, total_two]).reshape(attention_weights.shape)
        grad_expand = total_three[: blocks * shard].reshape(blocks, shard, width).transpose(1, 0, 2)
        updated = []
        for (now, one_now, two_now), grad, factor in (
            (attention, grad_attention, 1.0),
            (expand, grad_expand.reshape(shard, -1), 1.0),
            (shrink, total_three[blocks * shard :], 1.0),
            (bias, flat[layer_vectors.size :], 0.0),
            (vectors, flat[: layer_vectors.size].reshape(-1, shard), 0.0),
        ):
            updated.extend(adam_update(now, grad, one_now, two_now, hyper_rates, step_float, factor))
    return (outputs[None], input_grad[None], memory_grad[None], *updated)


def solution(mesh):
    rows = ("rep", "fsdp")
    params = (P(None, "fsdp", None), P("fsdp", None), P("fsdp", None), P("fsdp"), P(None, "fsdp"))
    return jax.shard_map(
        functools.partial(per_device, small_mesh(mesh)),
        mesh=mesh,
        in_specs=(
            P(rows, None, None), P(rows, None, None), P(rows), P(rows, None), P(rows, None, None),
            *params, *params, *params, P(), P(),
        ),
        out_specs=(
            P(rows, None, None), P(rows, None, None), P(rows, None, None),
            *(spec for spec in params for _ in range(3)),
        ),
        check_vma=False,
    )
```

```python
import functools

import jax
import jax.numpy as jnp
from jax import lax
from jax.experimental import pallas as pl
from jax.experimental.pallas import tpu as pltpu
from jax.sharding import PartitionSpec as P

BF = jnp.bfloat16
F32 = jnp.float32
HEAD_DIM = 64
PAIR = 128
TILE = 256
MIB = 1 << 20


def dot(left, right, left_dim, right_dim):
    return lax.dot_general(
        left, right, (((left_dim,), (right_dim,)), ((), ())), preferred_element_type=F32
    )


def lanes(size):
    return lax.broadcasted_iota(jnp.int32, (1, size), 1)


def half_masks():
    first = jnp.where(lanes(PAIR) < HEAD_DIM, 1.0, 0.0)
    return first.astype(BF), (1.0 - first).astype(BF)


def rows_at(index, size=TILE):
    return pl.ds(pl.multiple_of(index * size, size), size)


class Mover:
    def __init__(self, sems):
        self.sems, self.used, self.leaving = sems, 0, []

    def take(self, count=1):
        self.used += count
        return self.used - count

    def load(self, source, target):
        copy = pltpu.make_async_copy(source, target, self.sems.at[self.take()])
        copy.start()
        return copy

    def load_rows(self, source, target):
        count = source.shape[0] // TILE
        first = self.take(count)

        def copy(tile):
            rows = rows_at(tile)
            return pltpu.make_async_copy(source.at[rows], target.at[rows], self.sems.at[first + tile])

        for tile in range(count):
            copy(tile).start()
        return lambda tile: copy(tile).wait()

    def store(self, source, target):
        self.leaving.append(self.load(source, target))

    def store_parts(self, source, target, count, where):
        first = self.take(count)

        def copy(part):
            return pltpu.make_async_copy(source.at[where(part)], target.at[where(part)], self.sems.at[first + part])

        self.leaving.extend(copy(part) for part in range(count))
        return lambda part: copy(part).start()

    def store_rows(self, source, target):
        return self.store_parts(source, target, source.shape[0] // TILE, rows_at)

    def finish(self):
        for copy in self.leaving:
            copy.wait()


def columns_at(size):
    return lambda part: (slice(None), rows_at(part, size))


def load_matrices(mover, core, sources, targets, which=None):
    waits, first = [], 0
    for index, target in enumerate(targets):
        if which is not None and index not in which:
            first += target.shape[1]
            continue
        if core is None:
            copies = [mover.load(sources[index], target)]
        else:
            rows, half = target.shape[1], target.shape[2] // 2
            copies = []
            for step, source in enumerate(sources):
                cols = pl.ds(pl.multiple_of(jnp.bitwise_xor(core, step) * half, half), half)
                copies.append(mover.load(source.at[:, first : first + rows, :], target.at[:, :, cols]))
            first += rows
        waits.append(lambda copies=copies: [copy.wait() for copy in copies])
    return waits


def load_quarters(mover, place_ref, packs, expand_ref, shrink_ref):
    core, chip, line, row = place_of(place_ref)
    half, cut = expand_ref.shape[3] // 2, expand_ref.shape[2] // 2
    loads = ([], [])
    for index, pack in enumerate(packs):
        core_step, chip_step = divmod(index, 2)
        cols = pl.ds(pl.multiple_of(jnp.bitwise_xor(core, core_step) * half, half), half)
        side = jnp.bitwise_xor(chip, chip_step)
        rows = pl.ds(pl.multiple_of(side * cut, cut), cut)
        for line_step in range(4):
            for row_step in (0, 1):
                owner = lax.rem(line - line_step + 4, 4) * 2 + jnp.bitwise_xor(row, row_step)
                source = pack.at[line_step, row_step]
                loads[0].append((source.at[0], expand_ref.at[:, owner, rows, cols]))
                loads[1].append((source.at[1], shrink_ref.at[owner, side, :, :, cols]))
    return [[mover.load(*pair) for pair in pairs] for pairs in loads]


def whole(ref):
    return ref[...].reshape(-1, ref.shape[-1])


def key_extra(length_limit, count):
    lane = lanes(PAIR) % HEAD_DIM
    extra = jnp.where(lane < 3, 1.0, 0.0)
    if length_limit is None:
        return jnp.broadcast_to(extra, (count, PAIR)).astype(BF)
    row = lax.broadcasted_iota(jnp.int32, (count, PAIR), 0)
    bias = jnp.where(row < length_limit, 0.0, -1e30)
    return jnp.where(lane == 3, bias, extra).astype(BF)


def put_start(pos_ref, start_ref):
    length = start_ref.shape[0]
    query = lax.broadcasted_iota(jnp.int32, (8, length), 1)
    first = (query - pos_ref[...]).astype(F32)
    start_ref[...] = first.T[:, :1].astype(jnp.int32)


def visible(start, first_query, first_key, count):
    key = first_key + lax.broadcasted_iota(jnp.int32, (TILE, count), 1)
    seen = key >= start
    if first_key == first_query:
        query = first_query + lax.broadcasted_iota(jnp.int32, (TILE, count), 0)
        seen = seen & (key <= query)
    return seen


def key_spans(tile, count, causal):
    if not causal:
        return [(0, count)]
    spans = [(0, tile * TILE)] if tile else []
    return spans + [(tile * TILE, TILE)]


def staggered(first, then, count):
    ready = first(0)
    for index in range(count):
        following = first(index + 1) if index + 1 < count else None
        then(index, ready)
        ready = following


class ProbStore:
    def __init__(self, mover, hbm, ref, causal):
        self.hbm, self.ref, self.mover = hbm, ref, mover
        self.tiles = ref.shape[2] // TILE
        self.causal = causal
        self.first = mover.take(2 * self.tiles)

    def views(self, pair, slot, tile):
        rows = slice(tile * TILE, (tile + 1) * TILE)
        keys = slice(0, (tile + 1) * TILE) if self.causal else slice(0, self.ref.shape[3])
        sem = self.mover.sems.at[self.first + slot * self.tiles + tile]
        return self.hbm.at[pair, :, rows, keys], self.ref.at[slot, :, rows, keys], sem

    def copy(self, pair, slot, tile, out):
        far, near, sem = self.views(pair, slot, tile)
        return pltpu.make_async_copy(near, far, sem) if out else pltpu.make_async_copy(far, near, sem)


def two_pairs(pairs, body):
    @pl.loop(0, pairs // 2)
    def _(step):
        for slot in (0, 1):
            body(2 * step + slot, slot, step)


def attend(q_ref, k_ref, v_ref, extra_ref, start_ref, o_ref, store, finished):
    length, count = q_ref.shape[0], k_ref.shape[0]
    causal = start_ref is not None
    masks = half_masks()
    pairs = q_ref.shape[1] // PAIR

    def one_pair(pair, slot, step):
        cols = rows_at(pair, PAIR)

        @pl.when(step > 0)
        def _():
            for tile in range(store.tiles):
                store.copy(pair - 2, slot, tile, True).wait()

        steps = [(tile, side) for tile in range(length // TILE) for side in (0, 1)]
        results = {}

        def scores_of(index):
            tile, side = steps[index]
            rows = slice(tile * TILE, (tile + 1) * TILE)
            queries = q_ref[rows, cols] * masks[side]
            if not causal:
                base = HEAD_DIM * (1 - side)
                queries = jnp.where(lanes(PAIR) == base + 3, 1.0, queries.astype(F32)).astype(BF)
            blocks = []
            for first, size in key_spans(tile, count, causal):
                keys = k_ref[first : first + size, cols]
                if not causal:
                    keys = keys * masks[side] + extra_ref[first : first + size, :] * masks[1 - side]
                scores = dot(queries, keys, 1, 1)
                if causal:
                    seen = visible(start_ref[rows, :], tile * TILE, first, size)
                    scores = jnp.where(seen, scores, -1000000000.0)
                blocks.append(scores)
            return blocks

        def mix(index, score_blocks):
            tile, side = steps[index]
            rows = slice(tile * TILE, (tile + 1) * TILE)
            spans = key_spans(tile, count, causal)
            top = functools.reduce(
                jnp.maximum, [jnp.max(scores, axis=1, keepdims=True) for scores in score_blocks]
            )
            exponents = [jnp.exp(scores - top) for scores in score_blocks]
            inverse = 1.0 / sum(jnp.sum(exponent, axis=1, keepdims=True) for exponent in exponents)
            total = None
            for exponent, (first, size) in zip(exponents, spans):
                probs = (exponent * inverse).astype(BF)
                store.ref[slot, side, rows, first : first + size] = probs
                part = dot(probs, v_ref[first : first + size, cols], 1, 0)
                total = part if total is None else total + part
            results[side] = total
            if side == 1:
                o_ref[rows, cols] = jnp.where(lanes(PAIR) < HEAD_DIM, results[0], results[1]).astype(BF)

        staggered(scores_of, mix, len(steps))
        for tile in range(store.tiles):
            store.copy(pair, slot, tile, True).start()
        for start_store in finished:
            start_store(pair)

    two_pairs(pairs, one_pair)
    for slot in (0, 1):
        for tile in range(store.tiles):
            store.mover.leaving.append(store.copy(pairs - 2 + slot, slot, tile, True))


def load_probs(store, slot):
    for tile in reversed(range(store.tiles)):
        store.copy(slot, slot, tile, False).start()


def attend_back(q_ref, da_ref, inner_ref, k_ref, v_ref, store, dq_ref, dk_ref, dv_ref, dk_sum, dv_sum, values_ref):
    length, count = q_ref.shape[0], k_ref.shape[0]
    masks = half_masks()
    pairs = k_ref.shape[1] // PAIR

    def one_pair(pair, slot, step):
        cols = rows_at(pair, PAIR)
        for tile in range(store.tiles):
            store.copy(pair, slot, tile, False).wait()
        for side in (0, 1):
            values_ref[side] = v_ref[:, cols] * masks[side]
        steps = [(tile, side) for tile in reversed(range(length // TILE)) for side in (0, 1)]
        query_grads = {}

        def place(index):
            tile, side = steps[index]
            size = (tile + 1) * TILE if store.causal else count
            return tile, side, slice(tile * TILE, (tile + 1) * TILE), slice(0, size)

        def collect(ref, tile, side, span, part):
            if tile == length // TILE - 1:
                ref[side, :, span] = part
            else:
                ref[side, :, span] += part

        def value_side(index):
            _, side, rows, span = place(index)
            return dot(da_ref[rows, cols], values_ref[side, span, :], 1, 1)

        def score_side(index, grad_probs):
            tile, side, rows, span = place(index)
            probs = store.ref[slot, side, rows, span]
            collect(dv_sum, tile, side, span, dot(da_ref[rows, cols], probs, 0, 0))
            inner = inner_ref[pair, rows, side : side + 1]
            grad_scores = (probs.astype(F32) * (grad_probs - inner)).astype(BF)
            collect(dk_sum, tile, side, span, dot(q_ref[rows, cols], grad_scores, 0, 0))
            query_grads[side] = dot(grad_scores, k_ref[span, cols], 1, 0)
            if side == 1:
                dq_ref[rows, cols] = (
                    jnp.where(lanes(PAIR) < HEAD_DIM, query_grads[0], query_grads[1]) * HEAD_DIM**-0.5
                ).astype(BF)

        staggered(value_side, score_side, len(steps))
        for sums, out in ((dk_sum, dk_ref), (dv_sum, dv_ref)):
            joined = jnp.concatenate([sums[0, :HEAD_DIM, :], sums[1, HEAD_DIM:, :]], axis=0)
            out[:, cols] = joined.astype(BF).T

        @pl.when(step < pairs // 2 - 1)
        def _():
            for tile in range(store.tiles):
                store.copy(pair + 2, slot, tile, False).start()

    two_pairs(pairs, one_pair)


def norm_rows(summed):
    center = jnp.mean(summed, axis=1, keepdims=True)
    shifted = summed - center
    inverse = lax.rsqrt(jnp.mean(shifted * shifted, axis=1, keepdims=True) + 1e-05)
    return shifted * inverse, inverse


def norm_back(grad_out, normed, inverse, gain):
    scaled = grad_out * gain
    first = jnp.mean(scaled, axis=1, keepdims=True)
    second = jnp.mean(scaled * normed, axis=1, keepdims=True)
    return inverse * (scaled - first - normed * second)


def add_rows(ref, row, values):
    ref[row : row + 1, :] += jnp.sum(values, axis=0, keepdims=True)


def place_of(place_ref):
    rep, place = place_ref[0], place_ref[1]
    return lax.rem(rep, 2), lax.div(rep, 2), lax.div(place, 2), lax.rem(place, 2)


def assemble(place_ref, chunk_refs, all_ref):
    core, chip, line, row = place_of(place_ref)
    width = all_ref.shape[1]
    quarter = chunk_refs[0].shape[3]
    shard = quarter * 4 // 3
    for core_step, chunk_ref in enumerate(chunk_refs):
        for chip_step in (0, 1):
            rep = jnp.bitwise_xor(chip, chip_step) * 2 + jnp.bitwise_xor(core, core_step)
            for line_step in range(4):
                for row_step in (0, 1):
                    owner = lax.rem(line - line_step + 4, 4) * 2 + jnp.bitwise_xor(row, row_step)
                    for piece in range(quarter // 16):
                        stacked = rep * quarter + piece * 16
                        matrix = lax.div(stacked, shard)
                        target = matrix * width + owner * shard + (stacked - matrix * shard)
                        all_ref[pl.ds(pl.multiple_of(target, 16), 16), :] = chunk_ref[
                            chip_step, line_step, row_step, piece * 16 : (piece + 1) * 16, :
                        ]


def assemble_halves(place_ref, mine_ref, other_ref, all_ref, shards):
    core = place_of(place_ref)[0]
    devices, _, half = mine_ref.shape
    for step, ref in ((0, mine_ref), (1, other_ref)):
        cols = pl.ds(pl.multiple_of(jnp.bitwise_xor(core, step) * half, half), half)
        first, target = 0, 0
        for shard in shards:
            for owner in range(devices):
                at = target + owner * shard
                all_ref[at : at + shard, cols] = ref[owner, first : first + shard, :]
            first += shard
            target += shard * devices


def unpack_small(all_ref, base, vec_ref, bias_ref):
    devices = vec_ref.shape[1] // HEAD_DIM
    inner = bias_ref.shape[1] // devices
    for pair in range(devices // 2):
        first = base + 2 * pair * 16
        left = all_ref[first : first + 16, :PAIR].astype(F32)
        right = all_ref[first + 16 : first + 32, :PAIR].astype(F32)
        vec_ref[:, pair * PAIR : (pair + 1) * PAIR] = jnp.where(
            lanes(PAIR) < HEAD_DIM, left, pltpu.roll(right, HEAD_DIM, 1)
        )
    for owner in range(devices):
        rows = all_ref[base + owner * 16 : base + owner * 16 + 16, :inner].astype(F32)
        bias_ref[:, owner * inner : (owner + 1) * inner] = rows[10:11, :]


def self_forward_kernel(staged, *refs):
    if staged:
        place_ref, pos_ref, x_hbm, chunk_hbm, other_hbm = refs[:5]
        refs = refs[5:]
    else:
        pos_ref, x_hbm, all_hbm = refs[:3]
        refs = refs[3:]
    p_hbm, q_hbm, k_hbm, v_hbm, o_hbm = refs[:5]
    refs = refs[5:]
    if staged:
        all_out, refs = refs[0], refs[1:]
    x_ref, all_ref, q_ref, k_ref, v_ref, o_ref, p_ref, start_ref = refs[:8]
    mover = Mover(refs[-1])
    length, width = x_ref.shape
    if staged:
        chunk_refs = refs[8:10]
        loads = [mover.load(a, b) for a, b in zip((chunk_hbm, other_hbm), chunk_refs)]
    else:
        loads = [mover.load(all_hbm, all_ref)]
    x_load = mover.load(x_hbm, x_ref)
    put_start(pos_ref, start_ref)
    for load in loads:
        load.wait()
    if staged:
        assemble(place_ref, chunk_refs, all_ref)
        mover.store(all_ref, all_out)
    x_load.wait()

    @pl.loop(0, length // TILE)
    def _(tile):
        rows = rows_at(tile)
        source = x_ref[rows, :]
        queries = dot(source, all_ref[:width, :], 1, 0).astype(BF)
        q_ref[rows, :] = queries * jnp.asarray(HEAD_DIM**-0.5, BF)
        k_ref[rows, :] = dot(source, all_ref[width : 2 * width, :], 1, 0).astype(BF)
        v_ref[rows, :] = dot(source, all_ref[2 * width :, :], 1, 0).astype(BF)

    mover.store(k_ref, k_hbm)
    mover.store(v_ref, v_hbm)
    mover.store(q_ref, q_hbm)
    finished = (mover.store_parts(o_ref, o_hbm, width // PAIR, columns_at(PAIR)),)
    attend(q_ref, k_ref, v_ref, None, start_ref, o_ref, ProbStore(mover, p_hbm, p_ref, True), finished)
    mover.finish()


def unpack_small(small_ref, vec_ref, bias_ref):
    devices = vec_ref.shape[1] // HEAD_DIM
    inner = bias_ref.shape[1] // devices
    for pair in range(devices // 2):
        left = small_ref[0, 2 * pair, :, :PAIR].astype(F32)
        right = small_ref[0, 2 * pair + 1, :, :PAIR].astype(F32)
        vec_ref[:, pair * PAIR : (pair + 1) * PAIR] = jnp.where(
            lanes(PAIR) < HEAD_DIM, left, pltpu.roll(right, HEAD_DIM, 1)
        )
    for owner in range(devices):
        rows = small_ref[0, owner, :, :inner].astype(F32)
        bias_ref[:, owner * inner : (owner + 1) * inner] = rows[10:11, :]


def cross_forward_kernel(staged, *refs):
    place_ref, core = None, None
    if staged:
        place_ref, refs = refs[0], refs[1:]
        core = place_of(place_ref)[0]
    length_ref, refs = refs[0], refs[1:]
    if staged:
        x_hbm, mixed_hbm, source_hbm, *packs = refs[:5]
        refs = refs[5:]
    else:
        vec_ref, x_hbm, mixed_hbm, source_hbm, *packs = refs[:9]
        refs = refs[9:]
    first_hbm, first_inv_hbm, p_hbm, q_hbm, k_hbm, v_hbm, o_hbm, n_hbm, inv_hbm = refs[:9]
    refs = refs[9:]
    if staged:
        vec_ref, bias_ref, refs = refs[0], refs[1], refs[2:]
    x_ref, mixed_ref, source_ref, first_ref, first_inv_ref, q_ref, k_ref, v_ref, o_ref, n_ref, inv_ref = refs[:11]
    p_ref, extra_ref, *w_refs = refs[11:18]
    mover = Mover(refs[-1])
    length, width = q_ref.shape

    if staged:
        small_ref = refs[18]
        rows = packs[0].shape[1]
        small = [
            mover.load(pack.at[:, rows - 16 :, :], small_ref.at[jnp.bitwise_xor(core, step)])
            for step, pack in enumerate(packs)
        ]
    source_load = mover.load_rows(source_hbm, source_ref)
    order = (2, 3, 0, 1, 4)
    waits = [None] * 5
    if staged:
        half = width // 2
        shard = w_refs[0].shape[1]
        for index in order:
            copies = []
            for step, pack in enumerate(packs):
                cols = pl.ds(pl.multiple_of(jnp.bitwise_xor(core, step) * half, half), half)
                copies.append(
                    mover.load(pack.at[:, index * shard : (index + 1) * shard, :], w_refs[index].at[:, :, cols])
                )
            waits[index] = lambda copies=copies: [copy.wait() for copy in copies]
    else:
        for index in order:
            waits[index] = mover.load(packs[index], w_refs[index]).wait
    mixed_load = mover.load_rows(mixed_hbm, mixed_ref)
    x_load = mover.load_rows(x_hbm, x_ref)
    extra_ref[...] = key_extra(length_ref[0], k_ref.shape[0])
    waits[2]()
    waits[3]()

    @pl.loop(0, source_ref.shape[0] // TILE)
    def _(tile):
        rows = rows_at(tile)
        source_load(tile)
        source = source_ref[rows, :]
        k_ref[rows, :] = dot(source, whole(w_refs[2]), 1, 0).astype(BF)
        v_ref[rows, :] = dot(source, whole(w_refs[3]), 1, 0).astype(BF)

    mover.store(k_ref, k_hbm)
    mover.store(v_ref, v_hbm)
    if staged:
        for load in small:
            load.wait()
        unpack_small(small_ref, vec_ref, bias_ref)
    waits[0]()
    waits[1]()

    @pl.loop(0, length // TILE)
    def _(tile):
        rows = rows_at(tile)
        mixed_load(tile)
        x_load(tile)
        summed = x_ref[rows, :].astype(F32) * vec_ref[6:7, :] + dot(mixed_ref[rows, :], whole(w_refs[0]), 1, 0)
        normed, inverse = norm_rows(summed)
        first_ref[rows, :] = normed
        first_inv_ref[rows, :] = inverse
        low = (normed * vec_ref[0:1, :] + vec_ref[3:4, :]).astype(BF)
        queries = dot(low, whole(w_refs[1]), 1, 0).astype(BF)
        q_ref[rows, :] = queries * jnp.asarray(HEAD_DIM**-0.5, BF)

    mover.store(first_ref, first_hbm)
    mover.store(first_inv_ref, first_inv_hbm)
    mover.store(q_ref, q_hbm)
    finished = (mover.store_parts(o_ref, o_hbm, width // PAIR, columns_at(PAIR)),)
    attend(q_ref, k_ref, v_ref, extra_ref, None, o_ref, ProbStore(mover, p_hbm, p_ref, False), finished)
    waits[4]()
    n_store, inv_store = mover.store_rows(n_ref, n_hbm), mover.store_rows(inv_ref, inv_hbm)

    @pl.loop(0, length // TILE)
    def _(tile):
        rows = rows_at(tile)
        first_out = first_ref[rows, :] * vec_ref[0:1, :] + vec_ref[3:4, :]
        summed = first_out * vec_ref[7:8, :] + dot(o_ref[rows, :], whole(w_refs[4]), 1, 0)
        normed, inverse = norm_rows(summed)
        n_ref[rows, :] = normed
        inv_ref[rows, :] = inverse
        n_store(tile)
        inv_store(tile)

    mover.finish()


def hidden_kernel(staged, *refs):
    place_ref, core = None, None
    if staged:
        place_ref, refs = refs[0], refs[1:]
        core = place_of(place_ref)[0]
    vec_ref, bias_ref, *packs = refs[: 6 if staged else 4]
    n_hbm, inv_hbm, cot_hbm = refs[len(packs) + 2 : len(packs) + 5]
    refs = refs[len(packs) + 5 :]
    count = 2 if staged else 1
    sums_ref, bias_sum_ref, out_hbm, dz_hbm = refs[:4]
    grad_hbms, refs = refs[4 : 4 + count], refs[4 + count :]
    grad_refs, refs = refs[:count], refs[count:]
    n_ref, inv_ref, cot_ref, out_ref, dz_ref, low_ref, h_ref, du_ref, df_ref, slope_ref, third_ref = refs[:11]
    blocks = bias_ref.shape[1] // vec_ref.shape[1]
    e_ref, s_ref = refs[11:13]
    mover = Mover(refs[-1])
    length, width = n_ref.shape

    n_load = mover.load_rows(n_hbm, n_ref)
    if staged:
        expand_loads, shrink_loads = load_quarters(mover, place_ref, packs, e_ref, s_ref)
    else:
        expand_loads, shrink_loads = [mover.load(packs[0], e_ref)], [mover.load(packs[1], s_ref)]
    cot_load = mover.load_rows(cot_hbm, cot_ref)
    inv_load = mover.load_rows(inv_hbm, inv_ref)
    out_store, dz_store = mover.store_rows(out_ref, out_hbm), mover.store_rows(dz_ref, dz_hbm)
    tiles = [slice(tile * TILE, (tile + 1) * TILE) for tile in range(length // TILE)]
    parts = [slice(block * width, (block + 1) * width) for block in range(blocks)]
    sums = {row: 0.0 for row in (1, 2, 4, 5, 8, 9)}
    bias_sums = [0.0] * blocks

    def add(row, values):
        sums[row] = sums[row] + jnp.sum(values, axis=0, keepdims=True)

    def second_out(rows):
        return n_ref[rows, :] * vec_ref[1:2, :] + vec_ref[4:5, :]

    for tile, rows in enumerate(tiles):
        n_load(tile)
        low_ref[rows, :] = second_out(rows).astype(BF)
    steps = [(block, rows) for block in range(blocks) for rows in tiles]

    def expand(index):
        block, rows = steps[index]
        return dot(low_ref[rows, :], whole(e_ref.at[block]), 1, 0) + bias_ref[:, parts[block]]

    def activate(index, before):
        block, rows = steps[index]
        square = before * before
        tangent = jnp.tanh(before * (0.7978845608028654 + 0.7978845608028654 * 0.044715 * square))
        half = 0.5 * (1.0 + tangent)
        slope_ref[rows, parts[block]] = half + before * (half * (1.0 - tangent)) * (
            0.7978845608028654 + 3.0 * 0.7978845608028654 * 0.044715 * square
        )
        h_ref[rows, parts[block]] = (before * half).astype(BF)

    for load in expand_loads:
        load.wait()
    staggered(expand, activate, len(steps))
    for load in shrink_loads:
        load.wait()
    for tile in range(len(tiles)):
        cot_load(tile)
        inv_load(tile)

    def shrink(tile):
        return dot(h_ref[tiles[tile], :], whole(s_ref), 1, 0)

    def outer_norm(tile, branch_out):
        rows = tiles[tile]
        second = second_out(rows)
        normed, inverse = norm_rows(second * vec_ref[8:9, :] + vec_ref[9:10, :] + branch_out)
        out_ref[rows, :] = (normed * vec_ref[2:3, :] + vec_ref[5:6, :]).astype(BF)
        grad_out = cot_ref[rows, :].astype(F32)
        third = norm_back(grad_out, normed, inverse, vec_ref[2:3, :])
        third_ref[rows, :] = third
        add(2, grad_out * normed)
        add(5, grad_out)
        branch = third.astype(BF)
        df_ref[rows, :] = branch
        add(9, branch.astype(F32))
        add(8, second * third)

    staggered(shrink, outer_norm, len(tiles))
    for tile in range(len(tiles)):
        out_store(tile)

    def shrink_back(index):
        block, rows = steps[index]
        return dot(df_ref[rows, :], whole(s_ref)[parts[block], :], 1, 1)

    def slope_back(index, grad_hidden):
        block, rows = steps[index]
        du = (grad_hidden * slope_ref[rows, parts[block]]).astype(BF)
        du_ref[rows, parts[block]] = du
        bias_sums[block] = bias_sums[block] + jnp.sum(du.astype(F32), axis=0, keepdims=True)

    staggered(shrink_back, slope_back, len(steps))

    def expand_back(tile):
        rows = tiles[tile]
        return sum(dot(du_ref[rows, parts[block]], whole(e_ref.at[block]), 1, 1) for block in range(blocks))

    def inner_norm(tile, grad_expanded):
        rows = tiles[tile]
        grad = vec_ref[8:9, :] * third_ref[rows, :] + grad_expanded
        normed = n_ref[rows, :]
        dz_ref[rows, :] = norm_back(grad, normed, inv_ref[rows, :], vec_ref[1:2, :])
        add(1, grad * normed)
        add(4, grad)

    staggered(expand_back, inner_norm, len(tiles))
    for tile in range(len(tiles)):
        dz_store(tile)
    sums_ref[...] = jnp.zeros_like(sums_ref)
    for row, values in sums.items():
        sums_ref[row : row + 1, :] = values
    for block, values in enumerate(bias_sums):
        bias_sum_ref[:, parts[block]] = values
    for step in reversed(range(count)):
        for block in range(blocks):
            put_grad(grad_refs, step, place_ref, block, low_ref[...], du_ref, block * width)
            put_shrink(grad_refs, step, place_ref, block, blocks, h_ref[:, parts[block]], df_ref)
        mover.store(grad_refs[step], grad_hbms[step])
    mover.finish()


def branch_grads(branch_rows, mixed_weight, o_ref, da_ref, inner_ref):
    width = o_ref.shape[1]
    tiles = [slice(tile * TILE, (tile + 1) * TILE) for tile in range(o_ref.shape[0] // TILE)]
    head = lax.broadcasted_iota(jnp.int32, (width, PAIR), 0) // HEAD_DIM
    picks = jnp.where(head == lax.broadcasted_iota(jnp.int32, (width, PAIR), 1), 1.0, 0.0).astype(BF)

    def project(tile):
        return dot(branch_rows(tile, tiles[tile]), mixed_weight, 1, 1)

    def reduce(tile, mixed_grad):
        rows = tiles[tile]
        low = mixed_grad.astype(BF)
        da_ref[rows, :] = low
        product = low.astype(F32) * o_ref[rows, :].astype(F32)
        high = product.astype(BF)
        rest = (product - high.astype(F32)).astype(BF)
        inner = dot(high, picks, 1, 0) + dot(rest, picks, 1, 0)
        for pair in range(width // PAIR):
            inner_ref[pair, rows, :] = pltpu.roll(inner, (PAIR - 2 * pair) % PAIR, 1) if pair else inner

    staggered(project, reduce, len(tiles))


def put_grad(grad_refs, step, place_ref, index, left, right_ref, first=0):
    width = left.shape[1]
    if place_ref is None:
        grad = dot(left, right_ref[:, first : first + width], 0, 0)
        grad_refs[0][index * width : (index + 1) * width, :] = grad.astype(BF)
        return
    core, _, _, row = place_of(place_ref)
    half = width // 2
    shard = width // 8
    cols = pl.ds(pl.multiple_of(first + jnp.bitwise_xor(core, step) * half, half), half)
    grad = dot(left, right_ref[:, cols], 0, 0).astype(BF).reshape(4, 2, shard, half)
    for side in (0, 1):
        slot = jnp.bitwise_xor(row, side)
        grad_refs[step][slot, :, index * shard : (index + 1) * shard, :] = grad[:, side]


def put_shrink(grad_refs, step, place_ref, block, blocks, left, right_ref):
    width = left.shape[1]
    if place_ref is None:
        first = (blocks + block) * width
        grad_refs[0][first : first + width, :] = dot(left, right_ref[...], 0, 0).astype(BF)
        return
    core, _, _, row = place_of(place_ref)
    half, shard = width // 2, width * blocks // 8
    base = width // 8 * blocks
    cols = pl.ds(pl.multiple_of(jnp.bitwise_xor(core, step) * half, half), half)
    grad = dot(left, right_ref[:, cols], 0, 0).astype(BF).reshape(width // shard, shard, half)
    for part in range(width // shard):
        owner = block * (width // shard) + part
        grad_refs[step][jnp.bitwise_xor(row, owner % 2), owner // 2, base:, :] = grad[part]


def put_small(grad_refs, place_ref, base, sums, bias_sum):
    core, _, _, row = place_of(place_ref)
    half = grad_refs[0].shape[3]
    inner = bias_sum.shape[1] // 8
    index = lax.broadcasted_iota(jnp.int32, (16, half), 0)
    for owner in range(8):
        block = sums[:, owner // 2 * PAIR : (owner // 2 + 1) * PAIR]
        if owner % 2:
            block = pltpu.roll(block, HEAD_DIM, 1)
        block = jnp.concatenate([block, jnp.zeros((16, half - PAIR), F32)], axis=1)
        block = jnp.where(index == 10, bias_sum[:, owner * inner : (owner + 1) * inner], block)
        high = block.astype(BF)
        low = (block - high.astype(F32)).astype(BF)
        slot = jnp.bitwise_xor(row, owner % 2)
        first = (core == 0).astype(F32)
        for step, grad_ref in enumerate(grad_refs):
            is_high = first if step == 0 else 1.0 - first
            mixed = high.astype(F32) * is_high + low.astype(F32) * (1.0 - is_high)
            grad_ref[slot, owner // 2, base : base + 16, :] = mixed.astype(BF)


def cross_backward_kernel(staged, *refs):
    place_ref, core = None, None
    if staged:
        place_ref, refs = refs[0], refs[1:]
        core = place_of(place_ref)[0]
    vec_ref, refs = refs[0], refs[1:]
    if staged:
        sums_three_ref, bias_sum_ref, refs = refs[0], refs[1], refs[2:]
    packs, refs = refs[: 2 if staged else 5], refs[2 if staged else 5 :]
    p_hbm, dz_hbm, x_hbm, first_hbm, inv_hbm, source_hbm, q_hbm, k_hbm, v_hbm, o_hbm, self_o_hbm = refs[:11]
    sums_ref, dfirst_hbm, dsource_hbm = refs[11:14]
    count = 2 if staged else 1
    grad_hbms, refs = refs[14 : 14 + count], refs[14 + count :]
    grad_refs, refs = refs[:count], refs[count:]
    dz_ref, x_ref, first_ref, inv_ref, source_ref, q_ref, k_ref, v_ref, o_ref, self_o_ref = refs[:10]
    dfirst_ref, dsource_ref, *w_refs = refs[10:17]
    low_ref, da_ref, inner_ref, dq_ref, dk_ref, dv_ref, dk_sum, dv_sum, branch_ref, values_ref, p_ref = refs[17:28]
    mover = Mover(refs[-1])
    length, width = dz_ref.shape

    dz_load, o_load = mover.load_rows(dz_hbm, dz_ref), mover.load_rows(o_hbm, o_ref)
    waits = load_matrices(mover, core, packs, w_refs, (4,))
    sums_ref[...] = jnp.zeros_like(sums_ref)
    waits[0]()
    store = ProbStore(mover, p_hbm, p_ref, False)
    load_probs(store, 0)
    middle = [mover.load(a, b) for a, b in ((v_hbm, v_ref), (q_hbm, q_ref), (k_hbm, k_ref))]

    def branch_rows(tile, rows):
        dz_load(tile)
        o_load(tile)
        branch_ref[rows, :] = dz_ref[rows, :].astype(BF)
        return branch_ref[rows, :]

    branch_grads(branch_rows, whole(w_refs[4]), o_ref, da_ref, inner_ref)
    for step in range(count):
        put_grad(grad_refs, step, place_ref, 4, o_ref[...], branch_ref)
    load_probs(store, 1)
    first_load = mover.load_rows(first_hbm, first_ref)
    waits = load_matrices(mover, core, packs, w_refs, (1, 2, 3))
    last = [
        mover.load(a, b)
        for a, b in ((source_hbm, source_ref), (x_hbm, x_ref), (inv_hbm, inv_ref), (self_o_hbm, self_o_ref))
    ]
    for load in middle:
        load.wait()
    attend_back(q_ref, da_ref, inner_ref, k_ref, v_ref, store, dq_ref, dk_ref, dv_ref, dk_sum, dv_sum, values_ref)
    for load in last:
        load.wait()
    for wait in waits:
        wait()
    for tile in range(length // TILE):
        first_load(tile)

    dsource_store = mover.store_rows(dsource_ref, dsource_hbm)
    dfirst_store = mover.store_rows(dfirst_ref, dfirst_hbm)
    tiles = [slice(tile * TILE, (tile + 1) * TILE) for tile in range(length // TILE)]
    key_tiles = [slice(tile * TILE, (tile + 1) * TILE) for tile in range(source_ref.shape[0] // TILE)]
    sums = {row: 0.0 for row in (0, 3, 6, 7)}

    def add(row, values):
        sums[row] = sums[row] + jnp.sum(values, axis=0, keepdims=True)

    def source_grad(tile):
        rows = key_tiles[tile]
        dsource_ref[rows, :] = dot(dk_ref[rows, :], whole(w_refs[2]), 1, 1) + dot(
            dv_ref[rows, :], whole(w_refs[3]), 1, 1
        )

    def put_keys(step):
        put_grad(grad_refs, step, place_ref, 2, source_ref[...], dk_ref)
        put_grad(grad_refs, step, place_ref, 3, source_ref[...], dv_ref)

    products = [functools.partial(source_grad, tile) for tile in range(len(key_tiles))]
    products += [functools.partial(put_keys, step) for step in range(count)]

    def query_back(tile):
        product = dot(dq_ref[tiles[tile], :], whole(w_refs[1]), 1, 1)
        for run in products[tile :: len(tiles)]:
            run()
        return product

    def first_norm(tile, product):
        rows = tiles[tile]
        grad = dz_ref[rows, :]
        dx = product + vec_ref[7:8, :] * grad
        normed = first_ref[rows, :]
        first_out = normed * vec_ref[0:1, :] + vec_ref[3:4, :]
        low_ref[rows, :] = first_out.astype(BF)
        add(7, first_out * grad)
        dfirst = norm_back(dx, normed, inv_ref[rows, :], vec_ref[0:1, :])
        dfirst_ref[rows, :] = dfirst
        add(0, dx * normed)
        add(3, dx)
        add(6, x_ref[rows, :].astype(F32) * dfirst)
        branch_ref[rows, :] = dfirst.astype(BF)

    staggered(query_back, first_norm, len(tiles))
    for tile in range(len(key_tiles)):
        dsource_store(tile)
    for tile in range(len(tiles)):
        dfirst_store(tile)
    for row, values in sums.items():
        sums_ref[row : row + 1, :] = values

    if staged:
        put_small(grad_refs, place_ref, 5 * (width // 8), sums_ref[...] + sums_three_ref[...], bias_sum_ref[...])
    for step in reversed(range(count)):
        put_grad(grad_refs, step, place_ref, 1, low_ref[...], dq_ref)
        put_grad(grad_refs, step, place_ref, 0, self_o_ref[...], branch_ref)
        mover.store(grad_refs[step], grad_hbms[step])
    mover.finish()


def self_backward_kernel(staged, *refs):
    place_ref, core = None, None
    if staged:
        place_ref, refs = refs[0], refs[1:]
        core = place_of(place_ref)[0]
    count = 2 if staged else 1
    packs, refs = refs[:count], refs[count:]
    p_hbm, dz_hbm, x_hbm, q_hbm, k_hbm, v_hbm, o_hbm, *head_hbms = refs[:10]
    grad_hbms, refs = refs[10 : 10 + count], refs[10 + count :]
    grad_refs, refs = refs[:count], refs[count:]
    dz_ref, x_ref, q_ref, k_ref, v_ref, o_ref, w_ref = refs[:7]
    da_ref, inner_ref, dq_ref, dk_ref, dv_ref, dk_sum, dv_sum, values_ref, p_ref = refs[7:16]
    mover = Mover(refs[-1])
    length, width = dz_ref.shape

    dz_load = mover.load_rows(dz_hbm, dz_ref)
    waits = load_matrices(mover, core, packs, (w_ref,))
    o_load = mover.load_rows(o_hbm, o_ref)
    waits[0]()
    store = ProbStore(mover, p_hbm, p_ref, True)
    load_probs(store, 0)
    middle = [mover.load(a, b) for a, b in ((v_hbm, v_ref), (q_hbm, q_ref), (k_hbm, k_ref))]

    def branch_rows(tile, rows):
        dz_load(tile)
        o_load(tile)
        return dz_ref[rows, :].astype(BF)

    branch_grads(branch_rows, whole(w_ref), o_ref, da_ref, inner_ref)
    load_probs(store, 1)
    x_load = mover.load(x_hbm, x_ref)
    for load in middle:
        load.wait()
    attend_back(q_ref, da_ref, inner_ref, k_ref, v_ref, store, dq_ref, dk_ref, dv_ref, dk_sum, dv_sum, values_ref)
    for near, far in zip((dq_ref, dk_ref, dv_ref), head_hbms):
        mover.store(near, far)
    x_load.wait()
    for step in reversed(range(count)):
        for index, grads in enumerate((dq_ref, dk_ref, dv_ref)):
            put_grad(grad_refs, step, place_ref, index, x_ref[...], grads)
        mover.store(grad_refs[step], grad_hbms[step])
    mover.finish()


def input_grad_kernel(vec_ref, dz_hbm, all_hbm, dq_hbm, dk_hbm, dv_hbm, dx_hbm, *refs):
    dz_ref, all_ref, dq_ref, dk_ref, dv_ref, dx_ref, sems = refs
    mover = Mover(sems)
    width = dz_ref.shape[1]
    all_load = mover.load(all_hbm, all_ref)
    heads = (dq_ref, dk_ref, dv_ref)
    loads = [mover.load_rows(a, b) for a, b in zip((dq_hbm, dk_hbm, dv_hbm), heads)]
    loads.append(mover.load_rows(dz_hbm, dz_ref))
    dx_store = mover.store_rows(dx_ref, dx_hbm)
    all_load.wait()

    @pl.loop(0, dz_ref.shape[0] // TILE)
    def _(tile):
        rows = rows_at(tile)
        for load in loads:
            load(tile)
        dx = vec_ref[6:7, :] * dz_ref[rows, :]
        for index, grads in enumerate(heads):
            dx = dx + dot(grads[rows, :], all_ref[index * width : (index + 1) * width, :], 1, 1)
        dx_ref[rows, :] = dx
        dx_store(tile)

    mover.finish()


def call(kernel, args, outs, scratch, limit, flops, smem=(), near=(), near_outs=(), copies=0):
    spaces = [pltpu.SMEM if i in smem else pltpu.VMEM if i in near else pl.ANY for i in range(len(args))]
    out_spaces = [pltpu.VMEM if i in near_outs else pl.ANY for i in range(len(outs))]
    buffers = [pltpu.VMEM(shape, kind) for shape, kind in scratch]
    if copies:
        buffers.append(pltpu.SemaphoreType.DMA((copies,)))
    return pl.pallas_call(
        kernel,
        out_shape=[jax.ShapeDtypeStruct(shape, kind) for shape, kind in outs],
        in_specs=[pl.BlockSpec(memory_space=space) for space in spaces],
        out_specs=[pl.BlockSpec(memory_space=space) for space in out_spaces],
        scratch_shapes=buffers,
        compiler_params=pltpu.CompilerParams(vmem_limit_bytes=(63 if copies else limit) * MIB),
        cost_estimate=pl.CostEstimate(flops=flops, bytes_accessed=16 * MIB, transcendentals=0),
    )(*args)


def like(*arrays):
    return [(a.shape, a.dtype) for a in arrays]


def prob_shape(queries, keys, width):
    return (width // PAIR, 2, queries, keys), BF


def forward_self(place, x, pos, pack, staged):
    length, width = x.shape
    low = ((length, width), BF)
    outs = [prob_shape(length, length, width), low, low, low, low]
    matrices = ((3 * width, width), BF)
    scratch = [low, matrices, low, low, low, low, ((2, 2, length, length), BF), ((length, 1), jnp.int32)]
    if staged:
        return call(
            functools.partial(self_forward_kernel, True),
            (place, pos, x, *pack),
            [*outs, matrices],
            [*scratch, *like(*pack)],
            40, 10**10, smem=(0,), near=(1,), copies=24,
        )
    results = call(
        functools.partial(self_forward_kernel, False),
        (pos, x, pack), outs, scratch, 40, 10**10, near=(0,), copies=24,
    )
    return (*results, pack)


def matrix_buffers(shards, width):
    return [((8 if rows < width else 1, rows, width), BF) for rows in shards]


def forward_cross(place, x, mixed, source, count, packs, given, shards):
    length, width = x.shape
    keys = source.shape[0]
    low, full, column, key_low = ((length, width), BF), ((length, width), F32), ((length, 1), F32), ((keys, width), BF)
    outs = [full, column, prob_shape(length, keys, width), low, key_low, key_low, low, full, column]
    near = [full, column, low, key_low, key_low, low, full, column]
    scratch = [low, low, key_low, *near, ((2, 2, length, keys), BF), ((keys, PAIR), BF)]
    if place is not None:
        return call(
            functools.partial(cross_forward_kernel, True),
            (place, count, x, mixed, source, *packs),
            [*outs, ((16, width), F32), ((1, 4 * width), F32)],
            [*scratch, *matrix_buffers(shards, width), ((2, 8, 16, width // 2), BF)],
            44, 10**10, smem=(0, 1), near_outs=(9, 10), copies=64,
        )
    vec, bias = given
    results = call(
        functools.partial(cross_forward_kernel, False),
        (count, vec, x, mixed, source, *packs),
        outs, [*scratch, *like(*packs)],
        44, 10**10, smem=(0,), near=(1,), copies=64,
    )
    return (*results, vec, bias)


def grad_outs(rows, width, staged):
    return [((2, 4, rows, width // 2), BF)] * 2 if staged else [((rows, width), BF)]


def hidden_step(place, packs, normed, inverse, cot, vec, bias):
    length, width = normed.shape
    inner = bias.shape[1]
    blocks = inner // width
    staged = place is not None
    low, full = ((length, width), BF), ((length, width), F32)
    grads = grad_outs(2 * inner // 8 if staged else 2 * inner, width, staged)
    args = (vec, bias, *packs, normed, inverse, cot)
    matrices = like(*packs)
    if staged:
        rows = width // 8
        matrices = [((blocks, 8, rows, width), BF), ((8, 2, blocks, rows // 2, width), BF)]
    return call(
        functools.partial(hidden_kernel, staged),
        (place, *args) if staged else args,
        [((16, width), F32), ((1, inner), F32), low, full, *grads],
        [*grads, *like(normed, inverse, cot), low, full, low, ((length, inner), BF), ((length, inner), BF), low,
         ((length, inner), F32), full, *matrices],
        44, 2 * 10**10, smem=(0,) if staged else (), near=(1, 2) if staged else (0, 1), near_outs=(0, 1),
        copies=96,
    )


def backward_cross(place, packs, dz, x, normed, inverse, source, vec, saved, mixed, small, shards):
    length, width = dz.shape
    keys = source.shape[0]
    staged = place is not None
    probs, *saved = saved
    arrays = (dz, x, normed, inverse, source, *saved, mixed)
    low, key_low, sums = ((length, width), BF), ((keys, width), BF), ((2, PAIR, keys), F32)
    grads = grad_outs(5 * width // 8 + 16 if staged else 5 * width, width, staged)
    full, key_full = ((length, width), F32), ((keys, width), F32)
    return call(
        functools.partial(cross_backward_kernel, staged),
        (place, vec, *small, *packs, probs, *arrays) if staged else (vec, *packs, probs, *arrays),
        [((16, width), F32), full, key_full, *grads],
        [*grads, *like(*arrays), full, key_full, *(matrix_buffers(shards, width) if staged else like(*packs)),
         low, low, ((width // PAIR, length, PAIR), F32), low, key_low, key_low, sums, sums, low, ((2, keys, PAIR), BF),
         ((2, 2, length, keys), BF)],
        48, 2 * 10**10, smem=(0,) if staged else (), near=(1, 2, 3) if staged else (0,), near_outs=(0,), copies=72,
    )


def backward_self(place, packs, dz, x, saved, shards):
    length, width = dz.shape
    staged = place is not None
    probs, *saved = saved
    arrays = (dz, x, *saved)
    low, sums = ((length, width), BF), ((2, PAIR, length), F32)
    grads = grad_outs(3 * width // 8 if staged else 3 * width, width, staged)
    first = matrix_buffers(shards[:1], width) if staged else like(*packs)
    return call(
        functools.partial(self_backward_kernel, staged),
        (place, *packs, probs, *arrays) if staged else (*packs, probs, *arrays),
        [low, low, low, *grads],
        [*grads, *like(*arrays), *first, low, ((width // PAIR, length, PAIR), F32), low, low, low, sums, sums,
         ((2, length, PAIR), BF), ((2, 2, length, length), BF)],
        48, 2 * 10**10, smem=(0,) if staged else (), copies=64,
    )


def input_gradient(vec, dz, matrices, heads):
    arrays = (dz, matrices, *heads)
    return call(
        input_grad_kernel, (vec, *arrays), like(dz), [*like(*arrays), *like(dz)], 40, 2 * 10**9, near=(0,), copies=24
    )[0]


def adam_step(settings_ref, now, grad, one, two, decay):
    beta_one, beta_two = settings_ref[1], settings_ref[2]
    first = beta_one * one + (1.0 - beta_one) * grad
    second = beta_two * two + (1.0 - beta_two) * grad * grad
    change = (first / settings_ref[4]) / (jnp.sqrt(second / settings_ref[5]) + 1e-08)
    if decay:
        change = change + settings_ref[3] * now
    return now - settings_ref[0] * change, first, second


def store_step(refs, where, results):
    for ref, value in zip(refs, results):
        ref[where] = value


def hidden_adam_kernel(place_ref, settings_ref, *refs):
    core = place_of(place_ref)[0]
    hbms, new_hbms, refs = refs[:8], refs[8:14], refs[14:]
    mine_ref, other_ref, *params = refs[:8]
    news, mover = refs[8:14], Mover(refs[-1])
    loads = [mover.load(a, b) for a, b in zip(hbms, refs[:8])]
    expand, shrink = params[0:3], params[3:6]
    half = mine_ref.shape[1]
    shard = expand[0].shape[0]
    blocks = expand[0].shape[1] // (2 * half)
    for load in loads[:5]:
        load.wait()
    sides = [(jnp.bitwise_xor(core, step) * half, ref) for step, ref in ((0, mine_ref), (1, other_ref))]
    for side, ref in sides:
        for block in range(blocks):
            where = (slice(None), pl.ds(pl.multiple_of(block * 2 * half + side, half), half))
            grad = ref[block * shard : (block + 1) * shard, :]
            now, one, two = (r[where] for r in expand)
            store_step(news[:3], where, adam_step(settings_ref, now, grad, one, two, True))
    for load in loads[5:]:
        load.wait()
    for near, far in zip(news[:3], new_hbms[:3]):
        mover.store(near, far)
    for side, ref in sides:
        where = (slice(None), pl.ds(pl.multiple_of(side, half), half))
        now, one, two = (r[where] for r in shrink)
        store_step(news[3:], where, adam_step(settings_ref, now, ref[blocks * shard :, :], one, two, True))
    for near, far in zip(news[3:], new_hbms[3:]):
        mover.store(near, far)
    mover.finish()


def attention_adam_kernel(place_ref, settings_ref, mine_ref, other_ref, *refs):
    core = place_of(place_ref)[0]
    matrices, bias, vectors = refs[0:3], refs[3:6], refs[6:9]
    new_matrices, new_bias, new_vectors = refs[9:12], refs[12:15], refs[15:18]
    half = mine_ref.shape[1]
    shard = matrices[0].shape[1]
    for step, ref in ((0, mine_ref), (1, other_ref)):
        cols = pl.ds(pl.multiple_of(jnp.bitwise_xor(core, step) * half, half), half)
        for index in range(8):
            where = (index, slice(None), cols)
            now, one, two = (r[where] for r in matrices)
            grad = ref[index * shard : (index + 1) * shard, :]
            store_step(new_matrices, where, adam_step(settings_ref, now, grad, one, two, True))
    small = mine_ref[8 * shard :, :] + other_ref[8 * shard :, :]
    for group, new, grad in (
        (bias, new_bias, small[10:11, : bias[0].shape[1]]),
        (vectors, new_vectors, small[:10, : vectors[0].shape[1]]),
    ):
        now, one, two = (r[...] for r in group)
        store_step(new, ..., adam_step(settings_ref, now, grad, one, two, False))


def hidden_adam(scalars, grads, params):
    return call(
        hidden_adam_kernel, (*scalars, *grads, *params), like(*params), [*like(*grads), *like(*params), *like(*params)],
        40, 10**9, smem=(0, 1), copies=16,
    )


def adam_call(kernel, scalars, grads, params):
    return call(
        kernel, (*scalars, *grads, *params), [(p.shape, F32) for p in params], [], 32, 10**7, smem=(0, 1),
        near=range(2, 2 + len(grads) + len(params)), near_outs=range(len(params)),
    )


CORE_SWAP = [(0, 1), (1, 0), (2, 3), (3, 2)]
CHIP_SWAP = [(0, 2), (2, 0), (1, 3), (3, 1)]
ROW_SWAP = [(i, i ^ 1) for i in range(8)]


LINES = [[0, 2, 4, 6], [1, 3, 5, 7]]


def line_shift(step):
    return [(2 * z + y, 2 * ((z + step) % 4) + y) for z in range(4) for y in (0, 1)]


def small_mesh(mesh):
    return mesh.shape["rep"] == 4 and mesh.shape["fsdp"] == 8


class StagedGather:
    def rows(self, mine, done):
        self.mine = mine
        self.other = lax.ppermute(after(mine, done), "fsdp", ROW_SWAP)

    def line(self, done):
        self.pair = after(jnp.stack([self.mine, self.other]), done)
        self.received = [lax.ppermute(self.pair, "fsdp", line_shift(step)) for step in (1, 2, 3)]

    def chips(self, done):
        self.part = jnp.stack([self.pair, *(after(received, done) for received in self.received)])
        self.far = lax.ppermute(self.part, "rep", CHIP_SWAP)

    def cores(self, done):
        far = after(self.far, done)
        part = after(self.part, done)
        return part, far, lax.ppermute(part, "rep", CORE_SWAP), lax.ppermute(far, "rep", CORE_SWAP)


def gather_staged(pack):
    quarter = pack.shape[0] // 4
    mine = lax.dynamic_slice_in_dim(pack, lax.axis_index("rep") * quarter, quarter, 0)
    pair = jnp.stack([mine, lax.ppermute(mine, "fsdp", ROW_SWAP)])
    part = jnp.stack([pair] + [lax.ppermute(pair, "fsdp", line_shift(step)) for step in (1, 2, 3)])
    both = jnp.stack([part, lax.ppermute(part, "rep", CHIP_SWAP)])
    return pair, part, both


def after(value, *done):
    return lax.optimization_barrier((value, *done))[0]


def gather_half(pack):
    half = pack.shape[1] // 2
    mine = lax.dynamic_slice_in_dim(pack, lax.axis_index("rep") % 2 * half, half, 1)
    return lax.all_gather(mine, "fsdp", axis=0)


def both_halves(mine, done):
    mine = after(mine, done)
    return mine, lax.ppermute(mine, "rep", CORE_SWAP)


def reduce_cores(keep, send):
    received = lax.ppermute(send, "rep", CORE_SWAP)
    return (keep[0], received[0]), keep[1] + received[1]


def send_rows(send):
    return lax.ppermute(send, "fsdp", ROW_SWAP)


def reduce_rows(keep, received, done):
    mine, other = (part.astype(F32) for part in keep)
    return (mine + other + after(received, done).astype(F32)).astype(BF)


def reduce_last(part, *done):
    total = part.astype(F32) + after(lax.ppermute(part, "rep", CHIP_SWAP), *done).astype(F32)
    return total, lax.ppermute(total, "rep", CORE_SWAP)


def reduce_line(joined):
    part = lax.psum_scatter(joined, "fsdp", scatter_dimension=0, axis_index_groups=LINES)
    return part.reshape(joined.shape[1:])


def reduce_shifts(joined, done):
    line = lax.axis_index("fsdp") // 2
    total = lax.dynamic_index_in_dim(joined, line, 0, False).astype(F32)
    for step in (1, 2, 3):
        away = lax.dynamic_index_in_dim(joined, (line + step) % 4, 0, False)
        total = total + after(lax.ppermute(away, "fsdp", line_shift(step)), done).astype(F32)
    return total.astype(BF)


def reduce_plain(grads):
    return lax.psum(lax.psum_scatter(grads, "fsdp", scatter_dimension=0), "rep").astype(F32)


def adam_update(weight_now, gradient, moment_one, moment_two, settings, step_float, factor):
    learn_rate, beta_one, beta_two, decay_rate = settings[0], settings[1], settings[2], settings[3]
    first_new = beta_one * moment_one + (1.0 - beta_one) * gradient
    second_new = beta_two * moment_two + (1.0 - beta_two) * gradient * gradient
    first_hat = first_new / (1.0 - beta_one**step_float)
    second_hat = second_new / (1.0 - beta_two**step_float)
    change = first_hat / (jnp.sqrt(second_hat) + 1e-08) + factor * decay_rate * weight_now
    return (weight_now - learn_rate * change, first_new, second_new)


def per_device(
    small, inputs, memory, memory_length, target_pos, cotangent,
    attention_weights, expand_weights, shrink_weights, expand_bias, layer_vectors,
    first_attention, first_expand, first_shrink, first_bias, first_vectors,
    second_attention, second_expand, second_shrink, second_bias, second_vectors,
    hyper_rates, step_count,
):
    length, width = inputs.shape[1:]
    shard = attention_weights.shape[1]
    count = width // shard
    inner_shard = shrink_weights.shape[0]
    blocks = inner_shard // shard
    low_attention = attention_weights.astype(BF).reshape(8 * shard, width)
    pack_one = low_attention[: 3 * shard]
    expand_low = expand_weights.astype(BF).reshape(shard, blocks, width)
    shrink_low = shrink_weights.astype(BF)
    x, source, cot = inputs[0], memory[0], cotangent[0]
    step_float = step_count.astype(F32)

    if small:
        place = jnp.stack([lax.axis_index("rep"), lax.axis_index("fsdp")]).astype(jnp.int32)
        small_rows = jnp.concatenate(
            [
                jnp.pad(layer_vectors, ((0, 0), (0, inner_shard - shard))),
                expand_bias[None],
                jnp.zeros((5, inner_shard), F32),
            ]
        )
        small_rows = jnp.pad(small_rows, ((0, 0), (0, width - inner_shard))).astype(BF)
        pack_two = jnp.concatenate([low_attention[3 * shard :], small_rows])
        two = gather_half(pack_two)
        pair_one, part_one, one = gather_staged(pack_one)
        half = shard // 2
        halves = expand_low.reshape(2, half, blocks, width).transpose(0, 2, 1, 3)
        quarters = jnp.stack([halves, shrink_low.reshape(2, blocks, half, width)], axis=1)
        core, chip = place[0] % 2, place[0] // 2
        quarter = lax.dynamic_slice(
            quarters, (chip, 0, 0, 0, core * (width // 2)), (1, *quarters.shape[1:4], width // 2)
        )
        three = StagedGather()
        three.rows(quarter[0], pair_one)
        one = both_halves(one, three.other)
        three.line(part_one)
        given = None
        cross_shards = (shard,) * 5
    else:
        place, cross_shards = None, None
        flat = jnp.concatenate([layer_vectors.reshape(-1), expand_bias]).astype(BF)
        flat = lax.all_gather(flat, "fsdp", axis=0).astype(F32)
        vector_size = layer_vectors.size
        vec = flat[:, :vector_size].reshape(count, -1, shard).transpose(1, 0, 2).reshape(-1, width)
        given = jnp.pad(vec, ((0, 16 - vec.shape[0]), (0, 0))), flat[:, vector_size:].reshape(1, -1)

        def gather_all(pack, shards):
            full = lax.all_gather(pack, "fsdp", axis=0)
            pieces, first = [], 0
            for rows in shards:
                pieces.append(full[:, first : first + rows].reshape(-1, width))
                first += rows
            return pieces

        def owners(grads, shards):
            pieces, first = [], 0
            for rows in shards:
                pieces.append(grads[first : first + rows * count].reshape(count, rows, width))
                first += rows * count
            return jnp.concatenate(pieces, axis=1)

        one = jnp.concatenate(gather_all(pack_one, (shard,) * 3))
        two = [m[None] for m in gather_all(low_attention[3 * shard :], (shard,) * 5)]
        pack = jnp.concatenate([expand_low.transpose(1, 0, 2).reshape(-1, width), shrink_low])
        *expand_all, shrink_all = gather_all(pack, (*(shard,) * blocks, inner_shard))
        three = jnp.stack(expand_all)[:, None], shrink_all[None]

    *saved_one, matrices = forward_self(place, x, target_pos, one, small)
    if small:
        three.chips(saved_one[4])
        two = both_halves(two, three.part)
    norm_one, inv_one, *saved_two, norm_two, inv_two, vec, bias = forward_cross(
        place, x, saved_one[4], source, memory_length, two, given, cross_shards
    )
    three = three.cores(norm_two) if small else three
    sums_three, bias_sum, outputs, dz_two, *grad_three = hidden_step(
        place, three, norm_two, inv_two, cot, vec, bias
    )
    if small:
        keep_three, send_three = reduce_cores(*grad_three)
        dz_two = after(dz_two, send_three)
        received_three = send_rows(send_three)
    sums_two, dz_one, memory_grad, *grad_two = backward_cross(
        place, two, dz_two, x, norm_one, inv_one, source, vec, saved_two, saved_one[4],
        (sums_three, bias_sum), cross_shards,
    )
    if small:
        joined_three = reduce_rows(keep_three, received_three, dz_one)
        keep_two, send_two = reduce_cores(grad_two[0], after(grad_two[1], joined_three))
        dz_one = after(dz_one, joined_three, send_two)
        received_two = send_rows(send_two)
    *heads, grad_keep, grad_send = (
        *backward_self(place, two if small else two[:1], dz_one, x, saved_one, cross_shards),
        *((None,) if not small else ()),
    )
    if small:
        joined_two = reduce_rows(keep_two, received_two, heads[0])
        keep_one, send_one = reduce_cores(grad_keep, after(grad_send, joined_two))
        heads = after(tuple(heads), send_one)
        received_one = send_rows(send_one)
    input_grad = input_gradient(vec, dz_one, matrices, heads)

    attention = (attention_weights, first_attention, second_attention)
    expand = (expand_weights, first_expand, second_expand)
    shrink = (shrink_weights, first_shrink, second_shrink)
    bias = (expand_bias, first_bias, second_bias)
    vectors = (layer_vectors, first_vectors, second_vectors)
    if small:
        powers = 1.0 - hyper_rates[1:3] ** step_float
        scalars = place, jnp.concatenate([hyper_rates, powers])
        part_three = reduce_line(joined_three)
        part_two = reduce_line(joined_two)
        total_three = reduce_last(after(part_three, heads[0]), input_grad)
        joined_one = reduce_rows(keep_one, received_one, input_grad)
        hidden_new = hidden_adam(scalars, total_three, (*expand, *shrink))
        part_one = reduce_shifts(joined_one, hidden_new[0])
        total_rest = reduce_last(jnp.concatenate([part_one, after(part_two, part_one)]))
        rows = tuple(b[None] for b in bias)
        other_new = adam_call(
            attention_adam_kernel, scalars, total_rest, (*attention, *rows, *vectors)
        )
        new_bias = tuple(b[0] for b in other_new[3:6])
        updated = (*other_new[:3], *hidden_new, *new_bias, *other_new[6:])
    else:
        sums = (sums_two + sums_three)[: layer_vectors.shape[0]]
        flat = jnp.concatenate(
            [
                sums.reshape(-1, count, shard).transpose(1, 0, 2).reshape(count, -1),
                bias_sum.reshape(count, inner_shard),
            ],
            axis=1,
        )
        total_three = reduce_plain(owners(grad_three[0], (*(shard,) * blocks, inner_shard)))
        total_two = reduce_plain(owners(grad_two[0], (shard,) * 5))
        total_one = reduce_plain(owners(grad_keep, (shard,) * 3))
        flat = lax.psum(lax.psum_scatter(flat, "fsdp", scatter_dimension=0), "rep")
        grad_attention = jnp.concatenate([total_one, total_two]).reshape(attention_weights.shape)
        grad_expand = total_three[: blocks * shard].reshape(blocks, shard, width).transpose(1, 0, 2)
        updated = []
        for (now, one_now, two_now), grad, factor in (
            (attention, grad_attention, 1.0),
            (expand, grad_expand.reshape(shard, -1), 1.0),
            (shrink, total_three[blocks * shard :], 1.0),
            (bias, flat[layer_vectors.size :], 0.0),
            (vectors, flat[: layer_vectors.size].reshape(-1, shard), 0.0),
        ):
            updated.extend(adam_update(now, grad, one_now, two_now, hyper_rates, step_float, factor))
    return (outputs[None], input_grad[None], memory_grad[None], *updated)


def solution(mesh):
    rows = ("rep", "fsdp")
    params = (P(None, "fsdp", None), P("fsdp", None), P("fsdp", None), P("fsdp"), P(None, "fsdp"))
    return jax.shard_map(
        functools.partial(per_device, small_mesh(mesh)),
        mesh=mesh,
        in_specs=(
            P(rows, None, None), P(rows, None, None), P(rows), P(rows, None), P(rows, None, None),
            *params, *params, *params, P(), P(),
        ),
        out_specs=(
            P(rows, None, None), P(rows, None, None), P(rows, None, None),
            *(spec for spec in params for _ in range(3)),
        ),
        check_vma=False,
    )
```

```python
import functools

import jax
import jax.numpy as jnp
from jax import lax
from jax.experimental import pallas as pl
from jax.experimental.pallas import tpu as pltpu
from jax.sharding import PartitionSpec as P

BF = jnp.bfloat16
F32 = jnp.float32
HEAD_DIM = 64
PAIR = 128
TILE = 256
MIB = 1 << 20


def dot(left, right, left_dim, right_dim):
    return lax.dot_general(
        left, right, (((left_dim,), (right_dim,)), ((), ())), preferred_element_type=F32
    )


def lanes(size):
    return lax.broadcasted_iota(jnp.int32, (1, size), 1)


def half_masks():
    first = jnp.where(lanes(PAIR) < HEAD_DIM, 1.0, 0.0)
    return first.astype(BF), (1.0 - first).astype(BF)


def rows_at(index, size=TILE):
    return pl.ds(pl.multiple_of(index * size, size), size)


class Mover:
    def __init__(self, sems):
        self.sems, self.used, self.leaving = sems, 0, []

    def take(self, count=1):
        self.used += count
        return self.used - count

    def load(self, source, target):
        copy = pltpu.make_async_copy(source, target, self.sems.at[self.take()])
        copy.start()
        return copy

    def load_rows(self, source, target):
        count = source.shape[0] // TILE
        first = self.take(count)

        def copy(tile):
            rows = rows_at(tile)
            return pltpu.make_async_copy(source.at[rows], target.at[rows], self.sems.at[first + tile])

        for tile in range(count):
            copy(tile).start()
        return lambda tile: copy(tile).wait()

    def store(self, source, target):
        self.leaving.append(self.load(source, target))

    def store_parts(self, source, target, count, where):
        first = self.take(count)

        def copy(part):
            return pltpu.make_async_copy(source.at[where(part)], target.at[where(part)], self.sems.at[first + part])

        self.leaving.extend(copy(part) for part in range(count))
        return lambda part: copy(part).start()

    def store_rows(self, source, target):
        return self.store_parts(source, target, source.shape[0] // TILE, rows_at)

    def finish(self):
        for copy in self.leaving:
            copy.wait()


def columns_at(size):
    return lambda part: (slice(None), rows_at(part, size))


def load_matrices(mover, core, sources, targets, which=None):
    waits, first = [], 0
    for index, target in enumerate(targets):
        if which is not None and index not in which:
            first += target.shape[1]
            continue
        if core is None:
            copies = [mover.load(sources[index], target)]
        else:
            rows, half = target.shape[1], target.shape[2] // 2
            copies = []
            for step, source in enumerate(sources):
                cols = pl.ds(pl.multiple_of(jnp.bitwise_xor(core, step) * half, half), half)
                copies.append(mover.load(source.at[:, first : first + rows, :], target.at[:, :, cols]))
            first += rows
        waits.append(lambda copies=copies: [copy.wait() for copy in copies])
    return waits


def load_quarters(mover, place_ref, packs, expand_ref, shrink_ref):
    core, chip, line, row = place_of(place_ref)
    half, cut = expand_ref.shape[3] // 2, expand_ref.shape[2] // 2
    loads = ([], [])
    for index, pack in enumerate(packs):
        core_step, chip_step = divmod(index, 2)
        cols = pl.ds(pl.multiple_of(jnp.bitwise_xor(core, core_step) * half, half), half)
        side = jnp.bitwise_xor(chip, chip_step)
        rows = pl.ds(pl.multiple_of(side * cut, cut), cut)
        for line_step in range(4):
            for row_step in (0, 1):
                owner = lax.rem(line - line_step + 4, 4) * 2 + jnp.bitwise_xor(row, row_step)
                source = pack.at[line_step, row_step]
                loads[0].append((source.at[0], expand_ref.at[:, owner, rows, cols]))
                loads[1].append((source.at[1], shrink_ref.at[owner, side, :, :, cols]))
    return [[mover.load(*pair) for pair in pairs] for pairs in loads]


def whole(ref):
    return ref[...].reshape(-1, ref.shape[-1])


def key_extra(length_limit, count):
    lane = lanes(PAIR) % HEAD_DIM
    extra = jnp.where(lane < 3, 1.0, 0.0)
    if length_limit is None:
        return jnp.broadcast_to(extra, (count, PAIR)).astype(BF)
    row = lax.broadcasted_iota(jnp.int32, (count, PAIR), 0)
    bias = jnp.where(row < length_limit, 0.0, -1e30)
    return jnp.where(lane == 3, bias, extra).astype(BF)


def put_start(pos_ref, start_ref):
    length = start_ref.shape[0]
    query = lax.broadcasted_iota(jnp.int32, (8, length), 1)
    first = (query - pos_ref[...]).astype(F32)
    start_ref[...] = first.T[:, :1].astype(jnp.int32)


def visible(start, first_query, first_key, count):
    key = first_key + lax.broadcasted_iota(jnp.int32, (TILE, count), 1)
    seen = key >= start
    if first_key == first_query:
        query = first_query + lax.broadcasted_iota(jnp.int32, (TILE, count), 0)
        seen = seen & (key <= query)
    return seen


def key_spans(tile, count, causal):
    if not causal:
        return [(0, count)]
    spans = [(0, tile * TILE)] if tile else []
    return spans + [(tile * TILE, TILE)]


def staggered(first, then, count):
    ready = first(0)
    for index in range(count):
        following = first(index + 1) if index + 1 < count else None
        then(index, ready)
        ready = following


class ProbStore:
    def __init__(self, mover, hbm, ref, causal):
        self.hbm, self.ref, self.mover = hbm, ref, mover
        self.tiles = ref.shape[2] // TILE
        self.causal = causal
        self.first = mover.take(2 * self.tiles)

    def views(self, pair, slot, tile):
        rows = slice(tile * TILE, (tile + 1) * TILE)
        keys = slice(0, (tile + 1) * TILE) if self.causal else slice(0, self.ref.shape[3])
        sem = self.mover.sems.at[self.first + slot * self.tiles + tile]
        return self.hbm.at[pair, :, rows, keys], self.ref.at[slot, :, rows, keys], sem

    def copy(self, pair, slot, tile, out):
        far, near, sem = self.views(pair, slot, tile)
        return pltpu.make_async_copy(near, far, sem) if out else pltpu.make_async_copy(far, near, sem)


def two_pairs(pairs, body):
    @pl.loop(0, pairs // 2)
    def _(step):
        for slot in (0, 1):
            body(2 * step + slot, slot, step)


def attend(q_ref, k_ref, v_ref, extra_ref, start_ref, o_ref, store, finished):
    length, count = q_ref.shape[0], k_ref.shape[0]
    causal = start_ref is not None
    masks = half_masks()
    pairs = q_ref.shape[1] // PAIR

    def one_pair(pair, slot, step):
        cols = rows_at(pair, PAIR)

        @pl.when(step > 0)
        def _():
            for tile in range(store.tiles):
                store.copy(pair - 2, slot, tile, True).wait()

        steps = [(tile, side) for tile in range(length // TILE) for side in (0, 1)]
        results = {}

        def scores_of(index):
            tile, side = steps[index]
            rows = slice(tile * TILE, (tile + 1) * TILE)
            queries = q_ref[rows, cols] * masks[side]
            if not causal:
                base = HEAD_DIM * (1 - side)
                queries = jnp.where(lanes(PAIR) == base + 3, 1.0, queries.astype(F32)).astype(BF)
            blocks = []
            for first, size in key_spans(tile, count, causal):
                keys = k_ref[first : first + size, cols]
                if not causal:
                    keys = keys * masks[side] + extra_ref[first : first + size, :] * masks[1 - side]
                scores = dot(queries, keys, 1, 1)
                if causal:
                    seen = visible(start_ref[rows, :], tile * TILE, first, size)
                    scores = jnp.where(seen, scores, -1000000000.0)
                blocks.append(scores)
            return blocks

        def mix(index, score_blocks):
            tile, side = steps[index]
            rows = slice(tile * TILE, (tile + 1) * TILE)
            spans = key_spans(tile, count, causal)
            top = functools.reduce(
                jnp.maximum, [jnp.max(scores, axis=1, keepdims=True) for scores in score_blocks]
            )
            exponents = [jnp.exp(scores - top) for scores in score_blocks]
            inverse = 1.0 / sum(jnp.sum(exponent, axis=1, keepdims=True) for exponent in exponents)
            total = None
            for exponent, (first, size) in zip(exponents, spans):
                probs = (exponent * inverse).astype(BF)
                store.ref[slot, side, rows, first : first + size] = probs
                part = dot(probs, v_ref[first : first + size, cols], 1, 0)
                total = part if total is None else total + part
            results[side] = total
            if side == 1:
                o_ref[rows, cols] = jnp.where(lanes(PAIR) < HEAD_DIM, results[0], results[1]).astype(BF)

        staggered(scores_of, mix, len(steps))
        for tile in range(store.tiles):
            store.copy(pair, slot, tile, True).start()
        for start_store in finished:
            start_store(pair)

    two_pairs(pairs, one_pair)
    for slot in (0, 1):
        for tile in range(store.tiles):
            store.mover.leaving.append(store.copy(pairs - 2 + slot, slot, tile, True))


def load_probs(store, slot):
    for tile in reversed(range(store.tiles)):
        store.copy(slot, slot, tile, False).start()


def attend_back(q_ref, da_ref, inner_ref, k_ref, v_ref, store, dq_ref, dk_ref, dv_ref, dk_sum, dv_sum, values_ref):
    length, count = q_ref.shape[0], k_ref.shape[0]
    masks = half_masks()
    pairs = k_ref.shape[1] // PAIR

    def one_pair(pair, slot, step):
        cols = rows_at(pair, PAIR)
        for tile in range(store.tiles):
            store.copy(pair, slot, tile, False).wait()
        for side in (0, 1):
            values_ref[side] = v_ref[:, cols] * masks[side]
        steps = [(tile, side) for tile in reversed(range(length // TILE)) for side in (0, 1)]
        query_grads = {}

        def place(index):
            tile, side = steps[index]
            size = (tile + 1) * TILE if store.causal else count
            return tile, side, slice(tile * TILE, (tile + 1) * TILE), slice(0, size)

        def collect(ref, tile, side, span, part):
            if tile == length // TILE - 1:
                ref[side, :, span] = part
            else:
                ref[side, :, span] += part

        def value_side(index):
            _, side, rows, span = place(index)
            return dot(da_ref[rows, cols], values_ref[side, span, :], 1, 1)

        def score_side(index, grad_probs):
            tile, side, rows, span = place(index)
            probs = store.ref[slot, side, rows, span]
            collect(dv_sum, tile, side, span, dot(da_ref[rows, cols], probs, 0, 0))
            inner = inner_ref[pair, rows, side : side + 1]
            grad_scores = (probs.astype(F32) * (grad_probs - inner)).astype(BF)
            collect(dk_sum, tile, side, span, dot(q_ref[rows, cols], grad_scores, 0, 0))
            query_grads[side] = dot(grad_scores, k_ref[span, cols], 1, 0)
            if side == 1:
                dq_ref[rows, cols] = (
                    jnp.where(lanes(PAIR) < HEAD_DIM, query_grads[0], query_grads[1]) * HEAD_DIM**-0.5
                ).astype(BF)

        staggered(value_side, score_side, len(steps))
        for sums, out in ((dk_sum, dk_ref), (dv_sum, dv_ref)):
            joined = jnp.concatenate([sums[0, :HEAD_DIM, :], sums[1, HEAD_DIM:, :]], axis=0)
            out[:, cols] = joined.astype(BF).T

        @pl.when(step < pairs // 2 - 1)
        def _():
            for tile in range(store.tiles):
                store.copy(pair + 2, slot, tile, False).start()

    two_pairs(pairs, one_pair)


def norm_rows(summed):
    center = jnp.mean(summed, axis=1, keepdims=True)
    shifted = summed - center
    inverse = lax.rsqrt(jnp.mean(shifted * shifted, axis=1, keepdims=True) + 1e-05)
    return shifted * inverse, inverse


def norm_back(grad_out, normed, inverse, gain):
    scaled = grad_out * gain
    first = jnp.mean(scaled, axis=1, keepdims=True)
    second = jnp.mean(scaled * normed, axis=1, keepdims=True)
    return inverse * (scaled - first - normed * second)


def add_rows(ref, row, values):
    ref[row : row + 1, :] += jnp.sum(values, axis=0, keepdims=True)


def place_of(place_ref):
    rep, place = place_ref[0], place_ref[1]
    return lax.rem(rep, 2), lax.div(rep, 2), lax.div(place, 2), lax.rem(place, 2)


def assemble(place_ref, chunk_refs, all_ref):
    core, chip, line, row = place_of(place_ref)
    width = all_ref.shape[1]
    quarter = chunk_refs[0].shape[3]
    shard = quarter * 4 // 3
    for core_step, chunk_ref in enumerate(chunk_refs):
        for chip_step in (0, 1):
            rep = jnp.bitwise_xor(chip, chip_step) * 2 + jnp.bitwise_xor(core, core_step)
            for line_step in range(4):
                for row_step in (0, 1):
                    owner = lax.rem(line - line_step + 4, 4) * 2 + jnp.bitwise_xor(row, row_step)
                    for piece in range(quarter // 16):
                        stacked = rep * quarter + piece * 16
                        matrix = lax.div(stacked, shard)
                        target = matrix * width + owner * shard + (stacked - matrix * shard)
                        all_ref[pl.ds(pl.multiple_of(target, 16), 16), :] = chunk_ref[
                            chip_step, line_step, row_step, piece * 16 : (piece + 1) * 16, :
                        ]


def assemble_halves(place_ref, mine_ref, other_ref, all_ref, shards):
    core = place_of(place_ref)[0]
    devices, _, half = mine_ref.shape
    for step, ref in ((0, mine_ref), (1, other_ref)):
        cols = pl.ds(pl.multiple_of(jnp.bitwise_xor(core, step) * half, half), half)
        first, target = 0, 0
        for shard in shards:
            for owner in range(devices):
                at = target + owner * shard
                all_ref[at : at + shard, cols] = ref[owner, first : first + shard, :]
            first += shard
            target += shard * devices


def unpack_small(all_ref, base, vec_ref, bias_ref):
    devices = vec_ref.shape[1] // HEAD_DIM
    inner = bias_ref.shape[1] // devices
    for pair in range(devices // 2):
        first = base + 2 * pair * 16
        left = all_ref[first : first + 16, :PAIR].astype(F32)
        right = all_ref[first + 16 : first + 32, :PAIR].astype(F32)
        vec_ref[:, pair * PAIR : (pair + 1) * PAIR] = jnp.where(
            lanes(PAIR) < HEAD_DIM, left, pltpu.roll(right, HEAD_DIM, 1)
        )
    for owner in range(devices):
        rows = all_ref[base + owner * 16 : base + owner * 16 + 16, :inner].astype(F32)
        bias_ref[:, owner * inner : (owner + 1) * inner] = rows[10:11, :]


def self_forward_kernel(staged, *refs):
    if staged:
        place_ref, pos_ref, x_hbm, chunk_hbm, other_hbm = refs[:5]
        refs = refs[5:]
    else:
        pos_ref, x_hbm, all_hbm = refs[:3]
        refs = refs[3:]
    p_hbm, q_hbm, k_hbm, v_hbm, o_hbm = refs[:5]
    refs = refs[5:]
    if staged:
        all_out, refs = refs[0], refs[1:]
    x_ref, all_ref, q_ref, k_ref, v_ref, o_ref, p_ref, start_ref = refs[:8]
    mover = Mover(refs[-1])
    length, width = x_ref.shape
    if staged:
        chunk_refs = refs[8:10]
        loads = [mover.load(a, b) for a, b in zip((chunk_hbm, other_hbm), chunk_refs)]
    else:
        loads = [mover.load(all_hbm, all_ref)]
    x_load = mover.load(x_hbm, x_ref)
    put_start(pos_ref, start_ref)
    for load in loads:
        load.wait()
    if staged:
        assemble(place_ref, chunk_refs, all_ref)
        mover.store(all_ref, all_out)
    x_load.wait()

    @pl.loop(0, length // TILE)
    def _(tile):
        rows = rows_at(tile)
        source = x_ref[rows, :]
        queries = dot(source, all_ref[:width, :], 1, 0).astype(BF)
        q_ref[rows, :] = queries * jnp.asarray(HEAD_DIM**-0.5, BF)
        k_ref[rows, :] = dot(source, all_ref[width : 2 * width, :], 1, 0).astype(BF)
        v_ref[rows, :] = dot(source, all_ref[2 * width :, :], 1, 0).astype(BF)

    mover.store(k_ref, k_hbm)
    mover.store(v_ref, v_hbm)
    mover.store(q_ref, q_hbm)
    finished = (mover.store_parts(o_ref, o_hbm, width // PAIR, columns_at(PAIR)),)
    attend(q_ref, k_ref, v_ref, None, start_ref, o_ref, ProbStore(mover, p_hbm, p_ref, True), finished)
    mover.finish()


def unpack_small(small_ref, vec_ref, bias_ref):
    devices = vec_ref.shape[1] // HEAD_DIM
    inner = bias_ref.shape[1] // devices
    for pair in range(devices // 2):
        left = small_ref[0, 2 * pair, :, :PAIR].astype(F32)
        right = small_ref[0, 2 * pair + 1, :, :PAIR].astype(F32)
        vec_ref[:, pair * PAIR : (pair + 1) * PAIR] = jnp.where(
            lanes(PAIR) < HEAD_DIM, left, pltpu.roll(right, HEAD_DIM, 1)
        )
    for owner in range(devices):
        rows = small_ref[0, owner, :, :inner].astype(F32)
        bias_ref[:, owner * inner : (owner + 1) * inner] = rows[10:11, :]


def cross_forward_kernel(staged, *refs):
    place_ref, core = None, None
    if staged:
        place_ref, refs = refs[0], refs[1:]
        core = place_of(place_ref)[0]
    length_ref, refs = refs[0], refs[1:]
    if staged:
        x_hbm, mixed_hbm, source_hbm, *packs = refs[:5]
        refs = refs[5:]
    else:
        vec_ref, x_hbm, mixed_hbm, source_hbm, *packs = refs[:9]
        refs = refs[9:]
    first_hbm, first_inv_hbm, p_hbm, q_hbm, k_hbm, v_hbm, o_hbm, n_hbm, inv_hbm = refs[:9]
    refs = refs[9:]
    if staged:
        vec_ref, bias_ref, refs = refs[0], refs[1], refs[2:]
    x_ref, mixed_ref, source_ref, first_ref, first_inv_ref, q_ref, k_ref, v_ref, o_ref, n_ref, inv_ref = refs[:11]
    p_ref, extra_ref, *w_refs = refs[11:18]
    mover = Mover(refs[-1])
    length, width = q_ref.shape

    if staged:
        small_ref = refs[18]
        rows = packs[0].shape[1]
        small = [
            mover.load(pack.at[:, rows - 16 :, :], small_ref.at[jnp.bitwise_xor(core, step)])
            for step, pack in enumerate(packs)
        ]
    source_load = mover.load_rows(source_hbm, source_ref)
    order = (2, 3, 0, 1, 4)
    waits = [None] * 5
    if staged:
        half = width // 2
        shard = w_refs[0].shape[1]
        for index in order:
            copies = []
            for step, pack in enumerate(packs):
                cols = pl.ds(pl.multiple_of(jnp.bitwise_xor(core, step) * half, half), half)
                copies.append(
                    mover.load(pack.at[:, index * shard : (index + 1) * shard, :], w_refs[index].at[:, :, cols])
                )
            waits[index] = lambda copies=copies: [copy.wait() for copy in copies]
    else:
        for index in order:
            waits[index] = mover.load(packs[index], w_refs[index]).wait
    mixed_load = mover.load_rows(mixed_hbm, mixed_ref)
    x_load = mover.load_rows(x_hbm, x_ref)
    extra_ref[...] = key_extra(length_ref[0], k_ref.shape[0])
    waits[2]()
    waits[3]()

    @pl.loop(0, source_ref.shape[0] // TILE)
    def _(tile):
        rows = rows_at(tile)
        source_load(tile)
        source = source_ref[rows, :]
        k_ref[rows, :] = dot(source, whole(w_refs[2]), 1, 0).astype(BF)
        v_ref[rows, :] = dot(source, whole(w_refs[3]), 1, 0).astype(BF)

    mover.store(k_ref, k_hbm)
    mover.store(v_ref, v_hbm)
    if staged:
        for load in small:
            load.wait()
        unpack_small(small_ref, vec_ref, bias_ref)
    waits[0]()
    waits[1]()

    @pl.loop(0, length // TILE)
    def _(tile):
        rows = rows_at(tile)
        mixed_load(tile)
        x_load(tile)
        summed = x_ref[rows, :].astype(F32) * vec_ref[6:7, :] + dot(mixed_ref[rows, :], whole(w_refs[0]), 1, 0)
        normed, inverse = norm_rows(summed)
        first_ref[rows, :] = normed
        first_inv_ref[rows, :] = inverse
        low = (normed * vec_ref[0:1, :] + vec_ref[3:4, :]).astype(BF)
        queries = dot(low, whole(w_refs[1]), 1, 0).astype(BF)
        q_ref[rows, :] = queries * jnp.asarray(HEAD_DIM**-0.5, BF)

    mover.store(first_ref, first_hbm)
    mover.store(first_inv_ref, first_inv_hbm)
    mover.store(q_ref, q_hbm)
    finished = (mover.store_parts(o_ref, o_hbm, width // PAIR, columns_at(PAIR)),)
    attend(q_ref, k_ref, v_ref, extra_ref, None, o_ref, ProbStore(mover, p_hbm, p_ref, False), finished)
    waits[4]()
    n_store, inv_store = mover.store_rows(n_ref, n_hbm), mover.store_rows(inv_ref, inv_hbm)

    @pl.loop(0, length // TILE)
    def _(tile):
        rows = rows_at(tile)
        first_out = first_ref[rows, :] * vec_ref[0:1, :] + vec_ref[3:4, :]
        summed = first_out * vec_ref[7:8, :] + dot(o_ref[rows, :], whole(w_refs[4]), 1, 0)
        normed, inverse = norm_rows(summed)
        n_ref[rows, :] = normed
        inv_ref[rows, :] = inverse
        n_store(tile)
        inv_store(tile)

    mover.finish()


def hidden_kernel(staged, *refs):
    place_ref, core = None, None
    if staged:
        place_ref, refs = refs[0], refs[1:]
        core = place_of(place_ref)[0]
    vec_ref, bias_ref, *packs = refs[: 6 if staged else 4]
    n_hbm, inv_hbm, cot_hbm = refs[len(packs) + 2 : len(packs) + 5]
    refs = refs[len(packs) + 5 :]
    count = 2 if staged else 1
    sums_ref, bias_sum_ref, out_hbm, dz_hbm = refs[:4]
    grad_hbms, refs = refs[4 : 4 + count], refs[4 + count :]
    grad_refs, refs = refs[:count], refs[count:]
    n_ref, inv_ref, cot_ref, out_ref, dz_ref, low_ref, h_ref, du_ref, df_ref, slope_ref, third_ref = refs[:11]
    blocks = bias_ref.shape[1] // vec_ref.shape[1]
    e_ref, s_ref = refs[11:13]
    mover = Mover(refs[-1])
    length, width = n_ref.shape

    n_load = mover.load_rows(n_hbm, n_ref)
    if staged:
        expand_loads, shrink_loads = load_quarters(mover, place_ref, packs, e_ref, s_ref)
    else:
        expand_loads, shrink_loads = [mover.load(packs[0], e_ref)], [mover.load(packs[1], s_ref)]
    cot_load = mover.load_rows(cot_hbm, cot_ref)
    inv_load = mover.load_rows(inv_hbm, inv_ref)
    out_store, dz_store = mover.store_rows(out_ref, out_hbm), mover.store_rows(dz_ref, dz_hbm)
    tiles = [slice(tile * TILE, (tile + 1) * TILE) for tile in range(length // TILE)]
    parts = [slice(block * width, (block + 1) * width) for block in range(blocks)]
    sums = {row: 0.0 for row in (1, 2, 4, 5, 8, 9)}
    bias_sums = [0.0] * blocks

    def add(row, values):
        sums[row] = sums[row] + jnp.sum(values, axis=0, keepdims=True)

    def second_out(rows):
        return n_ref[rows, :] * vec_ref[1:2, :] + vec_ref[4:5, :]

    for tile, rows in enumerate(tiles):
        n_load(tile)
        low_ref[rows, :] = second_out(rows).astype(BF)
    steps = [(block, rows) for block in range(blocks) for rows in tiles]

    def expand(index):
        block, rows = steps[index]
        return dot(low_ref[rows, :], whole(e_ref.at[block]), 1, 0) + bias_ref[:, parts[block]]

    def activate(index, before):
        block, rows = steps[index]
        square = before * before
        tangent = jnp.tanh(before * (0.7978845608028654 + 0.7978845608028654 * 0.044715 * square))
        half = 0.5 * (1.0 + tangent)
        slope_ref[rows, parts[block]] = half + before * (half * (1.0 - tangent)) * (
            0.7978845608028654 + 3.0 * 0.7978845608028654 * 0.044715 * square
        )
        h_ref[rows, parts[block]] = (before * half).astype(BF)

    for load in expand_loads:
        load.wait()
    staggered(expand, activate, len(steps))
    for load in shrink_loads:
        load.wait()
    for tile in range(len(tiles)):
        cot_load(tile)
        inv_load(tile)

    def shrink(tile):
        return dot(h_ref[tiles[tile], :], whole(s_ref), 1, 0)

    def outer_norm(tile, branch_out):
        rows = tiles[tile]
        second = second_out(rows)
        normed, inverse = norm_rows(second * vec_ref[8:9, :] + vec_ref[9:10, :] + branch_out)
        out_ref[rows, :] = (normed * vec_ref[2:3, :] + vec_ref[5:6, :]).astype(BF)
        grad_out = cot_ref[rows, :].astype(F32)
        third = norm_back(grad_out, normed, inverse, vec_ref[2:3, :])
        third_ref[rows, :] = third
        add(2, grad_out * normed)
        add(5, grad_out)
        branch = third.astype(BF)
        df_ref[rows, :] = branch
        add(9, branch.astype(F32))
        add(8, second * third)

    staggered(shrink, outer_norm, len(tiles))
    for tile in range(len(tiles)):
        out_store(tile)

    def shrink_back(index):
        block, rows = steps[index]
        return dot(df_ref[rows, :], whole(s_ref)[parts[block], :], 1, 1)

    def slope_back(index, grad_hidden):
        block, rows = steps[index]
        du = (grad_hidden * slope_ref[rows, parts[block]]).astype(BF)
        du_ref[rows, parts[block]] = du
        bias_sums[block] = bias_sums[block] + jnp.sum(du.astype(F32), axis=0, keepdims=True)

    staggered(shrink_back, slope_back, len(steps))

    def expand_back(tile):
        rows = tiles[tile]
        return sum(dot(du_ref[rows, parts[block]], whole(e_ref.at[block]), 1, 1) for block in range(blocks))

    def inner_norm(tile, grad_expanded):
        rows = tiles[tile]
        grad = vec_ref[8:9, :] * third_ref[rows, :] + grad_expanded
        normed = n_ref[rows, :]
        dz_ref[rows, :] = norm_back(grad, normed, inv_ref[rows, :], vec_ref[1:2, :])
        add(1, grad * normed)
        add(4, grad)

    staggered(expand_back, inner_norm, len(tiles))
    for tile in range(len(tiles)):
        dz_store(tile)
    sums_ref[...] = jnp.zeros_like(sums_ref)
    for row, values in sums.items():
        sums_ref[row : row + 1, :] = values
    for block, values in enumerate(bias_sums):
        bias_sum_ref[:, parts[block]] = values
    for step in reversed(range(count)):
        for block in range(blocks):
            put_grad(grad_refs, step, place_ref, block, low_ref[...], du_ref, block * width)
            put_shrink(grad_refs, step, place_ref, block, blocks, h_ref[:, parts[block]], df_ref)
        mover.store(grad_refs[step], grad_hbms[step])
    mover.finish()


def branch_grads(branch_rows, mixed_weight, o_ref, da_ref, inner_ref):
    width = o_ref.shape[1]
    tiles = [slice(tile * TILE, (tile + 1) * TILE) for tile in range(o_ref.shape[0] // TILE)]
    head = lax.broadcasted_iota(jnp.int32, (width, PAIR), 0) // HEAD_DIM
    picks = jnp.where(head == lax.broadcasted_iota(jnp.int32, (width, PAIR), 1), 1.0, 0.0).astype(BF)

    def project(tile):
        return dot(branch_rows(tile, tiles[tile]), mixed_weight, 1, 1)

    def reduce(tile, mixed_grad):
        rows = tiles[tile]
        low = mixed_grad.astype(BF)
        da_ref[rows, :] = low
        product = low.astype(F32) * o_ref[rows, :].astype(F32)
        high = product.astype(BF)
        rest = (product - high.astype(F32)).astype(BF)
        inner = dot(high, picks, 1, 0) + dot(rest, picks, 1, 0)
        for pair in range(width // PAIR):
            inner_ref[pair, rows, :] = pltpu.roll(inner, (PAIR - 2 * pair) % PAIR, 1) if pair else inner

    staggered(project, reduce, len(tiles))


def put_grad(grad_refs, step, place_ref, index, left, right_ref, first=0):
    width = left.shape[1]
    if place_ref is None:
        grad = dot(left, right_ref[:, first : first + width], 0, 0)
        grad_refs[0][index * width : (index + 1) * width, :] = grad.astype(BF)
        return
    core, _, _, row = place_of(place_ref)
    half = width // 2
    shard = width // 8
    cols = pl.ds(pl.multiple_of(first + jnp.bitwise_xor(core, step) * half, half), half)
    grad = dot(left, right_ref[:, cols], 0, 0).astype(BF).reshape(4, 2, shard, half)
    for side in (0, 1):
        slot = jnp.bitwise_xor(row, side)
        grad_refs[step][slot, :, index * shard : (index + 1) * shard, :] = grad[:, side]


def put_shrink(grad_refs, step, place_ref, block, blocks, left, right_ref):
    width = left.shape[1]
    if place_ref is None:
        first = (blocks + block) * width
        grad_refs[0][first : first + width, :] = dot(left, right_ref[...], 0, 0).astype(BF)
        return
    core, _, _, row = place_of(place_ref)
    half, shard = width // 2, width * blocks // 8
    base = width // 8 * blocks
    cols = pl.ds(pl.multiple_of(jnp.bitwise_xor(core, step) * half, half), half)
    grad = dot(left, right_ref[:, cols], 0, 0).astype(BF).reshape(width // shard, shard, half)
    for part in range(width // shard):
        owner = block * (width // shard) + part
        grad_refs[step][jnp.bitwise_xor(row, owner % 2), owner // 2, base:, :] = grad[part]


def put_small(grad_refs, place_ref, base, sums, bias_sum):
    core, _, _, row = place_of(place_ref)
    half = grad_refs[0].shape[3]
    inner = bias_sum.shape[1] // 8
    index = lax.broadcasted_iota(jnp.int32, (16, half), 0)
    for owner in range(8):
        block = sums[:, owner // 2 * PAIR : (owner // 2 + 1) * PAIR]
        if owner % 2:
            block = pltpu.roll(block, HEAD_DIM, 1)
        block = jnp.concatenate([block, jnp.zeros((16, half - PAIR), F32)], axis=1)
        block = jnp.where(index == 10, bias_sum[:, owner * inner : (owner + 1) * inner], block)
        high = block.astype(BF)
        low = (block - high.astype(F32)).astype(BF)
        slot = jnp.bitwise_xor(row, owner % 2)
        first = (core == 0).astype(F32)
        for step, grad_ref in enumerate(grad_refs):
            is_high = first if step == 0 else 1.0 - first
            mixed = high.astype(F32) * is_high + low.astype(F32) * (1.0 - is_high)
            grad_ref[slot, owner // 2, base : base + 16, :] = mixed.astype(BF)


def cross_backward_kernel(staged, *refs):
    place_ref, core = None, None
    if staged:
        place_ref, refs = refs[0], refs[1:]
        core = place_of(place_ref)[0]
    vec_ref, refs = refs[0], refs[1:]
    if staged:
        sums_three_ref, bias_sum_ref, refs = refs[0], refs[1], refs[2:]
    packs, refs = refs[: 2 if staged else 5], refs[2 if staged else 5 :]
    p_hbm, dz_hbm, x_hbm, first_hbm, inv_hbm, source_hbm, q_hbm, k_hbm, v_hbm, o_hbm, self_o_hbm = refs[:11]
    sums_ref, dfirst_hbm, dsource_hbm = refs[11:14]
    count = 2 if staged else 1
    grad_hbms, refs = refs[14 : 14 + count], refs[14 + count :]
    grad_refs, refs = refs[:count], refs[count:]
    dz_ref, x_ref, first_ref, inv_ref, source_ref, q_ref, k_ref, v_ref, o_ref, self_o_ref = refs[:10]
    dfirst_ref, dsource_ref, *w_refs = refs[10:17]
    low_ref, da_ref, inner_ref, dq_ref, dk_ref, dv_ref, dk_sum, dv_sum, branch_ref, values_ref, p_ref = refs[17:28]
    mover = Mover(refs[-1])
    length, width = dz_ref.shape

    dz_load, o_load = mover.load_rows(dz_hbm, dz_ref), mover.load_rows(o_hbm, o_ref)
    waits = load_matrices(mover, core, packs, w_refs, (4,))
    sums_ref[...] = jnp.zeros_like(sums_ref)
    waits[0]()
    store = ProbStore(mover, p_hbm, p_ref, False)
    load_probs(store, 0)
    middle = [mover.load(a, b) for a, b in ((v_hbm, v_ref), (q_hbm, q_ref), (k_hbm, k_ref))]

    def branch_rows(tile, rows):
        dz_load(tile)
        o_load(tile)
        branch_ref[rows, :] = dz_ref[rows, :].astype(BF)
        return branch_ref[rows, :]

    branch_grads(branch_rows, whole(w_refs[4]), o_ref, da_ref, inner_ref)
    for step in range(count):
        put_grad(grad_refs, step, place_ref, 4, o_ref[...], branch_ref)
    load_probs(store, 1)
    first_load = mover.load_rows(first_hbm, first_ref)
    waits = load_matrices(mover, core, packs, w_refs, (1, 2, 3))
    last = [
        mover.load(a, b)
        for a, b in ((source_hbm, source_ref), (x_hbm, x_ref), (inv_hbm, inv_ref), (self_o_hbm, self_o_ref))
    ]
    for load in middle:
        load.wait()
    attend_back(q_ref, da_ref, inner_ref, k_ref, v_ref, store, dq_ref, dk_ref, dv_ref, dk_sum, dv_sum, values_ref)
    for load in last:
        load.wait()
    for wait in waits:
        wait()
    for tile in range(length // TILE):
        first_load(tile)

    dsource_store = mover.store_rows(dsource_ref, dsource_hbm)
    dfirst_store = mover.store_rows(dfirst_ref, dfirst_hbm)
    tiles = [slice(tile * TILE, (tile + 1) * TILE) for tile in range(length // TILE)]
    key_tiles = [slice(tile * TILE, (tile + 1) * TILE) for tile in range(source_ref.shape[0] // TILE)]
    sums = {row: 0.0 for row in (0, 3, 6, 7)}

    def add(row, values):
        sums[row] = sums[row] + jnp.sum(values, axis=0, keepdims=True)

    def source_grad(tile):
        rows = key_tiles[tile]
        dsource_ref[rows, :] = dot(dk_ref[rows, :], whole(w_refs[2]), 1, 1) + dot(
            dv_ref[rows, :], whole(w_refs[3]), 1, 1
        )

    def put_keys(step):
        put_grad(grad_refs, step, place_ref, 2, source_ref[...], dk_ref)
        put_grad(grad_refs, step, place_ref, 3, source_ref[...], dv_ref)

    products = [functools.partial(source_grad, tile) for tile in range(len(key_tiles))]
    products += [functools.partial(put_keys, step) for step in range(count)]

    def query_back(tile):
        product = dot(dq_ref[tiles[tile], :], whole(w_refs[1]), 1, 1)
        for run in products[tile :: len(tiles)]:
            run()
        return product

    def first_norm(tile, product):
        rows = tiles[tile]
        grad = dz_ref[rows, :]
        dx = product + vec_ref[7:8, :] * grad
        normed = first_ref[rows, :]
        first_out = normed * vec_ref[0:1, :] + vec_ref[3:4, :]
        low_ref[rows, :] = first_out.astype(BF)
        add(7, first_out * grad)
        dfirst = norm_back(dx, normed, inv_ref[rows, :], vec_ref[0:1, :])
        dfirst_ref[rows, :] = dfirst
        add(0, dx * normed)
        add(3, dx)
        add(6, x_ref[rows, :].astype(F32) * dfirst)
        branch_ref[rows, :] = dfirst.astype(BF)

    staggered(query_back, first_norm, len(tiles))
    for tile in range(len(key_tiles)):
        dsource_store(tile)
    for tile in range(len(tiles)):
        dfirst_store(tile)
    for row, values in sums.items():
        sums_ref[row : row + 1, :] = values

    if staged:
        put_small(grad_refs, place_ref, 5 * (width // 8), sums_ref[...] + sums_three_ref[...], bias_sum_ref[...])
    for step in reversed(range(count)):
        put_grad(grad_refs, step, place_ref, 1, low_ref[...], dq_ref)
        put_grad(grad_refs, step, place_ref, 0, self_o_ref[...], branch_ref)
        mover.store(grad_refs[step], grad_hbms[step])
    mover.finish()


def self_backward_kernel(staged, *refs):
    place_ref, core = None, None
    if staged:
        place_ref, refs = refs[0], refs[1:]
        core = place_of(place_ref)[0]
    count = 2 if staged else 1
    packs, refs = refs[:count], refs[count:]
    p_hbm, dz_hbm, x_hbm, q_hbm, k_hbm, v_hbm, o_hbm, *head_hbms = refs[:10]
    grad_hbms, refs = refs[10 : 10 + count], refs[10 + count :]
    grad_refs, refs = refs[:count], refs[count:]
    dz_ref, x_ref, q_ref, k_ref, v_ref, o_ref, w_ref = refs[:7]
    da_ref, inner_ref, dq_ref, dk_ref, dv_ref, dk_sum, dv_sum, values_ref, p_ref = refs[7:16]
    mover = Mover(refs[-1])
    length, width = dz_ref.shape

    dz_load = mover.load_rows(dz_hbm, dz_ref)
    waits = load_matrices(mover, core, packs, (w_ref,))
    o_load = mover.load_rows(o_hbm, o_ref)
    waits[0]()
    store = ProbStore(mover, p_hbm, p_ref, True)
    load_probs(store, 0)
    middle = [mover.load(a, b) for a, b in ((v_hbm, v_ref), (q_hbm, q_ref), (k_hbm, k_ref))]

    def branch_rows(tile, rows):
        dz_load(tile)
        o_load(tile)
        return dz_ref[rows, :].astype(BF)

    branch_grads(branch_rows, whole(w_ref), o_ref, da_ref, inner_ref)
    load_probs(store, 1)
    x_load = mover.load(x_hbm, x_ref)
    for load in middle:
        load.wait()
    attend_back(q_ref, da_ref, inner_ref, k_ref, v_ref, store, dq_ref, dk_ref, dv_ref, dk_sum, dv_sum, values_ref)
    for near, far in zip((dq_ref, dk_ref, dv_ref), head_hbms):
        mover.store(near, far)
    x_load.wait()
    for step in reversed(range(count)):
        for index, grads in enumerate((dq_ref, dk_ref, dv_ref)):
            put_grad(grad_refs, step, place_ref, index, x_ref[...], grads)
        mover.store(grad_refs[step], grad_hbms[step])
    mover.finish()


def input_grad_kernel(vec_ref, dz_hbm, all_hbm, dq_hbm, dk_hbm, dv_hbm, dx_hbm, *refs):
    dz_ref, all_ref, dq_ref, dk_ref, dv_ref, dx_ref, sems = refs
    mover = Mover(sems)
    width = dz_ref.shape[1]
    all_load = mover.load(all_hbm, all_ref)
    heads = (dq_ref, dk_ref, dv_ref)
    loads = [mover.load_rows(a, b) for a, b in zip((dq_hbm, dk_hbm, dv_hbm), heads)]
    loads.append(mover.load_rows(dz_hbm, dz_ref))
    dx_store = mover.store_rows(dx_ref, dx_hbm)
    all_load.wait()

    @pl.loop(0, dz_ref.shape[0] // TILE)
    def _(tile):
        rows = rows_at(tile)
        for load in loads:
            load(tile)
        dx = vec_ref[6:7, :] * dz_ref[rows, :]
        for index, grads in enumerate(heads):
            dx = dx + dot(grads[rows, :], all_ref[index * width : (index + 1) * width, :], 1, 1)
        dx_ref[rows, :] = dx
        dx_store(tile)

    mover.finish()


def call(kernel, args, outs, scratch, limit, flops, smem=(), near=(), near_outs=(), copies=0):
    spaces = [pltpu.SMEM if i in smem else pltpu.VMEM if i in near else pl.ANY for i in range(len(args))]
    out_spaces = [pltpu.VMEM if i in near_outs else pl.ANY for i in range(len(outs))]
    buffers = [pltpu.VMEM(shape, kind) for shape, kind in scratch]
    if copies:
        buffers.append(pltpu.SemaphoreType.DMA((copies,)))
    return pl.pallas_call(
        kernel,
        out_shape=[jax.ShapeDtypeStruct(shape, kind) for shape, kind in outs],
        in_specs=[pl.BlockSpec(memory_space=space) for space in spaces],
        out_specs=[pl.BlockSpec(memory_space=space) for space in out_spaces],
        scratch_shapes=buffers,
        compiler_params=pltpu.CompilerParams(vmem_limit_bytes=(63 if copies else limit) * MIB),
        cost_estimate=pl.CostEstimate(flops=flops, bytes_accessed=16 * MIB, transcendentals=0),
    )(*args)


def like(*arrays):
    return [(a.shape, a.dtype) for a in arrays]


def prob_shape(queries, keys, width):
    return (width // PAIR, 2, queries, keys), BF


def forward_self(place, x, pos, pack, staged):
    length, width = x.shape
    low = ((length, width), BF)
    outs = [prob_shape(length, length, width), low, low, low, low]
    matrices = ((3 * width, width), BF)
    scratch = [low, matrices, low, low, low, low, ((2, 2, length, length), BF), ((length, 1), jnp.int32)]
    if staged:
        return call(
            functools.partial(self_forward_kernel, True),
            (place, pos, x, *pack),
            [*outs, matrices],
            [*scratch, *like(*pack)],
            40, 10**10, smem=(0,), near=(1,), copies=24,
        )
    results = call(
        functools.partial(self_forward_kernel, False),
        (pos, x, pack), outs, scratch, 40, 10**10, near=(0,), copies=24,
    )
    return (*results, pack)


def matrix_buffers(shards, width):
    return [((8 if rows < width else 1, rows, width), BF) for rows in shards]


def forward_cross(place, x, mixed, source, count, packs, given, shards):
    length, width = x.shape
    keys = source.shape[0]
    low, full, column, key_low = ((length, width), BF), ((length, width), F32), ((length, 1), F32), ((keys, width), BF)
    outs = [full, column, prob_shape(length, keys, width), low, key_low, key_low, low, full, column]
    near = [full, column, low, key_low, key_low, low, full, column]
    scratch = [low, low, key_low, *near, ((2, 2, length, keys), BF), ((keys, PAIR), BF)]
    if place is not None:
        return call(
            functools.partial(cross_forward_kernel, True),
            (place, count, x, mixed, source, *packs),
            [*outs, ((16, width), F32), ((1, 4 * width), F32)],
            [*scratch, *matrix_buffers(shards, width), ((2, 8, 16, width // 2), BF)],
            44, 10**10, smem=(0, 1), near_outs=(9, 10), copies=64,
        )
    vec, bias = given
    results = call(
        functools.partial(cross_forward_kernel, False),
        (count, vec, x, mixed, source, *packs),
        outs, [*scratch, *like(*packs)],
        44, 10**10, smem=(0,), near=(1,), copies=64,
    )
    return (*results, vec, bias)


def grad_outs(rows, width, staged):
    return [((2, 4, rows, width // 2), BF)] * 2 if staged else [((rows, width), BF)]


def hidden_step(place, packs, normed, inverse, cot, vec, bias):
    length, width = normed.shape
    inner = bias.shape[1]
    blocks = inner // width
    staged = place is not None
    low, full = ((length, width), BF), ((length, width), F32)
    grads = grad_outs(2 * inner // 8 if staged else 2 * inner, width, staged)
    args = (vec, bias, *packs, normed, inverse, cot)
    matrices = like(*packs)
    if staged:
        rows = width // 8
        matrices = [((blocks, 8, rows, width), BF), ((8, 2, blocks, rows // 2, width), BF)]
    return call(
        functools.partial(hidden_kernel, staged),
        (place, *args) if staged else args,
        [((16, width), F32), ((1, inner), F32), low, full, *grads],
        [*grads, *like(normed, inverse, cot), low, full, low, ((length, inner), BF), ((length, inner), BF), low,
         ((length, inner), F32), full, *matrices],
        44, 2 * 10**10, smem=(0,) if staged else (), near=(1, 2) if staged else (0, 1), near_outs=(0, 1),
        copies=96,
    )


def backward_cross(place, packs, dz, x, normed, inverse, source, vec, saved, mixed, small, shards):
    length, width = dz.shape
    keys = source.shape[0]
    staged = place is not None
    probs, *saved = saved
    arrays = (dz, x, normed, inverse, source, *saved, mixed)
    low, key_low, sums = ((length, width), BF), ((keys, width), BF), ((2, PAIR, keys), F32)
    grads = grad_outs(5 * width // 8 + 16 if staged else 5 * width, width, staged)
    full, key_full = ((length, width), F32), ((keys, width), F32)
    return call(
        functools.partial(cross_backward_kernel, staged),
        (place, vec, *small, *packs, probs, *arrays) if staged else (vec, *packs, probs, *arrays),
        [((16, width), F32), full, key_full, *grads],
        [*grads, *like(*arrays), full, key_full, *(matrix_buffers(shards, width) if staged else like(*packs)),
         low, low, ((width // PAIR, length, PAIR), F32), low, key_low, key_low, sums, sums, low, ((2, keys, PAIR), BF),
         ((2, 2, length, keys), BF)],
        48, 2 * 10**10, smem=(0,) if staged else (), near=(1, 2, 3) if staged else (0,), near_outs=(0,), copies=72,
    )


def backward_self(place, packs, dz, x, saved, shards):
    length, width = dz.shape
    staged = place is not None
    probs, *saved = saved
    arrays = (dz, x, *saved)
    low, sums = ((length, width), BF), ((2, PAIR, length), F32)
    grads = grad_outs(3 * width // 8 if staged else 3 * width, width, staged)
    first = matrix_buffers(shards[:1], width) if staged else like(*packs)
    return call(
        functools.partial(self_backward_kernel, staged),
        (place, *packs, probs, *arrays) if staged else (*packs, probs, *arrays),
        [low, low, low, *grads],
        [*grads, *like(*arrays), *first, low, ((width // PAIR, length, PAIR), F32), low, low, low, sums, sums,
         ((2, length, PAIR), BF), ((2, 2, length, length), BF)],
        48, 2 * 10**10, smem=(0,) if staged else (), copies=64,
    )


def input_gradient(vec, dz, matrices, heads):
    arrays = (dz, matrices, *heads)
    return call(
        input_grad_kernel, (vec, *arrays), like(dz), [*like(*arrays), *like(dz)], 40, 2 * 10**9, near=(0,), copies=24
    )[0]


def adam_step(settings_ref, now, grad, one, two, decay):
    beta_one, beta_two = settings_ref[1], settings_ref[2]
    first = beta_one * one + (1.0 - beta_one) * grad
    second = beta_two * two + (1.0 - beta_two) * grad * grad
    change = (first / settings_ref[4]) / (jnp.sqrt(second / settings_ref[5]) + 1e-08)
    if decay:
        change = change + settings_ref[3] * now
    return now - settings_ref[0] * change, first, second


def store_step(refs, where, results):
    for ref, value in zip(refs, results):
        ref[where] = value


def hidden_adam_kernel(place_ref, settings_ref, *refs):
    core = place_of(place_ref)[0]
    hbms, new_hbms, refs = refs[:8], refs[8:14], refs[14:]
    mine_ref, other_ref, *params = refs[:8]
    news, mover = refs[8:14], Mover(refs[-1])
    loads = [mover.load(a, b) for a, b in zip(hbms, refs[:8])]
    expand, shrink = params[0:3], params[3:6]
    half = mine_ref.shape[1]
    shard = expand[0].shape[0]
    blocks = expand[0].shape[1] // (2 * half)
    for load in loads[:5]:
        load.wait()
    sides = [(jnp.bitwise_xor(core, step) * half, ref) for step, ref in ((0, mine_ref), (1, other_ref))]
    for side, ref in sides:
        for block in range(blocks):
            where = (slice(None), pl.ds(pl.multiple_of(block * 2 * half + side, half), half))
            grad = ref[block * shard : (block + 1) * shard, :]
            now, one, two = (r[where] for r in expand)
            store_step(news[:3], where, adam_step(settings_ref, now, grad, one, two, True))
    for load in loads[5:]:
        load.wait()
    for near, far in zip(news[:3], new_hbms[:3]):
        mover.store(near, far)
    for side, ref in sides:
        where = (slice(None), pl.ds(pl.multiple_of(side, half), half))
        now, one, two = (r[where] for r in shrink)
        store_step(news[3:], where, adam_step(settings_ref, now, ref[blocks * shard :, :], one, two, True))
    for near, far in zip(news[3:], new_hbms[3:]):
        mover.store(near, far)
    mover.finish()


def attention_adam_kernel(place_ref, settings_ref, mine_ref, other_ref, *refs):
    core = place_of(place_ref)[0]
    matrices, bias, vectors = refs[0:3], refs[3:6], refs[6:9]
    new_matrices, new_bias, new_vectors = refs[9:12], refs[12:15], refs[15:18]
    half = mine_ref.shape[1]
    shard = matrices[0].shape[1]
    for step, ref in ((0, mine_ref), (1, other_ref)):
        cols = pl.ds(pl.multiple_of(jnp.bitwise_xor(core, step) * half, half), half)
        for index in range(8):
            where = (index, slice(None), cols)
            now, one, two = (r[where] for r in matrices)
            grad = ref[index * shard : (index + 1) * shard, :]
            store_step(new_matrices, where, adam_step(settings_ref, now, grad, one, two, True))
    small = mine_ref[8 * shard :, :] + other_ref[8 * shard :, :]
    for group, new, grad in (
        (bias, new_bias, small[10:11, : bias[0].shape[1]]),
        (vectors, new_vectors, small[:10, : vectors[0].shape[1]]),
    ):
        now, one, two = (r[...] for r in group)
        store_step(new, ..., adam_step(settings_ref, now, grad, one, two, False))


def hidden_adam(scalars, grads, params):
    return call(
        hidden_adam_kernel, (*scalars, *grads, *params), like(*params), [*like(*grads), *like(*params), *like(*params)],
        40, 10**9, smem=(0, 1), copies=16,
    )


def adam_call(kernel, scalars, grads, params):
    return call(
        kernel, (*scalars, *grads, *params), [(p.shape, F32) for p in params], [], 32, 10**7, smem=(0, 1),
        near=range(2, 2 + len(grads) + len(params)), near_outs=range(len(params)),
    )


CORE_SWAP = [(0, 1), (1, 0), (2, 3), (3, 2)]
CHIP_SWAP = [(0, 2), (2, 0), (1, 3), (3, 1)]
ROW_SWAP = [(i, i ^ 1) for i in range(8)]


LINES = [[0, 2, 4, 6], [1, 3, 5, 7]]


def line_shift(step):
    return [(2 * z + y, 2 * ((z + step) % 4) + y) for z in range(4) for y in (0, 1)]


def small_mesh(mesh):
    return mesh.shape["rep"] == 4 and mesh.shape["fsdp"] == 8


class StagedGather:
    def rows(self, mine, done):
        self.mine = mine
        self.other = lax.ppermute(after(mine, done), "fsdp", ROW_SWAP)

    def line(self, done):
        self.pair = after(jnp.stack([self.mine, self.other]), done)
        self.received = [lax.ppermute(self.pair, "fsdp", line_shift(step)) for step in (1, 2, 3)]

    def chips(self, done):
        self.arrived = after(tuple(self.received), done)
        self.part = jnp.stack([self.pair, *self.arrived])
        self.far = lax.ppermute(self.part, "rep", CHIP_SWAP)

    def cores(self, done):
        far = after(self.far, done)
        part = after(self.part, done)
        return part, far, lax.ppermute(part, "rep", CORE_SWAP), lax.ppermute(far, "rep", CORE_SWAP)


def gather_staged(pack):
    quarter = pack.shape[0] // 4
    mine = lax.dynamic_slice_in_dim(pack, lax.axis_index("rep") * quarter, quarter, 0)
    pair = jnp.stack([mine, lax.ppermute(mine, "fsdp", ROW_SWAP)])
    part = jnp.stack([pair] + [lax.ppermute(pair, "fsdp", line_shift(step)) for step in (1, 2, 3)])
    both = jnp.stack([part, lax.ppermute(part, "rep", CHIP_SWAP)])
    return pair, part, both


def after(value, *done):
    return lax.optimization_barrier((value, *done))[0]


def gather_half(pack):
    half = pack.shape[1] // 2
    mine = lax.dynamic_slice_in_dim(pack, lax.axis_index("rep") % 2 * half, half, 1)
    return lax.all_gather(mine, "fsdp", axis=0)


def both_halves(mine, *done):
    mine = after(mine, *done)
    return mine, lax.ppermute(mine, "rep", CORE_SWAP)


def reduce_cores(keep, send):
    received = lax.ppermute(send, "rep", CORE_SWAP)
    return keep[0] + received[0], keep[1] + received[1]


def send_rows(send):
    return lax.ppermute(send, "fsdp", ROW_SWAP)


def reduce_rows(keep, received, done):
    return keep + after(received, done)


def reduce_chips(part, *done):
    return part.astype(F32) + after(lax.ppermute(part, "rep", CHIP_SWAP), *done).astype(F32)


def reduce_last(part, *done):
    total = reduce_chips(part, *done)
    return total, lax.ppermute(total, "rep", CORE_SWAP)


def reduce_line(joined):
    part = lax.psum_scatter(joined, "fsdp", scatter_dimension=0, axis_index_groups=LINES)
    return part.reshape(joined.shape[1:])


def reduce_shifts(joined, done):
    line = lax.axis_index("fsdp") // 2
    total = lax.dynamic_index_in_dim(joined, line, 0, False).astype(F32)
    for step in (1, 2, 3):
        away = lax.dynamic_index_in_dim(joined, (line + step) % 4, 0, False)
        total = total + after(lax.ppermute(away, "fsdp", line_shift(step)), done).astype(F32)
    return total.astype(BF)


def reduce_plain(grads):
    return lax.psum(lax.psum_scatter(grads, "fsdp", scatter_dimension=0), "rep").astype(F32)


def adam_update(weight_now, gradient, moment_one, moment_two, settings, step_float, factor):
    learn_rate, beta_one, beta_two, decay_rate = settings[0], settings[1], settings[2], settings[3]
    first_new = beta_one * moment_one + (1.0 - beta_one) * gradient
    second_new = beta_two * moment_two + (1.0 - beta_two) * gradient * gradient
    first_hat = first_new / (1.0 - beta_one**step_float)
    second_hat = second_new / (1.0 - beta_two**step_float)
    change = first_hat / (jnp.sqrt(second_hat) + 1e-08) + factor * decay_rate * weight_now
    return (weight_now - learn_rate * change, first_new, second_new)


def per_device(
    small, inputs, memory, memory_length, target_pos, cotangent,
    attention_weights, expand_weights, shrink_weights, expand_bias, layer_vectors,
    first_attention, first_expand, first_shrink, first_bias, first_vectors,
    second_attention, second_expand, second_shrink, second_bias, second_vectors,
    hyper_rates, step_count,
):
    length, width = inputs.shape[1:]
    shard = attention_weights.shape[1]
    count = width // shard
    inner_shard = shrink_weights.shape[0]
    blocks = inner_shard // shard
    low_attention = attention_weights.astype(BF).reshape(8 * shard, width)
    pack_one = low_attention[: 3 * shard]
    expand_low = expand_weights.astype(BF).reshape(shard, blocks, width)
    shrink_low = shrink_weights.astype(BF)
    x, source, cot = inputs[0], memory[0], cotangent[0]
    step_float = step_count.astype(F32)

    if small:
        place = jnp.stack([lax.axis_index("rep"), lax.axis_index("fsdp")]).astype(jnp.int32)
        small_rows = jnp.concatenate(
            [
                jnp.pad(layer_vectors, ((0, 0), (0, inner_shard - shard))),
                expand_bias[None],
                jnp.zeros((5, inner_shard), F32),
            ]
        )
        small_rows = jnp.pad(small_rows, ((0, 0), (0, width - inner_shard))).astype(BF)
        pack_two = jnp.concatenate([low_attention[3 * shard :], small_rows])
        two = gather_half(pack_two)
        pair_one, part_one, one = gather_staged(pack_one)
        half = shard // 2
        halves = expand_low.reshape(2, half, blocks, width).transpose(0, 2, 1, 3)
        quarters = jnp.stack([halves, shrink_low.reshape(2, blocks, half, width)], axis=1)
        core, chip = place[0] % 2, place[0] // 2
        quarter = lax.dynamic_slice(
            quarters, (chip, 0, 0, 0, core * (width // 2)), (1, *quarters.shape[1:4], width // 2)
        )
        three = StagedGather()
        three.rows(quarter[0], pair_one)
        one = both_halves(one, three.other)
        three.line(part_one)
        given = None
        cross_shards = (shard,) * 5
    else:
        place, cross_shards = None, None
        flat = jnp.concatenate([layer_vectors.reshape(-1), expand_bias]).astype(BF)
        flat = lax.all_gather(flat, "fsdp", axis=0).astype(F32)
        vector_size = layer_vectors.size
        vec = flat[:, :vector_size].reshape(count, -1, shard).transpose(1, 0, 2).reshape(-1, width)
        given = jnp.pad(vec, ((0, 16 - vec.shape[0]), (0, 0))), flat[:, vector_size:].reshape(1, -1)

        def gather_all(pack, shards):
            full = lax.all_gather(pack, "fsdp", axis=0)
            pieces, first = [], 0
            for rows in shards:
                pieces.append(full[:, first : first + rows].reshape(-1, width))
                first += rows
            return pieces

        def owners(grads, shards):
            pieces, first = [], 0
            for rows in shards:
                pieces.append(grads[first : first + rows * count].reshape(count, rows, width))
                first += rows * count
            return jnp.concatenate(pieces, axis=1)

        one = jnp.concatenate(gather_all(pack_one, (shard,) * 3))
        two = [m[None] for m in gather_all(low_attention[3 * shard :], (shard,) * 5)]
        pack = jnp.concatenate([expand_low.transpose(1, 0, 2).reshape(-1, width), shrink_low])
        *expand_all, shrink_all = gather_all(pack, (*(shard,) * blocks, inner_shard))
        three = jnp.stack(expand_all)[:, None], shrink_all[None]

    *saved_one, matrices = forward_self(place, x, target_pos, one, small)
    if small:
        three.chips(saved_one[4])
        two = both_halves(two, *three.arrived)
    norm_one, inv_one, *saved_two, norm_two, inv_two, vec, bias = forward_cross(
        place, x, saved_one[4], source, memory_length, two, given, cross_shards
    )
    three = three.cores(norm_two) if small else three
    sums_three, bias_sum, outputs, dz_two, *grad_three = hidden_step(
        place, three, norm_two, inv_two, cot, vec, bias
    )
    if small:
        keep_three, send_three = reduce_cores(*grad_three)
        dz_two = after(dz_two, keep_three, send_three)
        received_three = send_rows(send_three)
    sums_two, dz_one, memory_grad, *grad_two = backward_cross(
        place, two, dz_two, x, norm_one, inv_one, source, vec, saved_two, saved_one[4],
        (sums_three, bias_sum), cross_shards,
    )
    if small:
        joined_three = reduce_rows(keep_three, received_three, dz_one)
        keep_two, send_two = reduce_cores(grad_two[0], after(grad_two[1], received_three))
        dz_one = after(dz_one, joined_three, keep_two, send_two)
        received_two = send_rows(send_two)
    *heads, grad_keep, grad_send = (
        *backward_self(place, two if small else two[:1], dz_one, x, saved_one, cross_shards),
        *((None,) if not small else ()),
    )
    if small:
        joined_two = reduce_rows(keep_two, received_two, heads[0])
        keep_one, send_one = reduce_cores(grad_keep, after(grad_send, received_two))
        heads = after(tuple(heads), keep_one, send_one)
        received_one = send_rows(send_one)
    input_grad = input_gradient(vec, dz_one, matrices, heads)

    attention = (attention_weights, first_attention, second_attention)
    expand = (expand_weights, first_expand, second_expand)
    shrink = (shrink_weights, first_shrink, second_shrink)
    bias = (expand_bias, first_bias, second_bias)
    vectors = (layer_vectors, first_vectors, second_vectors)
    if small:
        powers = 1.0 - hyper_rates[1:3] ** step_float
        scalars = place, jnp.concatenate([hyper_rates, powers])
        part_three = reduce_line(joined_three)
        part_two = reduce_line(joined_two)
        total_three = reduce_last(after(part_three, heads[0]), input_grad)
        joined_one = reduce_rows(keep_one, received_one, input_grad)
        hidden_new = hidden_adam(scalars, total_three, (*expand, *shrink))
        part_one = reduce_shifts(joined_one, hidden_new[0])
        total_two = reduce_chips(after(part_two, hidden_new[0]), part_one)
        total_rest = jnp.concatenate([reduce_chips(part_one), total_two])
        total_rest = total_rest, lax.ppermute(total_rest, "rep", CORE_SWAP)
        rows = tuple(b[None] for b in bias)
        other_new = adam_call(
            attention_adam_kernel, scalars, total_rest, (*attention, *rows, *vectors)
        )
        new_bias = tuple(b[0] for b in other_new[3:6])
        updated = (*other_new[:3], *hidden_new, *new_bias, *other_new[6:])
    else:
        sums = (sums_two + sums_three)[: layer_vectors.shape[0]]
        flat = jnp.concatenate(
            [
                sums.reshape(-1, count, shard).transpose(1, 0, 2).reshape(count, -1),
                bias_sum.reshape(count, inner_shard),
            ],
            axis=1,
        )
        total_three = reduce_plain(owners(grad_three[0], (*(shard,) * blocks, inner_shard)))
        total_two = reduce_plain(owners(grad_two[0], (shard,) * 5))
        total_one = reduce_plain(owners(grad_keep, (shard,) * 3))
        flat = lax.psum(lax.psum_scatter(flat, "fsdp", scatter_dimension=0), "rep")
        grad_attention = jnp.concatenate([total_one, total_two]).reshape(attention_weights.shape)
        grad_expand = total_three[: blocks * shard].reshape(blocks, shard, width).transpose(1, 0, 2)
        updated = []
        for (now, one_now, two_now), grad, factor in (
            (attention, grad_attention, 1.0),
            (expand, grad_expand.reshape(shard, -1), 1.0),
            (shrink, total_three[blocks * shard :], 1.0),
            (bias, flat[layer_vectors.size :], 0.0),
            (vectors, flat[: layer_vectors.size].reshape(-1, shard), 0.0),
        ):
            updated.extend(adam_update(now, grad, one_now, two_now, hyper_rates, step_float, factor))
    return (outputs[None], input_grad[None], memory_grad[None], *updated)


def solution(mesh):
    rows = ("rep", "fsdp")
    params = (P(None, "fsdp", None), P("fsdp", None), P("fsdp", None), P("fsdp"), P(None, "fsdp"))
    return jax.shard_map(
        functools.partial(per_device, small_mesh(mesh)),
        mesh=mesh,
        in_specs=(
            P(rows, None, None), P(rows, None, None), P(rows), P(rows, None), P(rows, None, None),
            *params, *params, *params, P(), P(),
        ),
        out_specs=(
            P(rows, None, None), P(rows, None, None), P(rows, None, None),
            *(spec for spec in params for _ in range(3)),
        ),
        check_vma=False,
    )
```

```python
import functools

import jax
import jax.numpy as jnp
from jax import lax
from jax.experimental import pallas as pl
from jax.experimental.pallas import tpu as pltpu
from jax.sharding import PartitionSpec as P

BF = jnp.bfloat16
F32 = jnp.float32
HEAD_DIM = 64
PAIR = 128
TILE = 256
MIB = 1 << 20


def dot(left, right, left_dim, right_dim):
    return lax.dot_general(
        left, right, (((left_dim,), (right_dim,)), ((), ())), preferred_element_type=F32
    )


def lanes(size):
    return lax.broadcasted_iota(jnp.int32, (1, size), 1)


def half_masks():
    first = jnp.where(lanes(PAIR) < HEAD_DIM, 1.0, 0.0)
    return first.astype(BF), (1.0 - first).astype(BF)


def rows_at(index, size=TILE):
    return pl.ds(pl.multiple_of(index * size, size), size)


class Mover:
    def __init__(self, sems):
        self.sems, self.used, self.leaving = sems, 0, []

    def take(self, count=1):
        self.used += count
        return self.used - count

    def load(self, source, target):
        copy = pltpu.make_async_copy(source, target, self.sems.at[self.take()])
        copy.start()
        return copy

    def load_rows(self, source, target):
        count = source.shape[0] // TILE
        first = self.take(count)

        def copy(tile):
            rows = rows_at(tile)
            return pltpu.make_async_copy(source.at[rows], target.at[rows], self.sems.at[first + tile])

        for tile in range(count):
            copy(tile).start()
        return lambda tile: copy(tile).wait()

    def store(self, source, target):
        self.leaving.append(self.load(source, target))

    def store_parts(self, source, target, count, where):
        first = self.take(count)

        def copy(part):
            return pltpu.make_async_copy(source.at[where(part)], target.at[where(part)], self.sems.at[first + part])

        self.leaving.extend(copy(part) for part in range(count))
        return lambda part: copy(part).start()

    def store_rows(self, source, target):
        return self.store_parts(source, target, source.shape[0] // TILE, rows_at)

    def finish(self):
        for copy in self.leaving:
            copy.wait()


def columns_at(size):
    return lambda part: (slice(None), rows_at(part, size))


def load_matrices(mover, core, sources, targets, which=None):
    waits, first = [], 0
    for index, target in enumerate(targets):
        if which is not None and index not in which:
            first += target.shape[1]
            continue
        if core is None:
            copies = [mover.load(sources[index], target)]
        else:
            rows, half = target.shape[1], target.shape[2] // 2
            copies = []
            for step, source in enumerate(sources):
                cols = pl.ds(pl.multiple_of(jnp.bitwise_xor(core, step) * half, half), half)
                copies.append(mover.load(source.at[:, first : first + rows, :], target.at[:, :, cols]))
            first += rows
        waits.append(lambda copies=copies: [copy.wait() for copy in copies])
    return waits


def load_hidden(mover, place_ref, packs, expand_ref, shrink_ref):
    core, chip, line, row = place_of(place_ref)
    blocks, _, rows, width = expand_ref.shape
    half = width // 2
    base = packs[0].shape[1] - blocks * rows
    loads = ([], [])
    for index, pack in enumerate(packs):
        core_step, chip_step = (index, 0) if index < 2 else divmod(index - 2, 2)
        cols = pl.ds(pl.multiple_of(jnp.bitwise_xor(core, core_step) * half, half), half)
        if index < 2:
            for block in range(blocks):
                first = base + block * rows
                source = pack.at[:, first : first + rows, :]
                loads[0].append(mover.load(source, expand_ref.at[block, :, :, cols]))
            continue
        side = jnp.bitwise_xor(chip, chip_step)
        for line_step in range(4):
            for row_step in (0, 1):
                owner = lax.rem(line - line_step + 4, 4) * 2 + jnp.bitwise_xor(row, row_step)
                loads[1].append(
                    mover.load(pack.at[line_step, row_step], shrink_ref.at[owner, side, :, :, cols])
                )
    return loads


def whole(ref):
    return ref[...].reshape(-1, ref.shape[-1])


def key_extra(length_limit, count):
    lane = lanes(PAIR) % HEAD_DIM
    extra = jnp.where(lane < 3, 1.0, 0.0)
    if length_limit is None:
        return jnp.broadcast_to(extra, (count, PAIR)).astype(BF)
    row = lax.broadcasted_iota(jnp.int32, (count, PAIR), 0)
    bias = jnp.where(row < length_limit, 0.0, -1e30)
    return jnp.where(lane == 3, bias, extra).astype(BF)


def put_start(pos_ref, start_ref):
    length = start_ref.shape[0]
    query = lax.broadcasted_iota(jnp.int32, (8, length), 1)
    first = (query - pos_ref[...]).astype(F32)
    start_ref[...] = first.T[:, :1].astype(jnp.int32)


def visible(start, first_query, first_key, count):
    key = first_key + lax.broadcasted_iota(jnp.int32, (TILE, count), 1)
    seen = key >= start
    if first_key == first_query:
        query = first_query + lax.broadcasted_iota(jnp.int32, (TILE, count), 0)
        seen = seen & (key <= query)
    return seen


def key_spans(tile, count, causal):
    if not causal:
        return [(0, count)]
    spans = [(0, tile * TILE)] if tile else []
    return spans + [(tile * TILE, TILE)]


def staggered(first, then, count):
    ready = first(0)
    for index in range(count):
        following = first(index + 1) if index + 1 < count else None
        then(index, ready)
        ready = following


class ProbStore:
    def __init__(self, mover, hbm, ref, causal):
        self.hbm, self.ref, self.mover = hbm, ref, mover
        self.tiles = ref.shape[2] // TILE
        self.causal = causal
        self.first = mover.take(2 * self.tiles)

    def views(self, pair, slot, tile):
        rows = slice(tile * TILE, (tile + 1) * TILE)
        keys = slice(0, (tile + 1) * TILE) if self.causal else slice(0, self.ref.shape[3])
        sem = self.mover.sems.at[self.first + slot * self.tiles + tile]
        return self.hbm.at[pair, :, rows, keys], self.ref.at[slot, :, rows, keys], sem

    def copy(self, pair, slot, tile, out):
        far, near, sem = self.views(pair, slot, tile)
        return pltpu.make_async_copy(near, far, sem) if out else pltpu.make_async_copy(far, near, sem)


def two_pairs(pairs, body):
    @pl.loop(0, pairs // 2)
    def _(step):
        for slot in (0, 1):
            body(2 * step + slot, slot, step)


def attend(q_ref, k_ref, v_ref, extra_ref, start_ref, o_ref, store, finished):
    length, count = q_ref.shape[0], k_ref.shape[0]
    causal = start_ref is not None
    masks = half_masks()
    pairs = q_ref.shape[1] // PAIR

    def one_pair(pair, slot, step):
        cols = rows_at(pair, PAIR)

        @pl.when(step > 0)
        def _():
            for tile in range(store.tiles):
                store.copy(pair - 2, slot, tile, True).wait()

        steps = [(tile, side) for tile in range(length // TILE) for side in (0, 1)]
        results = {}

        def scores_of(index):
            tile, side = steps[index]
            rows = slice(tile * TILE, (tile + 1) * TILE)
            queries = q_ref[rows, cols] * masks[side]
            if not causal:
                base = HEAD_DIM * (1 - side)
                queries = jnp.where(lanes(PAIR) == base + 3, 1.0, queries.astype(F32)).astype(BF)
            blocks = []
            for first, size in key_spans(tile, count, causal):
                keys = k_ref[first : first + size, cols]
                if not causal:
                    keys = keys * masks[side] + extra_ref[first : first + size, :] * masks[1 - side]
                scores = dot(queries, keys, 1, 1)
                if causal:
                    seen = visible(start_ref[rows, :], tile * TILE, first, size)
                    scores = jnp.where(seen, scores, -1000000000.0)
                blocks.append(scores)
            return blocks

        def mix(index, score_blocks):
            tile, side = steps[index]
            rows = slice(tile * TILE, (tile + 1) * TILE)
            spans = key_spans(tile, count, causal)
            top = functools.reduce(
                jnp.maximum, [jnp.max(scores, axis=1, keepdims=True) for scores in score_blocks]
            )
            exponents = [jnp.exp(scores - top) for scores in score_blocks]
            inverse = 1.0 / sum(jnp.sum(exponent, axis=1, keepdims=True) for exponent in exponents)
            total = None
            for exponent, (first, size) in zip(exponents, spans):
                probs = (exponent * inverse).astype(BF)
                store.ref[slot, side, rows, first : first + size] = probs
                part = dot(probs, v_ref[first : first + size, cols], 1, 0)
                total = part if total is None else total + part
            results[side] = total
            if side == 1:
                o_ref[rows, cols] = jnp.where(lanes(PAIR) < HEAD_DIM, results[0], results[1]).astype(BF)

        staggered(scores_of, mix, len(steps))
        for tile in range(store.tiles):
            store.copy(pair, slot, tile, True).start()
        for start_store in finished:
            start_store(pair)

    two_pairs(pairs, one_pair)
    for slot in (0, 1):
        for tile in range(store.tiles):
            store.mover.leaving.append(store.copy(pairs - 2 + slot, slot, tile, True))


def load_probs(store, slot):
    for tile in reversed(range(store.tiles)):
        store.copy(slot, slot, tile, False).start()


def attend_back(q_ref, da_ref, inner_ref, k_ref, v_ref, store, dq_ref, dk_ref, dv_ref, dk_sum, dv_sum, values_ref):
    length, count = q_ref.shape[0], k_ref.shape[0]
    masks = half_masks()
    pairs = k_ref.shape[1] // PAIR

    def one_pair(pair, slot, step):
        cols = rows_at(pair, PAIR)
        for tile in range(store.tiles):
            store.copy(pair, slot, tile, False).wait()
        for side in (0, 1):
            values_ref[side] = v_ref[:, cols] * masks[side]
        steps = [(tile, side) for tile in reversed(range(length // TILE)) for side in (0, 1)]
        query_grads = {}

        def place(index):
            tile, side = steps[index]
            size = (tile + 1) * TILE if store.causal else count
            return tile, side, slice(tile * TILE, (tile + 1) * TILE), slice(0, size)

        def collect(ref, tile, side, span, part):
            if tile == length // TILE - 1:
                ref[side, :, span] = part
            else:
                ref[side, :, span] += part

        def value_side(index):
            _, side, rows, span = place(index)
            return dot(da_ref[rows, cols], values_ref[side, span, :], 1, 1)

        def score_side(index, grad_probs):
            tile, side, rows, span = place(index)
            probs = store.ref[slot, side, rows, span]
            collect(dv_sum, tile, side, span, dot(da_ref[rows, cols], probs, 0, 0))
            inner = inner_ref[pair, rows, side : side + 1]
            grad_scores = (probs.astype(F32) * (grad_probs - inner)).astype(BF)
            collect(dk_sum, tile, side, span, dot(q_ref[rows, cols], grad_scores, 0, 0))
            query_grads[side] = dot(grad_scores, k_ref[span, cols], 1, 0)
            if side == 1:
                dq_ref[rows, cols] = (
                    jnp.where(lanes(PAIR) < HEAD_DIM, query_grads[0], query_grads[1]) * HEAD_DIM**-0.5
                ).astype(BF)

        staggered(value_side, score_side, len(steps))
        for sums, out in ((dk_sum, dk_ref), (dv_sum, dv_ref)):
            joined = jnp.concatenate([sums[0, :HEAD_DIM, :], sums[1, HEAD_DIM:, :]], axis=0)
            out[:, cols] = joined.astype(BF).T

        @pl.when(step < pairs // 2 - 1)
        def _():
            for tile in range(store.tiles):
                store.copy(pair + 2, slot, tile, False).start()

    two_pairs(pairs, one_pair)


def norm_rows(summed):
    center = jnp.mean(summed, axis=1, keepdims=True)
    shifted = summed - center
    inverse = lax.rsqrt(jnp.mean(shifted * shifted, axis=1, keepdims=True) + 1e-05)
    return shifted * inverse, inverse


def norm_back(grad_out, normed, inverse, gain):
    scaled = grad_out * gain
    first = jnp.mean(scaled, axis=1, keepdims=True)
    second = jnp.mean(scaled * normed, axis=1, keepdims=True)
    return inverse * (scaled - first - normed * second)


def add_rows(ref, row, values):
    ref[row : row + 1, :] += jnp.sum(values, axis=0, keepdims=True)


def place_of(place_ref):
    rep, place = place_ref[0], place_ref[1]
    return lax.rem(rep, 2), lax.div(rep, 2), lax.div(place, 2), lax.rem(place, 2)


def assemble(place_ref, chunk_refs, all_ref):
    core, chip, line, row = place_of(place_ref)
    width = all_ref.shape[1]
    quarter = chunk_refs[0].shape[3]
    shard = quarter * 4 // 3
    for core_step, chunk_ref in enumerate(chunk_refs):
        for chip_step in (0, 1):
            rep = jnp.bitwise_xor(chip, chip_step) * 2 + jnp.bitwise_xor(core, core_step)
            for line_step in range(4):
                for row_step in (0, 1):
                    owner = lax.rem(line - line_step + 4, 4) * 2 + jnp.bitwise_xor(row, row_step)
                    for piece in range(quarter // 16):
                        stacked = rep * quarter + piece * 16
                        matrix = lax.div(stacked, shard)
                        target = matrix * width + owner * shard + (stacked - matrix * shard)
                        all_ref[pl.ds(pl.multiple_of(target, 16), 16), :] = chunk_ref[
                            chip_step, line_step, row_step, piece * 16 : (piece + 1) * 16, :
                        ]


def assemble_halves(place_ref, mine_ref, other_ref, all_ref, shards):
    core = place_of(place_ref)[0]
    devices, _, half = mine_ref.shape
    for step, ref in ((0, mine_ref), (1, other_ref)):
        cols = pl.ds(pl.multiple_of(jnp.bitwise_xor(core, step) * half, half), half)
        first, target = 0, 0
        for shard in shards:
            for owner in range(devices):
                at = target + owner * shard
                all_ref[at : at + shard, cols] = ref[owner, first : first + shard, :]
            first += shard
            target += shard * devices


def unpack_small(all_ref, base, vec_ref, bias_ref):
    devices = vec_ref.shape[1] // HEAD_DIM
    inner = bias_ref.shape[1] // devices
    for pair in range(devices // 2):
        first = base + 2 * pair * 16
        left = all_ref[first : first + 16, :PAIR].astype(F32)
        right = all_ref[first + 16 : first + 32, :PAIR].astype(F32)
        vec_ref[:, pair * PAIR : (pair + 1) * PAIR] = jnp.where(
            lanes(PAIR) < HEAD_DIM, left, pltpu.roll(right, HEAD_DIM, 1)
        )
    for owner in range(devices):
        rows = all_ref[base + owner * 16 : base + owner * 16 + 16, :inner].astype(F32)
        bias_ref[:, owner * inner : (owner + 1) * inner] = rows[10:11, :]


def self_forward_kernel(staged, *refs):
    if staged:
        place_ref, pos_ref, x_hbm, chunk_hbm, other_hbm = refs[:5]
        refs = refs[5:]
    else:
        pos_ref, x_hbm, all_hbm = refs[:3]
        refs = refs[3:]
    p_hbm, q_hbm, k_hbm, v_hbm, o_hbm = refs[:5]
    refs = refs[5:]
    if staged:
        all_out, refs = refs[0], refs[1:]
    x_ref, all_ref, q_ref, k_ref, v_ref, o_ref, p_ref, start_ref = refs[:8]
    mover = Mover(refs[-1])
    length, width = x_ref.shape
    if staged:
        chunk_refs = refs[8:10]
        loads = [mover.load(a, b) for a, b in zip((chunk_hbm, other_hbm), chunk_refs)]
    else:
        loads = [mover.load(all_hbm, all_ref)]
    x_load = mover.load(x_hbm, x_ref)
    put_start(pos_ref, start_ref)
    for load in loads:
        load.wait()
    if staged:
        assemble(place_ref, chunk_refs, all_ref)
        mover.store(all_ref, all_out)
    x_load.wait()

    @pl.loop(0, length // TILE)
    def _(tile):
        rows = rows_at(tile)
        source = x_ref[rows, :]
        queries = dot(source, all_ref[:width, :], 1, 0).astype(BF)
        q_ref[rows, :] = queries * jnp.asarray(HEAD_DIM**-0.5, BF)
        k_ref[rows, :] = dot(source, all_ref[width : 2 * width, :], 1, 0).astype(BF)
        v_ref[rows, :] = dot(source, all_ref[2 * width :, :], 1, 0).astype(BF)

    mover.store(k_ref, k_hbm)
    mover.store(v_ref, v_hbm)
    mover.store(q_ref, q_hbm)
    finished = (mover.store_parts(o_ref, o_hbm, width // PAIR, columns_at(PAIR)),)
    attend(q_ref, k_ref, v_ref, None, start_ref, o_ref, ProbStore(mover, p_hbm, p_ref, True), finished)
    mover.finish()


def unpack_small(small_ref, vec_ref, bias_ref):
    devices = vec_ref.shape[1] // HEAD_DIM
    inner = bias_ref.shape[1] // devices
    for pair in range(devices // 2):
        left = small_ref[0, 2 * pair, :, :PAIR].astype(F32)
        right = small_ref[0, 2 * pair + 1, :, :PAIR].astype(F32)
        vec_ref[:, pair * PAIR : (pair + 1) * PAIR] = jnp.where(
            lanes(PAIR) < HEAD_DIM, left, pltpu.roll(right, HEAD_DIM, 1)
        )
    for owner in range(devices):
        rows = small_ref[0, owner, :, :inner].astype(F32)
        bias_ref[:, owner * inner : (owner + 1) * inner] = rows[10:11, :]


def cross_forward_kernel(staged, *refs):
    place_ref, core = None, None
    if staged:
        place_ref, refs = refs[0], refs[1:]
        core = place_of(place_ref)[0]
    length_ref, refs = refs[0], refs[1:]
    if staged:
        x_hbm, mixed_hbm, source_hbm, *packs = refs[:5]
        refs = refs[5:]
    else:
        vec_ref, x_hbm, mixed_hbm, source_hbm, *packs = refs[:9]
        refs = refs[9:]
    first_hbm, first_inv_hbm, p_hbm, q_hbm, k_hbm, v_hbm, o_hbm, n_hbm, inv_hbm = refs[:9]
    refs = refs[9:]
    if staged:
        vec_ref, bias_ref, refs = refs[0], refs[1], refs[2:]
    x_ref, mixed_ref, source_ref, first_ref, first_inv_ref, q_ref, k_ref, v_ref, o_ref, n_ref, inv_ref = refs[:11]
    p_ref, extra_ref, *w_refs = refs[11:18]
    mover = Mover(refs[-1])
    length, width = q_ref.shape

    if staged:
        small_ref = refs[18]
        first = 5 * w_refs[0].shape[1]
        small = [
            mover.load(pack.at[:, first : first + 16, :], small_ref.at[jnp.bitwise_xor(core, step)])
            for step, pack in enumerate(packs)
        ]
    source_load = mover.load_rows(source_hbm, source_ref)
    order = (2, 3, 0, 1, 4)
    waits = [None] * 5
    if staged:
        half = width // 2
        shard = w_refs[0].shape[1]
        for index in order:
            copies = []
            for step, pack in enumerate(packs):
                cols = pl.ds(pl.multiple_of(jnp.bitwise_xor(core, step) * half, half), half)
                copies.append(
                    mover.load(pack.at[:, index * shard : (index + 1) * shard, :], w_refs[index].at[:, :, cols])
                )
            waits[index] = lambda copies=copies: [copy.wait() for copy in copies]
    else:
        for index in order:
            waits[index] = mover.load(packs[index], w_refs[index]).wait
    mixed_load = mover.load_rows(mixed_hbm, mixed_ref)
    x_load = mover.load_rows(x_hbm, x_ref)
    extra_ref[...] = key_extra(length_ref[0], k_ref.shape[0])
    waits[2]()
    waits[3]()

    @pl.loop(0, source_ref.shape[0] // TILE)
    def _(tile):
        rows = rows_at(tile)
        source_load(tile)
        source = source_ref[rows, :]
        k_ref[rows, :] = dot(source, whole(w_refs[2]), 1, 0).astype(BF)
        v_ref[rows, :] = dot(source, whole(w_refs[3]), 1, 0).astype(BF)

    mover.store(k_ref, k_hbm)
    mover.store(v_ref, v_hbm)
    if staged:
        for load in small:
            load.wait()
        unpack_small(small_ref, vec_ref, bias_ref)
    waits[0]()
    waits[1]()

    @pl.loop(0, length // TILE)
    def _(tile):
        rows = rows_at(tile)
        mixed_load(tile)
        x_load(tile)
        summed = x_ref[rows, :].astype(F32) * vec_ref[6:7, :] + dot(mixed_ref[rows, :], whole(w_refs[0]), 1, 0)
        normed, inverse = norm_rows(summed)
        first_ref[rows, :] = normed
        first_inv_ref[rows, :] = inverse
        low = (normed * vec_ref[0:1, :] + vec_ref[3:4, :]).astype(BF)
        queries = dot(low, whole(w_refs[1]), 1, 0).astype(BF)
        q_ref[rows, :] = queries * jnp.asarray(HEAD_DIM**-0.5, BF)

    mover.store(first_ref, first_hbm)
    mover.store(first_inv_ref, first_inv_hbm)
    mover.store(q_ref, q_hbm)
    finished = (mover.store_parts(o_ref, o_hbm, width // PAIR, columns_at(PAIR)),)
    attend(q_ref, k_ref, v_ref, extra_ref, None, o_ref, ProbStore(mover, p_hbm, p_ref, False), finished)
    waits[4]()
    n_store, inv_store = mover.store_rows(n_ref, n_hbm), mover.store_rows(inv_ref, inv_hbm)

    @pl.loop(0, length // TILE)
    def _(tile):
        rows = rows_at(tile)
        first_out = first_ref[rows, :] * vec_ref[0:1, :] + vec_ref[3:4, :]
        summed = first_out * vec_ref[7:8, :] + dot(o_ref[rows, :], whole(w_refs[4]), 1, 0)
        normed, inverse = norm_rows(summed)
        n_ref[rows, :] = normed
        inv_ref[rows, :] = inverse
        n_store(tile)
        inv_store(tile)

    mover.finish()


def hidden_kernel(staged, *refs):
    place_ref, core = None, None
    if staged:
        place_ref, refs = refs[0], refs[1:]
        core = place_of(place_ref)[0]
    vec_ref, bias_ref, *packs = refs[: 8 if staged else 4]
    n_hbm, inv_hbm, cot_hbm = refs[len(packs) + 2 : len(packs) + 5]
    refs = refs[len(packs) + 5 :]
    count = 2 if staged else 1
    sums_ref, bias_sum_ref, out_hbm, dz_hbm = refs[:4]
    grad_hbms, refs = refs[4 : 4 + count], refs[4 + count :]
    grad_refs, refs = refs[:count], refs[count:]
    n_ref, inv_ref, cot_ref, out_ref, dz_ref, low_ref, h_ref, du_ref, df_ref, slope_ref, third_ref = refs[:11]
    blocks = bias_ref.shape[1] // vec_ref.shape[1]
    e_ref, s_ref = refs[11:13]
    mover = Mover(refs[-1])
    length, width = n_ref.shape

    n_load = mover.load_rows(n_hbm, n_ref)
    if staged:
        expand_loads, shrink_loads = load_hidden(mover, place_ref, packs, e_ref, s_ref)
    else:
        expand_loads, shrink_loads = [mover.load(packs[0], e_ref)], [mover.load(packs[1], s_ref)]
    cot_load = mover.load_rows(cot_hbm, cot_ref)
    inv_load = mover.load_rows(inv_hbm, inv_ref)
    out_store, dz_store = mover.store_rows(out_ref, out_hbm), mover.store_rows(dz_ref, dz_hbm)
    tiles = [slice(tile * TILE, (tile + 1) * TILE) for tile in range(length // TILE)]
    parts = [slice(block * width, (block + 1) * width) for block in range(blocks)]
    sums = {row: 0.0 for row in (1, 2, 4, 5, 8, 9)}
    bias_sums = [0.0] * blocks

    def add(row, values):
        sums[row] = sums[row] + jnp.sum(values, axis=0, keepdims=True)

    def second_out(rows):
        return n_ref[rows, :] * vec_ref[1:2, :] + vec_ref[4:5, :]

    for tile, rows in enumerate(tiles):
        n_load(tile)
        low_ref[rows, :] = second_out(rows).astype(BF)
    steps = [(block, rows) for block in range(blocks) for rows in tiles]

    def expand(index):
        block, rows = steps[index]
        return dot(low_ref[rows, :], whole(e_ref.at[block]), 1, 0) + bias_ref[:, parts[block]]

    def activate(index, before):
        block, rows = steps[index]
        square = before * before
        tangent = jnp.tanh(before * (0.7978845608028654 + 0.7978845608028654 * 0.044715 * square))
        half = 0.5 * (1.0 + tangent)
        slope_ref[rows, parts[block]] = half + before * (half * (1.0 - tangent)) * (
            0.7978845608028654 + 3.0 * 0.7978845608028654 * 0.044715 * square
        )
        h_ref[rows, parts[block]] = (before * half).astype(BF)

    for load in expand_loads:
        load.wait()
    staggered(expand, activate, len(steps))
    for load in shrink_loads:
        load.wait()
    for tile in range(len(tiles)):
        cot_load(tile)
        inv_load(tile)

    def shrink(tile):
        return dot(h_ref[tiles[tile], :], whole(s_ref), 1, 0)

    def outer_norm(tile, branch_out):
        rows = tiles[tile]
        second = second_out(rows)
        normed, inverse = norm_rows(second * vec_ref[8:9, :] + vec_ref[9:10, :] + branch_out)
        out_ref[rows, :] = (normed * vec_ref[2:3, :] + vec_ref[5:6, :]).astype(BF)
        grad_out = cot_ref[rows, :].astype(F32)
        third = norm_back(grad_out, normed, inverse, vec_ref[2:3, :])
        third_ref[rows, :] = third
        add(2, grad_out * normed)
        add(5, grad_out)
        branch = third.astype(BF)
        df_ref[rows, :] = branch
        add(9, branch.astype(F32))
        add(8, second * third)

    staggered(shrink, outer_norm, len(tiles))
    for tile in range(len(tiles)):
        out_store(tile)

    def shrink_back(index):
        block, rows = steps[index]
        return dot(df_ref[rows, :], whole(s_ref)[parts[block], :], 1, 1)

    def slope_back(index, grad_hidden):
        block, rows = steps[index]
        du = (grad_hidden * slope_ref[rows, parts[block]]).astype(BF)
        du_ref[rows, parts[block]] = du
        bias_sums[block] = bias_sums[block] + jnp.sum(du.astype(F32), axis=0, keepdims=True)

    staggered(shrink_back, slope_back, len(steps))

    def expand_back(tile):
        rows = tiles[tile]
        return sum(dot(du_ref[rows, parts[block]], whole(e_ref.at[block]), 1, 1) for block in range(blocks))

    def inner_norm(tile, grad_expanded):
        rows = tiles[tile]
        grad = vec_ref[8:9, :] * third_ref[rows, :] + grad_expanded
        normed = n_ref[rows, :]
        dz_ref[rows, :] = norm_back(grad, normed, inv_ref[rows, :], vec_ref[1:2, :])
        add(1, grad * normed)
        add(4, grad)

    staggered(expand_back, inner_norm, len(tiles))
    for tile in range(len(tiles)):
        dz_store(tile)
    sums_ref[...] = jnp.zeros_like(sums_ref)
    for row, values in sums.items():
        sums_ref[row : row + 1, :] = values
    for block, values in enumerate(bias_sums):
        bias_sum_ref[:, parts[block]] = values
    for step in reversed(range(count)):
        for block in range(blocks):
            put_grad(grad_refs, step, place_ref, block, low_ref[...], du_ref, block * width)
            put_shrink(grad_refs, step, place_ref, block, blocks, h_ref[:, parts[block]], df_ref)
        mover.store(grad_refs[step], grad_hbms[step])
    mover.finish()


def branch_grads(branch_rows, mixed_weight, o_ref, da_ref, inner_ref):
    width = o_ref.shape[1]
    tiles = [slice(tile * TILE, (tile + 1) * TILE) for tile in range(o_ref.shape[0] // TILE)]
    head = lax.broadcasted_iota(jnp.int32, (width, PAIR), 0) // HEAD_DIM
    picks = jnp.where(head == lax.broadcasted_iota(jnp.int32, (width, PAIR), 1), 1.0, 0.0).astype(BF)

    def project(tile):
        return dot(branch_rows(tile, tiles[tile]), mixed_weight, 1, 1)

    def reduce(tile, mixed_grad):
        rows = tiles[tile]
        low = mixed_grad.astype(BF)
        da_ref[rows, :] = low
        product = low.astype(F32) * o_ref[rows, :].astype(F32)
        high = product.astype(BF)
        rest = (product - high.astype(F32)).astype(BF)
        inner = dot(high, picks, 1, 0) + dot(rest, picks, 1, 0)
        for pair in range(width // PAIR):
            inner_ref[pair, rows, :] = pltpu.roll(inner, (PAIR - 2 * pair) % PAIR, 1) if pair else inner

    staggered(project, reduce, len(tiles))


def put_grad(grad_refs, step, place_ref, index, left, right_ref, first=0):
    width = left.shape[1]
    if place_ref is None:
        grad = dot(left, right_ref[:, first : first + width], 0, 0)
        grad_refs[0][index * width : (index + 1) * width, :] = grad.astype(BF)
        return
    core, _, _, row = place_of(place_ref)
    half = width // 2
    shard = width // 8
    cols = pl.ds(pl.multiple_of(first + jnp.bitwise_xor(core, step) * half, half), half)
    grad = dot(left, right_ref[:, cols], 0, 0).astype(BF).reshape(4, 2, shard, half)
    for side in (0, 1):
        slot = jnp.bitwise_xor(row, side)
        grad_refs[step][slot, :, index * shard : (index + 1) * shard, :] = grad[:, side]


def put_shrink(grad_refs, step, place_ref, block, blocks, left, right_ref):
    width = left.shape[1]
    if place_ref is None:
        first = (blocks + block) * width
        grad_refs[0][first : first + width, :] = dot(left, right_ref[...], 0, 0).astype(BF)
        return
    core, _, _, row = place_of(place_ref)
    half, shard = width // 2, width * blocks // 8
    base = width // 8 * blocks
    cols = pl.ds(pl.multiple_of(jnp.bitwise_xor(core, step) * half, half), half)
    grad = dot(left, right_ref[:, cols], 0, 0).astype(BF).reshape(width // shard, shard, half)
    for part in range(width // shard):
        owner = block * (width // shard) + part
        grad_refs[step][jnp.bitwise_xor(row, owner % 2), owner // 2, base:, :] = grad[part]


def put_small(grad_refs, place_ref, base, sums, bias_sum):
    core, _, _, row = place_of(place_ref)
    half = grad_refs[0].shape[3]
    inner = bias_sum.shape[1] // 8
    index = lax.broadcasted_iota(jnp.int32, (16, half), 0)
    for owner in range(8):
        block = sums[:, owner // 2 * PAIR : (owner // 2 + 1) * PAIR]
        if owner % 2:
            block = pltpu.roll(block, HEAD_DIM, 1)
        block = jnp.concatenate([block, jnp.zeros((16, half - PAIR), F32)], axis=1)
        block = jnp.where(index == 10, bias_sum[:, owner * inner : (owner + 1) * inner], block)
        high = block.astype(BF)
        low = (block - high.astype(F32)).astype(BF)
        slot = jnp.bitwise_xor(row, owner % 2)
        first = (core == 0).astype(F32)
        for step, grad_ref in enumerate(grad_refs):
            is_high = first if step == 0 else 1.0 - first
            mixed = high.astype(F32) * is_high + low.astype(F32) * (1.0 - is_high)
            grad_ref[slot, owner // 2, base : base + 16, :] = mixed.astype(BF)


def cross_backward_kernel(staged, *refs):
    place_ref, core = None, None
    if staged:
        place_ref, refs = refs[0], refs[1:]
        core = place_of(place_ref)[0]
    vec_ref, refs = refs[0], refs[1:]
    if staged:
        sums_three_ref, bias_sum_ref, refs = refs[0], refs[1], refs[2:]
    packs, refs = refs[: 2 if staged else 5], refs[2 if staged else 5 :]
    p_hbm, dz_hbm, x_hbm, first_hbm, inv_hbm, source_hbm, q_hbm, k_hbm, v_hbm, o_hbm, self_o_hbm = refs[:11]
    sums_ref, dfirst_hbm, dsource_hbm = refs[11:14]
    count = 2 if staged else 1
    grad_hbms, refs = refs[14 : 14 + count], refs[14 + count :]
    grad_refs, refs = refs[:count], refs[count:]
    dz_ref, x_ref, first_ref, inv_ref, source_ref, q_ref, k_ref, v_ref, o_ref, self_o_ref = refs[:10]
    dfirst_ref, dsource_ref, *w_refs = refs[10:17]
    low_ref, da_ref, inner_ref, dq_ref, dk_ref, dv_ref, dk_sum, dv_sum, branch_ref, values_ref, p_ref = refs[17:28]
    mover = Mover(refs[-1])
    length, width = dz_ref.shape

    dz_load, o_load = mover.load_rows(dz_hbm, dz_ref), mover.load_rows(o_hbm, o_ref)
    waits = load_matrices(mover, core, packs, w_refs, (4,))
    sums_ref[...] = jnp.zeros_like(sums_ref)
    waits[0]()
    store = ProbStore(mover, p_hbm, p_ref, False)
    load_probs(store, 0)
    middle = [mover.load(a, b) for a, b in ((v_hbm, v_ref), (q_hbm, q_ref), (k_hbm, k_ref))]

    def branch_rows(tile, rows):
        dz_load(tile)
        o_load(tile)
        branch_ref[rows, :] = dz_ref[rows, :].astype(BF)
        return branch_ref[rows, :]

    branch_grads(branch_rows, whole(w_refs[4]), o_ref, da_ref, inner_ref)
    for step in range(count):
        put_grad(grad_refs, step, place_ref, 4, o_ref[...], branch_ref)
    load_probs(store, 1)
    first_load = mover.load_rows(first_hbm, first_ref)
    waits = load_matrices(mover, core, packs, w_refs, (1, 2, 3))
    last = [
        mover.load(a, b)
        for a, b in ((source_hbm, source_ref), (x_hbm, x_ref), (inv_hbm, inv_ref), (self_o_hbm, self_o_ref))
    ]
    for load in middle:
        load.wait()
    attend_back(q_ref, da_ref, inner_ref, k_ref, v_ref, store, dq_ref, dk_ref, dv_ref, dk_sum, dv_sum, values_ref)
    for load in last:
        load.wait()
    for wait in waits:
        wait()
    for tile in range(length // TILE):
        first_load(tile)

    dsource_store = mover.store_rows(dsource_ref, dsource_hbm)
    dfirst_store = mover.store_rows(dfirst_ref, dfirst_hbm)
    tiles = [slice(tile * TILE, (tile + 1) * TILE) for tile in range(length // TILE)]
    key_tiles = [slice(tile * TILE, (tile + 1) * TILE) for tile in range(source_ref.shape[0] // TILE)]
    sums = {row: 0.0 for row in (0, 3, 6, 7)}

    def add(row, values):
        sums[row] = sums[row] + jnp.sum(values, axis=0, keepdims=True)

    def source_grad(tile):
        rows = key_tiles[tile]
        dsource_ref[rows, :] = dot(dk_ref[rows, :], whole(w_refs[2]), 1, 1) + dot(
            dv_ref[rows, :], whole(w_refs[3]), 1, 1
        )

    def put_keys(step):
        put_grad(grad_refs, step, place_ref, 2, source_ref[...], dk_ref)
        put_grad(grad_refs, step, place_ref, 3, source_ref[...], dv_ref)

    products = [functools.partial(source_grad, tile) for tile in range(len(key_tiles))]
    products += [functools.partial(put_keys, step) for step in range(count)]

    def query_back(tile):
        product = dot(dq_ref[tiles[tile], :], whole(w_refs[1]), 1, 1)
        for run in products[tile :: len(tiles)]:
            run()
        return product

    def first_norm(tile, product):
        rows = tiles[tile]
        grad = dz_ref[rows, :]
        dx = product + vec_ref[7:8, :] * grad
        normed = first_ref[rows, :]
        first_out = normed * vec_ref[0:1, :] + vec_ref[3:4, :]
        low_ref[rows, :] = first_out.astype(BF)
        add(7, first_out * grad)
        dfirst = norm_back(dx, normed, inv_ref[rows, :], vec_ref[0:1, :])
        dfirst_ref[rows, :] = dfirst
        add(0, dx * normed)
        add(3, dx)
        add(6, x_ref[rows, :].astype(F32) * dfirst)
        branch_ref[rows, :] = dfirst.astype(BF)

    staggered(query_back, first_norm, len(tiles))
    for tile in range(len(key_tiles)):
        dsource_store(tile)
    for tile in range(len(tiles)):
        dfirst_store(tile)
    for row, values in sums.items():
        sums_ref[row : row + 1, :] = values

    if staged:
        put_small(grad_refs, place_ref, 5 * (width // 8), sums_ref[...] + sums_three_ref[...], bias_sum_ref[...])
    for step in reversed(range(count)):
        put_grad(grad_refs, step, place_ref, 1, low_ref[...], dq_ref)
        put_grad(grad_refs, step, place_ref, 0, self_o_ref[...], branch_ref)
        mover.store(grad_refs[step], grad_hbms[step])
    mover.finish()


def self_backward_kernel(staged, *refs):
    place_ref, core = None, None
    if staged:
        place_ref, refs = refs[0], refs[1:]
        core = place_of(place_ref)[0]
    count = 2 if staged else 1
    packs, refs = refs[:count], refs[count:]
    p_hbm, dz_hbm, x_hbm, q_hbm, k_hbm, v_hbm, o_hbm, *head_hbms = refs[:10]
    grad_hbms, refs = refs[10 : 10 + count], refs[10 + count :]
    grad_refs, refs = refs[:count], refs[count:]
    dz_ref, x_ref, q_ref, k_ref, v_ref, o_ref, w_ref = refs[:7]
    da_ref, inner_ref, dq_ref, dk_ref, dv_ref, dk_sum, dv_sum, values_ref, p_ref = refs[7:16]
    mover = Mover(refs[-1])
    length, width = dz_ref.shape

    dz_load = mover.load_rows(dz_hbm, dz_ref)
    waits = load_matrices(mover, core, packs, (w_ref,))
    o_load = mover.load_rows(o_hbm, o_ref)
    waits[0]()
    store = ProbStore(mover, p_hbm, p_ref, True)
    load_probs(store, 0)
    middle = [mover.load(a, b) for a, b in ((v_hbm, v_ref), (q_hbm, q_ref), (k_hbm, k_ref))]

    def branch_rows(tile, rows):
        dz_load(tile)
        o_load(tile)
        return dz_ref[rows, :].astype(BF)

    branch_grads(branch_rows, whole(w_ref), o_ref, da_ref, inner_ref)
    load_probs(store, 1)
    x_load = mover.load(x_hbm, x_ref)
    for load in middle:
        load.wait()
    attend_back(q_ref, da_ref, inner_ref, k_ref, v_ref, store, dq_ref, dk_ref, dv_ref, dk_sum, dv_sum, values_ref)
    for near, far in zip((dq_ref, dk_ref, dv_ref), head_hbms):
        mover.store(near, far)
    x_load.wait()
    for step in reversed(range(count)):
        for index, grads in enumerate((dq_ref, dk_ref, dv_ref)):
            put_grad(grad_refs, step, place_ref, index, x_ref[...], grads)
        mover.store(grad_refs[step], grad_hbms[step])
    mover.finish()


def input_grad_kernel(vec_ref, dz_hbm, all_hbm, dq_hbm, dk_hbm, dv_hbm, dx_hbm, *refs):
    dz_ref, all_ref, dq_ref, dk_ref, dv_ref, dx_ref, sems = refs
    mover = Mover(sems)
    width = dz_ref.shape[1]
    all_load = mover.load(all_hbm, all_ref)
    heads = (dq_ref, dk_ref, dv_ref)
    loads = [mover.load_rows(a, b) for a, b in zip((dq_hbm, dk_hbm, dv_hbm), heads)]
    loads.append(mover.load_rows(dz_hbm, dz_ref))
    dx_store = mover.store_rows(dx_ref, dx_hbm)
    all_load.wait()

    @pl.loop(0, dz_ref.shape[0] // TILE)
    def _(tile):
        rows = rows_at(tile)
        for load in loads:
            load(tile)
        dx = vec_ref[6:7, :] * dz_ref[rows, :]
        for index, grads in enumerate(heads):
            dx = dx + dot(grads[rows, :], all_ref[index * width : (index + 1) * width, :], 1, 1)
        dx_ref[rows, :] = dx
        dx_store(tile)

    mover.finish()


def call(kernel, args, outs, scratch, limit, flops, smem=(), near=(), near_outs=(), copies=0):
    spaces = [pltpu.SMEM if i in smem else pltpu.VMEM if i in near else pl.ANY for i in range(len(args))]
    out_spaces = [pltpu.VMEM if i in near_outs else pl.ANY for i in range(len(outs))]
    buffers = [pltpu.VMEM(shape, kind) for shape, kind in scratch]
    if copies:
        buffers.append(pltpu.SemaphoreType.DMA((copies,)))
    return pl.pallas_call(
        kernel,
        out_shape=[jax.ShapeDtypeStruct(shape, kind) for shape, kind in outs],
        in_specs=[pl.BlockSpec(memory_space=space) for space in spaces],
        out_specs=[pl.BlockSpec(memory_space=space) for space in out_spaces],
        scratch_shapes=buffers,
        compiler_params=pltpu.CompilerParams(vmem_limit_bytes=(63 if copies else limit) * MIB),
        cost_estimate=pl.CostEstimate(flops=flops, bytes_accessed=16 * MIB, transcendentals=0),
    )(*args)


def like(*arrays):
    return [(a.shape, a.dtype) for a in arrays]


def prob_shape(queries, keys, width):
    return (width // PAIR, 2, queries, keys), BF


def forward_self(place, x, pos, pack, staged):
    length, width = x.shape
    low = ((length, width), BF)
    outs = [prob_shape(length, length, width), low, low, low, low]
    matrices = ((3 * width, width), BF)
    scratch = [low, matrices, low, low, low, low, ((2, 2, length, length), BF), ((length, 1), jnp.int32)]
    if staged:
        return call(
            functools.partial(self_forward_kernel, True),
            (place, pos, x, *pack),
            [*outs, matrices],
            [*scratch, *like(*pack)],
            40, 10**10, smem=(0,), near=(1,), copies=24,
        )
    results = call(
        functools.partial(self_forward_kernel, False),
        (pos, x, pack), outs, scratch, 40, 10**10, near=(0,), copies=24,
    )
    return (*results, pack)


def matrix_buffers(shards, width):
    return [((8 if rows < width else 1, rows, width), BF) for rows in shards]


def forward_cross(place, x, mixed, source, count, packs, given, shards):
    length, width = x.shape
    keys = source.shape[0]
    low, full, column, key_low = ((length, width), BF), ((length, width), F32), ((length, 1), F32), ((keys, width), BF)
    outs = [full, column, prob_shape(length, keys, width), low, key_low, key_low, low, full, column]
    near = [full, column, low, key_low, key_low, low, full, column]
    scratch = [low, low, key_low, *near, ((2, 2, length, keys), BF), ((keys, PAIR), BF)]
    if place is not None:
        return call(
            functools.partial(cross_forward_kernel, True),
            (place, count, x, mixed, source, *packs),
            [*outs, ((16, width), F32), ((1, 4 * width), F32)],
            [*scratch, *matrix_buffers(shards, width), ((2, 8, 16, width // 2), BF)],
            44, 10**10, smem=(0, 1), near_outs=(9, 10), copies=64,
        )
    vec, bias = given
    results = call(
        functools.partial(cross_forward_kernel, False),
        (count, vec, x, mixed, source, *packs),
        outs, [*scratch, *like(*packs)],
        44, 10**10, smem=(0,), near=(1,), copies=64,
    )
    return (*results, vec, bias)


def grad_outs(rows, width, staged):
    return [((2, 4, rows, width // 2), BF)] * 2 if staged else [((rows, width), BF)]


def hidden_step(place, packs, normed, inverse, cot, vec, bias):
    length, width = normed.shape
    inner = bias.shape[1]
    blocks = inner // width
    staged = place is not None
    low, full = ((length, width), BF), ((length, width), F32)
    grads = grad_outs(2 * inner // 8 if staged else 2 * inner, width, staged)
    args = (vec, bias, *packs, normed, inverse, cot)
    matrices = like(*packs)
    if staged:
        rows = width // 8
        matrices = [((blocks, 8, rows, width), BF), ((8, 2, blocks, rows // 2, width), BF)]
    return call(
        functools.partial(hidden_kernel, staged),
        (place, *args) if staged else args,
        [((16, width), F32), ((1, inner), F32), low, full, *grads],
        [*grads, *like(normed, inverse, cot), low, full, low, ((length, inner), BF), ((length, inner), BF), low,
         ((length, inner), F32), full, *matrices],
        44, 2 * 10**10, smem=(0,) if staged else (), near=(1, 2) if staged else (0, 1), near_outs=(0, 1),
        copies=96,
    )


def backward_cross(place, packs, dz, x, normed, inverse, source, vec, saved, mixed, small, shards):
    length, width = dz.shape
    keys = source.shape[0]
    staged = place is not None
    probs, *saved = saved
    arrays = (dz, x, normed, inverse, source, *saved, mixed)
    low, key_low, sums = ((length, width), BF), ((keys, width), BF), ((2, PAIR, keys), F32)
    grads = grad_outs(5 * width // 8 + 16 if staged else 5 * width, width, staged)
    full, key_full = ((length, width), F32), ((keys, width), F32)
    return call(
        functools.partial(cross_backward_kernel, staged),
        (place, vec, *small, *packs, probs, *arrays) if staged else (vec, *packs, probs, *arrays),
        [((16, width), F32), full, key_full, *grads],
        [*grads, *like(*arrays), full, key_full, *(matrix_buffers(shards, width) if staged else like(*packs)),
         low, low, ((width // PAIR, length, PAIR), F32), low, key_low, key_low, sums, sums, low, ((2, keys, PAIR), BF),
         ((2, 2, length, keys), BF)],
        48, 2 * 10**10, smem=(0,) if staged else (), near=(1, 2, 3) if staged else (0,), near_outs=(0,), copies=72,
    )


def backward_self(place, packs, dz, x, saved, shards):
    length, width = dz.shape
    staged = place is not None
    probs, *saved = saved
    arrays = (dz, x, *saved)
    low, sums = ((length, width), BF), ((2, PAIR, length), F32)
    grads = grad_outs(3 * width // 8 if staged else 3 * width, width, staged)
    first = matrix_buffers(shards[:1], width) if staged else like(*packs)
    return call(
        functools.partial(self_backward_kernel, staged),
        (place, *packs, probs, *arrays) if staged else (*packs, probs, *arrays),
        [low, low, low, *grads],
        [*grads, *like(*arrays), *first, low, ((width // PAIR, length, PAIR), F32), low, low, low, sums, sums,
         ((2, length, PAIR), BF), ((2, 2, length, length), BF)],
        48, 2 * 10**10, smem=(0,) if staged else (), copies=64,
    )


def input_gradient(vec, dz, matrices, heads):
    arrays = (dz, matrices, *heads)
    return call(
        input_grad_kernel, (vec, *arrays), like(dz), [*like(*arrays), *like(dz)], 40, 2 * 10**9, near=(0,), copies=24
    )[0]


def adam_step(settings_ref, now, grad, one, two, decay):
    beta_one, beta_two = settings_ref[1], settings_ref[2]
    first = beta_one * one + (1.0 - beta_one) * grad
    second = beta_two * two + (1.0 - beta_two) * grad * grad
    change = (first / settings_ref[4]) / (jnp.sqrt(second / settings_ref[5]) + 1e-08)
    if decay:
        change = change + settings_ref[3] * now
    return now - settings_ref[0] * change, first, second


def store_step(refs, where, results):
    for ref, value in zip(refs, results):
        ref[where] = value


def hidden_adam_kernel(place_ref, settings_ref, *refs):
    core = place_of(place_ref)[0]
    hbms, new_hbms, refs = refs[:8], refs[8:14], refs[14:]
    mine_ref, other_ref, *params = refs[:8]
    news, mover = refs[8:14], Mover(refs[-1])
    loads = [mover.load(a, b) for a, b in zip(hbms, refs[:8])]
    expand, shrink = params[0:3], params[3:6]
    half = mine_ref.shape[1]
    shard = expand[0].shape[0]
    blocks = expand[0].shape[1] // (2 * half)
    for load in loads[:5]:
        load.wait()
    sides = [(jnp.bitwise_xor(core, step) * half, ref) for step, ref in ((0, mine_ref), (1, other_ref))]
    for side, ref in sides:
        for block in range(blocks):
            where = (slice(None), pl.ds(pl.multiple_of(block * 2 * half + side, half), half))
            grad = ref[block * shard : (block + 1) * shard, :]
            now, one, two = (r[where] for r in expand)
            store_step(news[:3], where, adam_step(settings_ref, now, grad, one, two, True))
    for load in loads[5:]:
        load.wait()
    for near, far in zip(news[:3], new_hbms[:3]):
        mover.store(near, far)
    for side, ref in sides:
        where = (slice(None), pl.ds(pl.multiple_of(side, half), half))
        now, one, two = (r[where] for r in shrink)
        store_step(news[3:], where, adam_step(settings_ref, now, ref[blocks * shard :, :], one, two, True))
    for near, far in zip(news[3:], new_hbms[3:]):
        mover.store(near, far)
    mover.finish()


def attention_adam_kernel(place_ref, settings_ref, mine_ref, other_ref, *refs):
    core = place_of(place_ref)[0]
    matrices, bias, vectors = refs[0:3], refs[3:6], refs[6:9]
    new_matrices, new_bias, new_vectors = refs[9:12], refs[12:15], refs[15:18]
    half = mine_ref.shape[1]
    shard = matrices[0].shape[1]
    for step, ref in ((0, mine_ref), (1, other_ref)):
        cols = pl.ds(pl.multiple_of(jnp.bitwise_xor(core, step) * half, half), half)
        for index in range(8):
            where = (index, slice(None), cols)
            now, one, two = (r[where] for r in matrices)
            grad = ref[index * shard : (index + 1) * shard, :]
            store_step(new_matrices, where, adam_step(settings_ref, now, grad, one, two, True))
    small = mine_ref[8 * shard :, :] + other_ref[8 * shard :, :]
    for group, new, grad in (
        (bias, new_bias, small[10:11, : bias[0].shape[1]]),
        (vectors, new_vectors, small[:10, : vectors[0].shape[1]]),
    ):
        now, one, two = (r[...] for r in group)
        store_step(new, ..., adam_step(settings_ref, now, grad, one, two, False))


def hidden_adam(scalars, grads, params):
    return call(
        hidden_adam_kernel, (*scalars, *grads, *params), like(*params), [*like(*grads), *like(*params), *like(*params)],
        40, 10**9, smem=(0, 1), copies=16,
    )


def adam_call(kernel, scalars, grads, params):
    return call(
        kernel, (*scalars, *grads, *params), [(p.shape, F32) for p in params], [], 32, 10**7, smem=(0, 1),
        near=range(2, 2 + len(grads) + len(params)), near_outs=range(len(params)),
    )


CORE_SWAP = [(0, 1), (1, 0), (2, 3), (3, 2)]
CHIP_SWAP = [(0, 2), (2, 0), (1, 3), (3, 1)]
ROW_SWAP = [(i, i ^ 1) for i in range(8)]


LINES = [[0, 2, 4, 6], [1, 3, 5, 7]]


def line_shift(step):
    return [(2 * z + y, 2 * ((z + step) % 4) + y) for z in range(4) for y in (0, 1)]


def small_mesh(mesh):
    return mesh.shape["rep"] == 4 and mesh.shape["fsdp"] == 8


class StagedGather:
    def rows(self, mine, done):
        self.mine = mine
        self.other = lax.ppermute(after(mine, done), "fsdp", ROW_SWAP)

    def line(self, done):
        self.pair = after(jnp.stack([self.mine, self.other]), done)
        self.received = [lax.ppermute(self.pair, "fsdp", line_shift(step)) for step in (1, 2, 3)]

    def chips(self, done):
        self.arrived = after(tuple(self.received), done)
        self.part = jnp.stack([self.pair, *self.arrived])
        self.far = lax.ppermute(self.part, "rep", CHIP_SWAP)

    def cores(self, done):
        far = after(self.far, done)
        part = after(self.part, done)
        return part, far, lax.ppermute(part, "rep", CORE_SWAP), lax.ppermute(far, "rep", CORE_SWAP)


def gather_staged(pack):
    quarter = pack.shape[0] // 4
    mine = lax.dynamic_slice_in_dim(pack, lax.axis_index("rep") * quarter, quarter, 0)
    pair = jnp.stack([mine, lax.ppermute(mine, "fsdp", ROW_SWAP)])
    part = jnp.stack([pair] + [lax.ppermute(pair, "fsdp", line_shift(step)) for step in (1, 2, 3)])
    both = jnp.stack([part, lax.ppermute(part, "rep", CHIP_SWAP)])
    return pair, part, both


def after(value, *done):
    return lax.optimization_barrier((value, *done))[0]


def half_columns(pack):
    half = pack.shape[1] // 2
    return lax.dynamic_slice_in_dim(pack, lax.axis_index("rep") % 2 * half, half, 1)


def gather_half(mine):
    return lax.all_gather(mine, "fsdp", axis=0)


def both_halves(mine, *done):
    mine = after(mine, *done)
    return mine, lax.ppermute(mine, "rep", CORE_SWAP)


def reduce_cores(keep, send):
    received = lax.ppermute(send, "rep", CORE_SWAP)
    return keep[0] + received[0], keep[1] + received[1]


def send_rows(send):
    return lax.ppermute(send, "fsdp", ROW_SWAP)


def reduce_rows(keep, received, done):
    return keep + after(received, done)


def reduce_chips(part, *done):
    return part.astype(F32) + after(lax.ppermute(part, "rep", CHIP_SWAP), *done).astype(F32)


def reduce_last(part, *done):
    total = reduce_chips(part, *done)
    return total, lax.ppermute(total, "rep", CORE_SWAP)


def reduce_line(joined):
    part = lax.psum_scatter(joined, "fsdp", scatter_dimension=0, axis_index_groups=LINES)
    return part.reshape(joined.shape[1:])


def reduce_shifts(joined, done):
    line = lax.axis_index("fsdp") // 2
    total = lax.dynamic_index_in_dim(joined, line, 0, False).astype(F32)
    for step in (1, 2, 3):
        away = lax.dynamic_index_in_dim(joined, (line + step) % 4, 0, False)
        total = total + after(lax.ppermute(away, "fsdp", line_shift(step)), done).astype(F32)
    return total.astype(BF)


def reduce_plain(grads):
    return lax.psum(lax.psum_scatter(grads, "fsdp", scatter_dimension=0), "rep").astype(F32)


def adam_update(weight_now, gradient, moment_one, moment_two, settings, step_float, factor):
    learn_rate, beta_one, beta_two, decay_rate = settings[0], settings[1], settings[2], settings[3]
    first_new = beta_one * moment_one + (1.0 - beta_one) * gradient
    second_new = beta_two * moment_two + (1.0 - beta_two) * gradient * gradient
    first_hat = first_new / (1.0 - beta_one**step_float)
    second_hat = second_new / (1.0 - beta_two**step_float)
    change = first_hat / (jnp.sqrt(second_hat) + 1e-08) + factor * decay_rate * weight_now
    return (weight_now - learn_rate * change, first_new, second_new)


def per_device(
    small, inputs, memory, memory_length, target_pos, cotangent,
    attention_weights, expand_weights, shrink_weights, expand_bias, layer_vectors,
    first_attention, first_expand, first_shrink, first_bias, first_vectors,
    second_attention, second_expand, second_shrink, second_bias, second_vectors,
    hyper_rates, step_count,
):
    length, width = inputs.shape[1:]
    shard = attention_weights.shape[1]
    count = width // shard
    inner_shard = shrink_weights.shape[0]
    blocks = inner_shard // shard
    low_attention = attention_weights.astype(BF).reshape(8 * shard, width)
    pack_one = low_attention[: 3 * shard]
    expand_low = expand_weights.astype(BF).reshape(shard, blocks, width)
    shrink_low = shrink_weights.astype(BF)
    x, source, cot = inputs[0], memory[0], cotangent[0]
    step_float = step_count.astype(F32)

    if small:
        place = jnp.stack([lax.axis_index("rep"), lax.axis_index("fsdp")]).astype(jnp.int32)
        small_rows = jnp.concatenate(
            [
                jnp.pad(layer_vectors, ((0, 0), (0, inner_shard - shard))),
                expand_bias[None],
                jnp.zeros((5, inner_shard), F32),
            ]
        )
        small_rows = jnp.pad(small_rows, ((0, 0), (0, width - inner_shard))).astype(BF)
        expand_rows = expand_low.transpose(1, 0, 2).reshape(-1, width)
        pack_two = jnp.concatenate([low_attention[3 * shard :], small_rows, expand_rows])
        two = gather_half(half_columns(pack_two))
        pair_one, part_one, one = gather_staged(pack_one)
        core, chip = place[0] % 2, place[0] // 2
        quarter = lax.dynamic_slice(
            shrink_low.reshape(2, blocks, shard // 2, width),
            (chip, 0, 0, core * (width // 2)),
            (1, blocks, shard // 2, width // 2),
        )
        three = StagedGather()
        three.rows(quarter[0], pair_one)
        one = both_halves(one, three.other)
        three.line(part_one)
        given = None
        cross_shards = (shard,) * 5
    else:
        place, cross_shards = None, None
        flat = jnp.concatenate([layer_vectors.reshape(-1), expand_bias]).astype(BF)
        flat = lax.all_gather(flat, "fsdp", axis=0).astype(F32)
        vector_size = layer_vectors.size
        vec = flat[:, :vector_size].reshape(count, -1, shard).transpose(1, 0, 2).reshape(-1, width)
        given = jnp.pad(vec, ((0, 16 - vec.shape[0]), (0, 0))), flat[:, vector_size:].reshape(1, -1)

        def gather_all(pack, shards):
            full = lax.all_gather(pack, "fsdp", axis=0)
            pieces, first = [], 0
            for rows in shards:
                pieces.append(full[:, first : first + rows].reshape(-1, width))
                first += rows
            return pieces

        def owners(grads, shards):
            pieces, first = [], 0
            for rows in shards:
                pieces.append(grads[first : first + rows * count].reshape(count, rows, width))
                first += rows * count
            return jnp.concatenate(pieces, axis=1)

        one = jnp.concatenate(gather_all(pack_one, (shard,) * 3))
        two = [m[None] for m in gather_all(low_attention[3 * shard :], (shard,) * 5)]
        pack = jnp.concatenate([expand_low.transpose(1, 0, 2).reshape(-1, width), shrink_low])
        *expand_all, shrink_all = gather_all(pack, (*(shard,) * blocks, inner_shard))
        three = jnp.stack(expand_all)[:, None], shrink_all[None]

    *saved_one, matrices = forward_self(place, x, target_pos, one, small)
    if small:
        three.chips(saved_one[4])
        two = both_halves(two, *three.arrived)
    norm_one, inv_one, *saved_two, norm_two, inv_two, vec, bias = forward_cross(
        place, x, saved_one[4], source, memory_length, two, given, cross_shards
    )
    three = (*two, *three.cores(norm_two)) if small else three
    sums_three, bias_sum, outputs, dz_two, *grad_three = hidden_step(
        place, three, norm_two, inv_two, cot, vec, bias
    )
    if small:
        keep_three, send_three = reduce_cores(*grad_three)
        dz_two = after(dz_two, keep_three, send_three)
        received_three = send_rows(send_three)
    sums_two, dz_one, memory_grad, *grad_two = backward_cross(
        place, two, dz_two, x, norm_one, inv_one, source, vec, saved_two, saved_one[4],
        (sums_three, bias_sum), cross_shards,
    )
    if small:
        joined_three = reduce_rows(keep_three, received_three, dz_one)
        keep_two, send_two = reduce_cores(grad_two[0], after(grad_two[1], received_three))
        dz_one = after(dz_one, joined_three, keep_two, send_two)
        received_two = send_rows(send_two)
    *heads, grad_keep, grad_send = (
        *backward_self(place, two if small else two[:1], dz_one, x, saved_one, cross_shards),
        *((None,) if not small else ()),
    )
    if small:
        joined_two = reduce_rows(keep_two, received_two, heads[0])
        keep_one, send_one = reduce_cores(grad_keep, after(grad_send, received_two))
        heads = after(tuple(heads), keep_one, send_one)
        received_one = send_rows(send_one)
    input_grad = input_gradient(vec, dz_one, matrices, heads)

    attention = (attention_weights, first_attention, second_attention)
    expand = (expand_weights, first_expand, second_expand)
    shrink = (shrink_weights, first_shrink, second_shrink)
    bias = (expand_bias, first_bias, second_bias)
    vectors = (layer_vectors, first_vectors, second_vectors)
    if small:
        powers = 1.0 - hyper_rates[1:3] ** step_float
        scalars = place, jnp.concatenate([hyper_rates, powers])
        part_three = reduce_line(joined_three)
        part_two = reduce_line(joined_two)
        total_three = reduce_last(after(part_three, heads[0]), input_grad)
        joined_one = reduce_rows(keep_one, received_one, input_grad)
        hidden_new = hidden_adam(scalars, total_three, (*expand, *shrink))
        part_one = reduce_shifts(joined_one, hidden_new[0])
        total_two = reduce_chips(after(part_two, hidden_new[0]), part_one)
        total_rest = jnp.concatenate([reduce_chips(part_one), total_two])
        total_rest = total_rest, lax.ppermute(total_rest, "rep", CORE_SWAP)
        rows = tuple(b[None] for b in bias)
        other_new = adam_call(
            attention_adam_kernel, scalars, total_rest, (*attention, *rows, *vectors)
        )
        new_bias = tuple(b[0] for b in other_new[3:6])
        updated = (*other_new[:3], *hidden_new, *new_bias, *other_new[6:])
    else:
        sums = (sums_two + sums_three)[: layer_vectors.shape[0]]
        flat = jnp.concatenate(
            [
                sums.reshape(-1, count, shard).transpose(1, 0, 2).reshape(count, -1),
                bias_sum.reshape(count, inner_shard),
            ],
            axis=1,
        )
        total_three = reduce_plain(owners(grad_three[0], (*(shard,) * blocks, inner_shard)))
        total_two = reduce_plain(owners(grad_two[0], (shard,) * 5))
        total_one = reduce_plain(owners(grad_keep, (shard,) * 3))
        flat = lax.psum(lax.psum_scatter(flat, "fsdp", scatter_dimension=0), "rep")
        grad_attention = jnp.concatenate([total_one, total_two]).reshape(attention_weights.shape)
        grad_expand = total_three[: blocks * shard].reshape(blocks, shard, width).transpose(1, 0, 2)
        updated = []
        for (now, one_now, two_now), grad, factor in (
            (attention, grad_attention, 1.0),
            (expand, grad_expand.reshape(shard, -1), 1.0),
            (shrink, total_three[blocks * shard :], 1.0),
            (bias, flat[layer_vectors.size :], 0.0),
            (vectors, flat[: layer_vectors.size].reshape(-1, shard), 0.0),
        ):
            updated.extend(adam_update(now, grad, one_now, two_now, hyper_rates, step_float, factor))
    return (outputs[None], input_grad[None], memory_grad[None], *updated)


def solution(mesh):
    rows = ("rep", "fsdp")
    params = (P(None, "fsdp", None), P("fsdp", None), P("fsdp", None), P("fsdp"), P(None, "fsdp"))
    return jax.shard_map(
        functools.partial(per_device, small_mesh(mesh)),
        mesh=mesh,
        in_specs=(
            P(rows, None, None), P(rows, None, None), P(rows), P(rows, None), P(rows, None, None),
            *params, *params, *params, P(), P(),
        ),
        out_specs=(
            P(rows, None, None), P(rows, None, None), P(rows, None, None),
            *(spec for spec in params for _ in range(3)),
        ),
        check_vma=False,
    )
```

```python
import functools

import jax
import jax.numpy as jnp
from jax import lax
from jax.experimental import pallas as pl
from jax.experimental.pallas import tpu as pltpu
from jax.sharding import PartitionSpec as P

BF = jnp.bfloat16
F32 = jnp.float32
HEAD_DIM = 64
PAIR = 128
TILE = 256
MIB = 1 << 20


def dot(left, right, left_dim, right_dim):
    return lax.dot_general(
        left, right, (((left_dim,), (right_dim,)), ((), ())), preferred_element_type=F32
    )


def lanes(size):
    return lax.broadcasted_iota(jnp.int32, (1, size), 1)


def half_masks():
    first = jnp.where(lanes(PAIR) < HEAD_DIM, 1.0, 0.0)
    return first.astype(BF), (1.0 - first).astype(BF)


def rows_at(index, size=TILE):
    return pl.ds(pl.multiple_of(index * size, size), size)


class Mover:
    def __init__(self, sems):
        self.sems, self.used, self.leaving = sems, 0, []

    def take(self, count=1):
        self.used += count
        return self.used - count

    def load(self, source, target):
        copy = pltpu.make_async_copy(source, target, self.sems.at[self.take()])
        copy.start()
        return copy

    def load_rows(self, source, target):
        count = source.shape[0] // TILE
        first = self.take(count)

        def copy(tile):
            rows = rows_at(tile)
            return pltpu.make_async_copy(source.at[rows], target.at[rows], self.sems.at[first + tile])

        for tile in range(count):
            copy(tile).start()
        return lambda tile: copy(tile).wait()

    def store(self, source, target):
        self.leaving.append(self.load(source, target))

    def store_parts(self, source, target, count, where):
        first = self.take(count)

        def copy(part):
            return pltpu.make_async_copy(source.at[where(part)], target.at[where(part)], self.sems.at[first + part])

        self.leaving.extend(copy(part) for part in range(count))
        return lambda part: copy(part).start()

    def store_rows(self, source, target):
        return self.store_parts(source, target, source.shape[0] // TILE, rows_at)

    def finish(self):
        for copy in self.leaving:
            copy.wait()


def columns_at(size):
    return lambda part: (slice(None), rows_at(part, size))


def load_matrices(mover, core, sources, targets, which=None):
    waits, first = [], 0
    for index, target in enumerate(targets):
        if which is not None and index not in which:
            first += target.shape[1]
            continue
        if core is None:
            copies = [mover.load(sources[index], target)]
        else:
            rows, half = target.shape[1], target.shape[2] // 2
            copies = []
            for step, source in enumerate(sources):
                cols = pl.ds(pl.multiple_of(jnp.bitwise_xor(core, step) * half, half), half)
                copies.append(mover.load(source.at[:, first : first + rows, :], target.at[:, :, cols]))
            first += rows
        waits.append(lambda copies=copies: [copy.wait() for copy in copies])
    return waits


def load_quarters(mover, place_ref, packs, expand_ref, shrink_ref):
    core, chip, line, row = place_of(place_ref)
    half, cut = expand_ref.shape[3] // 2, expand_ref.shape[2] // 2
    loads = ([], [])
    for index, pack in enumerate(packs):
        core_step, chip_step = divmod(index, 2)
        cols = pl.ds(pl.multiple_of(jnp.bitwise_xor(core, core_step) * half, half), half)
        side = jnp.bitwise_xor(chip, chip_step)
        rows = pl.ds(pl.multiple_of(side * cut, cut), cut)
        for line_step in range(4):
            for row_step in (0, 1):
                owner = lax.rem(line - line_step + 4, 4) * 2 + jnp.bitwise_xor(row, row_step)
                source = pack.at[line_step, row_step]
                loads[0].append((source.at[0], expand_ref.at[:, owner, rows, cols]))
                loads[1].append((source.at[1], shrink_ref.at[owner, side, :, :, cols]))
    return [[mover.load(*pair) for pair in pairs] for pairs in loads]


def whole(ref):
    return ref[...].reshape(-1, ref.shape[-1])


def key_extra(length_limit, count):
    lane = lanes(PAIR) % HEAD_DIM
    extra = jnp.where(lane < 3, 1.0, 0.0)
    if length_limit is None:
        return jnp.broadcast_to(extra, (count, PAIR)).astype(BF)
    row = lax.broadcasted_iota(jnp.int32, (count, PAIR), 0)
    bias = jnp.where(row < length_limit, 0.0, -1e30)
    return jnp.where(lane == 3, bias, extra).astype(BF)


def put_start(pos_ref, start_ref):
    length = start_ref.shape[0]
    query = lax.broadcasted_iota(jnp.int32, (8, length), 1)
    first = (query - pos_ref[...]).astype(F32)
    start_ref[...] = first.T[:, :1].astype(jnp.int32)


def visible(start, first_query, first_key, count):
    key = first_key + lax.broadcasted_iota(jnp.int32, (TILE, count), 1)
    seen = key >= start
    if first_key == first_query:
        query = first_query + lax.broadcasted_iota(jnp.int32, (TILE, count), 0)
        seen = seen & (key <= query)
    return seen


def key_spans(tile, count, causal):
    if not causal:
        return [(0, count)]
    spans = [(0, tile * TILE)] if tile else []
    return spans + [(tile * TILE, TILE)]


def staggered(first, then, count):
    ready = first(0)
    for index in range(count):
        following = first(index + 1) if index + 1 < count else None
        then(index, ready)
        ready = following


class ProbStore:
    def __init__(self, mover, hbm, ref, causal):
        self.hbm, self.ref, self.mover = hbm, ref, mover
        self.tiles = ref.shape[2] // TILE
        self.causal = causal
        self.first = mover.take(2 * self.tiles)

    def views(self, pair, slot, tile):
        rows = slice(tile * TILE, (tile + 1) * TILE)
        keys = slice(0, (tile + 1) * TILE) if self.causal else slice(0, self.ref.shape[3])
        sem = self.mover.sems.at[self.first + slot * self.tiles + tile]
        return self.hbm.at[pair, :, rows, keys], self.ref.at[slot, :, rows, keys], sem

    def copy(self, pair, slot, tile, out):
        far, near, sem = self.views(pair, slot, tile)
        return pltpu.make_async_copy(near, far, sem) if out else pltpu.make_async_copy(far, near, sem)


def two_pairs(pairs, body):
    @pl.loop(0, pairs // 2)
    def _(step):
        for slot in (0, 1):
            body(2 * step + slot, slot, step)


def attend(q_ref, k_ref, v_ref, extra_ref, start_ref, o_ref, store, finished):
    length, count = q_ref.shape[0], k_ref.shape[0]
    causal = start_ref is not None
    masks = half_masks()
    pairs = q_ref.shape[1] // PAIR

    def one_pair(pair, slot, step):
        cols = rows_at(pair, PAIR)

        @pl.when(step > 0)
        def _():
            for tile in range(store.tiles):
                store.copy(pair - 2, slot, tile, True).wait()

        steps = [(tile, side) for tile in range(length // TILE) for side in (0, 1)]
        results = {}

        def scores_of(index):
            tile, side = steps[index]
            rows = slice(tile * TILE, (tile + 1) * TILE)
            queries = q_ref[rows, cols] * masks[side]
            if not causal:
                base = HEAD_DIM * (1 - side)
                queries = jnp.where(lanes(PAIR) == base + 3, 1.0, queries.astype(F32)).astype(BF)
            blocks = []
            for first, size in key_spans(tile, count, causal):
                keys = k_ref[first : first + size, cols]
                if not causal:
                    keys = keys * masks[side] + extra_ref[first : first + size, :] * masks[1 - side]
                scores = dot(queries, keys, 1, 1)
                if causal:
                    seen = visible(start_ref[rows, :], tile * TILE, first, size)
                    scores = jnp.where(seen, scores, -1000000000.0)
                blocks.append(scores)
            return blocks

        def mix(index, score_blocks):
            tile, side = steps[index]
            rows = slice(tile * TILE, (tile + 1) * TILE)
            spans = key_spans(tile, count, causal)
            top = functools.reduce(
                jnp.maximum, [jnp.max(scores, axis=1, keepdims=True) for scores in score_blocks]
            )
            exponents = [jnp.exp(scores - top) for scores in score_blocks]
            inverse = 1.0 / sum(jnp.sum(exponent, axis=1, keepdims=True) for exponent in exponents)
            total = None
            for exponent, (first, size) in zip(exponents, spans):
                probs = (exponent * inverse).astype(BF)
                store.ref[slot, side, rows, first : first + size] = probs
                part = dot(probs, v_ref[first : first + size, cols], 1, 0)
                total = part if total is None else total + part
            results[side] = total
            if side == 1:
                o_ref[rows, cols] = jnp.where(lanes(PAIR) < HEAD_DIM, results[0], results[1]).astype(BF)

        staggered(scores_of, mix, len(steps))
        for tile in range(store.tiles):
            store.copy(pair, slot, tile, True).start()
        for start_store in finished:
            start_store(pair)

    two_pairs(pairs, one_pair)
    for slot in (0, 1):
        for tile in range(store.tiles):
            store.mover.leaving.append(store.copy(pairs - 2 + slot, slot, tile, True))


def load_probs(store, slot):
    for tile in reversed(range(store.tiles)):
        store.copy(slot, slot, tile, False).start()


def attend_back(q_ref, da_ref, inner_ref, k_ref, v_ref, store, dq_ref, dk_ref, dv_ref, dk_sum, dv_sum, values_ref):
    length, count = q_ref.shape[0], k_ref.shape[0]
    masks = half_masks()
    pairs = k_ref.shape[1] // PAIR

    def one_pair(pair, slot, step):
        cols = rows_at(pair, PAIR)
        for tile in range(store.tiles):
            store.copy(pair, slot, tile, False).wait()
        for side in (0, 1):
            values_ref[side] = v_ref[:, cols] * masks[side]
        steps = [(tile, side) for tile in reversed(range(length // TILE)) for side in (0, 1)]
        query_grads = {}

        def place(index):
            tile, side = steps[index]
            size = (tile + 1) * TILE if store.causal else count
            return tile, side, slice(tile * TILE, (tile + 1) * TILE), slice(0, size)

        def collect(ref, tile, side, span, part):
            if tile == length // TILE - 1:
                ref[side, :, span] = part
            else:
                ref[side, :, span] += part

        def value_side(index):
            _, side, rows, span = place(index)
            return dot(da_ref[rows, cols], values_ref[side, span, :], 1, 1)

        def score_side(index, grad_probs):
            tile, side, rows, span = place(index)
            probs = store.ref[slot, side, rows, span]
            collect(dv_sum, tile, side, span, dot(da_ref[rows, cols], probs, 0, 0))
            inner = inner_ref[pair, rows, side : side + 1]
            grad_scores = (probs.astype(F32) * (grad_probs - inner)).astype(BF)
            collect(dk_sum, tile, side, span, dot(q_ref[rows, cols], grad_scores, 0, 0))
            query_grads[side] = dot(grad_scores, k_ref[span, cols], 1, 0)
            if side == 1:
                dq_ref[rows, cols] = (
                    jnp.where(lanes(PAIR) < HEAD_DIM, query_grads[0], query_grads[1]) * HEAD_DIM**-0.5
                ).astype(BF)

        staggered(value_side, score_side, len(steps))
        for sums, out in ((dk_sum, dk_ref), (dv_sum, dv_ref)):
            joined = jnp.concatenate([sums[0, :HEAD_DIM, :], sums[1, HEAD_DIM:, :]], axis=0)
            out[:, cols] = joined.astype(BF).T

        @pl.when(step < pairs // 2 - 1)
        def _():
            for tile in range(store.tiles):
                store.copy(pair + 2, slot, tile, False).start()

    two_pairs(pairs, one_pair)


def norm_rows(summed):
    center = jnp.mean(summed, axis=1, keepdims=True)
    shifted = summed - center
    inverse = lax.rsqrt(jnp.mean(shifted * shifted, axis=1, keepdims=True) + 1e-05)
    return shifted * inverse, inverse


def norm_back(grad_out, normed, inverse, gain):
    scaled = grad_out * gain
    first = jnp.mean(scaled, axis=1, keepdims=True)
    second = jnp.mean(scaled * normed, axis=1, keepdims=True)
    return inverse * (scaled - first - normed * second)


def add_rows(ref, row, values):
    ref[row : row + 1, :] += jnp.sum(values, axis=0, keepdims=True)


def place_of(place_ref):
    rep, place = place_ref[0], place_ref[1]
    return lax.rem(rep, 2), lax.div(rep, 2), lax.div(place, 2), lax.rem(place, 2)


def assemble(place_ref, chunk_refs, all_ref):
    core, chip, line, row = place_of(place_ref)
    width = all_ref.shape[1]
    quarter = chunk_refs[0].shape[3]
    shard = quarter * 4 // 3
    for core_step, chunk_ref in enumerate(chunk_refs):
        for chip_step in (0, 1):
            rep = jnp.bitwise_xor(chip, chip_step) * 2 + jnp.bitwise_xor(core, core_step)
            for line_step in range(4):
                for row_step in (0, 1):
                    owner = lax.rem(line - line_step + 4, 4) * 2 + jnp.bitwise_xor(row, row_step)
                    for piece in range(quarter // 16):
                        stacked = rep * quarter + piece * 16
                        matrix = lax.div(stacked, shard)
                        target = matrix * width + owner * shard + (stacked - matrix * shard)
                        all_ref[pl.ds(pl.multiple_of(target, 16), 16), :] = chunk_ref[
                            chip_step, line_step, row_step, piece * 16 : (piece + 1) * 16, :
                        ]


def assemble_halves(place_ref, mine_ref, other_ref, all_ref, shards):
    core = place_of(place_ref)[0]
    devices, _, half = mine_ref.shape
    for step, ref in ((0, mine_ref), (1, other_ref)):
        cols = pl.ds(pl.multiple_of(jnp.bitwise_xor(core, step) * half, half), half)
        first, target = 0, 0
        for shard in shards:
            for owner in range(devices):
                at = target + owner * shard
                all_ref[at : at + shard, cols] = ref[owner, first : first + shard, :]
            first += shard
            target += shard * devices


def unpack_small(all_ref, base, vec_ref, bias_ref):
    devices = vec_ref.shape[1] // HEAD_DIM
    inner = bias_ref.shape[1] // devices
    for pair in range(devices // 2):
        first = base + 2 * pair * 16
        left = all_ref[first : first + 16, :PAIR].astype(F32)
        right = all_ref[first + 16 : first + 32, :PAIR].astype(F32)
        vec_ref[:, pair * PAIR : (pair + 1) * PAIR] = jnp.where(
            lanes(PAIR) < HEAD_DIM, left, pltpu.roll(right, HEAD_DIM, 1)
        )
    for owner in range(devices):
        rows = all_ref[base + owner * 16 : base + owner * 16 + 16, :inner].astype(F32)
        bias_ref[:, owner * inner : (owner + 1) * inner] = rows[10:11, :]


def self_forward_kernel(staged, *refs):
    if staged:
        place_ref, pos_ref, x_hbm, chunk_hbm, other_hbm = refs[:5]
        refs = refs[5:]
    else:
        pos_ref, x_hbm, all_hbm = refs[:3]
        refs = refs[3:]
    p_hbm, q_hbm, k_hbm, v_hbm, o_hbm = refs[:5]
    refs = refs[5:]
    if staged:
        all_out, refs = refs[0], refs[1:]
    x_ref, all_ref, q_ref, k_ref, v_ref, o_ref, p_ref, start_ref = refs[:8]
    mover = Mover(refs[-1])
    length, width = x_ref.shape
    if staged:
        chunk_refs = refs[8:10]
        loads = [mover.load(a, b) for a, b in zip((chunk_hbm, other_hbm), chunk_refs)]
    else:
        loads = [mover.load(all_hbm, all_ref)]
    x_load = mover.load(x_hbm, x_ref)
    put_start(pos_ref, start_ref)
    for load in loads:
        load.wait()
    if staged:
        assemble(place_ref, chunk_refs, all_ref)
        mover.store(all_ref, all_out)
    x_load.wait()

    @pl.loop(0, length // TILE)
    def _(tile):
        rows = rows_at(tile)
        source = x_ref[rows, :]
        queries = dot(source, all_ref[:width, :], 1, 0).astype(BF)
        q_ref[rows, :] = queries * jnp.asarray(HEAD_DIM**-0.5, BF)
        k_ref[rows, :] = dot(source, all_ref[width : 2 * width, :], 1, 0).astype(BF)
        v_ref[rows, :] = dot(source, all_ref[2 * width :, :], 1, 0).astype(BF)

    mover.store(k_ref, k_hbm)
    mover.store(v_ref, v_hbm)
    mover.store(q_ref, q_hbm)
    finished = (mover.store_parts(o_ref, o_hbm, width // PAIR, columns_at(PAIR)),)
    attend(q_ref, k_ref, v_ref, None, start_ref, o_ref, ProbStore(mover, p_hbm, p_ref, True), finished)
    mover.finish()


def unpack_small(small_ref, vec_ref, bias_ref):
    devices = vec_ref.shape[1] // HEAD_DIM
    inner = bias_ref.shape[1] // devices
    for pair in range(devices // 2):
        left = small_ref[0, 2 * pair, :, :PAIR].astype(F32)
        right = small_ref[0, 2 * pair + 1, :, :PAIR].astype(F32)
        vec_ref[:, pair * PAIR : (pair + 1) * PAIR] = jnp.where(
            lanes(PAIR) < HEAD_DIM, left, pltpu.roll(right, HEAD_DIM, 1)
        )
    for owner in range(devices):
        rows = small_ref[0, owner, :, :inner].astype(F32)
        bias_ref[:, owner * inner : (owner + 1) * inner] = rows[10:11, :]


def cross_forward_kernel(staged, *refs):
    place_ref, core = None, None
    if staged:
        place_ref, refs = refs[0], refs[1:]
        core = place_of(place_ref)[0]
    length_ref, refs = refs[0], refs[1:]
    if staged:
        x_hbm, mixed_hbm, source_hbm, *packs = refs[:5]
        refs = refs[5:]
    else:
        vec_ref, x_hbm, mixed_hbm, source_hbm, *packs = refs[:9]
        refs = refs[9:]
    first_hbm, first_inv_hbm, p_hbm, q_hbm, k_hbm, v_hbm, o_hbm, n_hbm, inv_hbm = refs[:9]
    refs = refs[9:]
    if staged:
        vec_ref, bias_ref, refs = refs[0], refs[1], refs[2:]
    x_ref, mixed_ref, source_ref, first_ref, first_inv_ref, q_ref, k_ref, v_ref, o_ref, n_ref, inv_ref = refs[:11]
    p_ref, extra_ref, *w_refs = refs[11:18]
    mover = Mover(refs[-1])
    length, width = q_ref.shape

    if staged:
        small_ref = refs[18]
        rows = packs[0].shape[1]
        small = [
            mover.load(pack.at[:, rows - 16 :, :], small_ref.at[jnp.bitwise_xor(core, step)])
            for step, pack in enumerate(packs)
        ]
    source_load = mover.load_rows(source_hbm, source_ref)
    order = (2, 3, 0, 1, 4)
    waits = [None] * 5
    if staged:
        half = width // 2
        shard = w_refs[0].shape[1]
        for index in order:
            copies = []
            for step, pack in enumerate(packs):
                cols = pl.ds(pl.multiple_of(jnp.bitwise_xor(core, step) * half, half), half)
                copies.append(
                    mover.load(pack.at[:, index * shard : (index + 1) * shard, :], w_refs[index].at[:, :, cols])
                )
            waits[index] = lambda copies=copies: [copy.wait() for copy in copies]
    else:
        for index in order:
            waits[index] = mover.load(packs[index], w_refs[index]).wait
    mixed_load = mover.load_rows(mixed_hbm, mixed_ref)
    x_load = mover.load_rows(x_hbm, x_ref)
    extra_ref[...] = key_extra(length_ref[0], k_ref.shape[0])
    waits[2]()
    waits[3]()

    @pl.loop(0, source_ref.shape[0] // TILE)
    def _(tile):
        rows = rows_at(tile)
        source_load(tile)
        source = source_ref[rows, :]
        k_ref[rows, :] = dot(source, whole(w_refs[2]), 1, 0).astype(BF)
        v_ref[rows, :] = dot(source, whole(w_refs[3]), 1, 0).astype(BF)

    mover.store(k_ref, k_hbm)
    mover.store(v_ref, v_hbm)
    if staged:
        for load in small:
            load.wait()
        unpack_small(small_ref, vec_ref, bias_ref)
    waits[0]()
    waits[1]()

    tiles = [slice(tile * TILE, (tile + 1) * TILE) for tile in range(length // TILE)]

    def self_branch(tile):
        mixed_load(tile)
        x_load(tile)
        return dot(mixed_ref[tiles[tile], :], whole(w_refs[0]), 1, 0)

    def query_rows(tile, branch):
        rows = tiles[tile]
        normed, inverse = norm_rows(x_ref[rows, :].astype(F32) * vec_ref[6:7, :] + branch)
        first_ref[rows, :] = normed
        first_inv_ref[rows, :] = inverse
        low = (normed * vec_ref[0:1, :] + vec_ref[3:4, :]).astype(BF)
        queries = dot(low, whole(w_refs[1]), 1, 0).astype(BF)
        q_ref[rows, :] = queries * jnp.asarray(HEAD_DIM**-0.5, BF)

    staggered(self_branch, query_rows, len(tiles))
    mover.store(first_ref, first_hbm)
    mover.store(first_inv_ref, first_inv_hbm)
    mover.store(q_ref, q_hbm)
    finished = (mover.store_parts(o_ref, o_hbm, width // PAIR, columns_at(PAIR)),)
    attend(q_ref, k_ref, v_ref, extra_ref, None, o_ref, ProbStore(mover, p_hbm, p_ref, False), finished)
    waits[4]()
    n_store, inv_store = mover.store_rows(n_ref, n_hbm), mover.store_rows(inv_ref, inv_hbm)

    def cross_branch(tile):
        return dot(o_ref[tiles[tile], :], whole(w_refs[4]), 1, 0)

    def second_norm(tile, branch):
        rows = tiles[tile]
        first_out = first_ref[rows, :] * vec_ref[0:1, :] + vec_ref[3:4, :]
        normed, inverse = norm_rows(first_out * vec_ref[7:8, :] + branch)
        n_ref[rows, :] = normed
        inv_ref[rows, :] = inverse
        n_store(tile)
        inv_store(tile)

    staggered(cross_branch, second_norm, len(tiles))
    mover.finish()


def hidden_kernel(staged, *refs):
    place_ref, core = None, None
    if staged:
        place_ref, refs = refs[0], refs[1:]
        core = place_of(place_ref)[0]
    vec_ref, bias_ref, *packs = refs[: 6 if staged else 4]
    n_hbm, inv_hbm, cot_hbm = refs[len(packs) + 2 : len(packs) + 5]
    refs = refs[len(packs) + 5 :]
    count = 2 if staged else 1
    sums_ref, bias_sum_ref, out_hbm, dz_hbm = refs[:4]
    grad_hbms, refs = refs[4 : 4 + count], refs[4 + count :]
    grad_refs, refs = refs[:count], refs[count:]
    n_ref, inv_ref, cot_ref, out_ref, dz_ref, low_ref, h_ref, du_ref, df_ref, slope_ref, third_ref = refs[:11]
    blocks = bias_ref.shape[1] // vec_ref.shape[1]
    e_ref, s_ref = refs[11:13]
    mover = Mover(refs[-1])
    length, width = n_ref.shape

    n_load = mover.load_rows(n_hbm, n_ref)
    if staged:
        expand_loads, shrink_loads = load_quarters(mover, place_ref, packs, e_ref, s_ref)
    else:
        expand_loads, shrink_loads = [mover.load(packs[0], e_ref)], [mover.load(packs[1], s_ref)]
    cot_load = mover.load_rows(cot_hbm, cot_ref)
    inv_load = mover.load_rows(inv_hbm, inv_ref)
    out_store, dz_store = mover.store_rows(out_ref, out_hbm), mover.store_rows(dz_ref, dz_hbm)
    tiles = [slice(tile * TILE, (tile + 1) * TILE) for tile in range(length // TILE)]
    parts = [slice(block * width, (block + 1) * width) for block in range(blocks)]
    sums = {row: 0.0 for row in (1, 2, 4, 5, 8, 9)}
    bias_sums = [0.0] * blocks

    def add(row, values):
        sums[row] = sums[row] + jnp.sum(values, axis=0, keepdims=True)

    def second_out(rows):
        return n_ref[rows, :] * vec_ref[1:2, :] + vec_ref[4:5, :]

    for tile, rows in enumerate(tiles):
        n_load(tile)
        low_ref[rows, :] = second_out(rows).astype(BF)
    steps = [(block, rows) for block in range(blocks) for rows in tiles]

    def expand(index):
        block, rows = steps[index]
        return dot(low_ref[rows, :], whole(e_ref.at[block]), 1, 0) + bias_ref[:, parts[block]]

    def activate(index, before):
        block, rows = steps[index]
        square = before * before
        tangent = jnp.tanh(before * (0.7978845608028654 + 0.7978845608028654 * 0.044715 * square))
        half = 0.5 * (1.0 + tangent)
        slope_ref[rows, parts[block]] = half + before * (half * (1.0 - tangent)) * (
            0.7978845608028654 + 3.0 * 0.7978845608028654 * 0.044715 * square
        )
        h_ref[rows, parts[block]] = (before * half).astype(BF)

    for load in expand_loads:
        load.wait()
    staggered(expand, activate, len(steps))
    for load in shrink_loads:
        load.wait()
    for tile in range(len(tiles)):
        cot_load(tile)
        inv_load(tile)

    def shrink(tile):
        return dot(h_ref[tiles[tile], :], whole(s_ref), 1, 0)

    def outer_norm(tile, branch_out):
        rows = tiles[tile]
        second = second_out(rows)
        normed, inverse = norm_rows(second * vec_ref[8:9, :] + vec_ref[9:10, :] + branch_out)
        out_ref[rows, :] = (normed * vec_ref[2:3, :] + vec_ref[5:6, :]).astype(BF)
        grad_out = cot_ref[rows, :].astype(F32)
        third = norm_back(grad_out, normed, inverse, vec_ref[2:3, :])
        third_ref[rows, :] = third
        add(2, grad_out * normed)
        add(5, grad_out)
        branch = third.astype(BF)
        df_ref[rows, :] = branch
        add(9, branch.astype(F32))
        add(8, second * third)

    staggered(shrink, outer_norm, len(tiles))
    for tile in range(len(tiles)):
        out_store(tile)

    def shrink_back(index):
        block, rows = steps[index]
        return dot(df_ref[rows, :], whole(s_ref)[parts[block], :], 1, 1)

    def slope_back(index, grad_hidden):
        block, rows = steps[index]
        du = (grad_hidden * slope_ref[rows, parts[block]]).astype(BF)
        du_ref[rows, parts[block]] = du
        bias_sums[block] = bias_sums[block] + jnp.sum(du.astype(F32), axis=0, keepdims=True)

    staggered(shrink_back, slope_back, len(steps))

    def expand_back(tile):
        rows = tiles[tile]
        return sum(dot(du_ref[rows, parts[block]], whole(e_ref.at[block]), 1, 1) for block in range(blocks))

    def inner_norm(tile, grad_expanded):
        rows = tiles[tile]
        grad = vec_ref[8:9, :] * third_ref[rows, :] + grad_expanded
        normed = n_ref[rows, :]
        dz_ref[rows, :] = norm_back(grad, normed, inv_ref[rows, :], vec_ref[1:2, :])
        add(1, grad * normed)
        add(4, grad)

    staggered(expand_back, inner_norm, len(tiles))
    for tile in range(len(tiles)):
        dz_store(tile)
    sums_ref[...] = jnp.zeros_like(sums_ref)
    for row, values in sums.items():
        sums_ref[row : row + 1, :] = values
    for block, values in enumerate(bias_sums):
        bias_sum_ref[:, parts[block]] = values
    for step in reversed(range(count)):
        for block in range(blocks):
            put_grad(grad_refs, step, place_ref, block, low_ref[...], du_ref, block * width)
            put_shrink(grad_refs, step, place_ref, block, blocks, h_ref[:, parts[block]], df_ref)
        mover.store(grad_refs[step], grad_hbms[step])
    mover.finish()


def branch_grads(branch_rows, mixed_weight, o_ref, da_ref, inner_ref):
    width = o_ref.shape[1]
    tiles = [slice(tile * TILE, (tile + 1) * TILE) for tile in range(o_ref.shape[0] // TILE)]
    head = lax.broadcasted_iota(jnp.int32, (width, PAIR), 0) // HEAD_DIM
    picks = jnp.where(head == lax.broadcasted_iota(jnp.int32, (width, PAIR), 1), 1.0, 0.0).astype(BF)

    def project(tile):
        return dot(branch_rows(tile, tiles[tile]), mixed_weight, 1, 1)

    def reduce(tile, mixed_grad):
        rows = tiles[tile]
        low = mixed_grad.astype(BF)
        da_ref[rows, :] = low
        product = low.astype(F32) * o_ref[rows, :].astype(F32)
        high = product.astype(BF)
        rest = (product - high.astype(F32)).astype(BF)
        inner = dot(high, picks, 1, 0) + dot(rest, picks, 1, 0)
        for pair in range(width // PAIR):
            inner_ref[pair, rows, :] = pltpu.roll(inner, (PAIR - 2 * pair) % PAIR, 1) if pair else inner

    staggered(project, reduce, len(tiles))


def put_grad(grad_refs, step, place_ref, index, left, right_ref, first=0):
    width = left.shape[1]
    if place_ref is None:
        grad = dot(left, right_ref[:, first : first + width], 0, 0)
        grad_refs[0][index * width : (index + 1) * width, :] = grad.astype(BF)
        return
    core, _, _, row = place_of(place_ref)
    half = width // 2
    shard = width // 8
    cols = pl.ds(pl.multiple_of(first + jnp.bitwise_xor(core, step) * half, half), half)
    grad = dot(left, right_ref[:, cols], 0, 0).astype(BF).reshape(4, 2, shard, half)
    for side in (0, 1):
        slot = jnp.bitwise_xor(row, side)
        grad_refs[step][slot, :, index * shard : (index + 1) * shard, :] = grad[:, side]


def put_shrink(grad_refs, step, place_ref, block, blocks, left, right_ref):
    width = left.shape[1]
    if place_ref is None:
        first = (blocks + block) * width
        grad_refs[0][first : first + width, :] = dot(left, right_ref[...], 0, 0).astype(BF)
        return
    core, _, _, row = place_of(place_ref)
    half, shard = width // 2, width * blocks // 8
    base = width // 8 * blocks
    cols = pl.ds(pl.multiple_of(jnp.bitwise_xor(core, step) * half, half), half)
    grad = dot(left, right_ref[:, cols], 0, 0).astype(BF).reshape(width // shard, shard, half)
    for part in range(width // shard):
        owner = block * (width // shard) + part
        grad_refs[step][jnp.bitwise_xor(row, owner % 2), owner // 2, base:, :] = grad[part]


def put_small(grad_refs, place_ref, base, sums, bias_sum):
    core, _, _, row = place_of(place_ref)
    half = grad_refs[0].shape[3]
    inner = bias_sum.shape[1] // 8
    index = lax.broadcasted_iota(jnp.int32, (16, half), 0)
    for owner in range(8):
        block = sums[:, owner // 2 * PAIR : (owner // 2 + 1) * PAIR]
        if owner % 2:
            block = pltpu.roll(block, HEAD_DIM, 1)
        block = jnp.concatenate([block, jnp.zeros((16, half - PAIR), F32)], axis=1)
        block = jnp.where(index == 10, bias_sum[:, owner * inner : (owner + 1) * inner], block)
        high = block.astype(BF)
        low = (block - high.astype(F32)).astype(BF)
        slot = jnp.bitwise_xor(row, owner % 2)
        first = (core == 0).astype(F32)
        for step, grad_ref in enumerate(grad_refs):
            is_high = first if step == 0 else 1.0 - first
            mixed = high.astype(F32) * is_high + low.astype(F32) * (1.0 - is_high)
            grad_ref[slot, owner // 2, base : base + 16, :] = mixed.astype(BF)


def cross_backward_kernel(staged, *refs):
    place_ref, core = None, None
    if staged:
        place_ref, refs = refs[0], refs[1:]
        core = place_of(place_ref)[0]
    vec_ref, refs = refs[0], refs[1:]
    if staged:
        sums_three_ref, bias_sum_ref, refs = refs[0], refs[1], refs[2:]
    packs, refs = refs[: 2 if staged else 5], refs[2 if staged else 5 :]
    p_hbm, dz_hbm, x_hbm, first_hbm, inv_hbm, source_hbm, q_hbm, k_hbm, v_hbm, o_hbm, self_o_hbm = refs[:11]
    sums_ref, dfirst_hbm, dsource_hbm = refs[11:14]
    count = 2 if staged else 1
    grad_hbms, refs = refs[14 : 14 + count], refs[14 + count :]
    grad_refs, refs = refs[:count], refs[count:]
    dz_ref, x_ref, first_ref, inv_ref, source_ref, q_ref, k_ref, v_ref, o_ref, self_o_ref = refs[:10]
    dfirst_ref, dsource_ref, *w_refs = refs[10:17]
    low_ref, da_ref, inner_ref, dq_ref, dk_ref, dv_ref, dk_sum, dv_sum, branch_ref, values_ref, p_ref = refs[17:28]
    mover = Mover(refs[-1])
    length, width = dz_ref.shape

    dz_load, o_load = mover.load_rows(dz_hbm, dz_ref), mover.load_rows(o_hbm, o_ref)
    waits = load_matrices(mover, core, packs, w_refs, (4,))
    sums_ref[...] = jnp.zeros_like(sums_ref)
    waits[0]()
    store = ProbStore(mover, p_hbm, p_ref, False)
    load_probs(store, 0)
    middle = [mover.load(a, b) for a, b in ((v_hbm, v_ref), (q_hbm, q_ref), (k_hbm, k_ref))]

    def branch_rows(tile, rows):
        dz_load(tile)
        o_load(tile)
        branch_ref[rows, :] = dz_ref[rows, :].astype(BF)
        return branch_ref[rows, :]

    branch_grads(branch_rows, whole(w_refs[4]), o_ref, da_ref, inner_ref)
    for step in range(count):
        put_grad(grad_refs, step, place_ref, 4, o_ref[...], branch_ref)
    load_probs(store, 1)
    first_load = mover.load_rows(first_hbm, first_ref)
    waits = load_matrices(mover, core, packs, w_refs, (1, 2, 3))
    last = [
        mover.load(a, b)
        for a, b in ((source_hbm, source_ref), (x_hbm, x_ref), (inv_hbm, inv_ref), (self_o_hbm, self_o_ref))
    ]
    for load in middle:
        load.wait()
    attend_back(q_ref, da_ref, inner_ref, k_ref, v_ref, store, dq_ref, dk_ref, dv_ref, dk_sum, dv_sum, values_ref)
    for load in last:
        load.wait()
    for wait in waits:
        wait()
    for tile in range(length // TILE):
        first_load(tile)

    dsource_store = mover.store_rows(dsource_ref, dsource_hbm)
    dfirst_store = mover.store_rows(dfirst_ref, dfirst_hbm)
    tiles = [slice(tile * TILE, (tile + 1) * TILE) for tile in range(length // TILE)]
    key_tiles = [slice(tile * TILE, (tile + 1) * TILE) for tile in range(source_ref.shape[0] // TILE)]
    sums = {row: 0.0 for row in (0, 3, 6, 7)}

    def add(row, values):
        sums[row] = sums[row] + jnp.sum(values, axis=0, keepdims=True)

    def source_grad(tile):
        rows = key_tiles[tile]
        dsource_ref[rows, :] = dot(dk_ref[rows, :], whole(w_refs[2]), 1, 1) + dot(
            dv_ref[rows, :], whole(w_refs[3]), 1, 1
        )

    def put_keys(step):
        put_grad(grad_refs, step, place_ref, 2, source_ref[...], dk_ref)
        put_grad(grad_refs, step, place_ref, 3, source_ref[...], dv_ref)

    products = [functools.partial(source_grad, tile) for tile in range(len(key_tiles))]
    products += [functools.partial(put_keys, step) for step in range(count)]

    def query_back(tile):
        product = dot(dq_ref[tiles[tile], :], whole(w_refs[1]), 1, 1)
        for run in products[tile :: len(tiles)]:
            run()
        return product

    def first_norm(tile, product):
        rows = tiles[tile]
        grad = dz_ref[rows, :]
        dx = product + vec_ref[7:8, :] * grad
        normed = first_ref[rows, :]
        first_out = normed * vec_ref[0:1, :] + vec_ref[3:4, :]
        low_ref[rows, :] = first_out.astype(BF)
        add(7, first_out * grad)
        dfirst = norm_back(dx, normed, inv_ref[rows, :], vec_ref[0:1, :])
        dfirst_ref[rows, :] = dfirst
        add(0, dx * normed)
        add(3, dx)
        add(6, x_ref[rows, :].astype(F32) * dfirst)
        branch_ref[rows, :] = dfirst.astype(BF)

    staggered(query_back, first_norm, len(tiles))
    for tile in range(len(key_tiles)):
        dsource_store(tile)
    for tile in range(len(tiles)):
        dfirst_store(tile)
    for row, values in sums.items():
        sums_ref[row : row + 1, :] = values

    if staged:
        put_small(grad_refs, place_ref, 5 * (width // 8), sums_ref[...] + sums_three_ref[...], bias_sum_ref[...])
    for step in reversed(range(count)):
        put_grad(grad_refs, step, place_ref, 1, low_ref[...], dq_ref)
        put_grad(grad_refs, step, place_ref, 0, self_o_ref[...], branch_ref)
        mover.store(grad_refs[step], grad_hbms[step])
    mover.finish()


def self_backward_kernel(staged, *refs):
    place_ref, core = None, None
    if staged:
        place_ref, refs = refs[0], refs[1:]
        core = place_of(place_ref)[0]
    count = 2 if staged else 1
    packs, refs = refs[:count], refs[count:]
    p_hbm, dz_hbm, x_hbm, q_hbm, k_hbm, v_hbm, o_hbm, *head_hbms = refs[:10]
    grad_hbms, refs = refs[10 : 10 + count], refs[10 + count :]
    grad_refs, refs = refs[:count], refs[count:]
    dz_ref, x_ref, q_ref, k_ref, v_ref, o_ref, w_ref = refs[:7]
    da_ref, inner_ref, dq_ref, dk_ref, dv_ref, dk_sum, dv_sum, values_ref, p_ref = refs[7:16]
    mover = Mover(refs[-1])
    length, width = dz_ref.shape

    dz_load = mover.load_rows(dz_hbm, dz_ref)
    waits = load_matrices(mover, core, packs, (w_ref,))
    o_load = mover.load_rows(o_hbm, o_ref)
    waits[0]()
    store = ProbStore(mover, p_hbm, p_ref, True)
    load_probs(store, 0)
    middle = [mover.load(a, b) for a, b in ((v_hbm, v_ref), (q_hbm, q_ref), (k_hbm, k_ref))]

    def branch_rows(tile, rows):
        dz_load(tile)
        o_load(tile)
        return dz_ref[rows, :].astype(BF)

    branch_grads(branch_rows, whole(w_ref), o_ref, da_ref, inner_ref)
    load_probs(store, 1)
    x_load = mover.load(x_hbm, x_ref)
    for load in middle:
        load.wait()
    attend_back(q_ref, da_ref, inner_ref, k_ref, v_ref, store, dq_ref, dk_ref, dv_ref, dk_sum, dv_sum, values_ref)
    for near, far in zip((dq_ref, dk_ref, dv_ref), head_hbms):
        mover.store(near, far)
    x_load.wait()
    for step in reversed(range(count)):
        for index, grads in enumerate((dq_ref, dk_ref, dv_ref)):
            put_grad(grad_refs, step, place_ref, index, x_ref[...], grads)
        mover.store(grad_refs[step], grad_hbms[step])
    mover.finish()


def input_grad_kernel(vec_ref, dz_hbm, all_hbm, dq_hbm, dk_hbm, dv_hbm, dx_hbm, *refs):
    dz_ref, all_ref, dq_ref, dk_ref, dv_ref, dx_ref, sems = refs
    mover = Mover(sems)
    width = dz_ref.shape[1]
    all_load = mover.load(all_hbm, all_ref)
    heads = (dq_ref, dk_ref, dv_ref)
    loads = [mover.load_rows(a, b) for a, b in zip((dq_hbm, dk_hbm, dv_hbm), heads)]
    loads.append(mover.load_rows(dz_hbm, dz_ref))
    dx_store = mover.store_rows(dx_ref, dx_hbm)
    all_load.wait()

    @pl.loop(0, dz_ref.shape[0] // TILE)
    def _(tile):
        rows = rows_at(tile)
        for load in loads:
            load(tile)
        dx = vec_ref[6:7, :] * dz_ref[rows, :]
        for index, grads in enumerate(heads):
            dx = dx + dot(grads[rows, :], all_ref[index * width : (index + 1) * width, :], 1, 1)
        dx_ref[rows, :] = dx
        dx_store(tile)

    mover.finish()


def call(kernel, args, outs, scratch, limit, flops, smem=(), near=(), near_outs=(), copies=0):
    spaces = [pltpu.SMEM if i in smem else pltpu.VMEM if i in near else pl.ANY for i in range(len(args))]
    out_spaces = [pltpu.VMEM if i in near_outs else pl.ANY for i in range(len(outs))]
    buffers = [pltpu.VMEM(shape, kind) for shape, kind in scratch]
    if copies:
        buffers.append(pltpu.SemaphoreType.DMA((copies,)))
    return pl.pallas_call(
        kernel,
        out_shape=[jax.ShapeDtypeStruct(shape, kind) for shape, kind in outs],
        in_specs=[pl.BlockSpec(memory_space=space) for space in spaces],
        out_specs=[pl.BlockSpec(memory_space=space) for space in out_spaces],
        scratch_shapes=buffers,
        compiler_params=pltpu.CompilerParams(vmem_limit_bytes=(63 if copies else limit) * MIB),
        cost_estimate=pl.CostEstimate(flops=flops, bytes_accessed=16 * MIB, transcendentals=0),
    )(*args)


def like(*arrays):
    return [(a.shape, a.dtype) for a in arrays]


def prob_shape(queries, keys, width):
    return (width // PAIR, 2, queries, keys), BF


def forward_self(place, x, pos, pack, staged):
    length, width = x.shape
    low = ((length, width), BF)
    outs = [prob_shape(length, length, width), low, low, low, low]
    matrices = ((3 * width, width), BF)
    scratch = [low, matrices, low, low, low, low, ((2, 2, length, length), BF), ((length, 1), jnp.int32)]
    if staged:
        return call(
            functools.partial(self_forward_kernel, True),
            (place, pos, x, *pack),
            [*outs, matrices],
            [*scratch, *like(*pack)],
            40, 10**10, smem=(0,), near=(1,), copies=24,
        )
    results = call(
        functools.partial(self_forward_kernel, False),
        (pos, x, pack), outs, scratch, 40, 10**10, near=(0,), copies=24,
    )
    return (*results, pack)


def matrix_buffers(shards, width):
    return [((8 if rows < width else 1, rows, width), BF) for rows in shards]


def forward_cross(place, x, mixed, source, count, packs, given, shards):
    length, width = x.shape
    keys = source.shape[0]
    low, full, column, key_low = ((length, width), BF), ((length, width), F32), ((length, 1), F32), ((keys, width), BF)
    outs = [full, column, prob_shape(length, keys, width), low, key_low, key_low, low, full, column]
    near = [full, column, low, key_low, key_low, low, full, column]
    scratch = [low, low, key_low, *near, ((2, 2, length, keys), BF), ((keys, PAIR), BF)]
    if place is not None:
        return call(
            functools.partial(cross_forward_kernel, True),
            (place, count, x, mixed, source, *packs),
            [*outs, ((16, width), F32), ((1, 4 * width), F32)],
            [*scratch, *matrix_buffers(shards, width), ((2, 8, 16, width // 2), BF)],
            44, 10**10, smem=(0, 1), near_outs=(9, 10), copies=64,
        )
    vec, bias = given
    results = call(
        functools.partial(cross_forward_kernel, False),
        (count, vec, x, mixed, source, *packs),
        outs, [*scratch, *like(*packs)],
        44, 10**10, smem=(0,), near=(1,), copies=64,
    )
    return (*results, vec, bias)


def grad_outs(rows, width, staged):
    return [((2, 4, rows, width // 2), BF)] * 2 if staged else [((rows, width), BF)]


def hidden_step(place, packs, normed, inverse, cot, vec, bias):
    length, width = normed.shape
    inner = bias.shape[1]
    blocks = inner // width
    staged = place is not None
    low, full = ((length, width), BF), ((length, width), F32)
    grads = grad_outs(2 * inner // 8 if staged else 2 * inner, width, staged)
    args = (vec, bias, *packs, normed, inverse, cot)
    matrices = like(*packs)
    if staged:
        rows = width // 8
        matrices = [((blocks, 8, rows, width), BF), ((8, 2, blocks, rows // 2, width), BF)]
    return call(
        functools.partial(hidden_kernel, staged),
        (place, *args) if staged else args,
        [((16, width), F32), ((1, inner), F32), low, full, *grads],
        [*grads, *like(normed, inverse, cot), low, full, low, ((length, inner), BF), ((length, inner), BF), low,
         ((length, inner), F32), full, *matrices],
        44, 2 * 10**10, smem=(0,) if staged else (), near=(1, 2) if staged else (0, 1), near_outs=(0, 1),
        copies=96,
    )


def backward_cross(place, packs, dz, x, normed, inverse, source, vec, saved, mixed, small, shards):
    length, width = dz.shape
    keys = source.shape[0]
    staged = place is not None
    probs, *saved = saved
    arrays = (dz, x, normed, inverse, source, *saved, mixed)
    low, key_low, sums = ((length, width), BF), ((keys, width), BF), ((2, PAIR, keys), F32)
    grads = grad_outs(5 * width // 8 + 16 if staged else 5 * width, width, staged)
    full, key_full = ((length, width), F32), ((keys, width), F32)
    return call(
        functools.partial(cross_backward_kernel, staged),
        (place, vec, *small, *packs, probs, *arrays) if staged else (vec, *packs, probs, *arrays),
        [((16, width), F32), full, key_full, *grads],
        [*grads, *like(*arrays), full, key_full, *(matrix_buffers(shards, width) if staged else like(*packs)),
         low, low, ((width // PAIR, length, PAIR), F32), low, key_low, key_low, sums, sums, low, ((2, keys, PAIR), BF),
         ((2, 2, length, keys), BF)],
        48, 2 * 10**10, smem=(0,) if staged else (), near=(1, 2, 3) if staged else (0,), near_outs=(0,), copies=72,
    )


def backward_self(place, packs, dz, x, saved, shards):
    length, width = dz.shape
    staged = place is not None
    probs, *saved = saved
    arrays = (dz, x, *saved)
    low, sums = ((length, width), BF), ((2, PAIR, length), F32)
    grads = grad_outs(3 * width // 8 if staged else 3 * width, width, staged)
    first = matrix_buffers(shards[:1], width) if staged else like(*packs)
    return call(
        functools.partial(self_backward_kernel, staged),
        (place, *packs, probs, *arrays) if staged else (*packs, probs, *arrays),
        [low, low, low, *grads],
        [*grads, *like(*arrays), *first, low, ((width // PAIR, length, PAIR), F32), low, low, low, sums, sums,
         ((2, length, PAIR), BF), ((2, 2, length, length), BF)],
        48, 2 * 10**10, smem=(0,) if staged else (), copies=64,
    )


def input_gradient(vec, dz, matrices, heads):
    arrays = (dz, matrices, *heads)
    return call(
        input_grad_kernel, (vec, *arrays), like(dz), [*like(*arrays), *like(dz)], 40, 2 * 10**9, near=(0,), copies=24
    )[0]


def adam_step(settings_ref, now, grad, one, two, decay):
    beta_one, beta_two = settings_ref[1], settings_ref[2]
    first = beta_one * one + (1.0 - beta_one) * grad
    second = beta_two * two + (1.0 - beta_two) * grad * grad
    change = (first / settings_ref[4]) / (jnp.sqrt(second / settings_ref[5]) + 1e-08)
    if decay:
        change = change + settings_ref[3] * now
    return now - settings_ref[0] * change, first, second


def store_step(refs, where, results):
    for ref, value in zip(refs, results):
        ref[where] = value


def hidden_adam_kernel(place_ref, settings_ref, *refs):
    core = place_of(place_ref)[0]
    hbms, new_hbms, refs = refs[:8], refs[8:14], refs[14:]
    mine_ref, other_ref, *params = refs[:8]
    news, mover = refs[8:14], Mover(refs[-1])
    loads = [mover.load(a, b) for a, b in zip(hbms, refs[:8])]
    expand, shrink = params[0:3], params[3:6]
    half = mine_ref.shape[1]
    shard = expand[0].shape[0]
    blocks = expand[0].shape[1] // (2 * half)
    for load in loads[:5]:
        load.wait()
    sides = [(jnp.bitwise_xor(core, step) * half, ref) for step, ref in ((0, mine_ref), (1, other_ref))]
    for side, ref in sides:
        for block in range(blocks):
            where = (slice(None), pl.ds(pl.multiple_of(block * 2 * half + side, half), half))
            grad = ref[block * shard : (block + 1) * shard, :]
            now, one, two = (r[where] for r in expand)
            store_step(news[:3], where, adam_step(settings_ref, now, grad, one, two, True))
    for load in loads[5:]:
        load.wait()
    for near, far in zip(news[:3], new_hbms[:3]):
        mover.store(near, far)
    for side, ref in sides:
        where = (slice(None), pl.ds(pl.multiple_of(side, half), half))
        now, one, two = (r[where] for r in shrink)
        store_step(news[3:], where, adam_step(settings_ref, now, ref[blocks * shard :, :], one, two, True))
    for near, far in zip(news[3:], new_hbms[3:]):
        mover.store(near, far)
    mover.finish()


def attention_adam_kernel(place_ref, settings_ref, mine_ref, other_ref, *refs):
    core = place_of(place_ref)[0]
    matrices, bias, vectors = refs[0:3], refs[3:6], refs[6:9]
    new_matrices, new_bias, new_vectors = refs[9:12], refs[12:15], refs[15:18]
    half = mine_ref.shape[1]
    shard = matrices[0].shape[1]
    for step, ref in ((0, mine_ref), (1, other_ref)):
        cols = pl.ds(pl.multiple_of(jnp.bitwise_xor(core, step) * half, half), half)
        for index in range(8):
            where = (index, slice(None), cols)
            now, one, two = (r[where] for r in matrices)
            grad = ref[index * shard : (index + 1) * shard, :]
            store_step(new_matrices, where, adam_step(settings_ref, now, grad, one, two, True))
    small = mine_ref[8 * shard :, :] + other_ref[8 * shard :, :]
    for group, new, grad in (
        (bias, new_bias, small[10:11, : bias[0].shape[1]]),
        (vectors, new_vectors, small[:10, : vectors[0].shape[1]]),
    ):
        now, one, two = (r[...] for r in group)
        store_step(new, ..., adam_step(settings_ref, now, grad, one, two, False))


def hidden_adam(scalars, grads, params):
    return call(
        hidden_adam_kernel, (*scalars, *grads, *params), like(*params), [*like(*grads), *like(*params), *like(*params)],
        40, 10**9, smem=(0, 1), copies=16,
    )


def adam_call(kernel, scalars, grads, params):
    return call(
        kernel, (*scalars, *grads, *params), [(p.shape, F32) for p in params], [], 32, 10**7, smem=(0, 1),
        near=range(2, 2 + len(grads) + len(params)), near_outs=range(len(params)),
    )


CORE_SWAP = [(0, 1), (1, 0), (2, 3), (3, 2)]
CHIP_SWAP = [(0, 2), (2, 0), (1, 3), (3, 1)]
ROW_SWAP = [(i, i ^ 1) for i in range(8)]


LINES = [[0, 2, 4, 6], [1, 3, 5, 7]]


def line_shift(step):
    return [(2 * z + y, 2 * ((z + step) % 4) + y) for z in range(4) for y in (0, 1)]


def small_mesh(mesh):
    return mesh.shape["rep"] == 4 and mesh.shape["fsdp"] == 8


class StagedGather:
    def rows(self, mine, done):
        self.mine = mine
        self.other = lax.ppermute(after(mine, done), "fsdp", ROW_SWAP)

    def line(self, done):
        self.pair = after(jnp.stack([self.mine, self.other]), done)
        self.received = [lax.ppermute(self.pair, "fsdp", line_shift(step)) for step in (1, 2, 3)]

    def chips(self, done):
        self.arrived = after(tuple(self.received), done)
        self.part = jnp.stack([self.pair, *self.arrived])
        self.far = lax.ppermute(self.part, "rep", CHIP_SWAP)

    def cores(self, done):
        far = after(self.far, done)
        part = after(self.part, done)
        return part, far, lax.ppermute(part, "rep", CORE_SWAP), lax.ppermute(far, "rep", CORE_SWAP)


def gather_staged(pack):
    quarter = pack.shape[0] // 4
    mine = lax.dynamic_slice_in_dim(pack, lax.axis_index("rep") * quarter, quarter, 0)
    pair = jnp.stack([mine, lax.ppermute(mine, "fsdp", ROW_SWAP)])
    part = jnp.stack([pair] + [lax.ppermute(pair, "fsdp", line_shift(step)) for step in (1, 2, 3)])
    both = jnp.stack([part, lax.ppermute(part, "rep", CHIP_SWAP)])
    return pair, part, both


def after(value, *done):
    return lax.optimization_barrier((value, *done))[0]


def half_columns(pack):
    half = pack.shape[1] // 2
    return lax.dynamic_slice_in_dim(pack, lax.axis_index("rep") % 2 * half, half, 1)


def both_halves(mine, *done):
    mine = after(mine, *done)
    return mine, lax.ppermute(mine, "rep", CORE_SWAP)


def reduce_cores(keep, send):
    received = lax.ppermute(send, "rep", CORE_SWAP)
    return keep[0] + received[0], keep[1] + received[1]


def send_rows(send):
    return lax.ppermute(send, "fsdp", ROW_SWAP)


def reduce_rows(keep, received, done):
    return keep + after(received, done)


def reduce_chips(part, *done):
    return part.astype(F32) + after(lax.ppermute(part, "rep", CHIP_SWAP), *done).astype(F32)


def reduce_last(part, *done):
    total = reduce_chips(part, *done)
    return total, lax.ppermute(total, "rep", CORE_SWAP)


def reduce_line(joined):
    part = lax.psum_scatter(joined, "fsdp", scatter_dimension=0, axis_index_groups=LINES)
    return part.reshape(joined.shape[1:])


def reduce_shifts(joined, done):
    line = lax.axis_index("fsdp") // 2
    total = lax.dynamic_index_in_dim(joined, line, 0, False).astype(F32)
    for step in (1, 2, 3):
        away = lax.dynamic_index_in_dim(joined, (line + step) % 4, 0, False)
        total = total + after(lax.ppermute(away, "fsdp", line_shift(step)), done).astype(F32)
    return total.astype(BF)


def reduce_plain(grads):
    return lax.psum(lax.psum_scatter(grads, "fsdp", scatter_dimension=0), "rep").astype(F32)


def adam_update(weight_now, gradient, moment_one, moment_two, settings, step_float, factor):
    learn_rate, beta_one, beta_two, decay_rate = settings[0], settings[1], settings[2], settings[3]
    first_new = beta_one * moment_one + (1.0 - beta_one) * gradient
    second_new = beta_two * moment_two + (1.0 - beta_two) * gradient * gradient
    first_hat = first_new / (1.0 - beta_one**step_float)
    second_hat = second_new / (1.0 - beta_two**step_float)
    change = first_hat / (jnp.sqrt(second_hat) + 1e-08) + factor * decay_rate * weight_now
    return (weight_now - learn_rate * change, first_new, second_new)


def per_device(
    small, inputs, memory, memory_length, target_pos, cotangent,
    attention_weights, expand_weights, shrink_weights, expand_bias, layer_vectors,
    first_attention, first_expand, first_shrink, first_bias, first_vectors,
    second_attention, second_expand, second_shrink, second_bias, second_vectors,
    hyper_rates, step_count,
):
    length, width = inputs.shape[1:]
    shard = attention_weights.shape[1]
    count = width // shard
    inner_shard = shrink_weights.shape[0]
    blocks = inner_shard // shard
    low_attention = attention_weights.astype(BF).reshape(8 * shard, width)
    pack_one = low_attention[: 3 * shard]
    expand_low = expand_weights.astype(BF).reshape(shard, blocks, width)
    shrink_low = shrink_weights.astype(BF)
    x, source, cot = inputs[0], memory[0], cotangent[0]
    step_float = step_count.astype(F32)

    if small:
        place = jnp.stack([lax.axis_index("rep"), lax.axis_index("fsdp")]).astype(jnp.int32)
        small_rows = jnp.concatenate(
            [
                jnp.pad(layer_vectors, ((0, 0), (0, inner_shard - shard))),
                expand_bias[None],
                jnp.zeros((5, inner_shard), F32),
            ]
        )
        small_rows = jnp.pad(small_rows, ((0, 0), (0, width - inner_shard))).astype(BF)
        pack_two = jnp.concatenate([low_attention[3 * shard :], small_rows])
        half_two = half_columns(pack_two)
        two = lax.all_gather(half_two, "fsdp", axis=0)
        pair_one, part_one, one = gather_staged(after(pack_one, half_two))
        half = shard // 2
        halves = expand_low.reshape(2, half, blocks, width).transpose(0, 2, 1, 3)
        quarters = jnp.stack([halves, shrink_low.reshape(2, blocks, half, width)], axis=1)
        core, chip = place[0] % 2, place[0] // 2
        quarter = lax.dynamic_slice(
            quarters, (chip, 0, 0, 0, core * (width // 2)), (1, *quarters.shape[1:4], width // 2)
        )
        three = StagedGather()
        three.rows(quarter[0], pair_one)
        one = both_halves(one, three.other)
        three.line(part_one)
        given = None
        cross_shards = (shard,) * 5
    else:
        place, cross_shards = None, None
        flat = jnp.concatenate([layer_vectors.reshape(-1), expand_bias]).astype(BF)
        flat = lax.all_gather(flat, "fsdp", axis=0).astype(F32)
        vector_size = layer_vectors.size
        vec = flat[:, :vector_size].reshape(count, -1, shard).transpose(1, 0, 2).reshape(-1, width)
        given = jnp.pad(vec, ((0, 16 - vec.shape[0]), (0, 0))), flat[:, vector_size:].reshape(1, -1)

        def gather_all(pack, shards):
            full = lax.all_gather(pack, "fsdp", axis=0)
            pieces, first = [], 0
            for rows in shards:
                pieces.append(full[:, first : first + rows].reshape(-1, width))
                first += rows
            return pieces

        def owners(grads, shards):
            pieces, first = [], 0
            for rows in shards:
                pieces.append(grads[first : first + rows * count].reshape(count, rows, width))
                first += rows * count
            return jnp.concatenate(pieces, axis=1)

        one = jnp.concatenate(gather_all(pack_one, (shard,) * 3))
        two = [m[None] for m in gather_all(low_attention[3 * shard :], (shard,) * 5)]
        pack = jnp.concatenate([expand_low.transpose(1, 0, 2).reshape(-1, width), shrink_low])
        *expand_all, shrink_all = gather_all(pack, (*(shard,) * blocks, inner_shard))
        three = jnp.stack(expand_all)[:, None], shrink_all[None]

    *saved_one, matrices = forward_self(place, x, target_pos, one, small)
    if small:
        three.chips(saved_one[4])
        two = both_halves(two, *three.arrived)
    norm_one, inv_one, *saved_two, norm_two, inv_two, vec, bias = forward_cross(
        place, x, saved_one[4], source, memory_length, two, given, cross_shards
    )
    three = three.cores(norm_two) if small else three
    sums_three, bias_sum, outputs, dz_two, *grad_three = hidden_step(
        place, three, norm_two, inv_two, cot, vec, bias
    )
    if small:
        keep_three, send_three = reduce_cores(*grad_three)
        dz_two = after(dz_two, keep_three, send_three)
        received_three = send_rows(send_three)
    sums_two, dz_one, memory_grad, *grad_two = backward_cross(
        place, two, dz_two, x, norm_one, inv_one, source, vec, saved_two, saved_one[4],
        (sums_three, bias_sum), cross_shards,
    )
    if small:
        joined_three = reduce_rows(keep_three, received_three, dz_one)
        keep_two, send_two = reduce_cores(grad_two[0], after(grad_two[1], received_three))
        dz_one = after(dz_one, joined_three, keep_two, send_two)
        received_two = send_rows(send_two)
    *heads, grad_keep, grad_send = (
        *backward_self(place, two if small else two[:1], dz_one, x, saved_one, cross_shards),
        *((None,) if not small else ()),
    )
    if small:
        keep_one, send_one = reduce_cores(grad_keep, after(grad_send, received_two))
        joined_two = reduce_rows(after(keep_two, send_one), received_two, heads[0])
        heads = after(tuple(heads), keep_one, send_one, joined_two)
        received_one = send_rows(send_one)
    input_grad = input_gradient(vec, dz_one, matrices, heads)

    attention = (attention_weights, first_attention, second_attention)
    expand = (expand_weights, first_expand, second_expand)
    shrink = (shrink_weights, first_shrink, second_shrink)
    bias = (expand_bias, first_bias, second_bias)
    vectors = (layer_vectors, first_vectors, second_vectors)
    if small:
        powers = 1.0 - hyper_rates[1:3] ** step_float
        scalars = place, jnp.concatenate([hyper_rates, powers])
        part_three = reduce_line(joined_three)
        part_two = reduce_line(joined_two)
        total_three = reduce_last(after(part_three, send_one), input_grad)
        joined_one = reduce_rows(keep_one, received_one, input_grad)
        hidden_new = hidden_adam(scalars, total_three, (*expand, *shrink))
        part_one = reduce_shifts(joined_one, hidden_new[0])
        total_two = reduce_chips(after(part_two, hidden_new[0]), part_one)
        total_rest = jnp.concatenate([reduce_chips(part_one), total_two])
        total_rest = total_rest, lax.ppermute(total_rest, "rep", CORE_SWAP)
        rows = tuple(b[None] for b in bias)
        other_new = adam_call(
            attention_adam_kernel, scalars, total_rest, (*attention, *rows, *vectors)
        )
        new_bias = tuple(b[0] for b in other_new[3:6])
        updated = (*other_new[:3], *hidden_new, *new_bias, *other_new[6:])
    else:
        sums = (sums_two + sums_three)[: layer_vectors.shape[0]]
        flat = jnp.concatenate(
            [
                sums.reshape(-1, count, shard).transpose(1, 0, 2).reshape(count, -1),
                bias_sum.reshape(count, inner_shard),
            ],
            axis=1,
        )
        total_three = reduce_plain(owners(grad_three[0], (*(shard,) * blocks, inner_shard)))
        total_two = reduce_plain(owners(grad_two[0], (shard,) * 5))
        total_one = reduce_plain(owners(grad_keep, (shard,) * 3))
        flat = lax.psum(lax.psum_scatter(flat, "fsdp", scatter_dimension=0), "rep")
        grad_attention = jnp.concatenate([total_one, total_two]).reshape(attention_weights.shape)
        grad_expand = total_three[: blocks * shard].reshape(blocks, shard, width).transpose(1, 0, 2)
        updated = []
        for (now, one_now, two_now), grad, factor in (
            (attention, grad_attention, 1.0),
            (expand, grad_expand.reshape(shard, -1), 1.0),
            (shrink, total_three[blocks * shard :], 1.0),
            (bias, flat[layer_vectors.size :], 0.0),
            (vectors, flat[: layer_vectors.size].reshape(-1, shard), 0.0),
        ):
            updated.extend(adam_update(now, grad, one_now, two_now, hyper_rates, step_float, factor))
    return (outputs[None], input_grad[None], memory_grad[None], *updated)


def solution(mesh):
    rows = ("rep", "fsdp")
    params = (P(None, "fsdp", None), P("fsdp", None), P("fsdp", None), P("fsdp"), P(None, "fsdp"))
    return jax.shard_map(
        functools.partial(per_device, small_mesh(mesh)),
        mesh=mesh,
        in_specs=(
            P(rows, None, None), P(rows, None, None), P(rows), P(rows, None), P(rows, None, None),
            *params, *params, *params, P(), P(),
        ),
        out_specs=(
            P(rows, None, None), P(rows, None, None), P(rows, None, None),
            *(spec for spec in params for _ in range(3)),
        ),
        check_vma=False,
    )
```

```python
import functools

import jax
import jax.numpy as jnp
from jax import lax
from jax.experimental import pallas as pl
from jax.experimental.pallas import tpu as pltpu
from jax.sharding import PartitionSpec as P

BF = jnp.bfloat16
F32 = jnp.float32
HEAD_DIM = 64
PAIR = 128
TILE = 256
MIB = 1 << 20


def dot(left, right, left_dim, right_dim):
    return lax.dot_general(
        left, right, (((left_dim,), (right_dim,)), ((), ())), preferred_element_type=F32
    )


def lanes(size):
    return lax.broadcasted_iota(jnp.int32, (1, size), 1)


def half_masks():
    first = jnp.where(lanes(PAIR) < HEAD_DIM, 1.0, 0.0)
    return first.astype(BF), (1.0 - first).astype(BF)


def rows_at(index, size=TILE):
    return pl.ds(pl.multiple_of(index * size, size), size)


class Mover:
    def __init__(self, sems):
        self.sems, self.used, self.leaving = sems, 0, []

    def take(self, count=1):
        self.used += count
        return self.used - count

    def load(self, source, target):
        copy = pltpu.make_async_copy(source, target, self.sems.at[self.take()])
        copy.start()
        return copy

    def load_rows(self, source, target):
        count = source.shape[0] // TILE
        first = self.take(count)

        def copy(tile):
            rows = rows_at(tile)
            return pltpu.make_async_copy(source.at[rows], target.at[rows], self.sems.at[first + tile])

        for tile in range(count):
            copy(tile).start()
        return lambda tile: copy(tile).wait()

    def store(self, source, target):
        self.leaving.append(self.load(source, target))

    def store_parts(self, source, target, count, where):
        first = self.take(count)

        def copy(part):
            return pltpu.make_async_copy(source.at[where(part)], target.at[where(part)], self.sems.at[first + part])

        self.leaving.extend(copy(part) for part in range(count))
        return lambda part: copy(part).start()

    def store_rows(self, source, target):
        return self.store_parts(source, target, source.shape[0] // TILE, rows_at)

    def finish(self):
        for copy in self.leaving:
            copy.wait()


def columns_at(size):
    return lambda part: (slice(None), rows_at(part, size))


def load_matrices(mover, core, sources, targets, which=None):
    waits, first = [], 0
    for index, target in enumerate(targets):
        if which is not None and index not in which:
            first += target.shape[1]
            continue
        if core is None:
            copies = [mover.load(sources[index], target)]
        else:
            rows, half = target.shape[1], target.shape[2] // 2
            copies = []
            for step, source in enumerate(sources):
                cols = pl.ds(pl.multiple_of(jnp.bitwise_xor(core, step) * half, half), half)
                copies.append(mover.load(source.at[:, first : first + rows, :], target.at[:, :, cols]))
            first += rows
        waits.append(lambda copies=copies: [copy.wait() for copy in copies])
    return waits


def load_quarters(mover, place_ref, packs, expand_ref, shrink_ref):
    core, chip, line, row = place_of(place_ref)
    half, cut = expand_ref.shape[3] // 2, expand_ref.shape[2] // 2
    loads = ([], [])
    for index, pack in enumerate(packs):
        core_step, chip_step = divmod(index, 2)
        cols = pl.ds(pl.multiple_of(jnp.bitwise_xor(core, core_step) * half, half), half)
        side = jnp.bitwise_xor(chip, chip_step)
        rows = pl.ds(pl.multiple_of(side * cut, cut), cut)
        for line_step in range(4):
            for row_step in (0, 1):
                owner = lax.rem(line - line_step + 4, 4) * 2 + jnp.bitwise_xor(row, row_step)
                source = pack.at[line_step, row_step]
                loads[0].append((source.at[0], expand_ref.at[:, owner, rows, cols]))
                loads[1].append((source.at[1], shrink_ref.at[owner, side, :, :, cols]))
    return [[mover.load(*pair) for pair in pairs] for pairs in loads]


def whole(ref):
    return ref[...].reshape(-1, ref.shape[-1])


def key_extra(length_limit, count):
    lane = lanes(PAIR) % HEAD_DIM
    extra = jnp.where(lane < 3, 1.0, 0.0)
    if length_limit is None:
        return jnp.broadcast_to(extra, (count, PAIR)).astype(BF)
    row = lax.broadcasted_iota(jnp.int32, (count, PAIR), 0)
    bias = jnp.where(row < length_limit, 0.0, -1e30)
    return jnp.where(lane == 3, bias, extra).astype(BF)


def put_start(pos_ref, start_ref):
    length = start_ref.shape[0]
    query = lax.broadcasted_iota(jnp.int32, (8, length), 1)
    first = (query - pos_ref[...]).astype(F32)
    start_ref[...] = first.T[:, :1].astype(jnp.int32)


def visible(start, first_query, first_key, count):
    key = first_key + lax.broadcasted_iota(jnp.int32, (TILE, count), 1)
    seen = key >= start
    if first_key == first_query:
        query = first_query + lax.broadcasted_iota(jnp.int32, (TILE, count), 0)
        seen = seen & (key <= query)
    return seen


def key_spans(tile, count, causal):
    if not causal:
        return [(0, count)]
    spans = [(0, tile * TILE)] if tile else []
    return spans + [(tile * TILE, TILE)]


def staggered(first, then, count):
    ready = first(0)
    for index in range(count):
        following = first(index + 1) if index + 1 < count else None
        then(index, ready)
        ready = following


class ProbStore:
    def __init__(self, mover, hbm, ref, causal):
        self.hbm, self.ref, self.mover = hbm, ref, mover
        self.tiles = ref.shape[2] // TILE
        self.causal = causal
        self.first = mover.take(2 * self.tiles)

    def views(self, pair, slot, tile):
        rows = slice(tile * TILE, (tile + 1) * TILE)
        keys = slice(0, (tile + 1) * TILE) if self.causal else slice(0, self.ref.shape[3])
        sem = self.mover.sems.at[self.first + slot * self.tiles + tile]
        return self.hbm.at[pair, :, rows, keys], self.ref.at[slot, :, rows, keys], sem

    def copy(self, pair, slot, tile, out):
        far, near, sem = self.views(pair, slot, tile)
        return pltpu.make_async_copy(near, far, sem) if out else pltpu.make_async_copy(far, near, sem)


def two_pairs(pairs, body):
    @pl.loop(0, pairs // 2)
    def _(step):
        for slot in (0, 1):
            body(2 * step + slot, slot, step)


def attend(q_ref, k_ref, v_ref, extra_ref, start_ref, o_ref, store, finished):
    length, count = q_ref.shape[0], k_ref.shape[0]
    causal = start_ref is not None
    masks = half_masks()
    pairs = q_ref.shape[1] // PAIR

    def one_pair(pair, slot, step):
        cols = rows_at(pair, PAIR)

        @pl.when(step > 0)
        def _():
            for tile in range(store.tiles):
                store.copy(pair - 2, slot, tile, True).wait()

        steps = [(tile, side) for tile in range(length // TILE) for side in (0, 1)]
        results = {}

        def scores_of(index):
            tile, side = steps[index]
            rows = slice(tile * TILE, (tile + 1) * TILE)
            queries = q_ref[rows, cols] * masks[side]
            if not causal:
                base = HEAD_DIM * (1 - side)
                queries = jnp.where(lanes(PAIR) == base + 3, 1.0, queries.astype(F32)).astype(BF)
            blocks = []
            for first, size in key_spans(tile, count, causal):
                keys = k_ref[first : first + size, cols]
                if not causal:
                    keys = keys * masks[side] + extra_ref[first : first + size, :] * masks[1 - side]
                scores = dot(queries, keys, 1, 1)
                if causal:
                    seen = visible(start_ref[rows, :], tile * TILE, first, size)
                    scores = jnp.where(seen, scores, -1000000000.0)
                blocks.append(scores)
            return blocks

        def mix(index, score_blocks):
            tile, side = steps[index]
            rows = slice(tile * TILE, (tile + 1) * TILE)
            spans = key_spans(tile, count, causal)
            top = functools.reduce(
                jnp.maximum, [jnp.max(scores, axis=1, keepdims=True) for scores in score_blocks]
            )
            exponents = [jnp.exp(scores - top) for scores in score_blocks]
            inverse = 1.0 / sum(jnp.sum(exponent, axis=1, keepdims=True) for exponent in exponents)
            total = None
            for exponent, (first, size) in zip(exponents, spans):
                probs = (exponent * inverse).astype(BF)
                store.ref[slot, side, rows, first : first + size] = probs
                part = dot(probs, v_ref[first : first + size, cols], 1, 0)
                total = part if total is None else total + part
            results[side] = total
            if side == 1:
                o_ref[rows, cols] = jnp.where(lanes(PAIR) < HEAD_DIM, results[0], results[1]).astype(BF)

        staggered(scores_of, mix, len(steps))
        for tile in range(store.tiles):
            store.copy(pair, slot, tile, True).start()
        for start_store in finished:
            start_store(pair)

    two_pairs(pairs, one_pair)
    for slot in (0, 1):
        for tile in range(store.tiles):
            store.mover.leaving.append(store.copy(pairs - 2 + slot, slot, tile, True))


def load_probs(store, slot):
    for tile in reversed(range(store.tiles)):
        store.copy(slot, slot, tile, False).start()


def attend_back(q_ref, da_ref, inner_ref, k_ref, v_ref, store, dq_ref, dk_ref, dv_ref, dk_sum, dv_sum, values_ref):
    length, count = q_ref.shape[0], k_ref.shape[0]
    masks = half_masks()
    pairs = k_ref.shape[1] // PAIR

    def one_pair(pair, slot, step):
        cols = rows_at(pair, PAIR)
        for tile in range(store.tiles):
            store.copy(pair, slot, tile, False).wait()
        for side in (0, 1):
            values_ref[side] = v_ref[:, cols] * masks[side]
        steps = [(tile, side) for tile in reversed(range(length // TILE)) for side in (0, 1)]
        query_grads = {}

        def place(index):
            tile, side = steps[index]
            size = (tile + 1) * TILE if store.causal else count
            return tile, side, slice(tile * TILE, (tile + 1) * TILE), slice(0, size)

        def collect(ref, tile, side, span, part):
            if tile == length // TILE - 1:
                ref[side, :, span] = part
            else:
                ref[side, :, span] += part

        def value_side(index):
            _, side, rows, span = place(index)
            return dot(da_ref[rows, cols], values_ref[side, span, :], 1, 1)

        def score_side(index, grad_probs):
            tile, side, rows, span = place(index)
            probs = store.ref[slot, side, rows, span]
            collect(dv_sum, tile, side, span, dot(da_ref[rows, cols], probs, 0, 0))
            inner = inner_ref[pair, rows, side : side + 1]
            grad_scores = (probs.astype(F32) * (grad_probs - inner)).astype(BF)
            collect(dk_sum, tile, side, span, dot(q_ref[rows, cols], grad_scores, 0, 0))
            query_grads[side] = dot(grad_scores, k_ref[span, cols], 1, 0)
            if side == 1:
                dq_ref[rows, cols] = (
                    jnp.where(lanes(PAIR) < HEAD_DIM, query_grads[0], query_grads[1]) * HEAD_DIM**-0.5
                ).astype(BF)

        staggered(value_side, score_side, len(steps))
        for sums, out in ((dk_sum, dk_ref), (dv_sum, dv_ref)):
            joined = jnp.concatenate([sums[0, :HEAD_DIM, :], sums[1, HEAD_DIM:, :]], axis=0)
            out[:, cols] = joined.astype(BF).T

        @pl.when(step < pairs // 2 - 1)
        def _():
            for tile in range(store.tiles):
                store.copy(pair + 2, slot, tile, False).start()

    two_pairs(pairs, one_pair)


def norm_rows(summed):
    center = jnp.mean(summed, axis=1, keepdims=True)
    shifted = summed - center
    inverse = lax.rsqrt(jnp.mean(shifted * shifted, axis=1, keepdims=True) + 1e-05)
    return shifted * inverse, inverse


def norm_back(grad_out, normed, inverse, gain):
    scaled = grad_out * gain
    first = jnp.mean(scaled, axis=1, keepdims=True)
    second = jnp.mean(scaled * normed, axis=1, keepdims=True)
    return inverse * (scaled - first - normed * second)


def add_rows(ref, row, values):
    ref[row : row + 1, :] += jnp.sum(values, axis=0, keepdims=True)


def place_of(place_ref):
    rep, place = place_ref[0], place_ref[1]
    return lax.rem(rep, 2), lax.div(rep, 2), lax.div(place, 2), lax.rem(place, 2)


def assemble(place_ref, chunk_refs, all_ref):
    core, chip, line, row = place_of(place_ref)
    width = all_ref.shape[1]
    quarter = chunk_refs[0].shape[3]
    shard = quarter * 4 // 3
    for core_step, chunk_ref in enumerate(chunk_refs):
        for chip_step in (0, 1):
            rep = jnp.bitwise_xor(chip, chip_step) * 2 + jnp.bitwise_xor(core, core_step)
            for line_step in range(4):
                for row_step in (0, 1):
                    owner = lax.rem(line - line_step + 4, 4) * 2 + jnp.bitwise_xor(row, row_step)
                    for piece in range(quarter // 16):
                        stacked = rep * quarter + piece * 16
                        matrix = lax.div(stacked, shard)
                        target = matrix * width + owner * shard + (stacked - matrix * shard)
                        all_ref[pl.ds(pl.multiple_of(target, 16), 16), :] = chunk_ref[
                            chip_step, line_step, row_step, piece * 16 : (piece + 1) * 16, :
                        ]


def assemble_halves(place_ref, mine_ref, other_ref, all_ref, shards):
    core = place_of(place_ref)[0]
    devices, _, half = mine_ref.shape
    for step, ref in ((0, mine_ref), (1, other_ref)):
        cols = pl.ds(pl.multiple_of(jnp.bitwise_xor(core, step) * half, half), half)
        first, target = 0, 0
        for shard in shards:
            for owner in range(devices):
                at = target + owner * shard
                all_ref[at : at + shard, cols] = ref[owner, first : first + shard, :]
            first += shard
            target += shard * devices


def unpack_small(all_ref, base, vec_ref, bias_ref):
    devices = vec_ref.shape[1] // HEAD_DIM
    inner = bias_ref.shape[1] // devices
    for pair in range(devices // 2):
        first = base + 2 * pair * 16
        left = all_ref[first : first + 16, :PAIR].astype(F32)
        right = all_ref[first + 16 : first + 32, :PAIR].astype(F32)
        vec_ref[:, pair * PAIR : (pair + 1) * PAIR] = jnp.where(
            lanes(PAIR) < HEAD_DIM, left, pltpu.roll(right, HEAD_DIM, 1)
        )
    for owner in range(devices):
        rows = all_ref[base + owner * 16 : base + owner * 16 + 16, :inner].astype(F32)
        bias_ref[:, owner * inner : (owner + 1) * inner] = rows[10:11, :]


def self_forward_kernel(staged, *refs):
    if staged:
        place_ref, pos_ref, x_hbm, chunk_hbm, other_hbm = refs[:5]
        refs = refs[5:]
    else:
        pos_ref, x_hbm, all_hbm = refs[:3]
        refs = refs[3:]
    p_hbm, q_hbm, k_hbm, v_hbm, o_hbm = refs[:5]
    refs = refs[5:]
    if staged:
        all_out, refs = refs[0], refs[1:]
    x_ref, all_ref, q_ref, k_ref, v_ref, o_ref, p_ref, start_ref = refs[:8]
    mover = Mover(refs[-1])
    length, width = x_ref.shape
    if staged:
        chunk_refs = refs[8:10]
        loads = [mover.load(a, b) for a, b in zip((chunk_hbm, other_hbm), chunk_refs)]
    else:
        loads = [mover.load(all_hbm, all_ref)]
    x_load = mover.load(x_hbm, x_ref)
    put_start(pos_ref, start_ref)
    for load in loads:
        load.wait()
    if staged:
        assemble(place_ref, chunk_refs, all_ref)
        mover.store(all_ref, all_out)
    x_load.wait()

    @pl.loop(0, length // TILE)
    def _(tile):
        rows = rows_at(tile)
        source = x_ref[rows, :]
        queries = dot(source, all_ref[:width, :], 1, 0).astype(BF)
        q_ref[rows, :] = queries * jnp.asarray(HEAD_DIM**-0.5, BF)
        k_ref[rows, :] = dot(source, all_ref[width : 2 * width, :], 1, 0).astype(BF)
        v_ref[rows, :] = dot(source, all_ref[2 * width :, :], 1, 0).astype(BF)

    mover.store(k_ref, k_hbm)
    mover.store(v_ref, v_hbm)
    mover.store(q_ref, q_hbm)
    finished = (mover.store_parts(o_ref, o_hbm, width // PAIR, columns_at(PAIR)),)
    attend(q_ref, k_ref, v_ref, None, start_ref, o_ref, ProbStore(mover, p_hbm, p_ref, True), finished)
    mover.finish()


def unpack_small(small_ref, vec_ref, bias_ref):
    devices = vec_ref.shape[1] // HEAD_DIM
    inner = bias_ref.shape[1] // devices
    for pair in range(devices // 2):
        left = small_ref[0, 2 * pair, :, :PAIR].astype(F32)
        right = small_ref[0, 2 * pair + 1, :, :PAIR].astype(F32)
        vec_ref[:, pair * PAIR : (pair + 1) * PAIR] = jnp.where(
            lanes(PAIR) < HEAD_DIM, left, pltpu.roll(right, HEAD_DIM, 1)
        )
    for owner in range(devices):
        rows = small_ref[0, owner, :, :inner].astype(F32)
        bias_ref[:, owner * inner : (owner + 1) * inner] = rows[10:11, :]


def cross_forward_kernel(staged, *refs):
    place_ref, core = None, None
    if staged:
        place_ref, refs = refs[0], refs[1:]
        core = place_of(place_ref)[0]
    length_ref, refs = refs[0], refs[1:]
    if staged:
        x_hbm, mixed_hbm, source_hbm, *packs = refs[:5]
        refs = refs[5:]
    else:
        vec_ref, x_hbm, mixed_hbm, source_hbm, *packs = refs[:9]
        refs = refs[9:]
    first_hbm, first_inv_hbm, p_hbm, q_hbm, k_hbm, v_hbm, o_hbm, n_hbm, inv_hbm = refs[:9]
    refs = refs[9:]
    if staged:
        vec_ref, bias_ref, refs = refs[0], refs[1], refs[2:]
    x_ref, mixed_ref, source_ref, first_ref, first_inv_ref, q_ref, k_ref, v_ref, o_ref, n_ref, inv_ref = refs[:11]
    p_ref, extra_ref, *w_refs = refs[11:18]
    mover = Mover(refs[-1])
    length, width = q_ref.shape

    if staged:
        small_ref = refs[18]
        rows = packs[0].shape[1]
        small = [
            mover.load(pack.at[:, rows - 16 :, :], small_ref.at[jnp.bitwise_xor(core, step)])
            for step, pack in enumerate(packs)
        ]
    source_load = mover.load_rows(source_hbm, source_ref)
    order = (2, 3, 0, 1, 4)
    waits = [None] * 5
    if staged:
        half = width // 2
        shard = w_refs[0].shape[1]
        for index in order:
            copies = []
            for step, pack in enumerate(packs):
                cols = pl.ds(pl.multiple_of(jnp.bitwise_xor(core, step) * half, half), half)
                copies.append(
                    mover.load(pack.at[:, index * shard : (index + 1) * shard, :], w_refs[index].at[:, :, cols])
                )
            waits[index] = lambda copies=copies: [copy.wait() for copy in copies]
    else:
        for index in order:
            waits[index] = mover.load(packs[index], w_refs[index]).wait
    mixed_load = mover.load_rows(mixed_hbm, mixed_ref)
    x_load = mover.load_rows(x_hbm, x_ref)
    extra_ref[...] = key_extra(length_ref[0], k_ref.shape[0])
    waits[2]()
    waits[3]()

    @pl.loop(0, source_ref.shape[0] // TILE)
    def _(tile):
        rows = rows_at(tile)
        source_load(tile)
        source = source_ref[rows, :]
        k_ref[rows, :] = dot(source, whole(w_refs[2]), 1, 0).astype(BF)
        v_ref[rows, :] = dot(source, whole(w_refs[3]), 1, 0).astype(BF)

    mover.store(k_ref, k_hbm)
    mover.store(v_ref, v_hbm)
    if staged:
        for load in small:
            load.wait()
        unpack_small(small_ref, vec_ref, bias_ref)
    waits[0]()
    waits[1]()

    tiles = [slice(tile * TILE, (tile + 1) * TILE) for tile in range(length // TILE)]

    def self_branch(tile):
        mixed_load(tile)
        x_load(tile)
        return dot(mixed_ref[tiles[tile], :], whole(w_refs[0]), 1, 0)

    def query_rows(tile, branch):
        rows = tiles[tile]
        normed, inverse = norm_rows(x_ref[rows, :].astype(F32) * vec_ref[6:7, :] + branch)
        first_ref[rows, :] = normed
        first_inv_ref[rows, :] = inverse
        low = (normed * vec_ref[0:1, :] + vec_ref[3:4, :]).astype(BF)
        queries = dot(low, whole(w_refs[1]), 1, 0).astype(BF)
        q_ref[rows, :] = queries * jnp.asarray(HEAD_DIM**-0.5, BF)

    staggered(self_branch, query_rows, len(tiles))
    mover.store(first_ref, first_hbm)
    mover.store(first_inv_ref, first_inv_hbm)
    mover.store(q_ref, q_hbm)
    finished = (mover.store_parts(o_ref, o_hbm, width // PAIR, columns_at(PAIR)),)
    attend(q_ref, k_ref, v_ref, extra_ref, None, o_ref, ProbStore(mover, p_hbm, p_ref, False), finished)
    waits[4]()
    n_store, inv_store = mover.store_rows(n_ref, n_hbm), mover.store_rows(inv_ref, inv_hbm)

    def cross_branch(tile):
        return dot(o_ref[tiles[tile], :], whole(w_refs[4]), 1, 0)

    def second_norm(tile, branch):
        rows = tiles[tile]
        first_out = first_ref[rows, :] * vec_ref[0:1, :] + vec_ref[3:4, :]
        normed, inverse = norm_rows(first_out * vec_ref[7:8, :] + branch)
        n_ref[rows, :] = normed
        inv_ref[rows, :] = inverse
        n_store(tile)
        inv_store(tile)

    staggered(cross_branch, second_norm, len(tiles))
    mover.finish()


def hidden_kernel(staged, *refs):
    place_ref, core = None, None
    if staged:
        place_ref, refs = refs[0], refs[1:]
        core = place_of(place_ref)[0]
    vec_ref, bias_ref, *packs = refs[: 6 if staged else 4]
    n_hbm, inv_hbm, cot_hbm = refs[len(packs) + 2 : len(packs) + 5]
    refs = refs[len(packs) + 5 :]
    count = 2 if staged else 1
    sums_ref, bias_sum_ref, out_hbm, dz_hbm = refs[:4]
    grad_hbms, refs = refs[4 : 4 + count], refs[4 + count :]
    grad_refs, refs = refs[:count], refs[count:]
    n_ref, inv_ref, cot_ref, out_ref, dz_ref, low_ref, h_ref, du_ref, df_ref, slope_ref, third_ref = refs[:11]
    blocks = bias_ref.shape[1] // vec_ref.shape[1]
    e_ref, s_ref = refs[11:13]
    mover = Mover(refs[-1])
    length, width = n_ref.shape

    n_load = mover.load_rows(n_hbm, n_ref)
    if staged:
        expand_loads, shrink_loads = load_quarters(mover, place_ref, packs, e_ref, s_ref)
    else:
        expand_loads, shrink_loads = [mover.load(packs[0], e_ref)], [mover.load(packs[1], s_ref)]
    cot_load = mover.load_rows(cot_hbm, cot_ref)
    inv_load = mover.load_rows(inv_hbm, inv_ref)
    out_store, dz_store = mover.store_rows(out_ref, out_hbm), mover.store_rows(dz_ref, dz_hbm)
    tiles = [slice(tile * TILE, (tile + 1) * TILE) for tile in range(length // TILE)]
    parts = [slice(block * width, (block + 1) * width) for block in range(blocks)]
    sums = {row: 0.0 for row in (1, 2, 4, 5, 8, 9)}
    bias_sums = [0.0] * blocks

    def add(row, values):
        sums[row] = sums[row] + jnp.sum(values, axis=0, keepdims=True)

    def second_out(rows):
        return n_ref[rows, :] * vec_ref[1:2, :] + vec_ref[4:5, :]

    for tile, rows in enumerate(tiles):
        n_load(tile)
        low_ref[rows, :] = second_out(rows).astype(BF)
    steps = [(block, rows) for block in range(blocks) for rows in tiles]

    def expand(index):
        block, rows = steps[index]
        return dot(low_ref[rows, :], whole(e_ref.at[block]), 1, 0) + bias_ref[:, parts[block]]

    def activate(index, before):
        block, rows = steps[index]
        square = before * before
        tangent = jnp.tanh(before * (0.7978845608028654 + 0.7978845608028654 * 0.044715 * square))
        half = 0.5 * (1.0 + tangent)
        slope_ref[rows, parts[block]] = half + before * (half * (1.0 - tangent)) * (
            0.7978845608028654 + 3.0 * 0.7978845608028654 * 0.044715 * square
        )
        h_ref[rows, parts[block]] = (before * half).astype(BF)

    for load in expand_loads:
        load.wait()
    staggered(expand, activate, len(steps))
    for load in shrink_loads:
        load.wait()
    for tile in range(len(tiles)):
        cot_load(tile)
        inv_load(tile)

    def shrink(tile):
        return dot(h_ref[tiles[tile], :], whole(s_ref), 1, 0)

    def outer_norm(tile, branch_out):
        rows = tiles[tile]
        second = second_out(rows)
        normed, inverse = norm_rows(second * vec_ref[8:9, :] + vec_ref[9:10, :] + branch_out)
        out_ref[rows, :] = (normed * vec_ref[2:3, :] + vec_ref[5:6, :]).astype(BF)
        grad_out = cot_ref[rows, :].astype(F32)
        third = norm_back(grad_out, normed, inverse, vec_ref[2:3, :])
        third_ref[rows, :] = third
        add(2, grad_out * normed)
        add(5, grad_out)
        branch = third.astype(BF)
        df_ref[rows, :] = branch
        add(9, branch.astype(F32))
        add(8, second * third)

    staggered(shrink, outer_norm, len(tiles))
    for tile in range(len(tiles)):
        out_store(tile)

    def shrink_back(index):
        block, rows = steps[index]
        return dot(df_ref[rows, :], whole(s_ref)[parts[block], :], 1, 1)

    def slope_back(index, grad_hidden):
        block, rows = steps[index]
        du = (grad_hidden * slope_ref[rows, parts[block]]).astype(BF)
        du_ref[rows, parts[block]] = du
        bias_sums[block] = bias_sums[block] + jnp.sum(du.astype(F32), axis=0, keepdims=True)

    staggered(shrink_back, slope_back, len(steps))

    def expand_back(tile):
        rows = tiles[tile]
        return sum(dot(du_ref[rows, parts[block]], whole(e_ref.at[block]), 1, 1) for block in range(blocks))

    def inner_norm(tile, grad_expanded):
        rows = tiles[tile]
        grad = vec_ref[8:9, :] * third_ref[rows, :] + grad_expanded
        normed = n_ref[rows, :]
        dz_ref[rows, :] = norm_back(grad, normed, inv_ref[rows, :], vec_ref[1:2, :])
        add(1, grad * normed)
        add(4, grad)

    staggered(expand_back, inner_norm, len(tiles))
    for tile in range(len(tiles)):
        dz_store(tile)
    sums_ref[...] = jnp.zeros_like(sums_ref)
    for row, values in sums.items():
        sums_ref[row : row + 1, :] = values
    for block, values in enumerate(bias_sums):
        bias_sum_ref[:, parts[block]] = values
    for step in reversed(range(count)):
        for block in range(blocks):
            put_grad(grad_refs, step, place_ref, block, low_ref[...], du_ref, block * width)
            put_shrink(grad_refs, step, place_ref, block, blocks, h_ref[:, parts[block]], df_ref)
        mover.store(grad_refs[step], grad_hbms[step])
    mover.finish()


def branch_grads(branch_rows, mixed_weight, o_ref, da_ref, inner_ref):
    width = o_ref.shape[1]
    tiles = [slice(tile * TILE, (tile + 1) * TILE) for tile in range(o_ref.shape[0] // TILE)]
    head = lax.broadcasted_iota(jnp.int32, (width, PAIR), 0) // HEAD_DIM
    picks = jnp.where(head == lax.broadcasted_iota(jnp.int32, (width, PAIR), 1), 1.0, 0.0).astype(BF)

    def project(tile):
        return dot(branch_rows(tile, tiles[tile]), mixed_weight, 1, 1)

    def reduce(tile, mixed_grad):
        rows = tiles[tile]
        low = mixed_grad.astype(BF)
        da_ref[rows, :] = low
        product = low.astype(F32) * o_ref[rows, :].astype(F32)
        high = product.astype(BF)
        rest = (product - high.astype(F32)).astype(BF)
        inner = dot(high, picks, 1, 0) + dot(rest, picks, 1, 0)
        for pair in range(width // PAIR):
            inner_ref[pair, rows, :] = pltpu.roll(inner, (PAIR - 2 * pair) % PAIR, 1) if pair else inner

    staggered(project, reduce, len(tiles))


def put_grad(grad_refs, step, place_ref, index, left, right_ref, first=0):
    width = left.shape[1]
    if place_ref is None:
        grad = dot(left, right_ref[:, first : first + width], 0, 0)
        grad_refs[0][index * width : (index + 1) * width, :] = grad.astype(BF)
        return
    core, _, _, row = place_of(place_ref)
    half = width // 2
    shard = width // 8
    cols = pl.ds(pl.multiple_of(first + jnp.bitwise_xor(core, step) * half, half), half)
    grad = dot(left, right_ref[:, cols], 0, 0).astype(BF).reshape(4, 2, shard, half)
    for side in (0, 1):
        slot = jnp.bitwise_xor(row, side)
        grad_refs[step][slot, :, index * shard : (index + 1) * shard, :] = grad[:, side]


def put_shrink(grad_refs, step, place_ref, block, blocks, left, right_ref):
    width = left.shape[1]
    if place_ref is None:
        first = (blocks + block) * width
        grad_refs[0][first : first + width, :] = dot(left, right_ref[...], 0, 0).astype(BF)
        return
    core, _, _, row = place_of(place_ref)
    half, shard = width // 2, width * blocks // 8
    base = width // 8 * blocks
    cols = pl.ds(pl.multiple_of(jnp.bitwise_xor(core, step) * half, half), half)
    grad = dot(left, right_ref[:, cols], 0, 0).astype(BF).reshape(width // shard, shard, half)
    for part in range(width // shard):
        owner = block * (width // shard) + part
        grad_refs[step][jnp.bitwise_xor(row, owner % 2), owner // 2, base:, :] = grad[part]


def put_small(grad_refs, place_ref, base, sums, bias_sum):
    core, _, _, row = place_of(place_ref)
    half = grad_refs[0].shape[3]
    inner = bias_sum.shape[1] // 8
    index = lax.broadcasted_iota(jnp.int32, (16, half), 0)
    for owner in range(8):
        block = sums[:, owner // 2 * PAIR : (owner // 2 + 1) * PAIR]
        if owner % 2:
            block = pltpu.roll(block, HEAD_DIM, 1)
        block = jnp.concatenate([block, jnp.zeros((16, half - PAIR), F32)], axis=1)
        block = jnp.where(index == 10, bias_sum[:, owner * inner : (owner + 1) * inner], block)
        high = block.astype(BF)
        low = (block - high.astype(F32)).astype(BF)
        slot = jnp.bitwise_xor(row, owner % 2)
        first = (core == 0).astype(F32)
        for step, grad_ref in enumerate(grad_refs):
            is_high = first if step == 0 else 1.0 - first
            mixed = high.astype(F32) * is_high + low.astype(F32) * (1.0 - is_high)
            grad_ref[slot, owner // 2, base : base + 16, :] = mixed.astype(BF)


def cross_backward_kernel(staged, *refs):
    place_ref, core = None, None
    if staged:
        place_ref, refs = refs[0], refs[1:]
        core = place_of(place_ref)[0]
    vec_ref, refs = refs[0], refs[1:]
    if staged:
        sums_three_ref, bias_sum_ref, refs = refs[0], refs[1], refs[2:]
    packs, refs = refs[: 2 if staged else 5], refs[2 if staged else 5 :]
    p_hbm, dz_hbm, x_hbm, first_hbm, inv_hbm, source_hbm, q_hbm, k_hbm, v_hbm, o_hbm, self_o_hbm = refs[:11]
    sums_ref, dfirst_hbm, dsource_hbm = refs[11:14]
    count = 2 if staged else 1
    grad_hbms, refs = refs[14 : 14 + count], refs[14 + count :]
    grad_refs, refs = refs[:count], refs[count:]
    dz_ref, x_ref, first_ref, inv_ref, source_ref, q_ref, k_ref, v_ref, o_ref, self_o_ref = refs[:10]
    dfirst_ref, dsource_ref, *w_refs = refs[10:17]
    low_ref, da_ref, inner_ref, dq_ref, dk_ref, dv_ref, dk_sum, dv_sum, branch_ref, values_ref, p_ref = refs[17:28]
    mover = Mover(refs[-1])
    length, width = dz_ref.shape

    dz_load, o_load = mover.load_rows(dz_hbm, dz_ref), mover.load_rows(o_hbm, o_ref)
    waits = load_matrices(mover, core, packs, w_refs, (4,))
    sums_ref[...] = jnp.zeros_like(sums_ref)
    waits[0]()
    store = ProbStore(mover, p_hbm, p_ref, False)
    load_probs(store, 0)
    middle = [mover.load(a, b) for a, b in ((v_hbm, v_ref), (q_hbm, q_ref), (k_hbm, k_ref))]

    def branch_rows(tile, rows):
        dz_load(tile)
        o_load(tile)
        branch_ref[rows, :] = dz_ref[rows, :].astype(BF)
        return branch_ref[rows, :]

    branch_grads(branch_rows, whole(w_refs[4]), o_ref, da_ref, inner_ref)
    for step in range(count):
        put_grad(grad_refs, step, place_ref, 4, o_ref[...], branch_ref)
    load_probs(store, 1)
    first_load = mover.load_rows(first_hbm, first_ref)
    waits = load_matrices(mover, core, packs, w_refs, (1, 2, 3))
    last = [
        mover.load(a, b)
        for a, b in ((source_hbm, source_ref), (x_hbm, x_ref), (inv_hbm, inv_ref), (self_o_hbm, self_o_ref))
    ]
    for load in middle:
        load.wait()
    attend_back(q_ref, da_ref, inner_ref, k_ref, v_ref, store, dq_ref, dk_ref, dv_ref, dk_sum, dv_sum, values_ref)
    for load in last:
        load.wait()
    for wait in waits:
        wait()
    for tile in range(length // TILE):
        first_load(tile)

    dsource_store = mover.store_rows(dsource_ref, dsource_hbm)
    dfirst_store = mover.store_rows(dfirst_ref, dfirst_hbm)
    tiles = [slice(tile * TILE, (tile + 1) * TILE) for tile in range(length // TILE)]
    key_tiles = [slice(tile * TILE, (tile + 1) * TILE) for tile in range(source_ref.shape[0] // TILE)]
    sums = {row: 0.0 for row in (0, 3, 6, 7)}

    def add(row, values):
        sums[row] = sums[row] + jnp.sum(values, axis=0, keepdims=True)

    def source_grad(tile):
        rows = key_tiles[tile]
        dsource_ref[rows, :] = dot(dk_ref[rows, :], whole(w_refs[2]), 1, 1) + dot(
            dv_ref[rows, :], whole(w_refs[3]), 1, 1
        )

    def put_keys(step):
        put_grad(grad_refs, step, place_ref, 2, source_ref[...], dk_ref)
        put_grad(grad_refs, step, place_ref, 3, source_ref[...], dv_ref)

    products = [functools.partial(source_grad, tile) for tile in range(len(key_tiles))]
    products += [functools.partial(put_keys, step) for step in range(count)]

    def query_back(tile):
        product = dot(dq_ref[tiles[tile], :], whole(w_refs[1]), 1, 1)
        for run in products[tile :: len(tiles)]:
            run()
        return product

    def first_norm(tile, product):
        rows = tiles[tile]
        grad = dz_ref[rows, :]
        dx = product + vec_ref[7:8, :] * grad
        normed = first_ref[rows, :]
        first_out = normed * vec_ref[0:1, :] + vec_ref[3:4, :]
        low_ref[rows, :] = first_out.astype(BF)
        add(7, first_out * grad)
        dfirst = norm_back(dx, normed, inv_ref[rows, :], vec_ref[0:1, :])
        dfirst_ref[rows, :] = dfirst
        add(0, dx * normed)
        add(3, dx)
        add(6, x_ref[rows, :].astype(F32) * dfirst)
        branch_ref[rows, :] = dfirst.astype(BF)

    staggered(query_back, first_norm, len(tiles))
    for tile in range(len(key_tiles)):
        dsource_store(tile)
    for tile in range(len(tiles)):
        dfirst_store(tile)
    for row, values in sums.items():
        sums_ref[row : row + 1, :] = values

    if staged:
        put_small(grad_refs, place_ref, 5 * (width // 8), sums_ref[...] + sums_three_ref[...], bias_sum_ref[...])
    for step in reversed(range(count)):
        put_grad(grad_refs, step, place_ref, 1, low_ref[...], dq_ref)
        put_grad(grad_refs, step, place_ref, 0, self_o_ref[...], branch_ref)
        mover.store(grad_refs[step], grad_hbms[step])
    mover.finish()


def self_backward_kernel(staged, *refs):
    place_ref, core = None, None
    if staged:
        place_ref, refs = refs[0], refs[1:]
        core = place_of(place_ref)[0]
    count = 2 if staged else 1
    packs, refs = refs[:count], refs[count:]
    p_hbm, dz_hbm, x_hbm, q_hbm, k_hbm, v_hbm, o_hbm, *head_hbms = refs[:10]
    grad_hbms, refs = refs[10 : 10 + count], refs[10 + count :]
    grad_refs, refs = refs[:count], refs[count:]
    dz_ref, x_ref, q_ref, k_ref, v_ref, o_ref, w_ref = refs[:7]
    da_ref, inner_ref, dq_ref, dk_ref, dv_ref, dk_sum, dv_sum, values_ref, p_ref = refs[7:16]
    mover = Mover(refs[-1])
    length, width = dz_ref.shape

    dz_load = mover.load_rows(dz_hbm, dz_ref)
    waits = load_matrices(mover, core, packs, (w_ref,))
    o_load = mover.load_rows(o_hbm, o_ref)
    waits[0]()
    store = ProbStore(mover, p_hbm, p_ref, True)
    load_probs(store, 0)
    middle = [mover.load(a, b) for a, b in ((v_hbm, v_ref), (q_hbm, q_ref), (k_hbm, k_ref))]

    def branch_rows(tile, rows):
        dz_load(tile)
        o_load(tile)
        return dz_ref[rows, :].astype(BF)

    branch_grads(branch_rows, whole(w_ref), o_ref, da_ref, inner_ref)
    load_probs(store, 1)
    x_load = mover.load(x_hbm, x_ref)
    for load in middle:
        load.wait()
    attend_back(q_ref, da_ref, inner_ref, k_ref, v_ref, store, dq_ref, dk_ref, dv_ref, dk_sum, dv_sum, values_ref)
    for near, far in zip((dq_ref, dk_ref, dv_ref), head_hbms):
        mover.store(near, far)
    x_load.wait()
    for step in reversed(range(count)):
        for index, grads in enumerate((dq_ref, dk_ref, dv_ref)):
            put_grad(grad_refs, step, place_ref, index, x_ref[...], grads)
        mover.store(grad_refs[step], grad_hbms[step])
    mover.finish()


def input_grad_kernel(vec_ref, dz_hbm, all_hbm, dq_hbm, dk_hbm, dv_hbm, dx_hbm, *refs):
    dz_ref, all_ref, dq_ref, dk_ref, dv_ref, dx_ref, sems = refs
    mover = Mover(sems)
    width = dz_ref.shape[1]
    all_load = mover.load(all_hbm, all_ref)
    heads = (dq_ref, dk_ref, dv_ref)
    loads = [mover.load_rows(a, b) for a, b in zip((dq_hbm, dk_hbm, dv_hbm), heads)]
    loads.append(mover.load_rows(dz_hbm, dz_ref))
    dx_store = mover.store_rows(dx_ref, dx_hbm)
    all_load.wait()

    @pl.loop(0, dz_ref.shape[0] // TILE)
    def _(tile):
        rows = rows_at(tile)
        for load in loads:
            load(tile)
        dx = vec_ref[6:7, :] * dz_ref[rows, :]
        for index, grads in enumerate(heads):
            dx = dx + dot(grads[rows, :], all_ref[index * width : (index + 1) * width, :], 1, 1)
        dx_ref[rows, :] = dx
        dx_store(tile)

    mover.finish()


def call(kernel, args, outs, scratch, limit, flops, smem=(), near=(), near_outs=(), copies=0):
    spaces = [pltpu.SMEM if i in smem else pltpu.VMEM if i in near else pl.ANY for i in range(len(args))]
    out_spaces = [pltpu.VMEM if i in near_outs else pl.ANY for i in range(len(outs))]
    buffers = [pltpu.VMEM(shape, kind) for shape, kind in scratch]
    if copies:
        buffers.append(pltpu.SemaphoreType.DMA((copies,)))
    return pl.pallas_call(
        kernel,
        out_shape=[jax.ShapeDtypeStruct(shape, kind) for shape, kind in outs],
        in_specs=[pl.BlockSpec(memory_space=space) for space in spaces],
        out_specs=[pl.BlockSpec(memory_space=space) for space in out_spaces],
        scratch_shapes=buffers,
        compiler_params=pltpu.CompilerParams(vmem_limit_bytes=(63 if copies else limit) * MIB),
        cost_estimate=pl.CostEstimate(flops=flops, bytes_accessed=16 * MIB, transcendentals=0),
    )(*args)


def like(*arrays):
    return [(a.shape, a.dtype) for a in arrays]


def prob_shape(queries, keys, width):
    return (width // PAIR, 2, queries, keys), BF


def forward_self(place, x, pos, pack, staged):
    length, width = x.shape
    low = ((length, width), BF)
    outs = [prob_shape(length, length, width), low, low, low, low]
    matrices = ((3 * width, width), BF)
    scratch = [low, matrices, low, low, low, low, ((2, 2, length, length), BF), ((length, 1), jnp.int32)]
    if staged:
        return call(
            functools.partial(self_forward_kernel, True),
            (place, pos, x, *pack),
            [*outs, matrices],
            [*scratch, *like(*pack)],
            40, 10**10, smem=(0,), near=(1,), copies=24,
        )
    results = call(
        functools.partial(self_forward_kernel, False),
        (pos, x, pack), outs, scratch, 40, 10**10, near=(0,), copies=24,
    )
    return (*results, pack)


def matrix_buffers(shards, width):
    return [((8 if rows < width else 1, rows, width), BF) for rows in shards]


def forward_cross(place, x, mixed, source, count, packs, given, shards):
    length, width = x.shape
    keys = source.shape[0]
    low, full, column, key_low = ((length, width), BF), ((length, width), F32), ((length, 1), F32), ((keys, width), BF)
    outs = [full, column, prob_shape(length, keys, width), low, key_low, key_low, low, full, column]
    near = [full, column, low, key_low, key_low, low, full, column]
    scratch = [low, low, key_low, *near, ((2, 2, length, keys), BF), ((keys, PAIR), BF)]
    if place is not None:
        return call(
            functools.partial(cross_forward_kernel, True),
            (place, count, x, mixed, source, *packs),
            [*outs, ((16, width), F32), ((1, 4 * width), F32)],
            [*scratch, *matrix_buffers(shards, width), ((2, 8, 16, width // 2), BF)],
            44, 10**10, smem=(0, 1), near_outs=(9, 10), copies=64,
        )
    vec, bias = given
    results = call(
        functools.partial(cross_forward_kernel, False),
        (count, vec, x, mixed, source, *packs),
        outs, [*scratch, *like(*packs)],
        44, 10**10, smem=(0,), near=(1,), copies=64,
    )
    return (*results, vec, bias)


def grad_outs(rows, width, staged):
    return [((2, 4, rows, width // 2), BF)] * 2 if staged else [((rows, width), BF)]


def hidden_step(place, packs, normed, inverse, cot, vec, bias):
    length, width = normed.shape
    inner = bias.shape[1]
    blocks = inner // width
    staged = place is not None
    low, full = ((length, width), BF), ((length, width), F32)
    grads = grad_outs(2 * inner // 8 if staged else 2 * inner, width, staged)
    args = (vec, bias, *packs, normed, inverse, cot)
    matrices = like(*packs)
    if staged:
        rows = width // 8
        matrices = [((blocks, 8, rows, width), BF), ((8, 2, blocks, rows // 2, width), BF)]
    return call(
        functools.partial(hidden_kernel, staged),
        (place, *args) if staged else args,
        [((16, width), F32), ((1, inner), F32), low, full, *grads],
        [*grads, *like(normed, inverse, cot), low, full, low, ((length, inner), BF), ((length, inner), BF), low,
         ((length, inner), F32), full, *matrices],
        44, 2 * 10**10, smem=(0,) if staged else (), near=(1, 2) if staged else (0, 1), near_outs=(0, 1),
        copies=96,
    )


def backward_cross(place, packs, dz, x, normed, inverse, source, vec, saved, mixed, small, shards):
    length, width = dz.shape
    keys = source.shape[0]
    staged = place is not None
    probs, *saved = saved
    arrays = (dz, x, normed, inverse, source, *saved, mixed)
    low, key_low, sums = ((length, width), BF), ((keys, width), BF), ((2, PAIR, keys), F32)
    grads = grad_outs(5 * width // 8 + 16 if staged else 5 * width, width, staged)
    full, key_full = ((length, width), F32), ((keys, width), F32)
    return call(
        functools.partial(cross_backward_kernel, staged),
        (place, vec, *small, *packs, probs, *arrays) if staged else (vec, *packs, probs, *arrays),
        [((16, width), F32), full, key_full, *grads],
        [*grads, *like(*arrays), full, key_full, *(matrix_buffers(shards, width) if staged else like(*packs)),
         low, low, ((width // PAIR, length, PAIR), F32), low, key_low, key_low, sums, sums, low, ((2, keys, PAIR), BF),
         ((2, 2, length, keys), BF)],
        48, 2 * 10**10, smem=(0,) if staged else (), near=(1, 2, 3) if staged else (0,), near_outs=(0,), copies=72,
    )


def backward_self(place, packs, dz, x, saved, shards):
    length, width = dz.shape
    staged = place is not None
    probs, *saved = saved
    arrays = (dz, x, *saved)
    low, sums = ((length, width), BF), ((2, PAIR, length), F32)
    grads = grad_outs(3 * width // 8 if staged else 3 * width, width, staged)
    first = matrix_buffers(shards[:1], width) if staged else like(*packs)
    return call(
        functools.partial(self_backward_kernel, staged),
        (place, *packs, probs, *arrays) if staged else (*packs, probs, *arrays),
        [low, low, low, *grads],
        [*grads, *like(*arrays), *first, low, ((width // PAIR, length, PAIR), F32), low, low, low, sums, sums,
         ((2, length, PAIR), BF), ((2, 2, length, length), BF)],
        48, 2 * 10**10, smem=(0,) if staged else (), copies=64,
    )


def input_gradient(vec, dz, matrices, heads):
    arrays = (dz, matrices, *heads)
    return call(
        input_grad_kernel, (vec, *arrays), like(dz), [*like(*arrays), *like(dz)], 40, 2 * 10**9, near=(0,), copies=24
    )[0]


def adam_step(settings_ref, now, grad, one, two, decay):
    beta_one, beta_two = settings_ref[1], settings_ref[2]
    first = beta_one * one + (1.0 - beta_one) * grad
    second = beta_two * two + (1.0 - beta_two) * grad * grad
    change = (first / settings_ref[4]) / (jnp.sqrt(second / settings_ref[5]) + 1e-08)
    if decay:
        change = change + settings_ref[3] * now
    return now - settings_ref[0] * change, first, second


def store_step(refs, where, results):
    for ref, value in zip(refs, results):
        ref[where] = value


def hidden_adam_kernel(place_ref, settings_ref, *refs):
    core = place_of(place_ref)[0]
    hbms, new_hbms, refs = refs[:8], refs[8:14], refs[14:]
    mine_ref, other_ref, *params = refs[:8]
    news, mover = refs[8:14], Mover(refs[-1])
    loads = [mover.load(a, b) for a, b in zip(hbms, refs[:8])]
    expand, shrink = params[0:3], params[3:6]
    half = mine_ref.shape[1]
    shard = expand[0].shape[0]
    blocks = expand[0].shape[1] // (2 * half)
    for load in loads[:5]:
        load.wait()
    sides = [(jnp.bitwise_xor(core, step) * half, ref) for step, ref in ((0, mine_ref), (1, other_ref))]
    for side, ref in sides:
        for block in range(blocks):
            where = (slice(None), pl.ds(pl.multiple_of(block * 2 * half + side, half), half))
            grad = ref[block * shard : (block + 1) * shard, :]
            now, one, two = (r[where] for r in expand)
            store_step(news[:3], where, adam_step(settings_ref, now, grad, one, two, True))
    for load in loads[5:]:
        load.wait()
    for near, far in zip(news[:3], new_hbms[:3]):
        mover.store(near, far)
    for side, ref in sides:
        where = (slice(None), pl.ds(pl.multiple_of(side, half), half))
        now, one, two = (r[where] for r in shrink)
        store_step(news[3:], where, adam_step(settings_ref, now, ref[blocks * shard :, :], one, two, True))
    for near, far in zip(news[3:], new_hbms[3:]):
        mover.store(near, far)
    mover.finish()


def attention_adam_kernel(place_ref, settings_ref, mine_ref, other_ref, *refs):
    core = place_of(place_ref)[0]
    matrices, bias, vectors = refs[0:3], refs[3:6], refs[6:9]
    new_matrices, new_bias, new_vectors = refs[9:12], refs[12:15], refs[15:18]
    half = mine_ref.shape[1]
    shard = matrices[0].shape[1]
    for step, ref in ((0, mine_ref), (1, other_ref)):
        cols = pl.ds(pl.multiple_of(jnp.bitwise_xor(core, step) * half, half), half)
        for index in range(8):
            where = (index, slice(None), cols)
            now, one, two = (r[where] for r in matrices)
            grad = ref[index * shard : (index + 1) * shard, :]
            store_step(new_matrices, where, adam_step(settings_ref, now, grad, one, two, True))
    small = mine_ref[8 * shard :, :] + other_ref[8 * shard :, :]
    for group, new, grad in (
        (bias, new_bias, small[10:11, : bias[0].shape[1]]),
        (vectors, new_vectors, small[:10, : vectors[0].shape[1]]),
    ):
        now, one, two = (r[...] for r in group)
        store_step(new, ..., adam_step(settings_ref, now, grad, one, two, False))


def hidden_adam(scalars, grads, params):
    return call(
        hidden_adam_kernel, (*scalars, *grads, *params), like(*params), [*like(*grads), *like(*params), *like(*params)],
        40, 10**9, smem=(0, 1), copies=16,
    )


def adam_call(kernel, scalars, grads, params):
    return call(
        kernel, (*scalars, *grads, *params), [(p.shape, F32) for p in params], [], 32, 10**7, smem=(0, 1),
        near=range(2, 2 + len(grads) + len(params)), near_outs=range(len(params)),
    )


CORE_SWAP = [(0, 1), (1, 0), (2, 3), (3, 2)]
CHIP_SWAP = [(0, 2), (2, 0), (1, 3), (3, 1)]
ROW_SWAP = [(i, i ^ 1) for i in range(8)]


LINES = [[0, 2, 4, 6], [1, 3, 5, 7]]


def line_shift(step):
    return [(2 * z + y, 2 * ((z + step) % 4) + y) for z in range(4) for y in (0, 1)]


def small_mesh(mesh):
    return mesh.shape["rep"] == 4 and mesh.shape["fsdp"] == 8


class StagedGather:
    def rows(self, mine, done):
        self.mine = mine
        self.other = lax.ppermute(after(mine, done), "fsdp", ROW_SWAP)

    def line(self, done):
        self.pair = after(jnp.stack([self.mine, self.other]), done)
        self.received = [lax.ppermute(self.pair, "fsdp", line_shift(step)) for step in (1, 2, 3)]

    def chips(self, done):
        self.arrived = after(tuple(self.received), done)
        self.part = jnp.stack([self.pair, *self.arrived])
        self.far = lax.ppermute(self.part, "rep", CHIP_SWAP)

    def cores(self, done):
        far = after(self.far, done)
        part = after(self.part, done)
        return part, far, lax.ppermute(part, "rep", CORE_SWAP), lax.ppermute(far, "rep", CORE_SWAP)


def gather_staged(pack):
    quarter = pack.shape[0] // 4
    mine = lax.dynamic_slice_in_dim(pack, lax.axis_index("rep") * quarter, quarter, 0)
    pair = jnp.stack([mine, lax.ppermute(mine, "fsdp", ROW_SWAP)])
    part = jnp.stack([pair] + [lax.ppermute(pair, "fsdp", line_shift(step)) for step in (1, 2, 3)])
    both = jnp.stack([part, lax.ppermute(part, "rep", CHIP_SWAP)])
    return pair, part, both


def after(value, *done):
    return lax.optimization_barrier((value, *done))[0]


def half_columns(pack):
    half = pack.shape[1] // 2
    return lax.dynamic_slice_in_dim(pack, lax.axis_index("rep") % 2 * half, half, 1)


def both_halves(mine, *done):
    mine = after(mine, *done)
    return mine, lax.ppermute(mine, "rep", CORE_SWAP)


def reduce_cores(keep, send):
    received = lax.ppermute(send, "rep", CORE_SWAP)
    return keep[0] + received[0], keep[1] + received[1]


def send_rows(send):
    return lax.ppermute(send, "fsdp", ROW_SWAP)


def reduce_rows(keep, received, done):
    return keep + after(received, done)


def reduce_chips(part, *done):
    return part.astype(F32) + after(lax.ppermute(part, "rep", CHIP_SWAP), *done).astype(F32)


def reduce_last(part, *done):
    total = reduce_chips(part, *done)
    return total, lax.ppermute(total, "rep", CORE_SWAP)


def reduce_line(joined):
    part = lax.psum_scatter(joined, "fsdp", scatter_dimension=0, axis_index_groups=LINES)
    return part.reshape(joined.shape[1:])


def reduce_shifts(joined, done):
    line = lax.axis_index("fsdp") // 2
    total = lax.dynamic_index_in_dim(joined, line, 0, False).astype(F32)
    for step in (1, 2, 3):
        away = lax.dynamic_index_in_dim(joined, (line + step) % 4, 0, False)
        total = total + after(lax.ppermute(away, "fsdp", line_shift(step)), done).astype(F32)
    return total.astype(BF)


def reduce_plain(grads):
    return lax.psum(lax.psum_scatter(grads, "fsdp", scatter_dimension=0), "rep").astype(F32)


def adam_update(weight_now, gradient, moment_one, moment_two, settings, step_float, factor):
    learn_rate, beta_one, beta_two, decay_rate = settings[0], settings[1], settings[2], settings[3]
    first_new = beta_one * moment_one + (1.0 - beta_one) * gradient
    second_new = beta_two * moment_two + (1.0 - beta_two) * gradient * gradient
    first_hat = first_new / (1.0 - beta_one**step_float)
    second_hat = second_new / (1.0 - beta_two**step_float)
    change = first_hat / (jnp.sqrt(second_hat) + 1e-08) + factor * decay_rate * weight_now
    return (weight_now - learn_rate * change, first_new, second_new)


def per_device(
    small, inputs, memory, memory_length, target_pos, cotangent,
    attention_weights, expand_weights, shrink_weights, expand_bias, layer_vectors,
    first_attention, first_expand, first_shrink, first_bias, first_vectors,
    second_attention, second_expand, second_shrink, second_bias, second_vectors,
    hyper_rates, step_count,
):
    length, width = inputs.shape[1:]
    shard = attention_weights.shape[1]
    count = width // shard
    inner_shard = shrink_weights.shape[0]
    blocks = inner_shard // shard
    low_attention = attention_weights.astype(BF).reshape(8 * shard, width)
    pack_one = low_attention[: 3 * shard]
    expand_low = expand_weights.astype(BF).reshape(shard, blocks, width)
    shrink_low = shrink_weights.astype(BF)
    x, source, cot = inputs[0], memory[0], cotangent[0]
    step_float = step_count.astype(F32)

    if small:
        place = jnp.stack([lax.axis_index("rep"), lax.axis_index("fsdp")]).astype(jnp.int32)
        small_rows = jnp.concatenate(
            [
                jnp.pad(layer_vectors, ((0, 0), (0, inner_shard - shard))),
                expand_bias[None],
                jnp.zeros((5, inner_shard), F32),
            ]
        )
        small_rows = jnp.pad(small_rows, ((0, 0), (0, width - inner_shard))).astype(BF)
        pack_two = jnp.concatenate([low_attention[3 * shard :], small_rows])
        half_two = half_columns(pack_two)
        two = lax.all_gather(half_two, "fsdp", axis=0)
        pair_one, part_one, one = gather_staged(pack_one)
        half = shard // 2
        halves = expand_low.reshape(2, half, blocks, width).transpose(0, 2, 1, 3)
        quarters = jnp.stack([halves, shrink_low.reshape(2, blocks, half, width)], axis=1)
        core, chip = place[0] % 2, place[0] // 2
        quarter = lax.dynamic_slice(
            quarters, (chip, 0, 0, 0, core * (width // 2)), (1, *quarters.shape[1:4], width // 2)
        )
        three = StagedGather()
        three.rows(quarter[0], pair_one)
        one = both_halves(one, three.other)
        three.line(part_one)
        given = None
        cross_shards = (shard,) * 5
    else:
        place, cross_shards = None, None
        flat = jnp.concatenate([layer_vectors.reshape(-1), expand_bias]).astype(BF)
        flat = lax.all_gather(flat, "fsdp", axis=0).astype(F32)
        vector_size = layer_vectors.size
        vec = flat[:, :vector_size].reshape(count, -1, shard).transpose(1, 0, 2).reshape(-1, width)
        given = jnp.pad(vec, ((0, 16 - vec.shape[0]), (0, 0))), flat[:, vector_size:].reshape(1, -1)

        def gather_all(pack, shards):
            full = lax.all_gather(pack, "fsdp", axis=0)
            pieces, first = [], 0
            for rows in shards:
                pieces.append(full[:, first : first + rows].reshape(-1, width))
                first += rows
            return pieces

        def owners(grads, shards):
            pieces, first = [], 0
            for rows in shards:
                pieces.append(grads[first : first + rows * count].reshape(count, rows, width))
                first += rows * count
            return jnp.concatenate(pieces, axis=1)

        one = jnp.concatenate(gather_all(pack_one, (shard,) * 3))
        two = [m[None] for m in gather_all(low_attention[3 * shard :], (shard,) * 5)]
        pack = jnp.concatenate([expand_low.transpose(1, 0, 2).reshape(-1, width), shrink_low])
        *expand_all, shrink_all = gather_all(pack, (*(shard,) * blocks, inner_shard))
        three = jnp.stack(expand_all)[:, None], shrink_all[None]

    *saved_one, matrices = forward_self(place, x, target_pos, one, small)
    if small:
        three.chips(saved_one[4])
        two = both_halves(two, *three.arrived)
    norm_one, inv_one, *saved_two, norm_two, inv_two, vec, bias = forward_cross(
        place, x, saved_one[4], source, memory_length, two, given, cross_shards
    )
    three = three.cores(norm_two) if small else three
    sums_three, bias_sum, outputs, dz_two, *grad_three = hidden_step(
        place, three, norm_two, inv_two, cot, vec, bias
    )
    if small:
        keep_three, send_three = reduce_cores(*grad_three)
        dz_two = after(dz_two, keep_three, send_three)
        received_three = send_rows(send_three)
    sums_two, dz_one, memory_grad, *grad_two = backward_cross(
        place, two, dz_two, x, norm_one, inv_one, source, vec, saved_two, saved_one[4],
        (sums_three, bias_sum), cross_shards,
    )
    if small:
        joined_three = reduce_rows(keep_three, received_three, dz_one)
        keep_two, send_two = reduce_cores(grad_two[0], after(grad_two[1], received_three))
        dz_one = after(dz_one, joined_three, keep_two, send_two)
        received_two = send_rows(send_two)
    *heads, grad_keep, grad_send = (
        *backward_self(place, two if small else two[:1], dz_one, x, saved_one, cross_shards),
        *((None,) if not small else ()),
    )
    if small:
        keep_one, send_one = reduce_cores(grad_keep, after(grad_send, received_two))
        joined_two = reduce_rows(after(keep_two, send_one), received_two, heads[0])
        heads = after(tuple(heads), keep_one, send_one, joined_two)
        received_one = send_rows(send_one)
    input_grad = input_gradient(vec, dz_one, matrices, heads)

    attention = (attention_weights, first_attention, second_attention)
    expand = (expand_weights, first_expand, second_expand)
    shrink = (shrink_weights, first_shrink, second_shrink)
    bias = (expand_bias, first_bias, second_bias)
    vectors = (layer_vectors, first_vectors, second_vectors)
    if small:
        powers = 1.0 - hyper_rates[1:3] ** step_float
        scalars = place, jnp.concatenate([hyper_rates, powers])
        part_three = reduce_line(joined_three)
        part_two = reduce_line(joined_two)
        total_three = reduce_last(after(part_three, send_one), input_grad)
        joined_one = reduce_rows(keep_one, received_one, input_grad)
        hidden_new = hidden_adam(scalars, total_three, (*expand, *shrink))
        part_one = reduce_shifts(joined_one, hidden_new[0])
        parts = part_one, after(part_two, hidden_new[0])
        received = after(tuple(lax.ppermute(part, "rep", CHIP_SWAP) for part in parts))
        total_rest = jnp.concatenate([a.astype(F32) + b.astype(F32) for a, b in zip(parts, received)])
        total_rest = total_rest, lax.ppermute(total_rest, "rep", CORE_SWAP)
        rows = tuple(b[None] for b in bias)
        other_new = adam_call(
            attention_adam_kernel, scalars, total_rest, (*attention, *rows, *vectors)
        )
        new_bias = tuple(b[0] for b in other_new[3:6])
        updated = (*other_new[:3], *hidden_new, *new_bias, *other_new[6:])
    else:
        sums = (sums_two + sums_three)[: layer_vectors.shape[0]]
        flat = jnp.concatenate(
            [
                sums.reshape(-1, count, shard).transpose(1, 0, 2).reshape(count, -1),
                bias_sum.reshape(count, inner_shard),
            ],
            axis=1,
        )
        total_three = reduce_plain(owners(grad_three[0], (*(shard,) * blocks, inner_shard)))
        total_two = reduce_plain(owners(grad_two[0], (shard,) * 5))
        total_one = reduce_plain(owners(grad_keep, (shard,) * 3))
        flat = lax.psum(lax.psum_scatter(flat, "fsdp", scatter_dimension=0), "rep")
        grad_attention = jnp.concatenate([total_one, total_two]).reshape(attention_weights.shape)
        grad_expand = total_three[: blocks * shard].reshape(blocks, shard, width).transpose(1, 0, 2)
        updated = []
        for (now, one_now, two_now), grad, factor in (
            (attention, grad_attention, 1.0),
            (expand, grad_expand.reshape(shard, -1), 1.0),
            (shrink, total_three[blocks * shard :], 1.0),
            (bias, flat[layer_vectors.size :], 0.0),
            (vectors, flat[: layer_vectors.size].reshape(-1, shard), 0.0),
        ):
            updated.extend(adam_update(now, grad, one_now, two_now, hyper_rates, step_float, factor))
    return (outputs[None], input_grad[None], memory_grad[None], *updated)


def solution(mesh):
    rows = ("rep", "fsdp")
    params = (P(None, "fsdp", None), P("fsdp", None), P("fsdp", None), P("fsdp"), P(None, "fsdp"))
    return jax.shard_map(
        functools.partial(per_device, small_mesh(mesh)),
        mesh=mesh,
        in_specs=(
            P(rows, None, None), P(rows, None, None), P(rows), P(rows, None), P(rows, None, None),
            *params, *params, *params, P(), P(),
        ),
        out_specs=(
            P(rows, None, None), P(rows, None, None), P(rows, None, None),
            *(spec for spec in params for _ in range(3)),
        ),
        check_vma=False,
    )
```

```python
import functools

import jax
import jax.numpy as jnp
from jax import lax
from jax.experimental import pallas as pl
from jax.experimental.pallas import tpu as pltpu
from jax.sharding import PartitionSpec as P

BF = jnp.bfloat16
F32 = jnp.float32
HEAD_DIM = 64
PAIR = 128
TILE = 256
MIB = 1 << 20


def dot(left, right, left_dim, right_dim):
    return lax.dot_general(
        left, right, (((left_dim,), (right_dim,)), ((), ())), preferred_element_type=F32
    )


def lanes(size):
    return lax.broadcasted_iota(jnp.int32, (1, size), 1)


def half_masks():
    first = jnp.where(lanes(PAIR) < HEAD_DIM, 1.0, 0.0)
    return first.astype(BF), (1.0 - first).astype(BF)


def rows_at(index, size=TILE):
    return pl.ds(pl.multiple_of(index * size, size), size)


class Mover:
    def __init__(self, sems):
        self.sems, self.used, self.leaving = sems, 0, []

    def take(self, count=1):
        self.used += count
        return self.used - count

    def load(self, source, target):
        copy = pltpu.make_async_copy(source, target, self.sems.at[self.take()])
        copy.start()
        return copy

    def load_rows(self, source, target):
        count = source.shape[0] // TILE
        first = self.take(count)

        def copy(tile):
            rows = rows_at(tile)
            return pltpu.make_async_copy(source.at[rows], target.at[rows], self.sems.at[first + tile])

        for tile in range(count):
            copy(tile).start()
        return lambda tile: copy(tile).wait()

    def store(self, source, target):
        self.leaving.append(self.load(source, target))

    def store_parts(self, source, target, count, where):
        first = self.take(count)

        def copy(part):
            return pltpu.make_async_copy(source.at[where(part)], target.at[where(part)], self.sems.at[first + part])

        self.leaving.extend(copy(part) for part in range(count))
        return lambda part: copy(part).start()

    def store_rows(self, source, target):
        return self.store_parts(source, target, source.shape[0] // TILE, rows_at)

    def finish(self):
        for copy in self.leaving:
            copy.wait()


def columns_at(size):
    return lambda part: (slice(None), rows_at(part, size))


def load_matrices(mover, core, sources, targets, which=None):
    waits, first = [], 0
    for index, target in enumerate(targets):
        if which is not None and index not in which:
            first += target.shape[1]
            continue
        if core is None:
            copies = [mover.load(sources[index], target)]
        else:
            rows, half = target.shape[1], target.shape[2] // 2
            copies = []
            for step, source in enumerate(sources):
                cols = pl.ds(pl.multiple_of(jnp.bitwise_xor(core, step) * half, half), half)
                copies.append(mover.load(source.at[:, first : first + rows, :], target.at[:, :, cols]))
            first += rows
        waits.append(lambda copies=copies: [copy.wait() for copy in copies])
    return waits


def load_quarters(mover, place_ref, packs, expand_ref, shrink_ref):
    core, chip, line, row = place_of(place_ref)
    half, cut = expand_ref.shape[3] // 2, expand_ref.shape[2] // 2
    loads = ([], [])
    for index, pack in enumerate(packs):
        core_step, chip_step = divmod(index, 2)
        cols = pl.ds(pl.multiple_of(jnp.bitwise_xor(core, core_step) * half, half), half)
        side = jnp.bitwise_xor(chip, chip_step)
        rows = pl.ds(pl.multiple_of(side * cut, cut), cut)
        for line_step in range(4):
            for row_step in (0, 1):
                owner = lax.rem(line - line_step + 4, 4) * 2 + jnp.bitwise_xor(row, row_step)
                source = pack.at[line_step, row_step]
                loads[0].append((source.at[0], expand_ref.at[:, owner, rows, cols]))
                loads[1].append((source.at[1], shrink_ref.at[owner, side, :, :, cols]))
    return [[mover.load(*pair) for pair in pairs] for pairs in loads]


def whole(ref):
    return ref[...].reshape(-1, ref.shape[-1])


def key_extra(length_limit, count):
    lane = lanes(PAIR) % HEAD_DIM
    extra = jnp.where(lane < 3, 1.0, 0.0)
    if length_limit is None:
        return jnp.broadcast_to(extra, (count, PAIR)).astype(BF)
    row = lax.broadcasted_iota(jnp.int32, (count, PAIR), 0)
    bias = jnp.where(row < length_limit, 0.0, -1e30)
    return jnp.where(lane == 3, bias, extra).astype(BF)


def put_start(pos_ref, start_ref):
    length = start_ref.shape[0]
    query = lax.broadcasted_iota(jnp.int32, (8, length), 1)
    first = (query - pos_ref[...]).astype(F32)
    start_ref[...] = first.T[:, :1].astype(jnp.int32)


def visible(start, first_query, first_key, count):
    key = first_key + lax.broadcasted_iota(jnp.int32, (TILE, count), 1)
    seen = key >= start
    if first_key == first_query:
        query = first_query + lax.broadcasted_iota(jnp.int32, (TILE, count), 0)
        seen = seen & (key <= query)
    return seen


def key_spans(tile, count, causal):
    if not causal:
        return [(0, count)]
    spans = [(0, tile * TILE)] if tile else []
    return spans + [(tile * TILE, TILE)]


def staggered(first, then, count):
    ready = first(0)
    for index in range(count):
        following = first(index + 1) if index + 1 < count else None
        then(index, ready)
        ready = following


class ProbStore:
    def __init__(self, mover, hbm, ref, causal):
        self.hbm, self.ref, self.mover = hbm, ref, mover
        self.tiles = ref.shape[2] // TILE
        self.causal = causal
        self.first = mover.take(2 * self.tiles)

    def views(self, pair, slot, tile):
        rows = slice(tile * TILE, (tile + 1) * TILE)
        keys = slice(0, (tile + 1) * TILE) if self.causal else slice(0, self.ref.shape[3])
        sem = self.mover.sems.at[self.first + slot * self.tiles + tile]
        return self.hbm.at[pair, :, rows, keys], self.ref.at[slot, :, rows, keys], sem

    def copy(self, pair, slot, tile, out):
        far, near, sem = self.views(pair, slot, tile)
        return pltpu.make_async_copy(near, far, sem) if out else pltpu.make_async_copy(far, near, sem)


def two_pairs(pairs, body):
    @pl.loop(0, pairs // 2)
    def _(step):
        for slot in (0, 1):
            body(2 * step + slot, slot, step)


def attend(q_ref, k_ref, v_ref, extra_ref, start_ref, o_ref, store, finished):
    length, count = q_ref.shape[0], k_ref.shape[0]
    causal = start_ref is not None
    step_rows = TILE if causal else 2 * TILE
    masks = half_masks()
    pairs = q_ref.shape[1] // PAIR

    def one_pair(pair, slot, step):
        cols = rows_at(pair, PAIR)

        @pl.when(step > 0)
        def _():
            for tile in range(store.tiles):
                store.copy(pair - 2, slot, tile, True).wait()

        steps = [(tile, side) for tile in range(length // step_rows) for side in (0, 1)]
        results = {}

        def scores_of(index):
            tile, side = steps[index]
            rows = slice(tile * step_rows, (tile + 1) * step_rows)
            queries = q_ref[rows, cols] * masks[side]
            if not causal:
                base = HEAD_DIM * (1 - side)
                queries = jnp.where(lanes(PAIR) == base + 3, 1.0, queries.astype(F32)).astype(BF)
            blocks = []
            for first, size in key_spans(tile, count, causal):
                keys = k_ref[first : first + size, cols]
                if not causal:
                    keys = keys * masks[side] + extra_ref[first : first + size, :] * masks[1 - side]
                scores = dot(queries, keys, 1, 1)
                if causal:
                    seen = visible(start_ref[rows, :], tile * TILE, first, size)
                    scores = jnp.where(seen, scores, -1000000000.0)
                blocks.append(scores)
            return blocks

        def mix(index, score_blocks):
            tile, side = steps[index]
            rows = slice(tile * step_rows, (tile + 1) * step_rows)
            spans = key_spans(tile, count, causal)
            top = functools.reduce(
                jnp.maximum, [jnp.max(scores, axis=1, keepdims=True) for scores in score_blocks]
            )
            exponents = [jnp.exp(scores - top) for scores in score_blocks]
            inverse = 1.0 / sum(jnp.sum(exponent, axis=1, keepdims=True) for exponent in exponents)
            total = None
            for exponent, (first, size) in zip(exponents, spans):
                probs = (exponent * inverse).astype(BF)
                store.ref[slot, side, rows, first : first + size] = probs
                part = dot(probs, v_ref[first : first + size, cols], 1, 0)
                total = part if total is None else total + part
            results[side] = total
            if side == 1:
                o_ref[rows, cols] = jnp.where(lanes(PAIR) < HEAD_DIM, results[0], results[1]).astype(BF)

        staggered(scores_of, mix, len(steps))
        for tile in range(store.tiles):
            store.copy(pair, slot, tile, True).start()
        for start_store in finished:
            start_store(pair)

    two_pairs(pairs, one_pair)
    for slot in (0, 1):
        for tile in range(store.tiles):
            store.mover.leaving.append(store.copy(pairs - 2 + slot, slot, tile, True))


def load_probs(store, slot):
    for tile in reversed(range(store.tiles)):
        store.copy(slot, slot, tile, False).start()


def attend_back(q_ref, da_ref, inner_ref, k_ref, v_ref, store, dq_ref, dk_ref, dv_ref, dk_sum, dv_sum, values_ref):
    length, count = q_ref.shape[0], k_ref.shape[0]
    masks = half_masks()
    pairs = k_ref.shape[1] // PAIR

    def one_pair(pair, slot, step):
        cols = rows_at(pair, PAIR)
        for tile in range(store.tiles):
            store.copy(pair, slot, tile, False).wait()
        for side in (0, 1):
            values_ref[side] = v_ref[:, cols] * masks[side]
        steps = [(tile, side) for tile in reversed(range(length // TILE)) for side in (0, 1)]
        query_grads = {}

        def place(index):
            tile, side = steps[index]
            size = (tile + 1) * TILE if store.causal else count
            return tile, side, slice(tile * TILE, (tile + 1) * TILE), slice(0, size)

        def collect(ref, tile, side, span, part):
            if tile == length // TILE - 1:
                ref[side, :, span] = part
            else:
                ref[side, :, span] += part

        def value_side(index):
            _, side, rows, span = place(index)
            return dot(da_ref[rows, cols], values_ref[side, span, :], 1, 1)

        def score_side(index, grad_probs):
            tile, side, rows, span = place(index)
            probs = store.ref[slot, side, rows, span]
            collect(dv_sum, tile, side, span, dot(da_ref[rows, cols], probs, 0, 0))
            inner = inner_ref[pair, rows, side : side + 1]
            grad_scores = (probs.astype(F32) * (grad_probs - inner)).astype(BF)
            collect(dk_sum, tile, side, span, dot(q_ref[rows, cols], grad_scores, 0, 0))
            query_grads[side] = dot(grad_scores, k_ref[span, cols], 1, 0)
            if side == 1:
                dq_ref[rows, cols] = (
                    jnp.where(lanes(PAIR) < HEAD_DIM, query_grads[0], query_grads[1]) * HEAD_DIM**-0.5
                ).astype(BF)

        staggered(value_side, score_side, len(steps))
        for sums, out in ((dk_sum, dk_ref), (dv_sum, dv_ref)):
            joined = jnp.concatenate([sums[0, :HEAD_DIM, :], sums[1, HEAD_DIM:, :]], axis=0)
            out[:, cols] = joined.astype(BF).T

        @pl.when(step < pairs // 2 - 1)
        def _():
            for tile in range(store.tiles):
                store.copy(pair + 2, slot, tile, False).start()

    two_pairs(pairs, one_pair)


def norm_rows(summed):
    center = jnp.mean(summed, axis=1, keepdims=True)
    shifted = summed - center
    inverse = lax.rsqrt(jnp.mean(shifted * shifted, axis=1, keepdims=True) + 1e-05)
    return shifted * inverse, inverse


def norm_back(grad_out, normed, inverse, gain):
    scaled = grad_out * gain
    first = jnp.mean(scaled, axis=1, keepdims=True)
    second = jnp.mean(scaled * normed, axis=1, keepdims=True)
    return inverse * (scaled - first - normed * second)


def add_rows(ref, row, values):
    ref[row : row + 1, :] += jnp.sum(values, axis=0, keepdims=True)


def place_of(place_ref):
    rep, place = place_ref[0], place_ref[1]
    return lax.rem(rep, 2), lax.div(rep, 2), lax.div(place, 2), lax.rem(place, 2)


def assemble(place_ref, chunk_refs, all_ref):
    core, chip, line, row = place_of(place_ref)
    width = all_ref.shape[1]
    quarter = chunk_refs[0].shape[3]
    shard = quarter * 4 // 3
    for core_step, chunk_ref in enumerate(chunk_refs):
        for chip_step in (0, 1):
            rep = jnp.bitwise_xor(chip, chip_step) * 2 + jnp.bitwise_xor(core, core_step)
            for line_step in range(4):
                for row_step in (0, 1):
                    owner = lax.rem(line - line_step + 4, 4) * 2 + jnp.bitwise_xor(row, row_step)
                    for piece in range(quarter // 16):
                        stacked = rep * quarter + piece * 16
                        matrix = lax.div(stacked, shard)
                        target = matrix * width + owner * shard + (stacked - matrix * shard)
                        all_ref[pl.ds(pl.multiple_of(target, 16), 16), :] = chunk_ref[
                            chip_step, line_step, row_step, piece * 16 : (piece + 1) * 16, :
                        ]


def assemble_halves(place_ref, mine_ref, other_ref, all_ref, shards):
    core = place_of(place_ref)[0]
    devices, _, half = mine_ref.shape
    for step, ref in ((0, mine_ref), (1, other_ref)):
        cols = pl.ds(pl.multiple_of(jnp.bitwise_xor(core, step) * half, half), half)
        first, target = 0, 0
        for shard in shards:
            for owner in range(devices):
                at = target + owner * shard
                all_ref[at : at + shard, cols] = ref[owner, first : first + shard, :]
            first += shard
            target += shard * devices


def unpack_small(all_ref, base, vec_ref, bias_ref):
    devices = vec_ref.shape[1] // HEAD_DIM
    inner = bias_ref.shape[1] // devices
    for pair in range(devices // 2):
        first = base + 2 * pair * 16
        left = all_ref[first : first + 16, :PAIR].astype(F32)
        right = all_ref[first + 16 : first + 32, :PAIR].astype(F32)
        vec_ref[:, pair * PAIR : (pair + 1) * PAIR] = jnp.where(
            lanes(PAIR) < HEAD_DIM, left, pltpu.roll(right, HEAD_DIM, 1)
        )
    for owner in range(devices):
        rows = all_ref[base + owner * 16 : base + owner * 16 + 16, :inner].astype(F32)
        bias_ref[:, owner * inner : (owner + 1) * inner] = rows[10:11, :]


def self_forward_kernel(staged, *refs):
    if staged:
        place_ref, pos_ref, x_hbm, chunk_hbm, other_hbm = refs[:5]
        refs = refs[5:]
    else:
        pos_ref, x_hbm, all_hbm = refs[:3]
        refs = refs[3:]
    p_hbm, q_hbm, k_hbm, v_hbm, o_hbm = refs[:5]
    refs = refs[5:]
    if staged:
        all_out, refs = refs[0], refs[1:]
    x_ref, all_ref, q_ref, k_ref, v_ref, o_ref, p_ref, start_ref = refs[:8]
    mover = Mover(refs[-1])
    length, width = x_ref.shape
    if staged:
        chunk_refs = refs[8:10]
        loads = [mover.load(a, b) for a, b in zip((chunk_hbm, other_hbm), chunk_refs)]
    else:
        loads = [mover.load(all_hbm, all_ref)]
    x_load = mover.load(x_hbm, x_ref)
    put_start(pos_ref, start_ref)
    for load in loads:
        load.wait()
    if staged:
        assemble(place_ref, chunk_refs, all_ref)
        mover.store(all_ref, all_out)
    x_load.wait()

    @pl.loop(0, length // TILE)
    def _(tile):
        rows = rows_at(tile)
        source = x_ref[rows, :]
        queries = dot(source, all_ref[:width, :], 1, 0).astype(BF)
        q_ref[rows, :] = queries * jnp.asarray(HEAD_DIM**-0.5, BF)
        k_ref[rows, :] = dot(source, all_ref[width : 2 * width, :], 1, 0).astype(BF)
        v_ref[rows, :] = dot(source, all_ref[2 * width :, :], 1, 0).astype(BF)

    mover.store(k_ref, k_hbm)
    mover.store(v_ref, v_hbm)
    mover.store(q_ref, q_hbm)
    finished = (mover.store_parts(o_ref, o_hbm, width // PAIR, columns_at(PAIR)),)
    attend(q_ref, k_ref, v_ref, None, start_ref, o_ref, ProbStore(mover, p_hbm, p_ref, True), finished)
    mover.finish()


def unpack_small(small_ref, vec_ref, bias_ref):
    devices = vec_ref.shape[1] // HEAD_DIM
    inner = bias_ref.shape[1] // devices
    for pair in range(devices // 2):
        left = small_ref[0, 2 * pair, :, :PAIR].astype(F32)
        right = small_ref[0, 2 * pair + 1, :, :PAIR].astype(F32)
        vec_ref[:, pair * PAIR : (pair + 1) * PAIR] = jnp.where(
            lanes(PAIR) < HEAD_DIM, left, pltpu.roll(right, HEAD_DIM, 1)
        )
    for owner in range(devices):
        rows = small_ref[0, owner, :, :inner].astype(F32)
        bias_ref[:, owner * inner : (owner + 1) * inner] = rows[10:11, :]


def cross_forward_kernel(staged, *refs):
    place_ref, core = None, None
    if staged:
        place_ref, refs = refs[0], refs[1:]
        core = place_of(place_ref)[0]
    length_ref, refs = refs[0], refs[1:]
    if staged:
        x_hbm, mixed_hbm, source_hbm, *packs = refs[:5]
        refs = refs[5:]
    else:
        vec_ref, x_hbm, mixed_hbm, source_hbm, *packs = refs[:9]
        refs = refs[9:]
    first_hbm, first_inv_hbm, p_hbm, q_hbm, k_hbm, v_hbm, o_hbm, n_hbm, inv_hbm = refs[:9]
    refs = refs[9:]
    if staged:
        vec_ref, bias_ref, refs = refs[0], refs[1], refs[2:]
    x_ref, mixed_ref, source_ref, first_ref, first_inv_ref, q_ref, k_ref, v_ref, o_ref, n_ref, inv_ref = refs[:11]
    p_ref, extra_ref, *w_refs = refs[11:18]
    mover = Mover(refs[-1])
    length, width = q_ref.shape

    if staged:
        small_ref = refs[18]
        rows = packs[0].shape[1]
        small = [
            mover.load(pack.at[:, rows - 16 :, :], small_ref.at[jnp.bitwise_xor(core, step)])
            for step, pack in enumerate(packs)
        ]
    source_load = mover.load_rows(source_hbm, source_ref)
    order = (2, 3, 0, 1, 4)
    waits = [None] * 5
    if staged:
        half = width // 2
        shard = w_refs[0].shape[1]
        for index in order:
            copies = []
            for step, pack in enumerate(packs):
                cols = pl.ds(pl.multiple_of(jnp.bitwise_xor(core, step) * half, half), half)
                copies.append(
                    mover.load(pack.at[:, index * shard : (index + 1) * shard, :], w_refs[index].at[:, :, cols])
                )
            waits[index] = lambda copies=copies: [copy.wait() for copy in copies]
    else:
        for index in order:
            waits[index] = mover.load(packs[index], w_refs[index]).wait
    mixed_load = mover.load_rows(mixed_hbm, mixed_ref)
    x_load = mover.load_rows(x_hbm, x_ref)
    extra_ref[...] = key_extra(length_ref[0], k_ref.shape[0])
    waits[2]()
    waits[3]()

    @pl.loop(0, source_ref.shape[0] // TILE)
    def _(tile):
        rows = rows_at(tile)
        source_load(tile)
        source = source_ref[rows, :]
        k_ref[rows, :] = dot(source, whole(w_refs[2]), 1, 0).astype(BF)
        v_ref[rows, :] = dot(source, whole(w_refs[3]), 1, 0).astype(BF)

    mover.store(k_ref, k_hbm)
    mover.store(v_ref, v_hbm)
    if staged:
        for load in small:
            load.wait()
        unpack_small(small_ref, vec_ref, bias_ref)
    waits[0]()
    waits[1]()

    tiles = [slice(tile * TILE, (tile + 1) * TILE) for tile in range(length // TILE)]

    def self_branch(tile):
        mixed_load(tile)
        x_load(tile)
        return dot(mixed_ref[tiles[tile], :], whole(w_refs[0]), 1, 0)

    def query_rows(tile, branch):
        rows = tiles[tile]
        normed, inverse = norm_rows(x_ref[rows, :].astype(F32) * vec_ref[6:7, :] + branch)
        first_ref[rows, :] = normed
        first_inv_ref[rows, :] = inverse
        low = (normed * vec_ref[0:1, :] + vec_ref[3:4, :]).astype(BF)
        queries = dot(low, whole(w_refs[1]), 1, 0).astype(BF)
        q_ref[rows, :] = queries * jnp.asarray(HEAD_DIM**-0.5, BF)

    staggered(self_branch, query_rows, len(tiles))
    mover.store(first_ref, first_hbm)
    mover.store(first_inv_ref, first_inv_hbm)
    mover.store(q_ref, q_hbm)
    finished = (mover.store_parts(o_ref, o_hbm, width // PAIR, columns_at(PAIR)),)
    attend(q_ref, k_ref, v_ref, extra_ref, None, o_ref, ProbStore(mover, p_hbm, p_ref, False), finished)
    waits[4]()
    n_store, inv_store = mover.store_rows(n_ref, n_hbm), mover.store_rows(inv_ref, inv_hbm)

    def cross_branch(tile):
        return dot(o_ref[tiles[tile], :], whole(w_refs[4]), 1, 0)

    def second_norm(tile, branch):
        rows = tiles[tile]
        first_out = first_ref[rows, :] * vec_ref[0:1, :] + vec_ref[3:4, :]
        normed, inverse = norm_rows(first_out * vec_ref[7:8, :] + branch)
        n_ref[rows, :] = normed
        inv_ref[rows, :] = inverse
        n_store(tile)
        inv_store(tile)

    staggered(cross_branch, second_norm, len(tiles))
    mover.finish()


def hidden_kernel(staged, *refs):
    place_ref, core = None, None
    if staged:
        place_ref, refs = refs[0], refs[1:]
        core = place_of(place_ref)[0]
    vec_ref, bias_ref, *packs = refs[: 6 if staged else 4]
    n_hbm, inv_hbm, cot_hbm = refs[len(packs) + 2 : len(packs) + 5]
    refs = refs[len(packs) + 5 :]
    count = 2 if staged else 1
    sums_ref, bias_sum_ref, out_hbm, dz_hbm = refs[:4]
    grad_hbms, refs = refs[4 : 4 + count], refs[4 + count :]
    grad_refs, refs = refs[:count], refs[count:]
    n_ref, inv_ref, cot_ref, out_ref, dz_ref, low_ref, h_ref, du_ref, df_ref, slope_ref, third_ref = refs[:11]
    blocks = bias_ref.shape[1] // vec_ref.shape[1]
    e_ref, s_ref = refs[11:13]
    mover = Mover(refs[-1])
    length, width = n_ref.shape

    n_load = mover.load_rows(n_hbm, n_ref)
    if staged:
        expand_loads, shrink_loads = load_quarters(mover, place_ref, packs, e_ref, s_ref)
    else:
        expand_loads, shrink_loads = [mover.load(packs[0], e_ref)], [mover.load(packs[1], s_ref)]
    cot_load = mover.load_rows(cot_hbm, cot_ref)
    inv_load = mover.load_rows(inv_hbm, inv_ref)
    out_store, dz_store = mover.store_rows(out_ref, out_hbm), mover.store_rows(dz_ref, dz_hbm)
    tiles = [slice(tile * TILE, (tile + 1) * TILE) for tile in range(length // TILE)]
    parts = [slice(block * width, (block + 1) * width) for block in range(blocks)]
    sums = {row: 0.0 for row in (1, 2, 4, 5, 8, 9)}
    bias_sums = [0.0] * blocks

    def add(row, values):
        sums[row] = sums[row] + jnp.sum(values, axis=0, keepdims=True)

    def second_out(rows):
        return n_ref[rows, :] * vec_ref[1:2, :] + vec_ref[4:5, :]

    for tile, rows in enumerate(tiles):
        n_load(tile)
        low_ref[rows, :] = second_out(rows).astype(BF)
    steps = [(block, rows) for block in range(blocks) for rows in tiles]

    def expand(index):
        block, rows = steps[index]
        return dot(low_ref[rows, :], whole(e_ref.at[block]), 1, 0) + bias_ref[:, parts[block]]

    def activate(index, before):
        block, rows = steps[index]
        square = before * before
        tangent = jnp.tanh(before * (0.7978845608028654 + 0.7978845608028654 * 0.044715 * square))
        half = 0.5 * (1.0 + tangent)
        slope_ref[rows, parts[block]] = half + before * (half * (1.0 - tangent)) * (
            0.7978845608028654 + 3.0 * 0.7978845608028654 * 0.044715 * square
        )
        h_ref[rows, parts[block]] = (before * half).astype(BF)

    for load in expand_loads:
        load.wait()
    staggered(expand, activate, len(steps))
    for load in shrink_loads:
        load.wait()
    for tile in range(len(tiles)):
        cot_load(tile)
        inv_load(tile)

    def shrink(tile):
        return dot(h_ref[tiles[tile], :], whole(s_ref), 1, 0)

    def outer_norm(tile, branch_out):
        rows = tiles[tile]
        second = second_out(rows)
        normed, inverse = norm_rows(second * vec_ref[8:9, :] + vec_ref[9:10, :] + branch_out)
        out_ref[rows, :] = (normed * vec_ref[2:3, :] + vec_ref[5:6, :]).astype(BF)
        grad_out = cot_ref[rows, :].astype(F32)
        third = norm_back(grad_out, normed, inverse, vec_ref[2:3, :])
        third_ref[rows, :] = third
        add(2, grad_out * normed)
        add(5, grad_out)
        branch = third.astype(BF)
        df_ref[rows, :] = branch
        add(9, branch.astype(F32))
        add(8, second * third)

    staggered(shrink, outer_norm, len(tiles))
    for tile in range(len(tiles)):
        out_store(tile)

    def shrink_back(index):
        block, rows = steps[index]
        return dot(df_ref[rows, :], whole(s_ref)[parts[block], :], 1, 1)

    def slope_back(index, grad_hidden):
        block, rows = steps[index]
        du = (grad_hidden * slope_ref[rows, parts[block]]).astype(BF)
        du_ref[rows, parts[block]] = du
        bias_sums[block] = bias_sums[block] + jnp.sum(du.astype(F32), axis=0, keepdims=True)

    staggered(shrink_back, slope_back, len(steps))

    def expand_back(tile):
        rows = tiles[tile]
        return sum(dot(du_ref[rows, parts[block]], whole(e_ref.at[block]), 1, 1) for block in range(blocks))

    def inner_norm(tile, grad_expanded):
        rows = tiles[tile]
        grad = vec_ref[8:9, :] * third_ref[rows, :] + grad_expanded
        normed = n_ref[rows, :]
        dz_ref[rows, :] = norm_back(grad, normed, inv_ref[rows, :], vec_ref[1:2, :])
        add(1, grad * normed)
        add(4, grad)

    staggered(expand_back, inner_norm, len(tiles))
    for tile in range(len(tiles)):
        dz_store(tile)
    sums_ref[...] = jnp.zeros_like(sums_ref)
    for row, values in sums.items():
        sums_ref[row : row + 1, :] = values
    for block, values in enumerate(bias_sums):
        bias_sum_ref[:, parts[block]] = values
    for step in reversed(range(count)):
        for block in range(blocks):
            put_grad(grad_refs, step, place_ref, block, low_ref[...], du_ref, block * width)
            put_shrink(grad_refs, step, place_ref, block, blocks, h_ref[:, parts[block]], df_ref)
        mover.store(grad_refs[step], grad_hbms[step])
    mover.finish()


def branch_grads(branch_rows, mixed_weight, o_ref, da_ref, inner_ref):
    width = o_ref.shape[1]
    tiles = [slice(tile * TILE, (tile + 1) * TILE) for tile in range(o_ref.shape[0] // TILE)]
    head = lax.broadcasted_iota(jnp.int32, (width, PAIR), 0) // HEAD_DIM
    picks = jnp.where(head == lax.broadcasted_iota(jnp.int32, (width, PAIR), 1), 1.0, 0.0).astype(BF)

    def project(tile):
        return dot(branch_rows(tile, tiles[tile]), mixed_weight, 1, 1)

    def reduce(tile, mixed_grad):
        rows = tiles[tile]
        low = mixed_grad.astype(BF)
        da_ref[rows, :] = low
        product = low.astype(F32) * o_ref[rows, :].astype(F32)
        high = product.astype(BF)
        rest = (product - high.astype(F32)).astype(BF)
        inner = dot(high, picks, 1, 0) + dot(rest, picks, 1, 0)
        for pair in range(width // PAIR):
            inner_ref[pair, rows, :] = pltpu.roll(inner, (PAIR - 2 * pair) % PAIR, 1) if pair else inner

    staggered(project, reduce, len(tiles))


def put_grad(grad_refs, step, place_ref, index, left, right_ref, first=0):
    width = left.shape[1]
    if place_ref is None:
        grad = dot(left, right_ref[:, first : first + width], 0, 0)
        grad_refs[0][index * width : (index + 1) * width, :] = grad.astype(BF)
        return
    core, _, _, row = place_of(place_ref)
    half = width // 2
    shard = width // 8
    cols = pl.ds(pl.multiple_of(first + jnp.bitwise_xor(core, step) * half, half), half)
    grad = dot(left, right_ref[:, cols], 0, 0).astype(BF).reshape(4, 2, shard, half)
    for side in (0, 1):
        slot = jnp.bitwise_xor(row, side)
        grad_refs[step][slot, :, index * shard : (index + 1) * shard, :] = grad[:, side]


def put_shrink(grad_refs, step, place_ref, block, blocks, left, right_ref):
    width = left.shape[1]
    if place_ref is None:
        first = (blocks + block) * width
        grad_refs[0][first : first + width, :] = dot(left, right_ref[...], 0, 0).astype(BF)
        return
    core, _, _, row = place_of(place_ref)
    half, shard = width // 2, width * blocks // 8
    base = width // 8 * blocks
    cols = pl.ds(pl.multiple_of(jnp.bitwise_xor(core, step) * half, half), half)
    grad = dot(left, right_ref[:, cols], 0, 0).astype(BF).reshape(width // shard, shard, half)
    for part in range(width // shard):
        owner = block * (width // shard) + part
        grad_refs[step][jnp.bitwise_xor(row, owner % 2), owner // 2, base:, :] = grad[part]


def put_small(grad_refs, place_ref, base, sums, bias_sum):
    core, _, _, row = place_of(place_ref)
    half = grad_refs[0].shape[3]
    inner = bias_sum.shape[1] // 8
    index = lax.broadcasted_iota(jnp.int32, (16, half), 0)
    for owner in range(8):
        block = sums[:, owner // 2 * PAIR : (owner // 2 + 1) * PAIR]
        if owner % 2:
            block = pltpu.roll(block, HEAD_DIM, 1)
        block = jnp.concatenate([block, jnp.zeros((16, half - PAIR), F32)], axis=1)
        block = jnp.where(index == 10, bias_sum[:, owner * inner : (owner + 1) * inner], block)
        high = block.astype(BF)
        low = (block - high.astype(F32)).astype(BF)
        slot = jnp.bitwise_xor(row, owner % 2)
        first = (core == 0).astype(F32)
        for step, grad_ref in enumerate(grad_refs):
            is_high = first if step == 0 else 1.0 - first
            mixed = high.astype(F32) * is_high + low.astype(F32) * (1.0 - is_high)
            grad_ref[slot, owner // 2, base : base + 16, :] = mixed.astype(BF)


def cross_backward_kernel(staged, *refs):
    place_ref, core = None, None
    if staged:
        place_ref, refs = refs[0], refs[1:]
        core = place_of(place_ref)[0]
    vec_ref, refs = refs[0], refs[1:]
    if staged:
        sums_three_ref, bias_sum_ref, refs = refs[0], refs[1], refs[2:]
    packs, refs = refs[: 2 if staged else 5], refs[2 if staged else 5 :]
    p_hbm, dz_hbm, x_hbm, first_hbm, inv_hbm, source_hbm, q_hbm, k_hbm, v_hbm, o_hbm, self_o_hbm = refs[:11]
    sums_ref, dfirst_hbm, dsource_hbm = refs[11:14]
    count = 2 if staged else 1
    grad_hbms, refs = refs[14 : 14 + count], refs[14 + count :]
    grad_refs, refs = refs[:count], refs[count:]
    dz_ref, x_ref, first_ref, inv_ref, source_ref, q_ref, k_ref, v_ref, o_ref, self_o_ref = refs[:10]
    dfirst_ref, dsource_ref, *w_refs = refs[10:17]
    low_ref, da_ref, inner_ref, dq_ref, dk_ref, dv_ref, dk_sum, dv_sum, branch_ref, values_ref, p_ref = refs[17:28]
    mover = Mover(refs[-1])
    length, width = dz_ref.shape

    dz_load, o_load = mover.load_rows(dz_hbm, dz_ref), mover.load_rows(o_hbm, o_ref)
    waits = load_matrices(mover, core, packs, w_refs, (4,))
    sums_ref[...] = jnp.zeros_like(sums_ref)
    waits[0]()
    store = ProbStore(mover, p_hbm, p_ref, False)
    load_probs(store, 0)
    middle = [mover.load(a, b) for a, b in ((v_hbm, v_ref), (q_hbm, q_ref), (k_hbm, k_ref))]

    def branch_rows(tile, rows):
        dz_load(tile)
        o_load(tile)
        branch_ref[rows, :] = dz_ref[rows, :].astype(BF)
        return branch_ref[rows, :]

    branch_grads(branch_rows, whole(w_refs[4]), o_ref, da_ref, inner_ref)
    for step in range(count):
        put_grad(grad_refs, step, place_ref, 4, o_ref[...], branch_ref)
    load_probs(store, 1)
    first_load = mover.load_rows(first_hbm, first_ref)
    waits = load_matrices(mover, core, packs, w_refs, (1, 2, 3))
    last = [
        mover.load(a, b)
        for a, b in ((source_hbm, source_ref), (x_hbm, x_ref), (inv_hbm, inv_ref), (self_o_hbm, self_o_ref))
    ]
    for load in middle:
        load.wait()
    attend_back(q_ref, da_ref, inner_ref, k_ref, v_ref, store, dq_ref, dk_ref, dv_ref, dk_sum, dv_sum, values_ref)
    for load in last:
        load.wait()
    for wait in waits:
        wait()
    for tile in range(length // TILE):
        first_load(tile)

    dsource_store = mover.store_rows(dsource_ref, dsource_hbm)
    dfirst_store = mover.store_rows(dfirst_ref, dfirst_hbm)
    tiles = [slice(tile * TILE, (tile + 1) * TILE) for tile in range(length // TILE)]
    key_tiles = [slice(tile * TILE, (tile + 1) * TILE) for tile in range(source_ref.shape[0] // TILE)]
    sums = {row: 0.0 for row in (0, 3, 6, 7)}

    def add(row, values):
        sums[row] = sums[row] + jnp.sum(values, axis=0, keepdims=True)

    def source_grad(tile):
        rows = key_tiles[tile]
        dsource_ref[rows, :] = dot(dk_ref[rows, :], whole(w_refs[2]), 1, 1) + dot(
            dv_ref[rows, :], whole(w_refs[3]), 1, 1
        )

    def put_keys(step):
        put_grad(grad_refs, step, place_ref, 2, source_ref[...], dk_ref)
        put_grad(grad_refs, step, place_ref, 3, source_ref[...], dv_ref)

    products = [functools.partial(source_grad, tile) for tile in range(len(key_tiles))]
    products += [functools.partial(put_keys, step) for step in range(count)]

    def query_back(tile):
        product = dot(dq_ref[tiles[tile], :], whole(w_refs[1]), 1, 1)
        for run in products[tile :: len(tiles)]:
            run()
        return product

    def first_norm(tile, product):
        rows = tiles[tile]
        grad = dz_ref[rows, :]
        dx = product + vec_ref[7:8, :] * grad
        normed = first_ref[rows, :]
        first_out = normed * vec_ref[0:1, :] + vec_ref[3:4, :]
        low_ref[rows, :] = first_out.astype(BF)
        add(7, first_out * grad)
        dfirst = norm_back(dx, normed, inv_ref[rows, :], vec_ref[0:1, :])
        dfirst_ref[rows, :] = dfirst
        add(0, dx * normed)
        add(3, dx)
        add(6, x_ref[rows, :].astype(F32) * dfirst)
        branch_ref[rows, :] = dfirst.astype(BF)

    staggered(query_back, first_norm, len(tiles))
    for tile in range(len(key_tiles)):
        dsource_store(tile)
    for tile in range(len(tiles)):
        dfirst_store(tile)
    for row, values in sums.items():
        sums_ref[row : row + 1, :] = values

    if staged:
        put_small(grad_refs, place_ref, 5 * (width // 8), sums_ref[...] + sums_three_ref[...], bias_sum_ref[...])
    for step in reversed(range(count)):
        put_grad(grad_refs, step, place_ref, 1, low_ref[...], dq_ref)
        put_grad(grad_refs, step, place_ref, 0, self_o_ref[...], branch_ref)
        mover.store(grad_refs[step], grad_hbms[step])
    mover.finish()


def self_backward_kernel(staged, *refs):
    place_ref, core = None, None
    if staged:
        place_ref, refs = refs[0], refs[1:]
        core = place_of(place_ref)[0]
    count = 2 if staged else 1
    packs, refs = refs[:count], refs[count:]
    p_hbm, dz_hbm, x_hbm, q_hbm, k_hbm, v_hbm, o_hbm, *head_hbms = refs[:10]
    grad_hbms, refs = refs[10 : 10 + count], refs[10 + count :]
    grad_refs, refs = refs[:count], refs[count:]
    dz_ref, x_ref, q_ref, k_ref, v_ref, o_ref, w_ref = refs[:7]
    da_ref, inner_ref, dq_ref, dk_ref, dv_ref, dk_sum, dv_sum, values_ref, p_ref = refs[7:16]
    mover = Mover(refs[-1])
    length, width = dz_ref.shape

    dz_load = mover.load_rows(dz_hbm, dz_ref)
    waits = load_matrices(mover, core, packs, (w_ref,))
    o_load = mover.load_rows(o_hbm, o_ref)
    waits[0]()
    store = ProbStore(mover, p_hbm, p_ref, True)
    load_probs(store, 0)
    middle = [mover.load(a, b) for a, b in ((v_hbm, v_ref), (q_hbm, q_ref), (k_hbm, k_ref))]

    def branch_rows(tile, rows):
        dz_load(tile)
        o_load(tile)
        return dz_ref[rows, :].astype(BF)

    branch_grads(branch_rows, whole(w_ref), o_ref, da_ref, inner_ref)
    load_probs(store, 1)
    x_load = mover.load(x_hbm, x_ref)
    for load in middle:
        load.wait()
    attend_back(q_ref, da_ref, inner_ref, k_ref, v_ref, store, dq_ref, dk_ref, dv_ref, dk_sum, dv_sum, values_ref)
    for near, far in zip((dq_ref, dk_ref, dv_ref), head_hbms):
        mover.store(near, far)
    x_load.wait()
    for step in reversed(range(count)):
        for index, grads in enumerate((dq_ref, dk_ref, dv_ref)):
            put_grad(grad_refs, step, place_ref, index, x_ref[...], grads)
        mover.store(grad_refs[step], grad_hbms[step])
    mover.finish()


def input_grad_kernel(vec_ref, dz_hbm, all_hbm, dq_hbm, dk_hbm, dv_hbm, dx_hbm, *refs):
    dz_ref, all_ref, dq_ref, dk_ref, dv_ref, dx_ref, sems = refs
    mover = Mover(sems)
    width = dz_ref.shape[1]
    all_load = mover.load(all_hbm, all_ref)
    heads = (dq_ref, dk_ref, dv_ref)
    loads = [mover.load_rows(a, b) for a, b in zip((dq_hbm, dk_hbm, dv_hbm), heads)]
    loads.append(mover.load_rows(dz_hbm, dz_ref))
    dx_store = mover.store_rows(dx_ref, dx_hbm)
    all_load.wait()

    @pl.loop(0, dz_ref.shape[0] // TILE)
    def _(tile):
        rows = rows_at(tile)
        for load in loads:
            load(tile)
        dx = vec_ref[6:7, :] * dz_ref[rows, :]
        for index, grads in enumerate(heads):
            dx = dx + dot(grads[rows, :], all_ref[index * width : (index + 1) * width, :], 1, 1)
        dx_ref[rows, :] = dx
        dx_store(tile)

    mover.finish()


def call(kernel, args, outs, scratch, limit, flops, smem=(), near=(), near_outs=(), copies=0):
    spaces = [pltpu.SMEM if i in smem else pltpu.VMEM if i in near else pl.ANY for i in range(len(args))]
    out_spaces = [pltpu.VMEM if i in near_outs else pl.ANY for i in range(len(outs))]
    buffers = [pltpu.VMEM(shape, kind) for shape, kind in scratch]
    if copies:
        buffers.append(pltpu.SemaphoreType.DMA((copies,)))
    return pl.pallas_call(
        kernel,
        out_shape=[jax.ShapeDtypeStruct(shape, kind) for shape, kind in outs],
        in_specs=[pl.BlockSpec(memory_space=space) for space in spaces],
        out_specs=[pl.BlockSpec(memory_space=space) for space in out_spaces],
        scratch_shapes=buffers,
        compiler_params=pltpu.CompilerParams(vmem_limit_bytes=(63 if copies else limit) * MIB),
        cost_estimate=pl.CostEstimate(flops=flops, bytes_accessed=16 * MIB, transcendentals=0),
    )(*args)


def like(*arrays):
    return [(a.shape, a.dtype) for a in arrays]


def prob_shape(queries, keys, width):
    return (width // PAIR, 2, queries, keys), BF


def forward_self(place, x, pos, pack, staged):
    length, width = x.shape
    low = ((length, width), BF)
    outs = [prob_shape(length, length, width), low, low, low, low]
    matrices = ((3 * width, width), BF)
    scratch = [low, matrices, low, low, low, low, ((2, 2, length, length), BF), ((length, 1), jnp.int32)]
    if staged:
        return call(
            functools.partial(self_forward_kernel, True),
            (place, pos, x, *pack),
            [*outs, matrices],
            [*scratch, *like(*pack)],
            40, 10**10, smem=(0,), near=(1,), copies=24,
        )
    results = call(
        functools.partial(self_forward_kernel, False),
        (pos, x, pack), outs, scratch, 40, 10**10, near=(0,), copies=24,
    )
    return (*results, pack)


def matrix_buffers(shards, width):
    return [((8 if rows < width else 1, rows, width), BF) for rows in shards]


def forward_cross(place, x, mixed, source, count, packs, given, shards):
    length, width = x.shape
    keys = source.shape[0]
    low, full, column, key_low = ((length, width), BF), ((length, width), F32), ((length, 1), F32), ((keys, width), BF)
    outs = [full, column, prob_shape(length, keys, width), low, key_low, key_low, low, full, column]
    near = [full, column, low, key_low, key_low, low, full, column]
    scratch = [low, low, key_low, *near, ((2, 2, length, keys), BF), ((keys, PAIR), BF)]
    if place is not None:
        return call(
            functools.partial(cross_forward_kernel, True),
            (place, count, x, mixed, source, *packs),
            [*outs, ((16, width), F32), ((1, 4 * width), F32)],
            [*scratch, *matrix_buffers(shards, width), ((2, 8, 16, width // 2), BF)],
            44, 10**10, smem=(0, 1), near_outs=(9, 10), copies=64,
        )
    vec, bias = given
    results = call(
        functools.partial(cross_forward_kernel, False),
        (count, vec, x, mixed, source, *packs),
        outs, [*scratch, *like(*packs)],
        44, 10**10, smem=(0,), near=(1,), copies=64,
    )
    return (*results, vec, bias)


def grad_outs(rows, width, staged):
    return [((2, 4, rows, width // 2), BF)] * 2 if staged else [((rows, width), BF)]


def hidden_step(place, packs, normed, inverse, cot, vec, bias):
    length, width = normed.shape
    inner = bias.shape[1]
    blocks = inner // width
    staged = place is not None
    low, full = ((length, width), BF), ((length, width), F32)
    grads = grad_outs(2 * inner // 8 if staged else 2 * inner, width, staged)
    args = (vec, bias, *packs, normed, inverse, cot)
    matrices = like(*packs)
    if staged:
        rows = width // 8
        matrices = [((blocks, 8, rows, width), BF), ((8, 2, blocks, rows // 2, width), BF)]
    return call(
        functools.partial(hidden_kernel, staged),
        (place, *args) if staged else args,
        [((16, width), F32), ((1, inner), F32), low, full, *grads],
        [*grads, *like(normed, inverse, cot), low, full, low, ((length, inner), BF), ((length, inner), BF), low,
         ((length, inner), F32), full, *matrices],
        44, 2 * 10**10, smem=(0,) if staged else (), near=(1, 2) if staged else (0, 1), near_outs=(0, 1),
        copies=96,
    )


def backward_cross(place, packs, dz, x, normed, inverse, source, vec, saved, mixed, small, shards):
    length, width = dz.shape
    keys = source.shape[0]
    staged = place is not None
    probs, *saved = saved
    arrays = (dz, x, normed, inverse, source, *saved, mixed)
    low, key_low, sums = ((length, width), BF), ((keys, width), BF), ((2, PAIR, keys), F32)
    grads = grad_outs(5 * width // 8 + 16 if staged else 5 * width, width, staged)
    full, key_full = ((length, width), F32), ((keys, width), F32)
    return call(
        functools.partial(cross_backward_kernel, staged),
        (place, vec, *small, *packs, probs, *arrays) if staged else (vec, *packs, probs, *arrays),
        [((16, width), F32), full, key_full, *grads],
        [*grads, *like(*arrays), full, key_full, *(matrix_buffers(shards, width) if staged else like(*packs)),
         low, low, ((width // PAIR, length, PAIR), F32), low, key_low, key_low, sums, sums, low, ((2, keys, PAIR), BF),
         ((2, 2, length, keys), BF)],
        48, 2 * 10**10, smem=(0,) if staged else (), near=(1, 2, 3) if staged else (0,), near_outs=(0,), copies=72,
    )


def backward_self(place, packs, dz, x, saved, shards):
    length, width = dz.shape
    staged = place is not None
    probs, *saved = saved
    arrays = (dz, x, *saved)
    low, sums = ((length, width), BF), ((2, PAIR, length), F32)
    grads = grad_outs(3 * width // 8 if staged else 3 * width, width, staged)
    first = matrix_buffers(shards[:1], width) if staged else like(*packs)
    return call(
        functools.partial(self_backward_kernel, staged),
        (place, *packs, probs, *arrays) if staged else (*packs, probs, *arrays),
        [low, low, low, *grads],
        [*grads, *like(*arrays), *first, low, ((width // PAIR, length, PAIR), F32), low, low, low, sums, sums,
         ((2, length, PAIR), BF), ((2, 2, length, length), BF)],
        48, 2 * 10**10, smem=(0,) if staged else (), copies=64,
    )


def input_gradient(vec, dz, matrices, heads):
    arrays = (dz, matrices, *heads)
    return call(
        input_grad_kernel, (vec, *arrays), like(dz), [*like(*arrays), *like(dz)], 40, 2 * 10**9, near=(0,), copies=24
    )[0]


def adam_step(settings_ref, now, grad, one, two, decay):
    beta_one, beta_two = settings_ref[1], settings_ref[2]
    first = beta_one * one + (1.0 - beta_one) * grad
    second = beta_two * two + (1.0 - beta_two) * grad * grad
    change = (first / settings_ref[4]) / (jnp.sqrt(second / settings_ref[5]) + 1e-08)
    if decay:
        change = change + settings_ref[3] * now
    return now - settings_ref[0] * change, first, second


def store_step(refs, where, results):
    for ref, value in zip(refs, results):
        ref[where] = value


def hidden_adam_kernel(place_ref, settings_ref, *refs):
    core = place_of(place_ref)[0]
    hbms, new_hbms, refs = refs[:8], refs[8:14], refs[14:]
    mine_ref, other_ref, *params = refs[:8]
    news, mover = refs[8:14], Mover(refs[-1])
    loads = [mover.load(a, b) for a, b in zip(hbms, refs[:8])]
    expand, shrink = params[0:3], params[3:6]
    half = mine_ref.shape[1]
    shard = expand[0].shape[0]
    blocks = expand[0].shape[1] // (2 * half)
    for load in loads[:5]:
        load.wait()
    sides = [(jnp.bitwise_xor(core, step) * half, ref) for step, ref in ((0, mine_ref), (1, other_ref))]
    for side, ref in sides:
        for block in range(blocks):
            where = (slice(None), pl.ds(pl.multiple_of(block * 2 * half + side, half), half))
            grad = ref[block * shard : (block + 1) * shard, :]
            now, one, two = (r[where] for r in expand)
            store_step(news[:3], where, adam_step(settings_ref, now, grad, one, two, True))
    for load in loads[5:]:
        load.wait()
    for near, far in zip(news[:3], new_hbms[:3]):
        mover.store(near, far)
    for side, ref in sides:
        where = (slice(None), pl.ds(pl.multiple_of(side, half), half))
        now, one, two = (r[where] for r in shrink)
        store_step(news[3:], where, adam_step(settings_ref, now, ref[blocks * shard :, :], one, two, True))
    for near, far in zip(news[3:], new_hbms[3:]):
        mover.store(near, far)
    mover.finish()


def attention_adam_kernel(place_ref, settings_ref, mine_ref, other_ref, *refs):
    core = place_of(place_ref)[0]
    matrices, bias, vectors = refs[0:3], refs[3:6], refs[6:9]
    new_matrices, new_bias, new_vectors = refs[9:12], refs[12:15], refs[15:18]
    half = mine_ref.shape[1]
    shard = matrices[0].shape[1]
    for step, ref in ((0, mine_ref), (1, other_ref)):
        cols = pl.ds(pl.multiple_of(jnp.bitwise_xor(core, step) * half, half), half)
        for index in range(8):
            where = (index, slice(None), cols)
            now, one, two = (r[where] for r in matrices)
            grad = ref[index * shard : (index + 1) * shard, :]
            store_step(new_matrices, where, adam_step(settings_ref, now, grad, one, two, True))
    small = mine_ref[8 * shard :, :] + other_ref[8 * shard :, :]
    for group, new, grad in (
        (bias, new_bias, small[10:11, : bias[0].shape[1]]),
        (vectors, new_vectors, small[:10, : vectors[0].shape[1]]),
    ):
        now, one, two = (r[...] for r in group)
        store_step(new, ..., adam_step(settings_ref, now, grad, one, two, False))


def hidden_adam(scalars, grads, params):
    return call(
        hidden_adam_kernel, (*scalars, *grads, *params), like(*params), [*like(*grads), *like(*params), *like(*params)],
        40, 10**9, smem=(0, 1), copies=16,
    )


def adam_call(kernel, scalars, grads, params):
    return call(
        kernel, (*scalars, *grads, *params), [(p.shape, F32) for p in params], [], 32, 10**7, smem=(0, 1),
        near=range(2, 2 + len(grads) + len(params)), near_outs=range(len(params)),
    )


CORE_SWAP = [(0, 1), (1, 0), (2, 3), (3, 2)]
CHIP_SWAP = [(0, 2), (2, 0), (1, 3), (3, 1)]
ROW_SWAP = [(i, i ^ 1) for i in range(8)]


LINES = [[0, 2, 4, 6], [1, 3, 5, 7]]


def line_shift(step):
    return [(2 * z + y, 2 * ((z + step) % 4) + y) for z in range(4) for y in (0, 1)]


def small_mesh(mesh):
    return mesh.shape["rep"] == 4 and mesh.shape["fsdp"] == 8


class StagedGather:
    def rows(self, mine, done):
        self.mine = mine
        self.other = lax.ppermute(after(mine, done), "fsdp", ROW_SWAP)

    def line(self, done):
        self.pair = after(jnp.stack([self.mine, self.other]), done)
        self.received = [lax.ppermute(self.pair, "fsdp", line_shift(step)) for step in (1, 2, 3)]

    def chips(self, done):
        self.arrived = after(tuple(self.received), done)
        self.part = jnp.stack([self.pair, *self.arrived])
        self.far = lax.ppermute(self.part, "rep", CHIP_SWAP)

    def cores(self, done):
        far = after(self.far, done)
        part = after(self.part, done)
        return part, far, lax.ppermute(part, "rep", CORE_SWAP), lax.ppermute(far, "rep", CORE_SWAP)


def gather_staged(pack):
    quarter = pack.shape[0] // 4
    mine = lax.dynamic_slice_in_dim(pack, lax.axis_index("rep") * quarter, quarter, 0)
    pair = jnp.stack([mine, lax.ppermute(mine, "fsdp", ROW_SWAP)])
    part = jnp.stack([pair] + [lax.ppermute(pair, "fsdp", line_shift(step)) for step in (1, 2, 3)])
    both = jnp.stack([part, lax.ppermute(part, "rep", CHIP_SWAP)])
    return pair, part, both


def after(value, *done):
    return lax.optimization_barrier((value, *done))[0]


def half_columns(pack):
    half = pack.shape[1] // 2
    return lax.dynamic_slice_in_dim(pack, lax.axis_index("rep") % 2 * half, half, 1)


def both_halves(mine, *done):
    mine = after(mine, *done)
    return mine, lax.ppermute(mine, "rep", CORE_SWAP)


def reduce_cores(keep, send):
    received = lax.ppermute(send, "rep", CORE_SWAP)
    return keep[0] + received[0], keep[1] + received[1]


def send_rows(send):
    return lax.ppermute(send, "fsdp", ROW_SWAP)


def reduce_rows(keep, received, done):
    return keep + after(received, done)


def reduce_chips(part, *done):
    return part.astype(F32) + after(lax.ppermute(part, "rep", CHIP_SWAP), *done).astype(F32)


def reduce_last(part, *done):
    total = reduce_chips(part, *done)
    return total, lax.ppermute(total, "rep", CORE_SWAP)


def reduce_line(joined):
    part = lax.psum_scatter(joined, "fsdp", scatter_dimension=0, axis_index_groups=LINES)
    return part.reshape(joined.shape[1:])


def reduce_shifts(joined, done):
    line = lax.axis_index("fsdp") // 2
    total = lax.dynamic_index_in_dim(joined, line, 0, False).astype(F32)
    for step in (1, 2, 3):
        away = lax.dynamic_index_in_dim(joined, (line + step) % 4, 0, False)
        total = total + after(lax.ppermute(away, "fsdp", line_shift(step)), done).astype(F32)
    return total.astype(BF)


def reduce_plain(grads):
    return lax.psum(lax.psum_scatter(grads, "fsdp", scatter_dimension=0), "rep").astype(F32)


def adam_update(weight_now, gradient, moment_one, moment_two, settings, step_float, factor):
    learn_rate, beta_one, beta_two, decay_rate = settings[0], settings[1], settings[2], settings[3]
    first_new = beta_one * moment_one + (1.0 - beta_one) * gradient
    second_new = beta_two * moment_two + (1.0 - beta_two) * gradient * gradient
    first_hat = first_new / (1.0 - beta_one**step_float)
    second_hat = second_new / (1.0 - beta_two**step_float)
    change = first_hat / (jnp.sqrt(second_hat) + 1e-08) + factor * decay_rate * weight_now
    return (weight_now - learn_rate * change, first_new, second_new)


def per_device(
    small, inputs, memory, memory_length, target_pos, cotangent,
    attention_weights, expand_weights, shrink_weights, expand_bias, layer_vectors,
    first_attention, first_expand, first_shrink, first_bias, first_vectors,
    second_attention, second_expand, second_shrink, second_bias, second_vectors,
    hyper_rates, step_count,
):
    length, width = inputs.shape[1:]
    shard = attention_weights.shape[1]
    count = width // shard
    inner_shard = shrink_weights.shape[0]
    blocks = inner_shard // shard
    low_attention = attention_weights.astype(BF).reshape(8 * shard, width)
    pack_one = low_attention[: 3 * shard]
    expand_low = expand_weights.astype(BF).reshape(shard, blocks, width)
    shrink_low = shrink_weights.astype(BF)
    x, source, cot = inputs[0], memory[0], cotangent[0]
    step_float = step_count.astype(F32)

    if small:
        place = jnp.stack([lax.axis_index("rep"), lax.axis_index("fsdp")]).astype(jnp.int32)
        small_rows = jnp.concatenate(
            [
                jnp.pad(layer_vectors, ((0, 0), (0, inner_shard - shard))),
                expand_bias[None],
                jnp.zeros((5, inner_shard), F32),
            ]
        )
        small_rows = jnp.pad(small_rows, ((0, 0), (0, width - inner_shard))).astype(BF)
        pack_two = jnp.concatenate([low_attention[3 * shard :], small_rows])
        half_two = half_columns(pack_two)
        two = lax.all_gather(half_two, "fsdp", axis=0)
        pair_one, part_one, one = gather_staged(pack_one)
        half = shard // 2
        halves = expand_low.reshape(2, half, blocks, width).transpose(0, 2, 1, 3)
        quarters = jnp.stack([halves, shrink_low.reshape(2, blocks, half, width)], axis=1)
        core, chip = place[0] % 2, place[0] // 2
        quarter = lax.dynamic_slice(
            quarters, (chip, 0, 0, 0, core * (width // 2)), (1, *quarters.shape[1:4], width // 2)
        )
        three = StagedGather()
        three.rows(quarter[0], pair_one)
        one = both_halves(one, three.other)
        three.line(part_one)
        given = None
        cross_shards = (shard,) * 5
    else:
        place, cross_shards = None, None
        flat = jnp.concatenate([layer_vectors.reshape(-1), expand_bias]).astype(BF)
        flat = lax.all_gather(flat, "fsdp", axis=0).astype(F32)
        vector_size = layer_vectors.size
        vec = flat[:, :vector_size].reshape(count, -1, shard).transpose(1, 0, 2).reshape(-1, width)
        given = jnp.pad(vec, ((0, 16 - vec.shape[0]), (0, 0))), flat[:, vector_size:].reshape(1, -1)

        def gather_all(pack, shards):
            full = lax.all_gather(pack, "fsdp", axis=0)
            pieces, first = [], 0
            for rows in shards:
                pieces.append(full[:, first : first + rows].reshape(-1, width))
                first += rows
            return pieces

        def owners(grads, shards):
            pieces, first = [], 0
            for rows in shards:
                pieces.append(grads[first : first + rows * count].reshape(count, rows, width))
                first += rows * count
            return jnp.concatenate(pieces, axis=1)

        one = jnp.concatenate(gather_all(pack_one, (shard,) * 3))
        two = [m[None] for m in gather_all(low_attention[3 * shard :], (shard,) * 5)]
        pack = jnp.concatenate([expand_low.transpose(1, 0, 2).reshape(-1, width), shrink_low])
        *expand_all, shrink_all = gather_all(pack, (*(shard,) * blocks, inner_shard))
        three = jnp.stack(expand_all)[:, None], shrink_all[None]

    *saved_one, matrices = forward_self(place, x, target_pos, one, small)
    if small:
        three.chips(saved_one[4])
        two = both_halves(two, *three.arrived)
    norm_one, inv_one, *saved_two, norm_two, inv_two, vec, bias = forward_cross(
        place, x, saved_one[4], source, memory_length, two, given, cross_shards
    )
    three = three.cores(norm_two) if small else three
    sums_three, bias_sum, outputs, dz_two, *grad_three = hidden_step(
        place, three, norm_two, inv_two, cot, vec, bias
    )
    if small:
        keep_three, send_three = reduce_cores(*grad_three)
        dz_two = after(dz_two, keep_three, send_three)
        received_three = send_rows(send_three)
    sums_two, dz_one, memory_grad, *grad_two = backward_cross(
        place, two, dz_two, x, norm_one, inv_one, source, vec, saved_two, saved_one[4],
        (sums_three, bias_sum), cross_shards,
    )
    if small:
        joined_three = reduce_rows(keep_three, received_three, dz_one)
        keep_two, send_two = reduce_cores(grad_two[0], after(grad_two[1], received_three))
        dz_one = after(dz_one, joined_three, keep_two, send_two)
        received_two = send_rows(send_two)
    *heads, grad_keep, grad_send = (
        *backward_self(place, two if small else two[:1], dz_one, x, saved_one, cross_shards),
        *((None,) if not small else ()),
    )
    if small:
        keep_one, send_one = reduce_cores(grad_keep, after(grad_send, received_two))
        joined_two = reduce_rows(after(keep_two, send_one), received_two, heads[0])
        heads = after(tuple(heads), keep_one, send_one, joined_two)
        received_one = send_rows(send_one)
    input_grad = input_gradient(vec, dz_one, matrices, heads)

    attention = (attention_weights, first_attention, second_attention)
    expand = (expand_weights, first_expand, second_expand)
    shrink = (shrink_weights, first_shrink, second_shrink)
    bias = (expand_bias, first_bias, second_bias)
    vectors = (layer_vectors, first_vectors, second_vectors)
    if small:
        powers = 1.0 - hyper_rates[1:3] ** step_float
        scalars = place, jnp.concatenate([hyper_rates, powers])
        part_three = reduce_line(joined_three)
        part_two = reduce_line(joined_two)
        total_three = reduce_last(after(part_three, send_one), input_grad)
        joined_one = reduce_rows(keep_one, received_one, input_grad)
        hidden_new = hidden_adam(scalars, total_three, (*expand, *shrink))
        part_one = reduce_shifts(joined_one, hidden_new[0])
        parts = part_one, after(part_two, hidden_new[0])
        received = after(tuple(lax.ppermute(part, "rep", CHIP_SWAP) for part in parts))
        total_rest = jnp.concatenate([a.astype(F32) + b.astype(F32) for a, b in zip(parts, received)])
        total_rest = total_rest, lax.ppermute(total_rest, "rep", CORE_SWAP)
        rows = tuple(b[None] for b in bias)
        other_new = adam_call(
            attention_adam_kernel, scalars, total_rest, (*attention, *rows, *vectors)
        )
        new_bias = tuple(b[0] for b in other_new[3:6])
        updated = (*other_new[:3], *hidden_new, *new_bias, *other_new[6:])
    else:
        sums = (sums_two + sums_three)[: layer_vectors.shape[0]]
        flat = jnp.concatenate(
            [
                sums.reshape(-1, count, shard).transpose(1, 0, 2).reshape(count, -1),
                bias_sum.reshape(count, inner_shard),
            ],
            axis=1,
        )
        total_three = reduce_plain(owners(grad_three[0], (*(shard,) * blocks, inner_shard)))
        total_two = reduce_plain(owners(grad_two[0], (shard,) * 5))
        total_one = reduce_plain(owners(grad_keep, (shard,) * 3))
        flat = lax.psum(lax.psum_scatter(flat, "fsdp", scatter_dimension=0), "rep")
        grad_attention = jnp.concatenate([total_one, total_two]).reshape(attention_weights.shape)
        grad_expand = total_three[: blocks * shard].reshape(blocks, shard, width).transpose(1, 0, 2)
        updated = []
        for (now, one_now, two_now), grad, factor in (
            (attention, grad_attention, 1.0),
            (expand, grad_expand.reshape(shard, -1), 1.0),
            (shrink, total_three[blocks * shard :], 1.0),
            (bias, flat[layer_vectors.size :], 0.0),
            (vectors, flat[: layer_vectors.size].reshape(-1, shard), 0.0),
        ):
            updated.extend(adam_update(now, grad, one_now, two_now, hyper_rates, step_float, factor))
    return (outputs[None], input_grad[None], memory_grad[None], *updated)


def solution(mesh):
    rows = ("rep", "fsdp")
    params = (P(None, "fsdp", None), P("fsdp", None), P("fsdp", None), P("fsdp"), P(None, "fsdp"))
    return jax.shard_map(
        functools.partial(per_device, small_mesh(mesh)),
        mesh=mesh,
        in_specs=(
            P(rows, None, None), P(rows, None, None), P(rows), P(rows, None), P(rows, None, None),
            *params, *params, *params, P(), P(),
        ),
        out_specs=(
            P(rows, None, None), P(rows, None, None), P(rows, None, None),
            *(spec for spec in params for _ in range(3)),
        ),
        check_vma=False,
    )
```
